128 devices in a mesh: dp: 64 (over y, x, z), tensor: 2 (over core).
Axes of the slice: x: 4, y: 4, z: 4, core: 2. Of those that a mesh axis runs over, the one named last changes fastest.
Arguments:
- tokens: bfloat16 [12288, 2048], P('dp'), may hold values from -6 to 6
- expert_ids: int32 [12288, 8], P('dp'), may hold values from 0 to 63, all different within a row
- capacity: int32 [64], replicated, may hold values from 12 to 24, as said below
- gain_attn: bfloat16 [2048], replicated, may hold values from 0.5 to 1.5
- w_qkv: bfloat16 [2048, 3, 2048], P(None, None, 'tensor'), may hold values from -0.125 to 0.125
- qk_gain: bfloat16 [2, 128], replicated, may hold values from 0.5 to 1.5
- w_out: bfloat16 [2048, 2048], P(None, 'tensor'), may hold values from -1 to 1
- gain_ffn: bfloat16 [2048], replicated, may hold values from 0.5 to 1.5
- w_router: bfloat16 [2048, 64], replicated, may hold values from -0.0625 to 0.0625
- w_gate_up: bfloat16 [64, 2048, 2, 1024], P('dp', None, None, 'tensor'), may hold values from -0.125 to 0.125
- w_down: bfloat16 [64, 1024, 2048], P('dp', 'tensor'), may hold values from -0.75 to 0.75
- cotangent: bfloat16 [12288, 2048], P('dp'), may hold values from -16 to 16
Outputs:
- output: bfloat16 [12288, 2048], P('dp')
- d_input: float32 [12288, 2048], P('dp')
- d_gain_attn: float32 [2048], P('dp')
- d_w_qkv: float32 [2048, 3, 2048], P('dp', None, 'tensor')
- d_qk_gain: float32 [2, 128], replicated
- d_w_out: float32 [2048, 2048], P('dp', 'tensor')
- d_gain_ffn: float32 [2048], P('dp')
- d_w_router: float32 [2048, 64], P('dp')
- d_w_gate_up: float32 [64, 2048, 2, 1024], P('dp', None, None, 'tensor')
- d_w_down: float32 [64, 1024, 2048], P('dp', 'tensor')
The draws below stay inside these ranges and needn't reach their ends.
Inputs may be any that keep to these rules, and one draw needn't show every extreme that they name: `expert_ids`: each row names 8 different experts, and every expert is named by some row. At least a quarter of the experts have capacity exactly 24.
All inputs are finite; a program needn't handle non-finite values.
Results may differ from the reference program's by a relative error of at most 0.023.
Values may be sent and summed in bfloat16 or wider, within the bound.
No kernel may reach another device: no remote copies, remote signals or barrier semaphores. Data moves between devices by JAX's collectives and lax.ppermute only.
A program may use at most 256 MiB of HBM per device.

```python
import math
import jax
import jax.numpy as jnp
from jax import lax

D = 2048
H = 16
DH = 128
FFE = 1024
TOP = 8
TOK_DEV = 192
EXPERTS = 64
CAP = 24
TOKENS = 12288
N_DP = 64


def draw_capacity(key, part):
    key_values, key_shuffle = jax.random.split(jax.random.fold_in(key, 11))
    lowest = max(CAP // 2, 2)
    values = jax.random.randint(key_values, (EXPERTS,), lowest, CAP + 1, dtype=jnp.int32)
    shuffled = jax.random.permutation(key_shuffle, EXPERTS)
    marked = jnp.zeros((EXPERTS,), jnp.int32).at[shuffled[:max(EXPERTS // 4, 1)]].set(1)
    return jnp.where(marked == 1, CAP, values).astype(jnp.int32)


def strengthened(values, rng, source, target, parts, factor):
    owner, partner = [(jnp.arange(values.shape[dim]) // (values.shape[dim] // parts)).reshape([-1 if axis == dim else 1 for axis in range(values.ndim)]) for dim in (source, target)]
    chosen = jax.random.permutation(rng, parts)[partner]
    strong = (owner == chosen) | (owner == (partner + parts // 2) % parts)
    return jnp.where(strong, factor * values, values)


def steps_of(stream_key, extent, pieces, smallest, top_value):
    factor_of, own = 1.0, jax.random.fold_in(stream_key, 6)
    for dim, blocks in pieces:
        heights = jnp.exp(jax.random.uniform(jax.random.fold_in(own, dim), (blocks,), jnp.float32, smallest / len(pieces), top_value / len(pieces)))
        factor_of = factor_of * jnp.repeat(heights, extent[dim] // blocks).reshape([-1 if axis == dim else 1 for axis in range(len(extent))])
    return factor_of


def picks_of(own_key, rows, count, top, lift):
    ranking = jax.random.permutation(jax.random.fold_in(own_key, 1), count)
    favour = ranking
    for power in range(3):
        favour = favour * favour // count
    favour = favour * lift // count
    tickets = jax.random.randint(jax.random.fold_in(own_key, 2), (rows, count), 0, 4096) + favour
    holders = jax.random.permutation(jax.random.fold_in(own_key, 3), rows)[jnp.arange(count) % rows]
    tickets = jnp.where(jnp.arange(rows)[:, None] == holders[None, :], 1 << 14, tickets)
    merit = tickets * count + jnp.arange(count)
    return lax.top_k(merit.astype(jnp.int32), top)[1].astype(jnp.int32)


def centred(stream_key, dims, scale, limit, cuts=(), kind=jnp.bfloat16):
    values = scale * jax.random.normal(stream_key, dims, jnp.float32)
    if cuts:
        values = values * steps_of(stream_key, dims, cuts, -0.22, 0.18)
    return jnp.clip(values, -limit, limit).astype(kind)


def heavy_noise(own_key, extent, width, bound, cuts, heavy, held_as=jnp.bfloat16):
    array = width * jax.random.normal(own_key, extent, jnp.float32)
    if cuts:
        array = array * steps_of(own_key, extent, cuts, -0.22, 0.18)
    return jnp.clip(strengthened(array, jax.random.fold_in(own_key, 3), *heavy), -bound, bound).astype(held_as)


def setup_inputs(seed: int = 0) -> dict:
    arg_keys = jax.random.split(jax.random.key(seed), 13)
    return {
        "tokens": centred(arg_keys[0], (TOKENS, D), 1.0, 6.0, ((0, 64),)),
        "expert_ids": picks_of(arg_keys[1], TOKENS, EXPERTS, TOP, 1024),
        "capacity": draw_capacity(jax.random.fold_in(arg_keys[12], 71), 0),
        "gain_attn": jnp.clip(1.0 + 0.1 * jax.random.normal(arg_keys[3], (D,), jnp.float32), 0.5, 1.5).astype(jnp.bfloat16),
        "w_qkv": centred(arg_keys[4], (D, 3, H * DH), D ** -0.5, 0.125, ((2, 2),)),
        "qk_gain": jnp.clip(1.0 + 0.1 * jax.random.normal(arg_keys[5], (2, DH), jnp.float32), 0.5, 1.5).astype(jnp.bfloat16),
        "w_out": centred(arg_keys[6], (D, H * DH), (H * DH * 4 // TOK_DEV) ** -0.5, 1.0, ((1, 2),)),
        "gain_ffn": jnp.clip(1.0 + 0.1 * jax.random.normal(arg_keys[7], (D,), jnp.float32), 0.5, 1.5).astype(jnp.bfloat16),
        "w_router": centred(arg_keys[8], (D, EXPERTS), (4 * D) ** -0.5, 0.0625),
        "w_gate_up": centred(arg_keys[9], (EXPERTS, D, 2, FFE), D ** -0.5, 0.125, ((0, 64), (3, 2))),
        "w_down": centred(arg_keys[10], (EXPERTS, FFE, D), (FFE // 16) ** -0.5, 0.75, ((0, 64), (1, 2))),
        "cotangent": heavy_noise(arg_keys[11], (TOKENS, D), 1.0, 16.0, ((0, 64),), (0, 1, 64, 4.0)),
    }


@jax.custom_vjp
def low(v):
    return lax.optimization_barrier(v.astype(jnp.bfloat16)).astype(jnp.float32)

@jax.custom_vjp
def low_back(v):
    return v

def low_keep(v):
    return (low(v), None)

def low_pass(kept, grad):
    return (grad,)

def back_keep(v):
    return (v, None)

def back_low(kept, grad):
    return (low(grad),)
low.defvjp(low_keep, low_pass)
low_back.defvjp(back_keep, back_low)

def rms_scale(values):
    return lax.rsqrt(lax.optimization_barrier(jnp.mean(values * values, axis=-1, keepdims=True)) + 1e-06)

def rotary(length, half_dim):
    position = jnp.arange(length).astype(jnp.float32)
    inverse = 50000.0 ** (-jnp.arange(half_dim).astype(jnp.float32) / half_dim)
    angles = position[:, None] * inverse[None, :]
    return (jnp.cos(angles)[:, None, :], jnp.sin(angles)[:, None, :])

def turn(values, cosine, sine):
    half_dim = values.shape[-1] // 2
    front = values[..., :half_dim]
    behind = values[..., half_dim:]
    return jnp.concatenate([front * cosine - behind * sine, behind * cosine + front * sine], axis=-1)

def attend(normed, weight_qkv, gains_qk, weight_out):
    projected = low_back(jnp.einsum('sd,dcn->scn', normed, weight_qkv, precision=lax.Precision.HIGHEST))
    projected = projected.reshape(TOK_DEV, 3, H, DH)
    query_raw = projected[:, 0]
    key_raw = projected[:, 1]
    value_in = low(projected[:, 2])
    cosine, sine = rotary(TOK_DEV, DH // 2)
    query_in = low(turn(query_raw * rms_scale(query_raw) * gains_qk[0], cosine, sine))
    key_in = low(turn(key_raw * rms_scale(key_raw) * gains_qk[1], cosine, sine))
    scores = low_back(jnp.einsum('qhd,khd->hqk', query_in, key_in, precision=lax.Precision.HIGHEST) * (1.0 / math.sqrt(DH)))
    weights = low(jax.nn.softmax(scores, axis=-1))
    attended = low_back(low(jnp.einsum('hqk,khd->qhd', weights, value_in, precision=lax.Precision.HIGHEST)))
    attended = attended.reshape(TOK_DEV, H * DH)
    return low_back(jnp.einsum('sn,dn->sd', attended, weight_out, precision=lax.Precision.HIGHEST))

def expert_step(carry, inputs, padded):
    token_index, slot_gate, weight_pair, weight_back = inputs
    rows = low_back(padded[token_index])
    gate_up = low_back(jnp.einsum('rd,dcf->rcf', rows, weight_pair, precision=lax.Precision.HIGHEST))
    hidden = low(jax.nn.silu(gate_up[:, 0]) * gate_up[:, 1])
    result = low_back(low(jnp.dot(hidden, weight_back, precision=lax.Precision.HIGHEST)))
    return (carry.at[token_index].add(slot_gate[:, None] * result, mode='drop'), None)

def slot_tables(expert_ids, capacity):
    flat_ids = expert_ids.reshape(N_DP, TOK_DEV * TOP)
    onehot = (flat_ids[:, :, None] == jnp.arange(EXPERTS, dtype=jnp.int32)[None, None, :]).astype(jnp.int32)
    earlier = jnp.cumsum(onehot, axis=1) - onehot
    ranks = lax.optimization_barrier(jnp.sum(earlier * onehot, axis=-1))
    keep = ranks < capacity[flat_ids]
    block_ids = jnp.arange(N_DP, dtype=jnp.int32)[:, None]
    slot_index = jnp.where(keep, flat_ids * (N_DP * CAP) + block_ids * CAP + ranks, EXPERTS * N_DP * CAP).astype(jnp.int32)
    pair_ids = jnp.arange(TOKENS * TOP, dtype=jnp.int32)
    pair_of_slot = jnp.full((EXPERTS * N_DP * CAP,), TOKENS * TOP, jnp.int32).at[slot_index.reshape(-1)].set(pair_ids, mode='drop')
    return pair_of_slot.reshape(EXPERTS, N_DP * CAP)

def reference(tokens, expert_ids, capacity, gain_attn, w_qkv, qk_gain, w_out, gain_ffn, w_router, w_gate_up, w_down, cotangent):
    pair_of_slot = slot_tables(expert_ids, capacity)
    token_of_slot = (pair_of_slot // TOP).astype(jnp.int32)
    attend_block = jax.checkpoint(attend)
    step_block = jax.checkpoint(expert_step)

    def forward(inputs, gain_one, weight_qkv, gains_qk, weight_out, gain_two, weight_router, weight_pair, weight_back):
        normed_one = low(inputs * rms_scale(inputs) * gain_one)
        attn_out = lax.map(lambda block: attend_block(block, weight_qkv, gains_qk, weight_out), normed_one.reshape(N_DP, TOK_DEV, D))
        middle = inputs + attn_out.reshape(TOKENS, D)
        normed_two = low(middle * rms_scale(middle) * gain_two)
        logits = low_back(jnp.dot(normed_two, weight_router, precision=lax.Precision.HIGHEST))
        probs = jax.nn.softmax(logits, axis=-1)
        picked = jnp.take_along_axis(probs, expert_ids, axis=1)
        gates = picked / lax.optimization_barrier(jnp.sum(picked, axis=-1, keepdims=True))
        gate_pad = jnp.concatenate([gates.reshape(-1), jnp.zeros((1,), jnp.float32)])
        slot_gates = gate_pad[pair_of_slot]
        padded = jnp.concatenate([normed_two, jnp.zeros((1, D), jnp.float32)], axis=0)
        mixture, unused = lax.scan(lambda carry, inputs_e: step_block(carry, inputs_e, padded), jnp.zeros((TOKENS, D), jnp.float32), (token_of_slot, slot_gates, weight_pair, weight_back))
        return middle + mixture
    primals = tuple((value.astype(jnp.float32) for value in (tokens, gain_attn, w_qkv, qk_gain, w_out, gain_ffn, w_router, w_gate_up, w_down)))
    result, pullback = jax.vjp(forward, *primals)
    grads = pullback(cotangent.astype(jnp.float32))
    return (result.astype(jnp.bfloat16), grads[0], grads[1], grads[2], grads[3], grads[4], grads[5], grads[6], grads[7], grads[8])
```

```python
import math

import jax
import jax.numpy as jnp
import numpy as np
from jax import lax
from jax.sharding import Mesh
from jax.sharding import PartitionSpec as P

AXES = ("y", "x", "z")
SIDE = 4
BF = jnp.bfloat16
F32 = jnp.float32


def dot(a, b, dims):
    return lax.dot_general(a, b, (dims, ((), ())), preferred_element_type=F32)


def rms_scale(values):
    return lax.rsqrt(jnp.mean(values * values, axis=-1, keepdims=True) + 1e-06)


def rotary(length, half_dim):
    position = np.arange(length, dtype=np.float32)
    inverse = np.float32(50000.0) ** (-np.arange(half_dim, dtype=np.float32) / np.float32(half_dim))
    angles = position[:, None] * inverse[None, :].astype(np.float32)
    return (
        jnp.asarray(np.cos(angles)[:, None, :], F32),
        jnp.asarray(np.sin(angles)[:, None, :], F32),
    )


def turn(values, cosine, sine):
    half_dim = values.shape[-1] // 2
    front = values[..., :half_dim]
    behind = values[..., half_dim:]
    return jnp.concatenate(
        [front * cosine - behind * sine, behind * cosine + front * sine], axis=-1
    )


def unturn(grads, cosine, sine):
    half_dim = grads.shape[-1] // 2
    front = grads[..., :half_dim]
    behind = grads[..., half_dim:]
    return jnp.concatenate(
        [front * cosine + behind * sine, behind * cosine - front * sine], axis=-1
    )


def norm_back(grad_normed, raw, scale, gain):
    unit = raw * scale
    weighted = grad_normed * gain
    d_raw = scale * (weighted - unit * jnp.mean(weighted * unit, axis=-1, keepdims=True))
    return (d_raw, grad_normed * unit)


def swap(value):
    return lax.ppermute(value, "tensor", [(0, 1), (1, 0)])


def shift(value, axis, step):
    return lax.ppermute(value, axis, [(i, (i + step) % SIDE) for i in range(SIDE)])


def side_by_side(own, peer, core):
    return jnp.where(
        core == 0,
        jnp.concatenate([own, peer], axis=-1),
        jnp.concatenate([peer, own], axis=-1),
    )


def block_at(value, index, dim):
    return lax.dynamic_index_in_dim(value, index, dim, keepdims=False)


def scatter_sum(value, axis, dim):
    here = lax.axis_index(axis)
    total = block_at(value, here, dim).astype(F32)
    for step in (1, 3, 2):
        sent = block_at(value, (here + step) % SIDE, dim)
        total = total + shift(sent, axis, step).astype(F32)
    return total


def all_sum(value, axis):
    here = lax.axis_index(axis)
    parts = [value] + [shift(value, axis, step) for step in (1, 2, 3)]
    stacked = jnp.stack(parts + parts)
    ordered = [block_at(stacked, (here - source) % SIDE, 0) for source in range(SIDE)]
    return (ordered[0] + ordered[1]) + (ordered[2] + ordered[3])


def exchange(value):
    return lax.all_to_all(value, AXES, split_axis=0, concat_axis=0, tiled=True)


def on_device(
    tokens,
    expert_ids,
    capacity,
    gain_attn,
    w_qkv,
    qk_gain,
    w_out,
    gain_ffn,
    w_router,
    w_gate_up,
    w_down,
    cotangent,
):
    length, width = tokens.shape
    expert_count = capacity.shape[0]
    slot_count = length * expert_ids.shape[1] // expert_count
    slots = expert_count * slot_count
    head_dim = qk_gain.shape[1]
    heads = w_qkv.shape[2] // head_dim
    inner = heads * head_dim
    hidden_here = w_down.shape[1]
    half = width // 2
    inverse_root = 1.0 / math.sqrt(head_dim)
    core = lax.axis_index("tensor")
    place = [lax.axis_index(a) for a in AXES]
    dp_index = (place[0] * SIDE + place[1]) * SIDE + place[2]

    def own_half(value):
        return lax.dynamic_slice_in_dim(value, core * half, half, axis=-1)

    experts = jnp.arange(expert_count, dtype=jnp.int32)
    member = jnp.sum((expert_ids[:, :, None] == experts).astype(F32), axis=1)
    earlier = jnp.asarray(np.tril(np.ones((length, length), np.float32), -1), BF)
    ranks = dot(earlier, member.astype(BF), ((1,), (0,)))
    kept = (member > 0.5) & (ranks < capacity.astype(F32)[None, :])
    code = jnp.where(kept, ranks, -1.0).T
    slot_hit = code[:, None, :] == jnp.arange(slot_count, dtype=jnp.int32).astype(F32)[None, :, None]
    select = slot_hit.astype(BF).reshape(slots, length)

    def dispatch(value):
        rows = dot(select, value, ((1,), (0,))).astype(BF)
        return exchange(rows.reshape(expert_count, slot_count, half)).reshape(slots, half)

    grad_own = dispatch(own_half(cotangent))

    residual_in = tokens.astype(F32)
    scale_one = rms_scale(residual_in)
    gain_one = gain_attn.astype(F32)
    normed_one = (residual_in * scale_one * gain_one).astype(BF)
    projected = jnp.einsum("sd,dcn->csn", normed_one, w_qkv, preferred_element_type=F32)
    projected = projected.reshape(3, length, heads, head_dim)
    query_raw = projected[0]
    key_raw = projected[1]
    value_in = projected[2].astype(BF)
    cosine, sine = rotary(length, head_dim // 2)
    qk_gains = qk_gain.astype(F32)
    query_scale = rms_scale(query_raw)
    key_scale = rms_scale(key_raw)
    query_in = turn(query_raw * query_scale * qk_gains[0], cosine, sine).astype(BF)
    key_in = turn(key_raw * key_scale * qk_gains[1], cosine, sine).astype(BF)
    scores = (
        jnp.einsum("qhd,khd->hqk", query_in, key_in, preferred_element_type=F32) * inverse_root
    )
    highest = jnp.max(scores, axis=-1, keepdims=True)
    raised = jnp.exp(scores - highest)
    probs_att = raised / jnp.sum(raised, axis=-1, keepdims=True)
    weights = probs_att.astype(BF)
    attended = jnp.einsum("hqk,khd->qhd", weights, value_in, preferred_element_type=F32)
    attended = attended.astype(BF).reshape(length, inner)
    partial_out = dot(attended, w_out, ((1,), (1,))).astype(BF)
    attn_out = partial_out.astype(F32) + swap(partial_out).astype(F32)
    middle = residual_in + attn_out
    scale_two = rms_scale(middle)
    gain_two = gain_ffn.astype(F32)
    normed_two = (middle * scale_two * gain_two).astype(BF)

    rows_own = dispatch(own_half(normed_two))

    logits = dot(normed_two, w_router, ((1,), (0,)))
    router_probs = jax.nn.softmax(logits, axis=-1)
    picked = router_probs * member
    picked_total = jnp.sum(picked, axis=-1, keepdims=True)
    gates = picked / picked_total
    gates_col = gates.T[:, None, :]
    slot_gates = jnp.sum(jnp.where(slot_hit, gates_col, 0.0), axis=-1)
    slot_gates = jnp.pad(slot_gates, ((0, 0), (0, 128 - slot_count)))
    slot_gates = jnp.broadcast_to(slot_gates[:, None, :], (expert_count, 8, 128))
    slot_gates = exchange(slot_gates)[:, 0, :slot_count].reshape(slots, 1)
    combine = jnp.where(slot_hit, gates_col, 0.0).astype(BF).reshape(slots, length)

    grad_rows = side_by_side(grad_own, swap(grad_own), core)
    down = w_down[0]
    pair = w_gate_up[0]
    d_hidden = dot(grad_rows, down, ((1,), (1,)))
    expert_rows = side_by_side(rows_own, swap(rows_own), core)
    gate_up = jnp.einsum("rd,dcf->rcf", expert_rows, pair, preferred_element_type=F32)
    gate_val = gate_up[:, 0]
    up_val = gate_up[:, 1]
    sig_gate = jax.nn.sigmoid(gate_val)
    silu_gate = gate_val * sig_gate
    acted = silu_gate * up_val
    hidden = acted.astype(BF)
    slot_grads = jnp.sum(d_hidden * hidden.astype(F32), axis=-1).reshape(expert_count, slot_count)
    slot_grads = jnp.pad(slot_grads, ((0, 0), (0, 128 - slot_count)))
    slot_grads = jnp.broadcast_to(slot_grads[:, None, :], (expert_count, 8, 128))
    slot_grads = exchange(slot_grads)[:, 0, :slot_count]
    d_gate_val = d_hidden * up_val * sig_gate * (1.0 + gate_val * (1.0 - sig_gate))
    d_up_val = d_hidden * silu_gate
    d_pair = jnp.stack([d_gate_val, d_up_val], axis=1)
    d_pair_low = d_pair.astype(BF)

    def to_sources(full):
        peer_first = lax.dynamic_slice_in_dim(full, (1 - core) * half, half, axis=1)
        own = lax.dynamic_slice_in_dim(full, core * half, half, axis=1)
        total = (own + swap(peer_first.astype(BF)).astype(F32)).astype(BF)
        return exchange(total.reshape(expert_count, slot_count, half)).reshape(slots, half)

    back_own = to_sources(
        jnp.einsum("rcf,dcf->rd", d_pair_low, pair, preferred_element_type=F32)
    )
    returned_own = to_sources(dot(hidden, down, ((1,), (0,))))

    gated_pair = (d_pair * slot_gates[:, :, None]).astype(BF)
    grad_gate_up = jnp.einsum("rd,rcf->dcf", expert_rows, gated_pair, preferred_element_type=F32)
    gated_hidden = (acted * slot_gates).astype(BF)
    grad_down = dot(gated_hidden, grad_rows, ((0,), (0,)))

    spread = jnp.sum(jnp.where(slot_hit, slot_grads[:, :, None], 0.0), axis=1).T
    d_gates = spread + swap(spread)
    d_picked = member * (d_gates - jnp.sum(d_gates * gates, axis=-1, keepdims=True)) / picked_total
    d_logits = (
        router_probs * (d_picked - jnp.sum(router_probs * d_picked, axis=-1, keepdims=True))
    ).astype(BF)
    grad_router = dot(normed_two, d_logits, ((0,), (0,)))

    mix_own = dot(combine, returned_own, ((0,), (0,)))
    out_own = (own_half(middle) + mix_own).astype(BF)
    output = side_by_side(out_own, swap(out_own), core)

    d_two_own = dot(combine, back_own, ((0,), (0,)))
    d_two_own = side_by_side(d_two_own, swap(d_two_own), core)
    d_normed_two = d_two_own + dot(d_logits, w_router, ((1,), (1,)))

    upstream = cotangent.astype(F32)
    d_middle_norm, gain_terms_two = norm_back(d_normed_two, middle, scale_two, gain_two)
    d_middle = upstream + d_middle_norm
    d_attn = d_middle.astype(BF)
    gain_two_local = jnp.sum(gain_terms_two, axis=0)

    grad_out = dot(d_attn, attended, ((0,), (0,))).astype(BF)
    d_attended = dot(d_attn, w_out, ((1,), (0,))).astype(BF).reshape(length, heads, head_dim)
    d_value = jnp.einsum("hqk,qhd->khd", weights, d_attended, preferred_element_type=F32)
    d_probs_att = jnp.einsum("qhd,khd->hqk", d_attended, value_in, preferred_element_type=F32)
    d_scores = (
        probs_att * (d_probs_att - jnp.sum(probs_att * d_probs_att, axis=-1, keepdims=True))
    ).astype(BF)
    d_query = unturn(
        jnp.einsum("hqk,khd->qhd", d_scores, key_in, preferred_element_type=F32) * inverse_root,
        cosine,
        sine,
    )
    d_key = unturn(
        jnp.einsum("hqk,qhd->khd", d_scores, query_in, preferred_element_type=F32) * inverse_root,
        cosine,
        sine,
    )
    d_query_raw, query_terms = norm_back(d_query, query_raw, query_scale, qk_gains[0])
    d_key_raw, key_terms = norm_back(d_key, key_raw, key_scale, qk_gains[1])
    grad_qk = jnp.stack([jnp.sum(query_terms, axis=(0, 1)), jnp.sum(key_terms, axis=(0, 1))])
    d_parts = [
        g.astype(BF).reshape(length, inner) for g in (d_query_raw, d_key_raw, d_value)
    ]

    packed = jnp.concatenate(
        [
            grad_router.reshape(SIDE**3, -1),
            gain_two_local.reshape(SIDE**3, -1),
            jnp.zeros((SIDE**3, 96), F32),
        ],
        axis=1,
    )
    columns = packed.shape[1]
    packed = exchange(packed.reshape(SIDE**3, columns // 128, 128))
    packed = jnp.sum(packed, axis=0).reshape(columns)
    router_rows = width // SIDE**3
    grad_router_out = packed[: router_rows * expert_count].reshape(router_rows, expert_count)
    grad_gain_two = packed[router_rows * expert_count : router_rows * (expert_count + 1)]

    grid = (SIDE, SIDE, SIDE, router_rows)
    cuts = (0, 384, 768, inner)
    orders = ((1, 2, 0), (2, 0, 1), (0, 1, 2))
    pieces = []
    for part, order in enumerate(orders):
        value = grad_out[:, cuts[part] : cuts[part + 1]].reshape(*grid, -1)
        names = [0, 1, 2]
        for axis in order:
            dim = names.index(axis)
            value = scatter_sum(value, AXES[axis], dim)
            names.remove(axis)
            if names:
                value = value.astype(BF)
        pieces.append(value)
    grad_out_here = jnp.concatenate(pieces, axis=1)

    grouped = normed_one.reshape(length, SIDE, SIDE, SIDE, router_rows)
    pieces = []
    for part, (group, second, third) in enumerate(((0, 1, 2), (1, 2, 0), (2, 0, 1))):
        here = place[group]
        total = None
        for step in (0, 1, 3, 2):
            left = block_at(grouped, (here + step) % SIDE, 1 + group).reshape(length, width // SIDE)
            right = d_parts[part]
            if step:
                left = shift(left, AXES[group], step)
                right = shift(right, AXES[group], step)
            product = dot(left, right, ((0,), (0,)))
            total = product if total is None else total + product
        value = total.astype(BF).reshape(SIDE, SIDE, router_rows, inner)
        names = [a for a in (0, 1, 2) if a != group]
        value = scatter_sum(value, AXES[second], names.index(second)).astype(BF)
        value = scatter_sum(value, AXES[third], 0)
        pieces.append(value)
    grad_qkv = jnp.stack(pieces, axis=1)
    rows_here = lax.dynamic_slice_in_dim(w_qkv, dp_index * router_rows, router_rows, axis=0)
    gain_here = lax.dynamic_slice_in_dim(gain_one, dp_index * router_rows, router_rows, axis=0)
    grad_gain_one = jnp.sum(grad_qkv * rows_here.astype(F32), axis=(1, 2))
    grad_gain_one = (grad_gain_one + swap(grad_gain_one)) / gain_here

    d_one = jnp.zeros((length, width), F32)
    for part in range(3):
        d_one = d_one + dot(d_parts[part], w_qkv[:, part], ((1,), (1,)))
    d_one = d_one.astype(BF)
    d_one = d_one.astype(F32) + swap(d_one).astype(F32)
    d_input_norm, _ = norm_back(d_one, residual_in, scale_one, gain_one)
    grad_input = d_middle + d_input_norm

    grad_qk = grad_qk + swap(grad_qk)
    for axis in AXES:
        grad_qk = all_sum(grad_qk, axis)

    return (
        output,
        grad_input,
        grad_gain_one,
        grad_qkv,
        grad_qk,
        grad_out_here,
        grad_gain_two,
        grad_router_out,
        grad_gate_up[None],
        grad_down[None],
    )


def solution(mesh):
    names = AXES + ("tensor",)
    torus = Mesh(mesh.devices.reshape(SIDE, SIDE, SIDE, 2), names)
    return jax.shard_map(
        on_device,
        mesh=torus,
        in_specs=(
            P(AXES, None),
            P(AXES, None),
            P(),
            P(),
            P(None, None, "tensor"),
            P(),
            P(None, "tensor"),
            P(),
            P(),
            P(AXES, None, None, "tensor"),
            P(AXES, "tensor", None),
            P(AXES, None),
        ),
        out_specs=(
            P(AXES, None),
            P(AXES, None),
            P(AXES),
            P(AXES, None, "tensor"),
            P(),
            P(AXES, "tensor"),
            P(AXES),
            P(AXES, None),
            P(AXES, None, None, "tensor"),
            P(AXES, "tensor", None),
        ),
        check_vma=False,
    )
```

```python
import functools
import math

import jax
import jax.numpy as jnp
import numpy as np
from jax import lax
from jax.experimental import pallas as pl
from jax.experimental.pallas import tpu as pltpu
from jax.sharding import Mesh
from jax.sharding import PartitionSpec as P

AXES = ("y", "x", "z")
SIDE = 4
LANE = 128
BF = jnp.bfloat16
F32 = jnp.float32
MIB = 1 << 20


def dot(a, b, dims):
    return lax.dot_general(a, b, (dims, ((), ())), preferred_element_type=F32)


NN = ((1,), (0,))
NT = ((1,), (1,))
TN = ((0,), (0,))


def rms(values):
    return lax.rsqrt(jnp.mean(values * values, axis=-1, keepdims=True) + 1e-06)


def rotary(length, half_dim):
    position = np.arange(length, dtype=np.float32)
    inverse = np.float32(50000.0) ** (-np.arange(half_dim, dtype=np.float32) / np.float32(half_dim))
    angles = position[:, None] * inverse[None, :].astype(np.float32)
    cosine = np.cos(angles).astype(np.float32)
    sine = np.sin(angles).astype(np.float32)
    return np.stack([np.concatenate([cosine, cosine], 1), np.concatenate([-sine, sine], 1)])


def swap(value):
    return lax.ppermute(value, "tensor", [(0, 1), (1, 0)])


def shift(value, axis, step):
    return lax.ppermute(value, axis, [(i, (i + step) % SIDE) for i in range(SIDE)])


def side_by_side(own, peer, core):
    return jnp.where(
        core == 0,
        jnp.concatenate([own, peer], axis=-1),
        jnp.concatenate([peer, own], axis=-1),
    )


def block_at(value, index, dim):
    return lax.dynamic_index_in_dim(value, index, dim, keepdims=False)


def together(*values):
    return lax.optimization_barrier(values)


def share(value, axis):
    return [value] + [shift(value, axis, step) for step in (1, 2, 3)]


def send_blocks(value, axis, dim):
    here = lax.axis_index(axis)
    own = block_at(value, here, dim)
    return [own] + [shift(block_at(value, (here + step) % SIDE, dim), axis, step) for step in (1, 2, 3)]


def in_order(parts, axis):
    here = lax.axis_index(axis)
    turned = jnp.stack([parts[0], parts[3], parts[2], parts[1]] * 2)
    return lax.dynamic_slice_in_dim(turned, (SIDE - here) % SIDE, SIDE, axis=0)


def exchange(value, axes):
    return lax.all_to_all(value, axes, split_axis=0, concat_axis=0, tiled=True)


def shape(dims, kind):
    return jax.ShapeDtypeStruct(dims, kind)


def main_memory(dims, kind):
    return pltpu.HBM(dims, kind)


def held(*values):
    return [pltpu.with_memory_space_constraint(value, pltpu.HBM) for value in values]


def kernel_call(body, grid, ins, outs, out_shapes, scratch=(), mib=40, scalars=0, name=None):
    return pl.pallas_call(
        body,
        grid_spec=pltpu.PrefetchScalarGridSpec(
            num_scalar_prefetch=scalars, grid=grid, in_specs=ins, out_specs=outs, scratch_shapes=list(scratch)
        ),
        out_shape=out_shapes,
        compiler_params=pltpu.CompilerParams(vmem_limit_bytes=mib * MIB),
        name=name,
    )


def whole(*dims):
    return pl.BlockSpec(dims, lambda *_: (0,) * len(dims))


def rope(values, table):
    return values * table[0] + pltpu.roll(values, values.shape[-1] // 2, 1) * table[1]


def unrope(values, table):
    return values * table[0] - pltpu.roll(values, values.shape[-1] // 2, 1) * table[1]


def attention_weights(query, key):
    scores = dot(query, key, NT) * (1.0 / math.sqrt(query.shape[-1]))
    raised = jnp.exp(scores - jnp.max(scores, axis=-1, keepdims=True))
    return raised / jnp.sum(raised, axis=-1, keepdims=True)


def attend_body(tokens, gain, w_qkv, w_out, gains, table, normed, raw, value_out, attended, partial, total):
    step = pl.program_id(0)

    @pl.when(step == 0)
    def _():
        x = tokens[...].astype(F32)
        normed[...] = (x * rms(x) * gain[...]).astype(BF)
        total[...] = jnp.zeros_like(total)

    h = normed[...]
    query_raw = dot(h, w_qkv[0], NN)
    key_raw = dot(h, w_qkv[1], NN)
    value = dot(h, w_qkv[2], NN).astype(BF)
    raw[0] = query_raw
    raw[1] = key_raw
    value_out[...] = value
    for at in range(query_raw.shape[1] // LANE):
        cut = slice(at * LANE, (at + 1) * LANE)
        q, k = query_raw[:, cut], key_raw[:, cut]
        query = rope(q * rms(q) * gains[0:1], table).astype(BF)
        key = rope(k * rms(k) * gains[1:2], table).astype(BF)
        weights = attention_weights(query, key).astype(BF)
        attended[:, cut] = dot(weights, value[:, cut], NN).astype(BF)
    total[...] += dot(attended[...], w_out[...], NT)

    @pl.when(step == pl.num_programs(0) - 1)
    def _():
        partial[...] = total[...].astype(BF)


def attend(tokens, gain, w_qkv, w_out, gains, table):
    length, width = tokens.shape
    inner = w_qkv.shape[2]
    cols = inner // SIDE
    return kernel_call(
        attend_body,
        (SIDE,),
        [
            whole(length, width),
            whole(1, width),
            pl.BlockSpec((3, width, cols), lambda i: (0, 0, i)),
            pl.BlockSpec((width, cols), lambda i: (0, i)),
            whole(2, LANE),
            whole(2, length, LANE),
        ],
        [
            whole(length, width),
            pl.BlockSpec((2, length, cols), lambda i: (0, 0, i)),
            pl.BlockSpec((length, cols), lambda i: (0, i)),
            pl.BlockSpec((length, cols), lambda i: (0, i)),
            whole(length, width),
        ],
        [
            shape((length, width), BF),
            shape((2, length, inner), F32),
            shape((length, inner), BF),
            shape((length, inner), BF),
            shape((length, width), BF),
        ],
        [pltpu.VMEM((length, width), F32)],
        name="attend",
    )(tokens, gain, w_qkv, w_out, gains, table)


def attend_back_body(d_attn, w_out, raw, value_in, gains, table, d_block, d_gains):
    step = pl.program_id(0)

    @pl.when(step == 0)
    def _():
        d_gains[...] = jnp.zeros_like(d_gains)

    d_attended = dot(d_attn[...], w_out[...], NN).astype(BF)
    for at in range(d_attended.shape[1] // LANE):
        cut = slice(at * LANE, (at + 1) * LANE)
        q, k = raw[0, :, cut], raw[1, :, cut]
        rq, rk = rms(q), rms(k)
        unit_q, unit_k = q * rq, k * rk
        query = rope(unit_q * gains[0:1], table).astype(BF)
        key = rope(unit_k * gains[1:2], table).astype(BF)
        weights = attention_weights(query, key)
        grad = d_attended[:, cut]
        d_value = dot(weights.astype(BF), grad, TN)
        d_weights = dot(grad, value_in[:, cut], NT)
        d_scores = (
            weights * (d_weights - jnp.sum(weights * d_weights, axis=-1, keepdims=True))
        ).astype(BF)
        root = 1.0 / math.sqrt(LANE)
        d_query = unrope(dot(d_scores, key, NN) * root, table)
        d_key = unrope(dot(d_scores, query, TN) * root, table)
        d_gains[0:1] += jnp.sum(d_query * unit_q, axis=0, keepdims=True)
        d_gains[1:2] += jnp.sum(d_key * unit_k, axis=0, keepdims=True)
        wq = d_query * gains[0:1]
        wk = d_key * gains[1:2]
        d_block[0, 0, :, cut] = (rq * (wq - unit_q * jnp.mean(wq * unit_q, axis=-1, keepdims=True))).astype(BF)
        d_block[0, 1, :, cut] = (rk * (wk - unit_k * jnp.mean(wk * unit_k, axis=-1, keepdims=True))).astype(BF)
        d_block[0, 2, :, cut] = d_value.astype(BF)


def attend_back(d_attn, w_out, raw, value_in, gains, table):
    length, width = d_attn.shape
    inner = w_out.shape[1]
    cols = inner // SIDE
    return kernel_call(
        attend_back_body,
        (SIDE,),
        [
            whole(length, width),
            pl.BlockSpec((width, cols), lambda i: (0, i)),
            pl.BlockSpec((2, length, cols), lambda i: (0, 0, i)),
            pl.BlockSpec((length, cols), lambda i: (0, i)),
            whole(2, LANE),
            whole(2, length, LANE),
        ],
        [pl.BlockSpec((1, 3, length, cols), lambda i: (i, 0, 0, 0)), whole(2, LANE)],
        [shape((SIDE, 3, length, cols), BF), shape((2, LANE), F32)],
        name="attend_back",
    )(d_attn, *held(w_out, raw, value_in, gains, table))


def input_grad_body(d_block, w_qkv, out, total):
    step = pl.program_id(0)
    value = dot(d_block[0, 0], w_qkv[0], NT) + dot(d_block[0, 1], w_qkv[1], NT) + dot(d_block[0, 2], w_qkv[2], NT)

    @pl.when(step == 0)
    def _():
        total[...] = value

    @pl.when(step > 0)
    def _():
        total[...] += value

    @pl.when(step == pl.num_programs(0) - 1)
    def _():
        out[...] = total[...].astype(BF)


def input_grad(d_blocks, w_qkv):
    _, _, length, cols = d_blocks.shape
    width = w_qkv.shape[1]
    return kernel_call(
        input_grad_body,
        (SIDE,),
        [
            pl.BlockSpec((1, 3, length, cols), lambda i: (i, 0, 0, 0)),
            pl.BlockSpec((3, width, cols), lambda i: (0, 0, i)),
        ],
        whole(length, width),
        shape((length, width), BF),
        [pltpu.VMEM((length, width), F32)],
        name="input_grad",
    )(d_blocks, *held(w_qkv))


def middle_body(core, tokens, own, peer, gain, select, w_router, member, expert_of,
                middle, normed, probs_out, gates_out, total_out, combine, rows):
    x2 = tokens[...].astype(F32) + (own[...].astype(F32) + peer[...].astype(F32))
    middle[...] = x2
    normed[...] = (x2 * rms(x2) * gain[...]).astype(BF)
    logits = dot(normed[...], w_router[...], NN)
    raised = jnp.exp(logits - jnp.max(logits, axis=-1, keepdims=True))
    probs = raised / jnp.sum(raised, axis=-1, keepdims=True)
    picked = probs * member[...]
    total = jnp.sum(picked, axis=-1, keepdims=True)
    gates = picked / total
    probs_out[...] = probs
    gates_out[...] = gates
    total_out[...] = total
    low = gates.astype(BF)
    half = rows.shape[1] - LANE
    for at in range(0, rows.shape[0], 256):
        cut = slice(at, at + 256)
        spread = dot(expert_of[cut], low, NT) * select[cut].astype(F32)
        combine[cut] = spread.astype(BF)
        gate = jnp.sum(spread, axis=-1, keepdims=True)
        rows[cut, half:] = jnp.broadcast_to(gate, (256, LANE)).astype(BF)
    for which in range(2):

        @pl.when(core[0] == which)
        def _():
            for at in range(0, rows.shape[0], 256):
                rows[at : at + 256, :half] = dot(
                    select[at : at + 256], normed[:, which * half : (which + 1) * half], NN
                ).astype(BF)


def middle_step(core, tokens, own, peer, gain, select, w_router, member, expert_of):
    length, width = tokens.shape
    slots, experts = expert_of.shape
    columns = width // 2 + LANE
    return kernel_call(
        middle_body,
        (1,),
        [whole(length, width)] * 3
        + [whole(1, width), whole(slots, length), whole(width, experts), whole(length, experts), whole(slots, experts)],
        [
            whole(length, width),
            whole(length, width),
            whole(length, experts),
            whole(length, experts),
            whole(length, 1),
            whole(slots, length),
            whole(slots, columns),
        ],
        [
            shape((length, width), F32),
            shape((length, width), BF),
            shape((length, experts), F32),
            shape((length, experts), F32),
            shape((length, 1), F32),
            shape((slots, length), BF),
            main_memory((slots, columns), BF),
        ],
        scalars=1,
        name="middle",
    )(core, *held(tokens), own, peer, *held(gain, select, w_router, member, expert_of))


def gather_back_body(back, combine, select, expert_of, out):
    half = combine.shape[1]
    half = out.shape[1] - LANE
    out[:, :half] = dot(combine[...], back[:, :half], TN)
    high = back[:, half : half + 1].astype(F32)
    low = back[:, half + 1 : half + 2].astype(F32)
    picked = select[...].astype(F32)
    experts = expert_of.shape[1]
    spread = dot((picked * high).astype(BF), expert_of[...], TN) + dot((picked * low).astype(BF), expert_of[...], TN)
    out[:, half : half + experts] = spread
    out[:, half + experts :] = jnp.zeros((out.shape[0], LANE - experts), F32)


def gather_back(back, combine, select, expert_of):
    slots, columns = back.shape
    length = combine.shape[1]
    experts = expert_of.shape[1]
    return kernel_call(
        gather_back_body,
        (1,),
        [whole(slots, columns), whole(slots, length), whole(slots, length), whole(slots, experts)],
        whole(length, columns),
        shape((length, columns), F32),
        name="gather_back",
    )(back, *held(combine, select, expert_of))


def middle_back_body(core, own, peer, probs, gates, total, member, w_router, middle, cotangent, gain,
                     d_logits_out, d_middle, d_attn, d_attn_blocks, d_gain):
    half = own.shape[1] - LANE
    experts = probs.shape[1]
    d_gates = own[:, half : half + experts] + peer[:, half : half + experts]
    g, p = gates[...], probs[...]
    d_picked = member[...] * (d_gates - jnp.sum(d_gates * g, axis=-1, keepdims=True)) / total[...]
    d_logits = (p * (d_picked - jnp.sum(p * d_picked, axis=-1, keepdims=True))).astype(BF)
    d_logits_out[...] = d_logits
    d_normed = dot(d_logits, w_router[...], NT)
    for which in range(2):

        @pl.when(core[0] == which)
        def _():
            first, second = (own, peer) if which == 0 else (peer, own)
            d_middle[:, :half] = first[:, :half]
            d_middle[:, half:] = second[:, :half]

    d_normed = d_normed + d_middle[...]
    x2 = middle[...]
    scale = rms(x2)
    unit = x2 * scale
    d_gain[...] = jnp.sum(d_normed * unit, axis=0, keepdims=True)
    weighted = d_normed * gain[...]
    value = cotangent[...].astype(F32) + scale * (
        weighted - unit * jnp.mean(weighted * unit, axis=-1, keepdims=True)
    )
    d_middle[...] = value
    low = value.astype(BF)
    d_attn[...] = low
    cut = d_attn_blocks.shape[2]
    for k in range(SIDE):
        d_attn_blocks[k] = low[:, k * cut : (k + 1) * cut]


def middle_back(core, own, peer, probs, gates, total, member, w_router, middle, cotangent, gain):
    length, width = middle.shape
    experts = probs.shape[1]
    columns = own.shape[1]
    return kernel_call(
        middle_back_body,
        (1,),
        [whole(length, columns)] * 2
        + [whole(length, experts)] * 2
        + [whole(length, 1), whole(length, experts), whole(width, experts), whole(length, width), whole(length, width), whole(1, width)],
        [
            whole(length, experts),
            whole(length, width),
            whole(length, width),
            whole(SIDE, length, width // SIDE),
            whole(1, width),
        ],
        [
            shape((length, experts), BF),
            shape((length, width), F32),
            shape((length, width), BF),
            shape((SIDE, length, width // SIDE), BF),
            shape((1, width), F32),
        ],
        scalars=1,
        name="middle_back",
    )(core, own, peer, *held(probs, gates, total, member, w_router, middle, cotangent, gain))


def hidden_grad_body(core, own, peer, down_own, down_peer, out):
    half = down_own.shape[1]
    out[...] = dot(own[:, :half], down_own[...], NT) + dot(peer[:, :half], down_peer[...], NT)


ROWS = 256


def hidden_grad(core, own, peer, down):
    slots, columns = own.shape
    hidden, width = down.shape
    half = width // 2
    return kernel_call(
        hidden_grad_body,
        (slots // ROWS,),
        [
            pl.BlockSpec((ROWS, columns), lambda i, c: (i, 0)),
            pl.BlockSpec((ROWS, columns), lambda i, c: (i, 0)),
            pl.BlockSpec((hidden, half), lambda i, c: (0, c[0])),
            pl.BlockSpec((hidden, half), lambda i, c: (0, 1 - c[0])),
        ],
        pl.BlockSpec((ROWS, hidden), lambda i, c: (i, 0)),
        main_memory((slots, hidden), F32),
        scalars=1,
        name="hidden_grad",
    )(core, own, peer, down, down)


def experts_body(core, own, peer, d_hidden, pair_own, pair_peer, acted, d_pair, back_own, back_peer, extra):
    hidden = d_hidden.shape[1]
    half = pair_own.shape[1]
    mine, other = own[:, :half], peer[:, :half]
    gate = dot(mine, pair_own[0], NN) + dot(other, pair_peer[0], NN)
    up = dot(mine, pair_own[1], NN) + dot(other, pair_peer[1], NN)
    sig = 1.0 / (1.0 + jnp.exp(-gate))
    silu = gate * sig
    act = (silu * up).astype(BF)
    acted[...] = act
    d_act = d_hidden[...]
    slot_grad = jnp.sum(d_act * act.astype(F32), axis=-1, keepdims=True)
    high = slot_grad.astype(BF)
    low = (slot_grad - high.astype(F32)).astype(BF)
    at = lax.broadcasted_iota(jnp.int32, extra.shape, 1)
    extra[...] = jnp.where(at == 0, high.astype(F32), jnp.where(at == 1, low.astype(F32), 0.0)).astype(BF)
    d_gate = (d_act * up * sig * (1.0 + gate * (1.0 - sig))).astype(BF)
    d_up = (d_act * silu).astype(BF)
    d_pair[:, :hidden] = d_gate
    d_pair[:, hidden:] = d_up
    back_peer[...] = (dot(d_gate, pair_peer[0], NT) + dot(d_up, pair_peer[1], NT)).astype(BF)
    back_own[...] = (dot(d_gate, pair_own[0], NT) + dot(d_up, pair_own[1], NT)).astype(BF)


def experts_out_body(core, acted, down_own, down_peer, out_own, out_peer):
    out_peer[...] = dot(acted[...], down_peer[...], NN).astype(BF)
    out_own[...] = dot(acted[...], down_own[...], NN).astype(BF)


def experts_out(core, acted, down):
    slots, hidden = acted.shape
    half = down.shape[1] // 2
    rows = lambda n: pl.BlockSpec((ROWS, n), lambda i, c: (i, 0))
    return kernel_call(
        experts_out_body,
        (slots // ROWS,),
        [
            rows(hidden),
            pl.BlockSpec((hidden, half), lambda i, c: (0, c[0])),
            pl.BlockSpec((hidden, half), lambda i, c: (0, 1 - c[0])),
        ],
        [rows(half), rows(half)],
        [shape((slots, half), BF)] * 2,
        scalars=1,
        name="experts_out",
    )(core, acted, down, down)


def experts_step(core, own, peer, d_hidden, pair):
    slots, columns = own.shape
    half = columns - LANE
    hidden = pair.shape[2]
    rows = lambda n: pl.BlockSpec((ROWS, n), lambda i, c: (i, 0))
    return kernel_call(
        experts_body,
        (slots // ROWS,),
        [
            rows(columns),
            rows(columns),
            rows(hidden),
            pl.BlockSpec((2, half, hidden), lambda i, c: (0, c[0], 0)),
            pl.BlockSpec((2, half, hidden), lambda i, c: (0, 1 - c[0], 0)),
        ],
        [rows(hidden), rows(2 * hidden), rows(half), rows(half), rows(LANE)],
        [
            shape((slots, hidden), BF),
            shape((slots, 2 * hidden), BF),
            shape((slots, half), BF),
            shape((slots, half), BF),
            shape((slots, LANE), BF),
        ],
        scalars=1,
        name="experts",
    )(core, *held(own), peer, *held(d_hidden, pair, pair))


def add_pack_body(own, peer, extra, out):
    half = own.shape[1]
    out[:, :half] = (own[...].astype(F32) + peer[...].astype(F32)).astype(BF)
    out[:, half:] = extra[...]


def add_pack(own, peer, extra):
    slots, half = own.shape
    rows = lambda n: pl.BlockSpec((ROWS, n), lambda i: (i, 0))
    return kernel_call(
        add_pack_body,
        (slots // ROWS,),
        [rows(half), rows(half), rows(LANE)],
        rows(half + LANE),
        main_memory((slots, half + LANE), BF),
        name="add_pack",
    )(own, peer, extra)


def expert_grads_body(core, own, peer, grad_own, grad_peer, acted, d_pair, gates, grad_pair, grad_down, pair_low, act_low):
    step = pl.program_id(0)
    hidden = acted.shape[1]

    @pl.when(step == 0)
    def _():
        gate = gates[:, :1].astype(F32)
        pair_low[...] = (d_pair[...].astype(F32) * gate).astype(BF)
        act_low[...] = (acted[...].astype(F32) * gate).astype(BF)

    def part(rows, grads):
        value = dot(rows[...], pair_low[...], TN)
        grad_pair[:, 0, :] = value[:, :hidden]
        grad_pair[:, 1, :] = value[:, hidden:]
        grad_down[...] = dot(act_low[...], grads[...], TN)

    @pl.when(step < SIDE)
    def _():
        part(own, grad_own)

    @pl.when(step >= SIDE)
    def _():
        part(peer, grad_peer)


def expert_grads(core, own, peer, grad_own, grad_peer, acted, d_pair, gates):
    slots, half = grad_own.shape
    hidden = acted.shape[1]
    cut = half // SIDE
    first = pl.BlockSpec((slots, cut), lambda i, c: (0, jnp.minimum(i, SIDE - 1)))
    second = pl.BlockSpec((slots, cut), lambda i, c: (0, jnp.maximum(i - SIDE, 0)))

    def target(i, c):
        return jnp.where(i < SIDE, c[0] * SIDE + i, (1 - c[0]) * SIDE + i - SIDE)

    return kernel_call(
        expert_grads_body,
        (2 * SIDE,),
        [first, second, first, second, whole(slots, hidden), whole(slots, 2 * hidden), pl.BlockSpec((slots, LANE), lambda i, c: (0, half // LANE))],
        [
            pl.BlockSpec((cut, 2, hidden), lambda i, c: (target(i, c), 0, 0)),
            pl.BlockSpec((hidden, cut), lambda i, c: (0, target(i, c))),
        ],
        [shape((2 * half, 2, hidden), F32), shape((hidden, 2 * half), F32)],
        [pltpu.VMEM((slots, 2 * hidden), BF), pltpu.VMEM((slots, hidden), BF)],
        mib=48,
        scalars=1,
        name="expert_grads",
    )(core, own, peer, grad_own, grad_peer, acted, d_pair, gates)


EXTRA = 16


def group_grads_body(core, own, peer, *refs):
    step = pl.program_id(0)
    d_group = refs[:SIDE]
    normed_two, d_logits, d_gain, d_qk, out = refs[SIDE:]
    cols = d_group[0].shape[2]
    targets = out.shape[0]
    rows = out.shape[1] - EXTRA

    def put(value, at):
        for k in range(targets):
            out[k, :rows, at * cols : (at + 1) * cols] = value[k * rows : (k + 1) * rows].astype(BF)

    def part(normed):
        members, length, cut = normed.shape
        left = normed[...].reshape(members * length, cut)
        for which in range(3):
            put(dot(left, jnp.concatenate([block[which] for block in d_group], axis=0), TN), which)

    @pl.when(step < SIDE)
    def _():
        part(own)

    @pl.when(step >= SIDE)
    def _():
        part(peer)

    router = dot(d_logits[...], normed_two[...], TN).astype(BF)
    for k in range(targets):
        cut = slice(k * rows, (k + 1) * rows)
        out[k, rows:, :LANE] = router[:EXTRA, cut]
        out[k, rows:, LANE : 2 * LANE] = router[EXTRA:, cut]
        out[k, rows:, 2 * LANE : 3 * LANE] = jnp.broadcast_to(d_gain[:, cut], (EXTRA, LANE)).astype(BF)
        out[k, rows:, 3 * LANE : 4 * LANE] = jnp.concatenate([d_qk[...]] * (EXTRA // 2), axis=0).astype(BF)
        out[k, rows:, 4 * LANE :] = jnp.zeros((EXTRA, out.shape[2] - 4 * LANE), BF)


def group_grads(core, own, peer, d_group, normed_two, d_logits, d_gain, d_qk):
    members, length, half = own.shape
    cols = d_group[0].shape[2]
    cut = half // SIDE
    places = SIDE * SIDE
    rows = 2 * half // places

    def target(i, c):
        return jnp.where(i < SIDE, c[0] * SIDE + i, (1 - c[0]) * SIDE + i - SIDE)

    return kernel_call(
        group_grads_body,
        (2 * SIDE,),
        [
            pl.BlockSpec((members, length, cut), lambda i, c: (0, 0, jnp.minimum(i, SIDE - 1))),
            pl.BlockSpec((members, length, cut), lambda i, c: (0, 0, jnp.maximum(i - SIDE, 0))),
        ]
        + [whole(3, length, cols)] * SIDE
        + [
            pl.BlockSpec((length, cut), lambda i, c: (0, target(i, c))),
            whole(length, d_logits.shape[1]),
            pl.BlockSpec((1, cut), lambda i, c: (0, target(i, c))),
            whole(2, LANE),
        ],
        pl.BlockSpec((cut // rows, rows + EXTRA, 3 * cols), lambda i, c: (target(i, c), 0, 0)),
        main_memory((places, rows + EXTRA, 3 * cols), BF),
        scalars=1,
        name="group_grads",
    )(core, *held(own, peer), *d_group, *held(normed_two), d_logits, d_gain, d_qk)


def out_grads_body(*refs):
    left = jnp.concatenate([part[...] for part in refs[:SIDE]], axis=0)
    right = jnp.concatenate([part[...] for part in refs[SIDE : 2 * SIDE]], axis=0)
    refs[2 * SIDE][...] = dot(left, right, TN).astype(BF)


def out_grads(d_attn, attended):
    length, rows = d_attn[0].shape
    inner = attended[0].shape[1]
    return kernel_call(
        out_grads_body,
        (1,),
        [whole(length, rows)] * SIDE + [whole(length, inner)] * SIDE,
        whole(rows, inner),
        shape((rows, inner), BF),
        name="out_grads",
    )(*d_attn, *attended)


def sum_arrived_body(rows, z_index, arrived, *outs):
    value = arrived[0].astype(F32)
    for k in range(1, arrived.shape[0]):
        value = value + arrived[k].astype(F32)
    value = value.astype(BF)
    main = SIDE * rows
    for which in range(SIDE):

        @pl.when(z_index[0] == which)
        def _():
            for step in range(SIDE):
                at = (which + step) % SIDE * rows
                outs[step][:rows] = value[at : at + rows]

    for step in range(SIDE):
        outs[step][rows:] = value[main:]


def sum_arrived(z_index, arrived, rows):
    places, height, columns = arrived.shape
    cols = columns // 3
    return kernel_call(
        functools.partial(sum_arrived_body, rows),
        (3,),
        [pl.BlockSpec((places, height, cols), lambda i, z: (0, 0, i))],
        [pl.BlockSpec((rows + EXTRA, cols), lambda i, z: (0, i))] * SIDE,
        [shape((rows + EXTRA, columns), BF)] * SIDE,
        scalars=1,
        name="sum_arrived",
    )(z_index, arrived)


def finish_body(z_index, *refs):
    parts, w_here, grad, small = refs[:SIDE], refs[SIDE], refs[SIDE + 1], refs[SIDE + 2]
    rows = grad.shape[1]
    cols = parts[0].shape[1] // 3
    for which in range(SIDE):

        @pl.when(z_index[0] == which)
        def _():
            ordered = [parts[(which - source) % SIDE] for source in range(SIDE)]
            for source in range(SIDE):
                for kind in range(3):
                    grad[kind, :, source * cols : (source + 1) * cols] = ordered[source][
                        :rows, kind * cols : (kind + 1) * cols
                    ].astype(F32)
            extra = [part[rows:].astype(F32) for part in ordered]
            total = (extra[0] + extra[1]) + (extra[2] + extra[3])
            small[:EXTRA] = total[:, :LANE]
            small[EXTRA : 2 * EXTRA] = total[:, LANE : 2 * LANE]
            small[2 * EXTRA + 1 : 2 * EXTRA + 2] = total[0:1, 2 * LANE : 3 * LANE]
            small[2 * EXTRA + 2 : 2 * EXTRA + 4] = total[0:2, 3 * LANE : 4 * LANE]

    product = jnp.sum(grad[0] * w_here[0].astype(F32) + grad[1] * w_here[1].astype(F32) + grad[2] * w_here[2].astype(F32), axis=-1, keepdims=True)
    at_row = lax.broadcasted_iota(jnp.int32, (rows, LANE), 0)
    at_lane = lax.broadcasted_iota(jnp.int32, (rows, LANE), 1)
    small[2 * EXTRA : 2 * EXTRA + 1] = jnp.sum(jnp.where(at_row == at_lane, product, 0.0), axis=0, keepdims=True)
    small[2 * EXTRA + 4 :] = jnp.zeros((small.shape[0] - 2 * EXTRA - 4, LANE), F32)


def finish(z_index, parts, w_here):
    kinds, rows, inner = w_here.shape
    height, columns = parts[0].shape
    return kernel_call(
        finish_body,
        (1,),
        [whole(height, columns)] * SIDE + [whole(kinds, rows, inner)],
        [whole(kinds, rows, inner), whole(2 * EXTRA + 8, LANE)],
        [shape((kinds, rows, inner), F32), shape((2 * EXTRA + 8, LANE), F32)],
        scalars=1,
        name="finish",
    )(z_index, *parts, w_here)


def on_device(
    tokens,
    expert_ids,
    capacity,
    gain_attn,
    w_qkv,
    qk_gain,
    w_out,
    gain_ffn,
    w_router,
    w_gate_up,
    w_down,
    cotangent,
):
    length, width = tokens.shape
    expert_count = capacity.shape[0]
    slot_count = length * expert_ids.shape[1] // expert_count
    slots = expert_count * slot_count
    inner = w_qkv.shape[2]
    half = width // 2
    cols = inner // SIDE
    core_index = lax.axis_index("tensor")
    core = core_index.astype(jnp.int32).reshape(1)
    place = [lax.axis_index(a) for a in AXES]
    dp_index = (place[0] * SIDE + place[1]) * SIDE + place[2]
    rows_here_count = width // SIDE**3

    def own_half(value):
        return lax.dynamic_slice_in_dim(value, core_index * half, half, axis=-1)

    experts = jnp.arange(expert_count, dtype=jnp.int32)
    member = jnp.sum((expert_ids[:, :, None] == experts).astype(F32), axis=1)
    earlier = jnp.asarray(np.tril(np.ones((length, length), np.float32), -1), BF)
    ranks = dot(earlier, member.astype(BF), NN)
    kept = (member > 0.5) & (ranks < capacity.astype(F32)[None, :])
    code = jnp.where(kept, ranks, -1.0).T
    slot_hit = code[:, None, :] == jnp.arange(slot_count, dtype=jnp.int32).astype(F32)[None, :, None]
    select = slot_hit.astype(BF).reshape(slots, length)
    expert_of = jnp.asarray(np.repeat(np.eye(expert_count, dtype=np.float32), slot_count, 0), BF)

    def to_owners(rows):
        columns = rows.shape[1]
        return exchange(rows.reshape(expert_count, slot_count, columns), AXES).reshape(slots, columns)

    grad_own = to_owners(dot(select, own_half(cotangent), NN).astype(BF))

    table = jnp.asarray(rotary(length, LANE // 2))
    gains = qk_gain.astype(F32)
    gain_one = gain_attn.astype(F32)
    gain_two = gain_ffn.astype(F32).reshape(1, width)
    w_parts = w_qkv.transpose(1, 0, 2)
    normed_one, raw, value_in, attended, partial = attend(
        tokens, gain_one.reshape(1, width), w_parts, w_out, gains, table
    )
    partial_peer = swap(partial)
    middle, normed_two, probs, gates, picked_total, combine, rows_send = middle_step(
        core, tokens, partial, partial_peer, gain_two, select, w_router, member, expert_of
    )
    rows_own = to_owners(rows_send)

    normed_early, attended_late, pair, grad_late, down, _ = together(
        own_half(normed_one), attended, w_gate_up, grad_own, w_down, rows_send
    )
    down = down[0]
    pair = pair[0].transpose(1, 0, 2)
    grad_peer = swap(grad_late)
    d_hidden = hidden_grad(core, grad_late, grad_peer, down)
    rows_own, d_hidden, pair, attended_late = together(rows_own, d_hidden, pair, attended_late)
    attended_group = share(attended_late, "y")
    rows_peer = swap(rows_own)
    acted, d_pair, back_own, back_peer, extra = experts_step(core, rows_own, rows_peer, d_hidden, pair)
    back_peer, normed_early, *attended_group = together(back_peer, normed_early, *attended_group)
    normed_group = share(normed_early, "z")
    back_send = add_pack(back_own, swap(back_peer), extra)
    out_own, out_peer = experts_out(core, acted, down)
    back_send, out_own, out_peer, *normed_group = together(back_send, out_own, out_peer, *normed_group)
    back = to_owners(back_send)

    returned = (out_own.astype(F32) + swap(out_peer).astype(F32)).astype(BF)
    normed_group = jnp.stack(normed_group)
    normed_group, normed_group_peer, returned = together(normed_group, swap(normed_group), returned)
    returned = to_owners(returned)
    back, normed_group_peer = together(back, normed_group_peer)

    gathered = gather_back(back, combine, select, expert_of)
    d_logits, d_middle, d_attn, d_attn_blocks, gain_two_local = middle_back(
        core, gathered, swap(gathered), probs, gates, picked_total, member, w_router, middle, cotangent, gain_two
    )

    d_blocks, grad_qk = attend_back(d_attn, w_out, raw, value_in, gains, table)
    d_group = send_blocks(d_blocks, "z", 0)
    returned, *d_group = together(returned, *d_group)

    d_attn_blocks, _ = together(d_attn_blocks, d_blocks)
    grad_out = out_grads(send_blocks(d_attn_blocks, "y", 0), attended_group)
    grad_out, *d_group = together(grad_out, *d_group)

    columns_here = expert_count // 2
    my_logits = lax.dynamic_slice_in_dim(d_logits, core_index * columns_here, columns_here, axis=1)
    partial_grads = group_grads(
        core,
        normed_group,
        normed_group_peer,
        d_group,
        normed_two,
        my_logits,
        gain_two_local,
        grad_qk,
    )
    late_blocks, late_returned, acted_late, _ = together(d_blocks, returned, acted, partial_grads)
    arrived = exchange(partial_grads, ("y", "x"))

    grad_out = send_blocks(grad_out.reshape(SIDE, SIDE, rows_here_count, inner), "z", 1)

    z_index = place[2].astype(jnp.int32).reshape(1)
    parts = sum_arrived(z_index, arrived, rows_here_count)
    parts = [parts[0]] + [shift(parts[step], "z", step) for step in (1, 2, 3)]
    w_here = lax.dynamic_slice_in_dim(w_parts, dp_index * rows_here_count, rows_here_count, axis=1)
    grad_qkv, small = finish(z_index, parts, w_here)
    grad_qkv = grad_qkv.transpose(1, 0, 2)
    small_peer = swap(small)
    gain_here = lax.dynamic_slice_in_dim(gain_one, dp_index * rows_here_count, rows_here_count, axis=0)
    grad_gain_one = (small[2 * EXTRA] + small_peer[2 * EXTRA])[:rows_here_count] / gain_here
    cut = lambda value: lax.dynamic_slice_in_dim(value, place[2] * rows_here_count, rows_here_count, axis=-1)
    grad_router = jnp.where(
        core_index == 0,
        jnp.concatenate([small[: 2 * EXTRA], small_peer[: 2 * EXTRA]], axis=0),
        jnp.concatenate([small_peer[: 2 * EXTRA], small[: 2 * EXTRA]], axis=0),
    )
    grad_router = cut(grad_router).T
    grad_gain_two = cut(small[2 * EXTRA + 1])
    grad_qk = small[2 * EXTRA + 2 : 2 * EXTRA + 4] + small_peer[2 * EXTRA + 2 : 2 * EXTRA + 4]

    d_one = input_grad(late_blocks, w_parts)
    d_one = d_one.astype(F32) + swap(d_one).astype(F32)

    grad_gate_up, grad_down = expert_grads(
        core, rows_own, rows_peer, grad_late, grad_peer, acted_late, d_pair, rows_own
    )
    *grad_out, _ = together(*grad_out, grad_down)
    grad_out = sum(part.astype(F32) for part in grad_out).astype(BF)
    grad_out = sum(part.astype(F32) for part in send_blocks(grad_out, "x", 0))

    residual_in = tokens.astype(F32)
    scale_one = rms(residual_in)
    unit_one = residual_in * scale_one
    weighted = d_one * gain_one
    grad_input = d_middle + scale_one * (
        weighted - unit_one * jnp.mean(weighted * unit_one, axis=-1, keepdims=True)
    )

    mix_own = dot(combine, late_returned, TN)
    result_own = (own_half(middle) + mix_own).astype(BF)
    output = side_by_side(result_own, swap(result_own), core_index)

    return (
        output,
        grad_input,
        grad_gain_one,
        grad_qkv,
        grad_qk,
        grad_out,
        grad_gain_two,
        grad_router,
        grad_gate_up[None],
        grad_down[None],
    )


def solution(mesh):
    names = AXES + ("tensor",)
    torus = Mesh(mesh.devices.reshape(SIDE, SIDE, SIDE, 2), names)
    return jax.shard_map(
        on_device,
        mesh=torus,
        in_specs=(
            P(AXES, None),
            P(AXES, None),
            P(),
            P(),
            P(None, None, "tensor"),
            P(),
            P(None, "tensor"),
            P(),
            P(),
            P(AXES, None, None, "tensor"),
            P(AXES, "tensor", None),
            P(AXES, None),
        ),
        out_specs=(
            P(AXES, None),
            P(AXES, None),
            P(AXES),
            P(AXES, None, "tensor"),
            P(),
            P(AXES, "tensor"),
            P(AXES),
            P(AXES, None),
            P(AXES, None, None, "tensor"),
            P(AXES, "tensor", None),
        ),
        check_vma=False,
    )
```

```python
import functools
import math

import jax
import jax.numpy as jnp
import numpy as np
from jax import lax
from jax.experimental import pallas as pl
from jax.experimental.pallas import tpu as pltpu
from jax.sharding import Mesh
from jax.sharding import PartitionSpec as P

AXES = ("y", "x", "z")
SIDE = 4
LANE = 128
BF = jnp.bfloat16
F32 = jnp.float32
MIB = 1 << 20


def dot(a, b, dims):
    return lax.dot_general(a, b, (dims, ((), ())), preferred_element_type=F32)


NN = ((1,), (0,))
NT = ((1,), (1,))
TN = ((0,), (0,))


def rms(values):
    return lax.rsqrt(jnp.mean(values * values, axis=-1, keepdims=True) + 1e-06)


def rotary(length, half_dim):
    position = np.arange(length, dtype=np.float32)
    inverse = np.float32(50000.0) ** (-np.arange(half_dim, dtype=np.float32) / np.float32(half_dim))
    angles = position[:, None] * inverse[None, :].astype(np.float32)
    cosine = np.cos(angles).astype(np.float32)
    sine = np.sin(angles).astype(np.float32)
    return np.stack([np.concatenate([cosine, cosine], 1), np.concatenate([-sine, sine], 1)])


def swap(value):
    return lax.ppermute(value, "tensor", [(0, 1), (1, 0)])


def shift(value, axis, step):
    return lax.ppermute(value, axis, [(i, (i + step) % SIDE) for i in range(SIDE)])


def side_by_side(own, peer, core):
    return jnp.where(
        core == 0,
        jnp.concatenate([own, peer], axis=-1),
        jnp.concatenate([peer, own], axis=-1),
    )


def block_at(value, index, dim):
    return lax.dynamic_index_in_dim(value, index, dim, keepdims=False)


def together(*values):
    return lax.optimization_barrier(values)


def share(value, axis):
    return [value] + [shift(value, axis, step) for step in (1, 2, 3)]


def send_blocks(value, axis, dim):
    here = lax.axis_index(axis)
    own = block_at(value, here, dim)
    return [own] + [shift(block_at(value, (here + step) % SIDE, dim), axis, step) for step in (1, 2, 3)]


def send_steps(blocks, axis):
    return [blocks[0]] + [shift(blocks[step], axis, step) for step in (1, 2, 3)]


def exchange(value, axes):
    return lax.all_to_all(value, axes, split_axis=0, concat_axis=0, tiled=True)


def shape(dims, kind):
    return jax.ShapeDtypeStruct(dims, kind)


def main_memory(dims, kind):
    return pltpu.HBM(dims, kind)


def held(*values):
    return [pltpu.with_memory_space_constraint(value, pltpu.HBM) for value in values]


def kernel_call(body, grid, ins, outs, out_shapes, scratch=(), mib=40, scalars=0, name=None):
    return pl.pallas_call(
        body,
        grid_spec=pltpu.PrefetchScalarGridSpec(
            num_scalar_prefetch=scalars, grid=grid, in_specs=ins, out_specs=outs, scratch_shapes=list(scratch)
        ),
        out_shape=out_shapes,
        compiler_params=pltpu.CompilerParams(vmem_limit_bytes=mib * MIB),
        name=name,
    )


def whole(*dims):
    return pl.BlockSpec(dims, lambda *_: (0,) * len(dims))


def rope(values, table):
    return values * table[0] + pltpu.roll(values, values.shape[-1] // 2, 1) * table[1]


def unrope(values, table):
    return values * table[0] - pltpu.roll(values, values.shape[-1] // 2, 1) * table[1]


def attention_weights(query, key):
    scores = dot(query, key, NT) * (1.0 / math.sqrt(query.shape[-1]))
    raised = jnp.exp(scores - jnp.max(scores, axis=-1, keepdims=True))
    return raised / jnp.sum(raised, axis=-1, keepdims=True)


def attend_body(tokens, gain, w_qkv, w_out, gains, table, normed, raw, value_out, attended, partial, total):
    step = pl.program_id(0)

    @pl.when(step == 0)
    def _():
        x = tokens[...].astype(F32)
        normed[...] = (x * rms(x) * gain[...]).astype(BF)
        total[...] = jnp.zeros_like(total)

    h = normed[...]
    query_raw = dot(h, w_qkv[0], NN)
    key_raw = dot(h, w_qkv[1], NN)
    value = dot(h, w_qkv[2], NN).astype(BF)
    raw[0] = query_raw
    raw[1] = key_raw
    value_out[...] = value
    for at in range(query_raw.shape[1] // LANE):
        cut = slice(at * LANE, (at + 1) * LANE)
        q, k = query_raw[:, cut], key_raw[:, cut]
        query = rope(q * rms(q) * gains[0:1], table).astype(BF)
        key = rope(k * rms(k) * gains[1:2], table).astype(BF)
        weights = attention_weights(query, key).astype(BF)
        attended[:, cut] = dot(weights, value[:, cut], NN).astype(BF)
    total[...] += dot(attended[...], w_out[...], NT)

    @pl.when(step == pl.num_programs(0) - 1)
    def _():
        partial[...] = total[...].astype(BF)


def attend(tokens, gain, w_qkv, w_out, gains, table):
    length, width = tokens.shape
    inner = w_qkv.shape[2]
    cols = inner // SIDE
    return kernel_call(
        attend_body,
        (SIDE,),
        [
            whole(length, width),
            whole(1, width),
            pl.BlockSpec((3, width, cols), lambda i: (0, 0, i)),
            pl.BlockSpec((width, cols), lambda i: (0, i)),
            whole(2, LANE),
            whole(2, length, LANE),
        ],
        [
            whole(length, width),
            pl.BlockSpec((2, length, cols), lambda i: (0, 0, i)),
            pl.BlockSpec((length, cols), lambda i: (0, i)),
            pl.BlockSpec((length, cols), lambda i: (0, i)),
            whole(length, width),
        ],
        [
            shape((length, width), BF),
            shape((2, length, inner), F32),
            shape((length, inner), BF),
            shape((length, inner), BF),
            shape((length, width), BF),
        ],
        [pltpu.VMEM((length, width), F32)],
        name="attend",
    )(tokens, gain, w_qkv, w_out, gains, table)


def attend_back_body(z_index, d_attn, w_out, raw, value_in, gains, table, *outs):
    d_gains = outs[SIDE]
    step = pl.program_id(0)
    parts = ([], [], [])

    @pl.when(step == 0)
    def _():
        d_gains[...] = jnp.zeros_like(d_gains)

    d_attended = dot(d_attn[...], w_out[...], NN).astype(BF)
    for at in range(d_attended.shape[1] // LANE):
        cut = slice(at * LANE, (at + 1) * LANE)
        q, k = raw[0, :, cut], raw[1, :, cut]
        rq, rk = rms(q), rms(k)
        unit_q, unit_k = q * rq, k * rk
        query = rope(unit_q * gains[0:1], table).astype(BF)
        key = rope(unit_k * gains[1:2], table).astype(BF)
        weights = attention_weights(query, key)
        grad = d_attended[:, cut]
        d_value = dot(weights.astype(BF), grad, TN)
        d_weights = dot(grad, value_in[:, cut], NT)
        d_scores = (
            weights * (d_weights - jnp.sum(weights * d_weights, axis=-1, keepdims=True))
        ).astype(BF)
        root = 1.0 / math.sqrt(LANE)
        d_query = unrope(dot(d_scores, key, NN) * root, table)
        d_key = unrope(dot(d_scores, query, TN) * root, table)
        d_gains[0:1] += jnp.sum(d_query * unit_q, axis=0, keepdims=True)
        d_gains[1:2] += jnp.sum(d_key * unit_k, axis=0, keepdims=True)
        wq = d_query * gains[0:1]
        wk = d_key * gains[1:2]
        parts[0].append((rq * (wq - unit_q * jnp.mean(wq * unit_q, axis=-1, keepdims=True))).astype(BF))
        parts[1].append((rk * (wk - unit_k * jnp.mean(wk * unit_k, axis=-1, keepdims=True))).astype(BF))
        parts[2].append(d_value.astype(BF))
    for k in range(SIDE):

        @pl.when((z_index[0] + k) % SIDE == step)
        def _():
            for kind in range(3):
                outs[k][kind] = jnp.concatenate(parts[kind], axis=1)


def attend_back(z_index, d_attn, w_out, raw, value_in, gains, table):
    length, width = d_attn.shape
    inner = w_out.shape[1]
    cols = inner // SIDE
    return kernel_call(
        attend_back_body,
        (SIDE,),
        [
            whole(length, width),
            pl.BlockSpec((width, cols), lambda i, z: (0, i)),
            pl.BlockSpec((2, length, cols), lambda i, z: (0, 0, i)),
            pl.BlockSpec((length, cols), lambda i, z: (0, i)),
            whole(2, LANE),
            whole(2, length, LANE),
        ],
        [whole(3, length, cols)] * SIDE + [whole(2, LANE)],
        [shape((3, length, cols), BF)] * SIDE + [shape((2, LANE), F32)],
        scalars=1,
        name="attend_back",
    )(z_index, d_attn, *held(w_out, raw, value_in, gains, table))


def input_grad_body(z_index, *refs):
    w_qkv, out, total = refs[SIDE:]
    step = pl.program_id(0)

    @pl.when(step == 0)
    def _():
        total[...] = jnp.zeros_like(total)

    for k in range(SIDE):

        @pl.when(step == k)
        def _():
            block = refs[k]
            total[...] += dot(block[0], w_qkv[0], NT) + dot(block[1], w_qkv[1], NT) + dot(block[2], w_qkv[2], NT)

    @pl.when(step == pl.num_programs(0) - 1)
    def _():
        out[...] = total[...].astype(BF)


def input_grad(z_index, d_blocks, w_qkv):
    _, length, cols = d_blocks[0].shape
    width = w_qkv.shape[1]
    return kernel_call(
        input_grad_body,
        (SIDE,),
        [whole(3, length, cols)] * SIDE
        + [pl.BlockSpec((3, width, cols), lambda i, z: (0, 0, lax.rem(z[0] + i, SIDE)))],
        whole(length, width),
        shape((length, width), BF),
        [pltpu.VMEM((length, width), F32)],
        scalars=1,
        name="input_grad",
    )(z_index, *d_blocks, *held(w_qkv))


def routing_body(core, capacity, ids, later, expert_of, cotangent, member_out, select, rows):
    experts = expert_of.shape[1]
    length = ids.shape[1]
    at_expert = lax.broadcasted_iota(jnp.int32, (experts, length), 0)
    member = jnp.zeros((experts, length), F32)
    for j in range(ids.shape[0]):
        member = member + (ids[j : j + 1, :] == at_expert).astype(F32)
    member_out[...] = member.T
    ranks = dot(member.astype(BF), later[...], NN)
    row = lax.broadcasted_iota(jnp.int32, (experts, experts), 0)
    column = lax.broadcasted_iota(jnp.int32, (experts, experts), 1)
    limit = jnp.sum(jnp.where(row == column, capacity[...].astype(F32), 0.0), axis=1, keepdims=True)
    code = jnp.where((member > 0.5) & (ranks < limit), ranks, -1.0).astype(BF)
    slots, half = rows.shape
    depth = slots // experts
    chunk = 8 * depth
    slot = lax.broadcasted_iota(jnp.int32, (chunk, length), 0).astype(F32)
    slot = slot - depth * jnp.floor((slot + 0.5) * (1.0 / depth))
    for which in range(2):

        @pl.when(core[0] == which)
        def _():
            for at in range(0, slots, chunk):
                cut = slice(at, at + chunk)
                hit = (dot(expert_of[cut], code, NN) == slot).astype(F32).astype(BF)
                select[cut] = hit
                rows[cut] = dot(hit, cotangent[:, which * half : (which + 1) * half], NN).astype(BF)


def routing(core, capacity, ids, expert_of, cotangent):
    length, width = cotangent.shape
    slots, experts = expert_of.shape
    later = jnp.asarray(np.triu(np.ones((length, length), np.float32), 1), BF)
    return kernel_call(
        routing_body,
        (1,),
        [
            whole(1, experts),
            whole(*ids.shape),
            whole(length, length),
            whole(slots, experts),
            whole(length, width),
        ],
        [whole(length, experts), whole(slots, length), whole(slots, width // 2)],
        [shape((length, experts), F32), shape((slots, length), BF), main_memory((slots, width // 2), BF)],
        scalars=1,
        name="routing",
    )(core, *held(capacity.reshape(1, experts), ids, later, expert_of, cotangent))


def middle_body(core, tokens, own, peer, gain, select, w_router, member, expert_of,
                middle, normed, probs_out, gates_out, total_out, combine, rows):
    x2 = tokens[...].astype(F32) + (own[...].astype(F32) + peer[...].astype(F32))
    middle[...] = x2
    normed[...] = (x2 * rms(x2) * gain[...]).astype(BF)
    logits = dot(normed[...], w_router[...], NN)
    raised = jnp.exp(logits - jnp.max(logits, axis=-1, keepdims=True))
    probs = raised / jnp.sum(raised, axis=-1, keepdims=True)
    picked = probs * member[...]
    total = jnp.sum(picked, axis=-1, keepdims=True)
    gates = picked / total
    probs_out[...] = probs
    gates_out[...] = gates
    total_out[...] = total
    low = gates.astype(BF)
    half = rows.shape[1] - LANE
    for at in range(0, rows.shape[0], 256):
        cut = slice(at, at + 256)
        spread = dot(expert_of[cut], low, NT) * select[cut].astype(F32)
        combine[cut] = spread.astype(BF)
        gate = jnp.sum(spread, axis=-1, keepdims=True)
        rows[cut, half:] = jnp.broadcast_to(gate, (256, LANE)).astype(BF)
    for which in range(2):

        @pl.when(core[0] == which)
        def _():
            for at in range(0, rows.shape[0], 256):
                rows[at : at + 256, :half] = dot(
                    select[at : at + 256], normed[:, which * half : (which + 1) * half], NN
                ).astype(BF)


def middle_step(core, tokens, own, peer, gain, select, w_router, member, expert_of):
    length, width = tokens.shape
    slots, experts = expert_of.shape
    columns = width // 2 + LANE
    return kernel_call(
        middle_body,
        (1,),
        [whole(length, width)] * 3
        + [whole(1, width), whole(slots, length), whole(width, experts), whole(length, experts), whole(slots, experts)],
        [
            whole(length, width),
            whole(length, width),
            whole(length, experts),
            whole(length, experts),
            whole(length, 1),
            whole(slots, length),
            whole(slots, columns),
        ],
        [
            shape((length, width), F32),
            shape((length, width), BF),
            shape((length, experts), F32),
            shape((length, experts), F32),
            shape((length, 1), F32),
            shape((slots, length), BF),
            main_memory((slots, columns), BF),
        ],
        scalars=1,
        name="middle",
    )(core, *held(tokens), own, peer, *held(gain, select, w_router, member, expert_of))


def gather_back_body(back, combine, select, expert_of, out):
    half = combine.shape[1]
    half = out.shape[1] - LANE
    out[:, :half] = dot(combine[...], back[:, :half], TN)
    high = back[:, half : half + 1].astype(F32)
    low = back[:, half + 1 : half + 2].astype(F32)
    picked = select[...].astype(F32)
    experts = expert_of.shape[1]
    spread = dot((picked * high).astype(BF), expert_of[...], TN) + dot((picked * low).astype(BF), expert_of[...], TN)
    out[:, half : half + experts] = spread
    out[:, half + experts :] = jnp.zeros((out.shape[0], LANE - experts), F32)


def gather_back(back, combine, select, expert_of):
    slots, columns = back.shape
    length = combine.shape[1]
    experts = expert_of.shape[1]
    return kernel_call(
        gather_back_body,
        (1,),
        [whole(slots, columns), whole(slots, length), whole(slots, length), whole(slots, experts)],
        whole(length, columns),
        shape((length, columns), F32),
        name="gather_back",
    )(back, *held(combine, select, expert_of))


def middle_back_body(core, own, peer, probs, gates, total, member, w_router, middle, cotangent, gain,
                     d_logits_out, d_middle, d_attn, d_gain, *d_attn_blocks):
    half = own.shape[1] - LANE
    experts = probs.shape[1]
    d_gates = own[:, half : half + experts] + peer[:, half : half + experts]
    g, p = gates[...], probs[...]
    d_picked = member[...] * (d_gates - jnp.sum(d_gates * g, axis=-1, keepdims=True)) / total[...]
    d_logits = (p * (d_picked - jnp.sum(p * d_picked, axis=-1, keepdims=True))).astype(BF)
    d_logits_out[...] = d_logits
    d_normed = dot(d_logits, w_router[...], NT)
    for which in range(2):

        @pl.when(core[0] == which)
        def _():
            first, second = (own, peer) if which == 0 else (peer, own)
            d_middle[:, :half] = first[:, :half]
            d_middle[:, half:] = second[:, :half]

    d_normed = d_normed + d_middle[...]
    x2 = middle[...]
    scale = rms(x2)
    unit = x2 * scale
    d_gain[...] = jnp.sum(d_normed * unit, axis=0, keepdims=True)
    weighted = d_normed * gain[...]
    value = cotangent[...].astype(F32) + scale * (
        weighted - unit * jnp.mean(weighted * unit, axis=-1, keepdims=True)
    )
    d_middle[...] = value
    low = value.astype(BF)
    d_attn[...] = low
    cut = d_attn_blocks[0].shape[1]
    for which in range(SIDE):

        @pl.when(core[1] == which)
        def _():
            for k in range(SIDE):
                at = (which + k) % SIDE * cut
                d_attn_blocks[k][...] = low[:, at : at + cut]


def middle_back(core, own, peer, probs, gates, total, member, w_router, middle, cotangent, gain):
    length, width = middle.shape
    experts = probs.shape[1]
    columns = own.shape[1]
    return kernel_call(
        middle_back_body,
        (1,),
        [whole(length, columns)] * 2
        + [whole(length, experts)] * 2
        + [whole(length, 1), whole(length, experts), whole(width, experts), whole(length, width), whole(length, width), whole(1, width)],
        [
            whole(length, experts),
            whole(length, width),
            whole(length, width),
            whole(1, width),
        ]
        + [whole(length, width // SIDE)] * SIDE,
        [
            shape((length, experts), BF),
            shape((length, width), F32),
            shape((length, width), BF),
            shape((1, width), F32),
        ]
        + [shape((length, width // SIDE), BF)] * SIDE,
        scalars=1,
        name="middle_back",
    )(core, own, peer, *held(probs, gates, total, member, w_router, middle, cotangent, gain))


def hidden_grad_body(core, own, peer, down_own, down_peer, out):
    half = down_own.shape[1]
    out[...] = dot(own[:, :half], down_own[...], NT) + dot(peer[:, :half], down_peer[...], NT)


ROWS = 256


def hidden_grad(core, own, peer, down):
    slots, columns = own.shape
    hidden, width = down.shape
    half = width // 2
    return kernel_call(
        hidden_grad_body,
        (slots // ROWS,),
        [
            pl.BlockSpec((ROWS, columns), lambda i, c: (i, 0)),
            pl.BlockSpec((ROWS, columns), lambda i, c: (i, 0)),
            pl.BlockSpec((hidden, half), lambda i, c: (0, c[0])),
            pl.BlockSpec((hidden, half), lambda i, c: (0, 1 - c[0])),
        ],
        pl.BlockSpec((ROWS, hidden), lambda i, c: (i, 0)),
        main_memory((slots, hidden), F32),
        scalars=1,
        name="hidden_grad",
    )(core, own, peer, down, down)


def experts_body(core, own, peer, d_hidden, pair_own, pair_peer, acted, d_pair, back_own, back_peer, extra):
    hidden = d_hidden.shape[1]
    half = pair_own.shape[1]
    mine, other = own[:, :half], peer[:, :half]
    gate = dot(mine, pair_own[0], NN) + dot(other, pair_peer[0], NN)
    up = dot(mine, pair_own[1], NN) + dot(other, pair_peer[1], NN)
    sig = 1.0 / (1.0 + jnp.exp(-gate))
    silu = gate * sig
    act = (silu * up).astype(BF)
    acted[...] = act
    d_act = d_hidden[...]
    slot_grad = jnp.sum(d_act * act.astype(F32), axis=-1, keepdims=True)
    high = slot_grad.astype(BF)
    low = (slot_grad - high.astype(F32)).astype(BF)
    at = lax.broadcasted_iota(jnp.int32, extra.shape, 1)
    extra[...] = jnp.where(at == 0, high.astype(F32), jnp.where(at == 1, low.astype(F32), 0.0)).astype(BF)
    d_gate = (d_act * up * sig * (1.0 + gate * (1.0 - sig))).astype(BF)
    d_up = (d_act * silu).astype(BF)
    d_pair[:, :hidden] = d_gate
    d_pair[:, hidden:] = d_up
    back_peer[...] = (dot(d_gate, pair_peer[0], NT) + dot(d_up, pair_peer[1], NT)).astype(BF)
    back_own[...] = (dot(d_gate, pair_own[0], NT) + dot(d_up, pair_own[1], NT)).astype(BF)


def experts_out_body(core, acted, down_own, down_peer, out_own, out_peer):
    out_peer[...] = dot(acted[...], down_peer[...], NN).astype(BF)
    out_own[...] = dot(acted[...], down_own[...], NN).astype(BF)


def experts_out(core, acted, down):
    slots, hidden = acted.shape
    half = down.shape[1] // 2
    rows = lambda n: pl.BlockSpec((ROWS, n), lambda i, c: (i, 0))
    return kernel_call(
        experts_out_body,
        (slots // ROWS,),
        [
            rows(hidden),
            pl.BlockSpec((hidden, half), lambda i, c: (0, c[0])),
            pl.BlockSpec((hidden, half), lambda i, c: (0, 1 - c[0])),
        ],
        [rows(half), rows(half)],
        [shape((slots, half), BF)] * 2,
        scalars=1,
        name="experts_out",
    )(core, acted, down, down)


def experts_step(core, own, peer, d_hidden, pair):
    slots, columns = own.shape
    half = columns - LANE
    hidden = pair.shape[2]
    rows = lambda n: pl.BlockSpec((ROWS, n), lambda i, c: (i, 0))
    return kernel_call(
        experts_body,
        (slots // ROWS,),
        [
            rows(columns),
            rows(columns),
            rows(hidden),
            pl.BlockSpec((2, half, hidden), lambda i, c: (0, c[0], 0)),
            pl.BlockSpec((2, half, hidden), lambda i, c: (0, 1 - c[0], 0)),
        ],
        [rows(hidden), rows(2 * hidden), rows(half), rows(half), rows(LANE)],
        [
            shape((slots, hidden), BF),
            shape((slots, 2 * hidden), BF),
            shape((slots, half), BF),
            shape((slots, half), BF),
            shape((slots, LANE), BF),
        ],
        scalars=1,
        name="experts",
    )(core, *held(own), peer, *held(d_hidden, pair, pair))


def add_pack_body(own, peer, extra, out):
    half = own.shape[1]
    out[:, :half] = (own[...].astype(F32) + peer[...].astype(F32)).astype(BF)
    out[:, half:] = extra[...]


def add_pack(own, peer, extra):
    slots, half = own.shape
    rows = lambda n: pl.BlockSpec((ROWS, n), lambda i: (i, 0))
    return kernel_call(
        add_pack_body,
        (slots // ROWS,),
        [rows(half), rows(half), rows(LANE)],
        rows(half + LANE),
        main_memory((slots, half + LANE), BF),
        name="add_pack",
    )(own, peer, extra)


def expert_grads_body(core, own, peer, grad_own, grad_peer, acted, d_pair, gates, grad_pair, grad_down, pair_low, act_low):
    step = pl.program_id(0)
    hidden = acted.shape[1]

    @pl.when(step == 0)
    def _():
        gate = gates[:, :1].astype(F32)
        pair_low[...] = (d_pair[...].astype(F32) * gate).astype(BF)
        act_low[...] = (acted[...].astype(F32) * gate).astype(BF)

    def part(rows, grads):
        value = dot(rows[...], pair_low[...], TN)
        grad_pair[:, 0, :] = value[:, :hidden]
        grad_pair[:, 1, :] = value[:, hidden:]
        grad_down[...] = dot(act_low[...], grads[...], TN)

    @pl.when(step < SIDE)
    def _():
        part(own, grad_own)

    @pl.when(step >= SIDE)
    def _():
        part(peer, grad_peer)


def expert_grads(core, own, peer, grad_own, grad_peer, acted, d_pair, gates):
    slots, half = grad_own.shape
    hidden = acted.shape[1]
    cut = half // SIDE
    first = pl.BlockSpec((slots, cut), lambda i, c: (0, jnp.minimum(i, SIDE - 1)))
    second = pl.BlockSpec((slots, cut), lambda i, c: (0, jnp.maximum(i - SIDE, 0)))

    def target(i, c):
        return jnp.where(i < SIDE, c[0] * SIDE + i, (1 - c[0]) * SIDE + i - SIDE)

    return kernel_call(
        expert_grads_body,
        (2 * SIDE,),
        [first, second, first, second, whole(slots, hidden), whole(slots, 2 * hidden), pl.BlockSpec((slots, LANE), lambda i, c: (0, half // LANE))],
        [
            pl.BlockSpec((cut, 2, hidden), lambda i, c: (target(i, c), 0, 0)),
            pl.BlockSpec((hidden, cut), lambda i, c: (0, target(i, c))),
        ],
        [shape((2 * half, 2, hidden), F32), shape((hidden, 2 * half), F32)],
        [pltpu.VMEM((slots, 2 * hidden), BF), pltpu.VMEM((slots, hidden), BF)],
        mib=48,
        scalars=1,
        name="expert_grads",
    )(core, own, peer, grad_own, grad_peer, acted, d_pair, gates)


EXTRA = 16


def group_grads_body(core, own, peer, *refs):
    step = pl.program_id(0)
    d_group = refs[:SIDE]
    normed_two, d_logits, d_gain, d_qk, out = refs[SIDE:]
    cols = d_group[0].shape[2]
    targets = out.shape[0]
    rows = out.shape[1] - EXTRA

    def put(value, at):
        for k in range(targets):
            out[k, :rows, at * cols : (at + 1) * cols] = value[k * rows : (k + 1) * rows].astype(BF)

    def part(normed):
        members, length, cut = normed.shape
        left = normed[...].reshape(members * length, cut)
        for which in range(3):
            put(dot(left, jnp.concatenate([block[which] for block in d_group], axis=0), TN), which)

    @pl.when(step < SIDE)
    def _():
        part(own)

    @pl.when(step >= SIDE)
    def _():
        part(peer)

    router = dot(d_logits[...], normed_two[...], TN).astype(BF)
    for k in range(targets):
        cut = slice(k * rows, (k + 1) * rows)
        out[k, rows:, :LANE] = router[:EXTRA, cut]
        out[k, rows:, LANE : 2 * LANE] = router[EXTRA:, cut]
        out[k, rows:, 2 * LANE : 3 * LANE] = jnp.broadcast_to(d_gain[:, cut], (EXTRA, LANE)).astype(BF)
        out[k, rows:, 3 * LANE : 4 * LANE] = jnp.concatenate([d_qk[...]] * (EXTRA // 2), axis=0).astype(BF)
        out[k, rows:, 4 * LANE :] = jnp.zeros((EXTRA, out.shape[2] - 4 * LANE), BF)


def group_grads(core, own, peer, d_group, normed_two, d_logits, d_gain, d_qk):
    members, length, half = own.shape
    cols = d_group[0].shape[2]
    cut = half // SIDE
    places = SIDE * SIDE
    rows = 2 * half // places

    def target(i, c):
        return jnp.where(i < SIDE, c[0] * SIDE + i, (1 - c[0]) * SIDE + i - SIDE)

    return kernel_call(
        group_grads_body,
        (2 * SIDE,),
        [
            pl.BlockSpec((members, length, cut), lambda i, c: (0, 0, jnp.minimum(i, SIDE - 1))),
            pl.BlockSpec((members, length, cut), lambda i, c: (0, 0, jnp.maximum(i - SIDE, 0))),
        ]
        + [whole(3, length, cols)] * SIDE
        + [
            pl.BlockSpec((length, cut), lambda i, c: (0, target(i, c))),
            whole(length, d_logits.shape[1]),
            pl.BlockSpec((1, cut), lambda i, c: (0, target(i, c))),
            whole(2, LANE),
        ],
        pl.BlockSpec((cut // rows, rows + EXTRA, 3 * cols), lambda i, c: (target(i, c), 0, 0)),
        main_memory((places, rows + EXTRA, 3 * cols), BF),
        scalars=1,
        name="group_grads",
    )(core, *held(own, peer), *d_group, *held(normed_two), d_logits, d_gain, d_qk)


def out_grads_body(*refs):
    left = jnp.concatenate([part[...] for part in refs[:SIDE]], axis=0)
    right = jnp.concatenate([part[...] for part in refs[SIDE : 2 * SIDE]], axis=0)
    refs[2 * SIDE][...] = dot(left, right, TN).astype(BF)


def out_grads(d_attn, attended):
    length, rows = d_attn[0].shape
    inner = attended[0].shape[1]
    return kernel_call(
        out_grads_body,
        (1,),
        [whole(length, rows)] * SIDE + [whole(length, inner)] * SIDE,
        whole(rows, inner),
        shape((rows, inner), BF),
        name="out_grads",
    )(*d_attn, *attended)


def sum_arrived_body(rows, z_index, arrived, *outs):
    value = arrived[0].astype(F32)
    for k in range(1, arrived.shape[0]):
        value = value + arrived[k].astype(F32)
    value = value.astype(BF)
    main = SIDE * rows
    for which in range(SIDE):

        @pl.when(z_index[0] == which)
        def _():
            for step in range(SIDE):
                at = (which + step) % SIDE * rows
                outs[step][:rows] = value[at : at + rows]

    for step in range(SIDE):
        outs[step][rows:] = value[main:]


def sum_arrived(z_index, arrived, rows):
    places, height, columns = arrived.shape
    cols = columns // 3
    return kernel_call(
        functools.partial(sum_arrived_body, rows),
        (3,),
        [pl.BlockSpec((places, height, cols), lambda i, z: (0, 0, i))],
        [pl.BlockSpec((rows + EXTRA, cols), lambda i, z: (0, i))] * SIDE,
        [shape((rows + EXTRA, columns), BF)] * SIDE,
        scalars=1,
        name="sum_arrived",
    )(z_index, arrived)


def finish_body(z_index, *refs):
    parts, w_here, grad, small = refs[:SIDE], refs[SIDE], refs[SIDE + 1], refs[SIDE + 2]
    rows = grad.shape[1]
    cols = parts[0].shape[1] // 3
    for which in range(SIDE):

        @pl.when(z_index[0] == which)
        def _():
            ordered = [parts[(which - source) % SIDE] for source in range(SIDE)]
            for source in range(SIDE):
                for kind in range(3):
                    grad[kind, :, source * cols : (source + 1) * cols] = ordered[source][
                        :rows, kind * cols : (kind + 1) * cols
                    ].astype(F32)
            extra = [part[rows:].astype(F32) for part in ordered]
            total = (extra[0] + extra[1]) + (extra[2] + extra[3])
            small[:EXTRA] = total[:, :LANE]
            small[EXTRA : 2 * EXTRA] = total[:, LANE : 2 * LANE]
            small[2 * EXTRA + 1 : 2 * EXTRA + 2] = total[0:1, 2 * LANE : 3 * LANE]
            small[2 * EXTRA + 2 : 2 * EXTRA + 4] = total[0:2, 3 * LANE : 4 * LANE]

    product = jnp.sum(grad[0] * w_here[0].astype(F32) + grad[1] * w_here[1].astype(F32) + grad[2] * w_here[2].astype(F32), axis=-1, keepdims=True)
    at_row = lax.broadcasted_iota(jnp.int32, (rows, LANE), 0)
    at_lane = lax.broadcasted_iota(jnp.int32, (rows, LANE), 1)
    small[2 * EXTRA : 2 * EXTRA + 1] = jnp.sum(jnp.where(at_row == at_lane, product, 0.0), axis=0, keepdims=True)
    small[2 * EXTRA + 4 :] = jnp.zeros((small.shape[0] - 2 * EXTRA - 4, LANE), F32)


def finish(z_index, parts, w_here):
    kinds, rows, inner = w_here.shape
    height, columns = parts[0].shape
    return kernel_call(
        finish_body,
        (1,),
        [whole(height, columns)] * SIDE + [whole(kinds, rows, inner)],
        [whole(kinds, rows, inner), whole(2 * EXTRA + 8, LANE)],
        [shape((kinds, rows, inner), F32), shape((2 * EXTRA + 8, LANE), F32)],
        scalars=1,
        name="finish",
    )(z_index, *parts, w_here)


def on_device(
    tokens,
    expert_ids,
    capacity,
    gain_attn,
    w_qkv,
    qk_gain,
    w_out,
    gain_ffn,
    w_router,
    w_gate_up,
    w_down,
    cotangent,
):
    length, width = tokens.shape
    expert_count = capacity.shape[0]
    slot_count = length * expert_ids.shape[1] // expert_count
    slots = expert_count * slot_count
    inner = w_qkv.shape[2]
    half = width // 2
    cols = inner // SIDE
    core_index = lax.axis_index("tensor")
    core = core_index.astype(jnp.int32).reshape(1)
    place = [lax.axis_index(a) for a in AXES]
    dp_index = (place[0] * SIDE + place[1]) * SIDE + place[2]
    rows_here_count = width // SIDE**3

    def own_half(value):
        return lax.dynamic_slice_in_dim(value, core_index * half, half, axis=-1)

    expert_of = jnp.asarray(np.repeat(np.eye(expert_count, dtype=np.float32), slot_count, 0), BF)

    def to_owners(rows):
        columns = rows.shape[1]
        return exchange(rows.reshape(expert_count, slot_count, columns), AXES).reshape(slots, columns)

    member, select, grad_send = routing(core, capacity, expert_ids.T, expert_of, cotangent)
    grad_own = to_owners(grad_send)

    table = jnp.asarray(rotary(length, LANE // 2))
    gains = qk_gain.astype(F32)
    gain_one = gain_attn.astype(F32)
    gain_two = gain_ffn.astype(F32).reshape(1, width)
    w_parts = w_qkv.transpose(1, 0, 2)
    normed_one, raw, value_in, attended, partial = attend(
        tokens, gain_one.reshape(1, width), w_parts, w_out, gains, table
    )
    partial_peer = swap(partial)
    middle, normed_two, probs, gates, picked_total, combine, rows_send = middle_step(
        core, tokens, partial, partial_peer, gain_two, select, w_router, member, expert_of
    )
    rows_own = to_owners(rows_send)

    normed_early, attended_late, pair, grad_late, down, _ = together(
        own_half(normed_one), attended, w_gate_up, grad_own, w_down, rows_send
    )
    down = down[0]
    pair = pair[0].transpose(1, 0, 2)
    grad_peer = swap(grad_late)
    d_hidden = hidden_grad(core, grad_late, grad_peer, down)
    rows_own, d_hidden, pair, attended_late = together(rows_own, d_hidden, pair, attended_late)
    attended_group = share(attended_late, "y")
    rows_peer = swap(rows_own)
    acted, d_pair, back_own, back_peer, extra = experts_step(core, rows_own, rows_peer, d_hidden, pair)
    back_peer, normed_early, *attended_group = together(back_peer, normed_early, *attended_group)
    from_one, from_three = shift(normed_early, "z", 1), shift(normed_early, "z", 3)
    back_send = add_pack(back_own, swap(back_peer), extra)
    out_own, out_peer = experts_out(core, acted, down)
    back_send, out_own, out_peer, from_one, from_three = together(
        back_send, out_own, out_peer, from_one, from_three
    )
    back = to_owners(back_send)

    acted_late, own_late, peer_late, _ = together(acted, rows_own, rows_peer, back_send)
    grad_gate_up, grad_down = expert_grads(
        core, own_late, peer_late, grad_late, grad_peer, acted_late, d_pair, own_late
    )
    returned = (out_own.astype(F32) + swap(out_peer).astype(F32)).astype(BF)
    returned, grad_gate_up, grad_down = together(returned, grad_gate_up, grad_down)
    returned = to_owners(returned)
    from_two = shift(from_one, "z", 1)

    gathered = gather_back(back, combine, select, expert_of)
    core_y = jnp.stack([core[0], place[0].astype(jnp.int32)])
    d_logits, d_middle, d_attn, gain_two_local, *d_attn_blocks = middle_back(
        core_y, gathered, swap(gathered), probs, gates, picked_total, member, w_router, middle, cotangent, gain_two
    )

    z_index = place[2].astype(jnp.int32).reshape(1)
    *d_blocks, grad_qk = attend_back(z_index, d_attn, w_out, raw, value_in, gains, table)
    from_two, *d_blocks = together(from_two, *d_blocks)
    d_group = send_steps(d_blocks, "z")
    normed_group = jnp.stack([normed_early, from_one, from_two, from_three])
    normed_group, normed_group_peer, returned, *d_group = together(
        normed_group, swap(normed_group), returned, *d_group
    )

    columns_here = expert_count // 2
    my_logits = lax.dynamic_slice_in_dim(d_logits, core_index * columns_here, columns_here, axis=1)
    partial_grads = group_grads(
        core,
        normed_group,
        normed_group_peer,
        d_group,
        normed_two,
        my_logits,
        gain_two_local,
        grad_qk,
    )
    d_attn_blocks, _ = together(d_attn_blocks, d_blocks)
    d_attn_group = send_steps(d_attn_blocks, "y")
    partial_grads, *d_attn_group = together(partial_grads, *d_attn_group)
    arrived = exchange(partial_grads, ("y", "x"))
    d_attn_group, late_blocks, late_returned, _ = together(d_attn_group, d_blocks, returned, partial_grads)

    grad_out = out_grads(d_attn_group, attended_group)

    grad_out = send_blocks(grad_out.reshape(SIDE, SIDE, rows_here_count, inner), "z", 1)

    d_one = input_grad(z_index, late_blocks, w_parts)
    d_one = d_one.astype(F32) + swap(d_one).astype(F32)

    residual_in = tokens.astype(F32)
    scale_one = rms(residual_in)
    unit_one = residual_in * scale_one
    weighted = d_one * gain_one
    grad_input = d_middle + scale_one * (
        weighted - unit_one * jnp.mean(weighted * unit_one, axis=-1, keepdims=True)
    )

    mix_own = dot(combine, late_returned, TN)
    result_own = (own_half(middle) + mix_own).astype(BF)
    output = side_by_side(result_own, swap(result_own), core_index)

    arrived, grad_input, output, grad_out = together(arrived, grad_input, output, grad_out)
    grad_out = sum(part.astype(F32) for part in grad_out).astype(BF)
    grad_out = sum(part.astype(F32) for part in send_blocks(grad_out, "x", 0))
    parts = send_steps(sum_arrived(z_index, arrived, rows_here_count), "z")
    w_here = lax.dynamic_slice_in_dim(w_parts, dp_index * rows_here_count, rows_here_count, axis=1)
    grad_qkv, small = finish(z_index, parts, w_here)
    grad_qkv = grad_qkv.transpose(1, 0, 2)
    small_peer = swap(small)
    gain_here = lax.dynamic_slice_in_dim(gain_one, dp_index * rows_here_count, rows_here_count, axis=0)
    grad_gain_one = (small[2 * EXTRA] + small_peer[2 * EXTRA])[:rows_here_count] / gain_here
    cut = lambda value: lax.dynamic_slice_in_dim(value, place[2] * rows_here_count, rows_here_count, axis=-1)
    grad_router = jnp.where(
        core_index == 0,
        jnp.concatenate([small[: 2 * EXTRA], small_peer[: 2 * EXTRA]], axis=0),
        jnp.concatenate([small_peer[: 2 * EXTRA], small[: 2 * EXTRA]], axis=0),
    )
    grad_router = cut(grad_router).T
    grad_gain_two = cut(small[2 * EXTRA + 1])
    grad_qk = small[2 * EXTRA + 2 : 2 * EXTRA + 4] + small_peer[2 * EXTRA + 2 : 2 * EXTRA + 4]

    return (
        output,
        grad_input,
        grad_gain_one,
        grad_qkv,
        grad_qk,
        grad_out,
        grad_gain_two,
        grad_router,
        grad_gate_up[None],
        grad_down[None],
    )


def solution(mesh):
    names = AXES + ("tensor",)
    torus = Mesh(mesh.devices.reshape(SIDE, SIDE, SIDE, 2), names)
    return jax.shard_map(
        on_device,
        mesh=torus,
        in_specs=(
            P(AXES, None),
            P(AXES, None),
            P(),
            P(),
            P(None, None, "tensor"),
            P(),
            P(None, "tensor"),
            P(),
            P(),
            P(AXES, None, None, "tensor"),
            P(AXES, "tensor", None),
            P(AXES, None),
        ),
        out_specs=(
            P(AXES, None),
            P(AXES, None),
            P(AXES),
            P(AXES, None, "tensor"),
            P(),
            P(AXES, "tensor"),
            P(AXES),
            P(AXES, None),
            P(AXES, None, None, "tensor"),
            P(AXES, "tensor", None),
        ),
        check_vma=False,
    )
```

```python
import functools
import math

import jax
import jax.numpy as jnp
import numpy as np
from jax import lax
from jax.experimental import pallas as pl
from jax.experimental.pallas import tpu as pltpu
from jax.sharding import Mesh
from jax.sharding import PartitionSpec as P

AXES = ("y", "x", "z")
SIDE = 4
LANE = 128
BF = jnp.bfloat16
F32 = jnp.float32
MIB = 1 << 20


def dot(a, b, dims):
    return lax.dot_general(a, b, (dims, ((), ())), preferred_element_type=F32)


NN = ((1,), (0,))
NT = ((1,), (1,))
TN = ((0,), (0,))


def rms(values):
    return lax.rsqrt(jnp.mean(values * values, axis=-1, keepdims=True) + 1e-06)


def rotary(length, half_dim):
    position = np.arange(length, dtype=np.float32)
    inverse = np.float32(50000.0) ** (-np.arange(half_dim, dtype=np.float32) / np.float32(half_dim))
    angles = position[:, None] * inverse[None, :].astype(np.float32)
    cosine = np.cos(angles).astype(np.float32)
    sine = np.sin(angles).astype(np.float32)
    return np.stack([np.concatenate([cosine, cosine], 1), np.concatenate([-sine, sine], 1)])


def swap(value):
    return lax.ppermute(value, "tensor", [(0, 1), (1, 0)])


def shift(value, axis, step):
    return lax.ppermute(value, axis, [(i, (i + step) % SIDE) for i in range(SIDE)])


def side_by_side(own, peer, core):
    return jnp.where(
        core == 0,
        jnp.concatenate([own, peer], axis=-1),
        jnp.concatenate([peer, own], axis=-1),
    )


def block_at(value, index, dim):
    return lax.dynamic_index_in_dim(value, index, dim, keepdims=False)


def together(*values):
    return lax.optimization_barrier(values)


def share(value, axis):
    return [value] + [shift(value, axis, step) for step in (1, 2, 3)]


def send_blocks(value, axis, dim):
    here = lax.axis_index(axis)
    own = block_at(value, here, dim)
    return [own] + [shift(block_at(value, (here + step) % SIDE, dim), axis, step) for step in (1, 2, 3)]


def send_steps(blocks, axis):
    return [blocks[0]] + [shift(blocks[step], axis, step) for step in (1, 2, 3)]


def exchange(value, axes):
    return lax.all_to_all(value, axes, split_axis=0, concat_axis=0, tiled=True)


def shape(dims, kind):
    return jax.ShapeDtypeStruct(dims, kind)


def main_memory(dims, kind):
    return pltpu.HBM(dims, kind)


def held(*values):
    return [pltpu.with_memory_space_constraint(value, pltpu.HBM) for value in values]


def kernel_call(body, grid, ins, outs, out_shapes, scratch=(), mib=40, scalars=0, name=None):
    return pl.pallas_call(
        body,
        grid_spec=pltpu.PrefetchScalarGridSpec(
            num_scalar_prefetch=scalars, grid=grid, in_specs=ins, out_specs=outs, scratch_shapes=list(scratch)
        ),
        out_shape=out_shapes,
        compiler_params=pltpu.CompilerParams(vmem_limit_bytes=mib * MIB),
        name=name,
    )


def whole(*dims):
    return pl.BlockSpec(dims, lambda *_: (0,) * len(dims))


def rope(values, table):
    return values * table[0] + pltpu.roll(values, values.shape[-1] // 2, 1) * table[1]


def unrope(values, table):
    return values * table[0] - pltpu.roll(values, values.shape[-1] // 2, 1) * table[1]


def attention_weights(query, key):
    scores = dot(query, key, NT) * (1.0 / math.sqrt(query.shape[-1]))
    raised = jnp.exp(scores - jnp.max(scores, axis=-1, keepdims=True))
    return raised / jnp.sum(raised, axis=-1, keepdims=True)


def attend_body(tokens, gain, w_qkv, w_out, gains, table, normed, raw, value_out, attended, partial, total):
    step = pl.program_id(0)

    @pl.when(step == 0)
    def _():
        x = tokens[...].astype(F32)
        normed[...] = (x * rms(x) * gain[...]).astype(BF)
        total[...] = jnp.zeros_like(total)

    h = normed[...]
    query_raw = dot(h, w_qkv[0], NN)
    key_raw = dot(h, w_qkv[1], NN)
    value = dot(h, w_qkv[2], NN).astype(BF)
    raw[0] = query_raw
    raw[1] = key_raw
    value_out[...] = value
    for at in range(query_raw.shape[1] // LANE):
        cut = slice(at * LANE, (at + 1) * LANE)
        q, k = query_raw[:, cut], key_raw[:, cut]
        query = rope(q * rms(q) * gains[0:1], table).astype(BF)
        key = rope(k * rms(k) * gains[1:2], table).astype(BF)
        weights = attention_weights(query, key).astype(BF)
        attended[:, cut] = dot(weights, value[:, cut], NN).astype(BF)
    total[...] += dot(attended[...], w_out[...], NT)

    @pl.when(step == pl.num_programs(0) - 1)
    def _():
        partial[...] = total[...].astype(BF)


def attend(tokens, gain, w_qkv, w_out, gains, table):
    length, width = tokens.shape
    inner = w_qkv.shape[2]
    cols = inner // SIDE
    return kernel_call(
        attend_body,
        (SIDE,),
        [
            whole(length, width),
            whole(1, width),
            pl.BlockSpec((3, width, cols), lambda i: (0, 0, i)),
            pl.BlockSpec((width, cols), lambda i: (0, i)),
            whole(2, LANE),
            whole(2, length, LANE),
        ],
        [
            whole(length, width),
            pl.BlockSpec((2, length, cols), lambda i: (0, 0, i)),
            pl.BlockSpec((length, cols), lambda i: (0, i)),
            pl.BlockSpec((length, cols), lambda i: (0, i)),
            whole(length, width),
        ],
        [
            shape((length, width), BF),
            shape((2, length, inner), F32),
            shape((length, inner), BF),
            shape((length, inner), BF),
            shape((length, width), BF),
        ],
        [pltpu.VMEM((length, width), F32)],
        name="attend",
    )(tokens, gain, w_qkv, w_out, gains, table)


def attend_back_body(z_index, d_attn, w_out, raw, value_in, gains, table, *outs):
    d_gains = outs[SIDE]
    step = pl.program_id(0)
    parts = ([], [], [])

    @pl.when(step == 0)
    def _():
        d_gains[...] = jnp.zeros_like(d_gains)

    d_attended = dot(d_attn[...], w_out[...], NN).astype(BF)
    for at in range(d_attended.shape[1] // LANE):
        cut = slice(at * LANE, (at + 1) * LANE)
        q, k = raw[0, :, cut], raw[1, :, cut]
        rq, rk = rms(q), rms(k)
        unit_q, unit_k = q * rq, k * rk
        query = rope(unit_q * gains[0:1], table).astype(BF)
        key = rope(unit_k * gains[1:2], table).astype(BF)
        weights = attention_weights(query, key)
        grad = d_attended[:, cut]
        d_value = dot(weights.astype(BF), grad, TN)
        d_weights = dot(grad, value_in[:, cut], NT)
        d_scores = (
            weights * (d_weights - jnp.sum(weights * d_weights, axis=-1, keepdims=True))
        ).astype(BF)
        root = 1.0 / math.sqrt(LANE)
        d_query = unrope(dot(d_scores, key, NN) * root, table)
        d_key = unrope(dot(d_scores, query, TN) * root, table)
        d_gains[0:1] += jnp.sum(d_query * unit_q, axis=0, keepdims=True)
        d_gains[1:2] += jnp.sum(d_key * unit_k, axis=0, keepdims=True)
        wq = d_query * gains[0:1]
        wk = d_key * gains[1:2]
        parts[0].append((rq * (wq - unit_q * jnp.mean(wq * unit_q, axis=-1, keepdims=True))).astype(BF))
        parts[1].append((rk * (wk - unit_k * jnp.mean(wk * unit_k, axis=-1, keepdims=True))).astype(BF))
        parts[2].append(d_value.astype(BF))
    for k in range(SIDE):

        @pl.when((z_index[0] + k) % SIDE == step)
        def _():
            for kind in range(3):
                outs[k][kind] = jnp.concatenate(parts[kind], axis=1)


def attend_back(z_index, d_attn, w_out, raw, value_in, gains, table):
    length, width = d_attn.shape
    inner = w_out.shape[1]
    cols = inner // SIDE
    return kernel_call(
        attend_back_body,
        (SIDE,),
        [
            whole(length, width),
            pl.BlockSpec((width, cols), lambda i, z: (0, i)),
            pl.BlockSpec((2, length, cols), lambda i, z: (0, 0, i)),
            pl.BlockSpec((length, cols), lambda i, z: (0, i)),
            whole(2, LANE),
            whole(2, length, LANE),
        ],
        [whole(3, length, cols)] * SIDE + [whole(2, LANE)],
        [shape((3, length, cols), BF)] * SIDE + [shape((2, LANE), F32)],
        scalars=1,
        name="attend_back",
    )(z_index, d_attn, *held(w_out, raw, value_in, gains, table))


def input_grad_body(z_index, *refs):
    w_qkv, out, total = refs[SIDE:]
    step = pl.program_id(0)

    @pl.when(step == 0)
    def _():
        total[...] = jnp.zeros_like(total)

    for k in range(SIDE):

        @pl.when(step == k)
        def _():
            block = refs[k]
            total[...] += dot(block[0], w_qkv[0], NT) + dot(block[1], w_qkv[1], NT) + dot(block[2], w_qkv[2], NT)

    @pl.when(step == pl.num_programs(0) - 1)
    def _():
        out[...] = total[...].astype(BF)


def input_grad(z_index, d_blocks, w_qkv):
    _, length, cols = d_blocks[0].shape
    width = w_qkv.shape[1]
    return kernel_call(
        input_grad_body,
        (SIDE,),
        [whole(3, length, cols)] * SIDE
        + [pl.BlockSpec((3, width, cols), lambda i, z: (0, 0, lax.rem(z[0] + i, SIDE)))],
        whole(length, width),
        shape((length, width), BF),
        [pltpu.VMEM((length, width), F32)],
        scalars=1,
        name="input_grad",
    )(z_index, *d_blocks, *held(w_qkv))


def routing_body(core, capacity, ids, later, expert_of, cotangent, member_out, select, rows):
    experts = expert_of.shape[1]
    length = ids.shape[1]
    at_expert = lax.broadcasted_iota(jnp.int32, (experts, length), 0)
    member = jnp.zeros((experts, length), F32)
    for j in range(ids.shape[0]):
        member = member + (ids[j : j + 1, :] == at_expert).astype(F32)
    member_out[...] = member.T
    ranks = dot(member.astype(BF), later[...], NN)
    row = lax.broadcasted_iota(jnp.int32, (experts, experts), 0)
    column = lax.broadcasted_iota(jnp.int32, (experts, experts), 1)
    limit = jnp.sum(jnp.where(row == column, capacity[...].astype(F32), 0.0), axis=1, keepdims=True)
    code = jnp.where((member > 0.5) & (ranks < limit), ranks, -1.0).astype(BF)
    slots, half = rows.shape
    depth = slots // experts
    chunk = 8 * depth
    slot = lax.broadcasted_iota(jnp.int32, (chunk, length), 0).astype(F32)
    slot = slot - depth * jnp.floor((slot + 0.5) * (1.0 / depth))
    for which in range(2):

        @pl.when(core[0] == which)
        def _():
            for at in range(0, slots, chunk):
                cut = slice(at, at + chunk)
                hit = (dot(expert_of[cut], code, NN) == slot).astype(F32).astype(BF)
                select[cut] = hit
                rows[cut] = dot(hit, cotangent[:, which * half : (which + 1) * half], NN).astype(BF)


def routing(core, capacity, ids, expert_of, cotangent):
    length, width = cotangent.shape
    slots, experts = expert_of.shape
    later = jnp.asarray(np.triu(np.ones((length, length), np.float32), 1), BF)
    return kernel_call(
        routing_body,
        (1,),
        [
            whole(1, experts),
            whole(*ids.shape),
            whole(length, length),
            whole(slots, experts),
            whole(length, width),
        ],
        [whole(length, experts), whole(slots, length), whole(slots, width // 2)],
        [shape((length, experts), F32), main_memory((slots, length), BF), main_memory((slots, width // 2), BF)],
        scalars=1,
        name="routing",
    )(core, *held(capacity.reshape(1, experts), ids, later, expert_of, cotangent))


def middle_body(core, tokens, own, peer, gain, select, w_router, member, expert_of,
                middle, normed, probs_out, gates_out, total_out, combine, rows):
    x2 = tokens[...].astype(F32) + (own[...].astype(F32) + peer[...].astype(F32))
    middle[...] = x2
    normed[...] = (x2 * rms(x2) * gain[...]).astype(BF)
    logits = dot(normed[...], w_router[...], NN)
    raised = jnp.exp(logits - jnp.max(logits, axis=-1, keepdims=True))
    probs = raised / jnp.sum(raised, axis=-1, keepdims=True)
    picked = probs * member[...]
    total = jnp.sum(picked, axis=-1, keepdims=True)
    gates = picked / total
    probs_out[...] = probs
    gates_out[...] = gates
    total_out[...] = total
    low = gates.astype(BF)
    half = rows.shape[1] - LANE
    for at in range(0, rows.shape[0], 256):
        cut = slice(at, at + 256)
        spread = dot(expert_of[cut], low, NT) * select[cut].astype(F32)
        combine[cut] = spread.astype(BF)
        gate = jnp.sum(spread, axis=-1, keepdims=True)
        rows[cut, half:] = jnp.broadcast_to(gate, (256, LANE)).astype(BF)
    for which in range(2):

        @pl.when(core[0] == which)
        def _():
            for at in range(0, rows.shape[0], 256):
                rows[at : at + 256, :half] = dot(
                    select[at : at + 256], normed[:, which * half : (which + 1) * half], NN
                ).astype(BF)


def middle_step(core, tokens, own, peer, gain, select, w_router, member, expert_of):
    length, width = tokens.shape
    slots, experts = expert_of.shape
    columns = width // 2 + LANE
    return kernel_call(
        middle_body,
        (1,),
        [whole(length, width)] * 3
        + [whole(1, width), whole(slots, length), whole(width, experts), whole(length, experts), whole(slots, experts)],
        [
            whole(length, width),
            whole(length, width),
            whole(length, experts),
            whole(length, experts),
            whole(length, 1),
            whole(slots, length),
            whole(slots, columns),
        ],
        [
            main_memory((length, width), F32),
            main_memory((length, width), BF),
            shape((length, experts), F32),
            shape((length, experts), F32),
            shape((length, 1), F32),
            main_memory((slots, length), BF),
            main_memory((slots, columns), BF),
        ],
        scalars=1,
        name="middle",
    )(core, *held(tokens), own, peer, *held(gain, select, w_router, member, expert_of))


def gather_back_body(back, combine, select, expert_of, out):
    half = combine.shape[1]
    half = out.shape[1] - LANE
    out[:, :half] = dot(combine[...], back[:, :half], TN)
    high = back[:, half : half + 1].astype(F32)
    low = back[:, half + 1 : half + 2].astype(F32)
    picked = select[...].astype(F32)
    experts = expert_of.shape[1]
    spread = dot((picked * high).astype(BF), expert_of[...], TN) + dot((picked * low).astype(BF), expert_of[...], TN)
    out[:, half : half + experts] = spread
    out[:, half + experts :] = jnp.zeros((out.shape[0], LANE - experts), F32)


def gather_back(back, combine, select, expert_of):
    slots, columns = back.shape
    length = combine.shape[1]
    experts = expert_of.shape[1]
    return kernel_call(
        gather_back_body,
        (1,),
        [whole(slots, columns), whole(slots, length), whole(slots, length), whole(slots, experts)],
        whole(length, columns),
        shape((length, columns), F32),
        name="gather_back",
    )(back, *held(combine, select, expert_of))


def middle_back_body(core, own, peer, probs, gates, total, member, w_router, middle, cotangent, gain,
                     d_logits_out, d_middle, d_attn, d_gain, *d_attn_blocks):
    half = own.shape[1] - LANE
    experts = probs.shape[1]
    d_gates = own[:, half : half + experts] + peer[:, half : half + experts]
    g, p = gates[...], probs[...]
    d_picked = member[...] * (d_gates - jnp.sum(d_gates * g, axis=-1, keepdims=True)) / total[...]
    d_logits = (p * (d_picked - jnp.sum(p * d_picked, axis=-1, keepdims=True))).astype(BF)
    d_logits_out[...] = d_logits
    d_normed = dot(d_logits, w_router[...], NT)
    for which in range(2):

        @pl.when(core[0] == which)
        def _():
            first, second = (own, peer) if which == 0 else (peer, own)
            d_middle[:, :half] = first[:, :half]
            d_middle[:, half:] = second[:, :half]

    d_normed = d_normed + d_middle[...]
    x2 = middle[...]
    scale = rms(x2)
    unit = x2 * scale
    d_gain[...] = jnp.sum(d_normed * unit, axis=0, keepdims=True)
    weighted = d_normed * gain[...]
    value = cotangent[...].astype(F32) + scale * (
        weighted - unit * jnp.mean(weighted * unit, axis=-1, keepdims=True)
    )
    d_middle[...] = value
    low = value.astype(BF)
    d_attn[...] = low
    cut = d_attn_blocks[0].shape[1]
    for which in range(SIDE):

        @pl.when(core[1] == which)
        def _():
            for k in range(SIDE):
                at = (which + k) % SIDE * cut
                d_attn_blocks[k][...] = low[:, at : at + cut]


def middle_back(core, own, peer, probs, gates, total, member, w_router, middle, cotangent, gain):
    length, width = middle.shape
    experts = probs.shape[1]
    columns = own.shape[1]
    return kernel_call(
        middle_back_body,
        (1,),
        [whole(length, columns)] * 2
        + [whole(length, experts)] * 2
        + [whole(length, 1), whole(length, experts), whole(width, experts), whole(length, width), whole(length, width), whole(1, width)],
        [
            whole(length, experts),
            whole(length, width),
            whole(length, width),
            whole(1, width),
        ]
        + [whole(length, width // SIDE)] * SIDE,
        [
            shape((length, experts), BF),
            shape((length, width), F32),
            shape((length, width), BF),
            shape((1, width), F32),
        ]
        + [shape((length, width // SIDE), BF)] * SIDE,
        scalars=1,
        name="middle_back",
    )(core, *held(own, peer, probs, gates, total, member, w_router, middle, cotangent, gain))


def hidden_grad_body(core, own, peer, down_own, down_peer, out):
    half = down_own.shape[1]
    out[...] = dot(own[:, :half], down_own[...], NT) + dot(peer[:, :half], down_peer[...], NT)


ROWS = 256


def hidden_grad(core, own, peer, down):
    slots, columns = own.shape
    hidden, width = down.shape
    half = width // 2
    return kernel_call(
        hidden_grad_body,
        (slots // ROWS,),
        [
            pl.BlockSpec((ROWS, columns), lambda i, c: (i, 0)),
            pl.BlockSpec((ROWS, columns), lambda i, c: (i, 0)),
            pl.BlockSpec((hidden, half), lambda i, c: (0, c[0])),
            pl.BlockSpec((hidden, half), lambda i, c: (0, 1 - c[0])),
        ],
        pl.BlockSpec((ROWS, hidden), lambda i, c: (i, 0)),
        main_memory((slots, hidden), F32),
        scalars=1,
        name="hidden_grad",
    )(core, *held(own, peer, down, down))


def experts_body(core, own, peer, d_hidden, pair_own, pair_peer, acted, d_pair, back_own, back_peer, extra):
    hidden = d_hidden.shape[1]
    half = pair_own.shape[1]
    mine, other = own[:, :half], peer[:, :half]
    gate = dot(mine, pair_own[0], NN) + dot(other, pair_peer[0], NN)
    up = dot(mine, pair_own[1], NN) + dot(other, pair_peer[1], NN)
    sig = 1.0 / (1.0 + jnp.exp(-gate))
    silu = gate * sig
    act = (silu * up).astype(BF)
    acted[...] = act
    d_act = d_hidden[...]
    slot_grad = jnp.sum(d_act * act.astype(F32), axis=-1, keepdims=True)
    high = slot_grad.astype(BF)
    low = (slot_grad - high.astype(F32)).astype(BF)
    at = lax.broadcasted_iota(jnp.int32, extra.shape, 1)
    extra[...] = jnp.where(at == 0, high.astype(F32), jnp.where(at == 1, low.astype(F32), 0.0)).astype(BF)
    d_gate = (d_act * up * sig * (1.0 + gate * (1.0 - sig))).astype(BF)
    d_up = (d_act * silu).astype(BF)
    d_pair[:, :hidden] = d_gate
    d_pair[:, hidden:] = d_up
    back_peer[...] = (dot(d_gate, pair_peer[0], NT) + dot(d_up, pair_peer[1], NT)).astype(BF)
    back_own[...] = (dot(d_gate, pair_own[0], NT) + dot(d_up, pair_own[1], NT)).astype(BF)


def experts_out_body(core, acted, down_own, down_peer, out_own, out_peer):
    out_peer[...] = dot(acted[...], down_peer[...], NN).astype(BF)
    out_own[...] = dot(acted[...], down_own[...], NN).astype(BF)


def experts_out(core, acted, down):
    slots, hidden = acted.shape
    half = down.shape[1] // 2
    rows = lambda n: pl.BlockSpec((ROWS, n), lambda i, c: (i, 0))
    return kernel_call(
        experts_out_body,
        (slots // ROWS,),
        [
            rows(hidden),
            pl.BlockSpec((hidden, half), lambda i, c: (0, c[0])),
            pl.BlockSpec((hidden, half), lambda i, c: (0, 1 - c[0])),
        ],
        [rows(half), rows(half)],
        [main_memory((slots, half), BF)] * 2,
        scalars=1,
        name="experts_out",
    )(core, *held(acted, down, down))


def experts_step(core, own, peer, d_hidden, pair):
    slots, columns = own.shape
    half = columns - LANE
    hidden = pair.shape[2]
    rows = lambda n: pl.BlockSpec((ROWS, n), lambda i, c: (i, 0))
    return kernel_call(
        experts_body,
        (slots // ROWS,),
        [
            rows(columns),
            rows(columns),
            rows(hidden),
            pl.BlockSpec((2, half, hidden), lambda i, c: (0, c[0], 0)),
            pl.BlockSpec((2, half, hidden), lambda i, c: (0, 1 - c[0], 0)),
        ],
        [rows(hidden), rows(2 * hidden), rows(half), rows(half), rows(LANE)],
        [
            main_memory((slots, hidden), BF),
            main_memory((slots, 2 * hidden), BF),
            main_memory((slots, half), BF),
            main_memory((slots, half), BF),
            shape((slots, LANE), BF),
        ],
        scalars=1,
        name="experts",
    )(core, *held(own, peer, d_hidden, pair, pair))


def add_pack_body(own, peer, extra, out):
    half = own.shape[1]
    out[:, :half] = (own[...].astype(F32) + peer[...].astype(F32)).astype(BF)
    out[:, half:] = extra[...]


def add_pack(own, peer, extra):
    slots, half = own.shape
    rows = lambda n: pl.BlockSpec((ROWS, n), lambda i: (i, 0))
    return kernel_call(
        add_pack_body,
        (slots // ROWS,),
        [rows(half), rows(half), rows(LANE)],
        rows(half + LANE),
        main_memory((slots, half + LANE), BF),
        name="add_pack",
    )(own, peer, extra)


def expert_grads_body(core, own, peer, grad_own, grad_peer, acted, d_pair, gates, grad_pair, grad_down, pair_low, act_low):
    step = pl.program_id(0)
    hidden = acted.shape[1]

    @pl.when(step == 0)
    def _():
        gate = gates[:, :1].astype(F32)
        pair_low[...] = (d_pair[...].astype(F32) * gate).astype(BF)
        act_low[...] = (acted[...].astype(F32) * gate).astype(BF)

    def part(rows, grads):
        value = dot(rows[...], pair_low[...], TN)
        grad_pair[:, 0, :] = value[:, :hidden]
        grad_pair[:, 1, :] = value[:, hidden:]
        grad_down[...] = dot(act_low[...], grads[...], TN)

    @pl.when(step < SIDE)
    def _():
        part(own, grad_own)

    @pl.when(step >= SIDE)
    def _():
        part(peer, grad_peer)


def expert_grads(core, own, peer, grad_own, grad_peer, acted, d_pair, gates):
    slots, half = grad_own.shape
    hidden = acted.shape[1]
    cut = half // SIDE
    first = pl.BlockSpec((slots, cut), lambda i, c: (0, jnp.minimum(i, SIDE - 1)))
    second = pl.BlockSpec((slots, cut), lambda i, c: (0, jnp.maximum(i - SIDE, 0)))

    def target(i, c):
        return jnp.where(i < SIDE, c[0] * SIDE + i, (1 - c[0]) * SIDE + i - SIDE)

    return kernel_call(
        expert_grads_body,
        (2 * SIDE,),
        [first, second, first, second, whole(slots, hidden), whole(slots, 2 * hidden), pl.BlockSpec((slots, LANE), lambda i, c: (0, half // LANE))],
        [
            pl.BlockSpec((cut, 2, hidden), lambda i, c: (target(i, c), 0, 0)),
            pl.BlockSpec((hidden, cut), lambda i, c: (0, target(i, c))),
        ],
        [shape((2 * half, 2, hidden), F32), shape((hidden, 2 * half), F32)],
        [pltpu.VMEM((slots, 2 * hidden), BF), pltpu.VMEM((slots, hidden), BF)],
        mib=48,
        scalars=1,
        name="expert_grads",
    )(core, *held(own, peer, grad_own, grad_peer, acted, d_pair, gates))


EXTRA = 16


def group_grads_body(core, own, peer, *refs):
    step = pl.program_id(0)
    d_group = refs[:SIDE]
    normed_two, d_logits, d_gain, d_qk, out = refs[SIDE:]
    cols = d_group[0].shape[2]
    targets = out.shape[0]
    rows = out.shape[1] - EXTRA

    def put(value, at):
        for k in range(targets):
            out[k, :rows, at * cols : (at + 1) * cols] = value[k * rows : (k + 1) * rows].astype(BF)

    def part(normed):
        for which in range(3):
            put(dot(normed[...], jnp.concatenate([block[which] for block in d_group], axis=0), NN), which)

    @pl.when(step < SIDE)
    def _():
        part(own)

    @pl.when(step >= SIDE)
    def _():
        part(peer)

    router = dot(d_logits[...], normed_two[...], TN).astype(BF)
    for k in range(targets):
        cut = slice(k * rows, (k + 1) * rows)
        out[k, rows:, :LANE] = router[:EXTRA, cut]
        out[k, rows:, LANE : 2 * LANE] = router[EXTRA:, cut]
        out[k, rows:, 2 * LANE : 3 * LANE] = jnp.broadcast_to(d_gain[:, cut], (EXTRA, LANE)).astype(BF)
        out[k, rows:, 3 * LANE : 4 * LANE] = jnp.concatenate([d_qk[...]] * (EXTRA // 2), axis=0).astype(BF)
        out[k, rows:, 4 * LANE :] = jnp.zeros((EXTRA, out.shape[2] - 4 * LANE), BF)


def turn_parts_body(*refs):
    value = jnp.concatenate([part[...].astype(F32) for part in refs[:SIDE]], axis=0)
    refs[SIDE][...] = value.T.astype(BF)


def turn_parts(parts):
    length, width = parts[0].shape
    cut = 256
    return kernel_call(
        turn_parts_body,
        (width // cut,),
        [pl.BlockSpec((length, cut), lambda i: (0, i))] * SIDE,
        pl.BlockSpec((cut, SIDE * length), lambda i: (i, 0)),
        main_memory((width, SIDE * length), BF),
        name="turn_parts",
    )(*held(*parts))


def group_grads(core, own, peer, d_group, normed_two, d_logits, d_gain, d_qk):
    half, depth = own.shape
    length = depth // SIDE
    cols = d_group[0].shape[2]
    cut = half // SIDE
    places = SIDE * SIDE
    rows = 2 * half // places

    def target(i, c):
        return jnp.where(i < SIDE, c[0] * SIDE + i, (1 - c[0]) * SIDE + i - SIDE)

    return kernel_call(
        group_grads_body,
        (2 * SIDE,),
        [
            pl.BlockSpec((cut, depth), lambda i, c: (jnp.minimum(i, SIDE - 1), 0)),
            pl.BlockSpec((cut, depth), lambda i, c: (jnp.maximum(i - SIDE, 0), 0)),
        ]
        + [whole(3, length, cols)] * SIDE
        + [
            pl.BlockSpec((length, cut), lambda i, c: (0, target(i, c))),
            whole(length, d_logits.shape[1]),
            pl.BlockSpec((1, cut), lambda i, c: (0, target(i, c))),
            whole(2, LANE),
        ],
        pl.BlockSpec((cut // rows, rows + EXTRA, 3 * cols), lambda i, c: (target(i, c), 0, 0)),
        main_memory((places, rows + EXTRA, 3 * cols), BF),
        scalars=1,
        name="group_grads",
    )(core, *held(own, peer), *d_group, *held(normed_two), d_logits, d_gain, d_qk)


def out_grads_body(*refs):
    left = jnp.concatenate([part[...] for part in refs[:SIDE]], axis=0)
    right = jnp.concatenate([part[...] for part in refs[SIDE : 2 * SIDE]], axis=0)
    refs[2 * SIDE][...] = dot(left, right, TN).astype(BF)


def out_grads(d_attn, attended):
    length, rows = d_attn[0].shape
    inner = attended[0].shape[1]
    return kernel_call(
        out_grads_body,
        (1,),
        [whole(length, rows)] * SIDE + [whole(length, inner)] * SIDE,
        whole(rows, inner),
        shape((rows, inner), BF),
        name="out_grads",
    )(*d_attn, *held(*attended))


def sum_arrived_body(rows, z_index, arrived, *outs):
    value = arrived[0].astype(F32)
    for k in range(1, arrived.shape[0]):
        value = value + arrived[k].astype(F32)
    value = value.astype(BF)
    main = SIDE * rows
    for which in range(SIDE):

        @pl.when(z_index[0] == which)
        def _():
            for step in range(SIDE):
                at = (which + step) % SIDE * rows
                outs[step][:rows] = value[at : at + rows]

    for step in range(SIDE):
        outs[step][rows:] = value[main:]


def sum_arrived(z_index, arrived, rows):
    places, height, columns = arrived.shape
    cols = columns // 3
    return kernel_call(
        functools.partial(sum_arrived_body, rows),
        (3,),
        [pl.BlockSpec((places, height, cols), lambda i, z: (0, 0, i))],
        [pl.BlockSpec((rows + EXTRA, cols), lambda i, z: (0, i))] * SIDE,
        [shape((rows + EXTRA, columns), BF)] * SIDE,
        scalars=1,
        name="sum_arrived",
    )(z_index, arrived)


def finish_body(z_index, *refs):
    parts, w_here, grad, small = refs[:SIDE], refs[SIDE], refs[SIDE + 1], refs[SIDE + 2]
    rows = grad.shape[1]
    cols = parts[0].shape[1] // 3
    for which in range(SIDE):

        @pl.when(z_index[0] == which)
        def _():
            ordered = [parts[(which - source) % SIDE] for source in range(SIDE)]
            for source in range(SIDE):
                for kind in range(3):
                    grad[kind, :, source * cols : (source + 1) * cols] = ordered[source][
                        :rows, kind * cols : (kind + 1) * cols
                    ].astype(F32)
            extra = [part[rows:].astype(F32) for part in ordered]
            total = (extra[0] + extra[1]) + (extra[2] + extra[3])
            small[:EXTRA] = total[:, :LANE]
            small[EXTRA : 2 * EXTRA] = total[:, LANE : 2 * LANE]
            small[2 * EXTRA + 1 : 2 * EXTRA + 2] = total[0:1, 2 * LANE : 3 * LANE]
            small[2 * EXTRA + 2 : 2 * EXTRA + 4] = total[0:2, 3 * LANE : 4 * LANE]

    product = jnp.sum(grad[0] * w_here[0].astype(F32) + grad[1] * w_here[1].astype(F32) + grad[2] * w_here[2].astype(F32), axis=-1, keepdims=True)
    at_row = lax.broadcasted_iota(jnp.int32, (rows, LANE), 0)
    at_lane = lax.broadcasted_iota(jnp.int32, (rows, LANE), 1)
    small[2 * EXTRA : 2 * EXTRA + 1] = jnp.sum(jnp.where(at_row == at_lane, product, 0.0), axis=0, keepdims=True)
    small[2 * EXTRA + 4 :] = jnp.zeros((small.shape[0] - 2 * EXTRA - 4, LANE), F32)


def finish(z_index, parts, w_here):
    kinds, rows, inner = w_here.shape
    height, columns = parts[0].shape
    return kernel_call(
        finish_body,
        (1,),
        [whole(height, columns)] * SIDE + [whole(kinds, rows, inner)],
        [whole(kinds, rows, inner), whole(2 * EXTRA + 8, LANE)],
        [shape((kinds, rows, inner), F32), shape((2 * EXTRA + 8, LANE), F32)],
        scalars=1,
        name="finish",
    )(z_index, *parts, w_here)


def on_device(
    tokens,
    expert_ids,
    capacity,
    gain_attn,
    w_qkv,
    qk_gain,
    w_out,
    gain_ffn,
    w_router,
    w_gate_up,
    w_down,
    cotangent,
):
    length, width = tokens.shape
    expert_count = capacity.shape[0]
    slot_count = length * expert_ids.shape[1] // expert_count
    slots = expert_count * slot_count
    inner = w_qkv.shape[2]
    half = width // 2
    cols = inner // SIDE
    core_index = lax.axis_index("tensor")
    core = core_index.astype(jnp.int32).reshape(1)
    place = [lax.axis_index(a) for a in AXES]
    dp_index = (place[0] * SIDE + place[1]) * SIDE + place[2]
    rows_here_count = width // SIDE**3

    def own_half(value):
        return lax.dynamic_slice_in_dim(value, core_index * half, half, axis=-1)

    expert_of = jnp.asarray(np.repeat(np.eye(expert_count, dtype=np.float32), slot_count, 0), BF)

    def to_owners(rows):
        columns = rows.shape[1]
        return exchange(rows.reshape(expert_count, slot_count, columns), AXES).reshape(slots, columns)

    member, select, grad_send = routing(core, capacity, expert_ids.T, expert_of, cotangent)
    grad_own = to_owners(grad_send)

    table = jnp.asarray(rotary(length, LANE // 2))
    gains = qk_gain.astype(F32)
    gain_one = gain_attn.astype(F32)
    gain_two = gain_ffn.astype(F32).reshape(1, width)
    w_parts = w_qkv.transpose(1, 0, 2)
    normed_one, raw, value_in, attended, partial = attend(
        tokens, gain_one.reshape(1, width), w_parts, w_out, gains, table
    )
    partial_peer = swap(partial)
    middle, normed_two, probs, gates, picked_total, combine, rows_send = middle_step(
        core, tokens, partial, partial_peer, gain_two, select, w_router, member, expert_of
    )
    rows_own = to_owners(rows_send)

    normed_early, attended_late, pair, grad_late, down, _ = together(
        own_half(normed_one), attended, w_gate_up, grad_own, w_down, rows_send
    )
    down = down[0]
    pair = pair[0].transpose(1, 0, 2)
    grad_peer = swap(grad_late)
    d_hidden = hidden_grad(core, grad_late, grad_peer, down)
    rows_own, d_hidden, pair, attended_late = together(rows_own, d_hidden, pair, attended_late)
    attended_group = share(attended_late, "y")
    rows_peer = swap(rows_own)
    acted, d_pair, back_own, back_peer, extra = experts_step(core, rows_own, rows_peer, d_hidden, pair)
    back_peer, normed_early, *attended_group = together(back_peer, normed_early, *attended_group)
    from_one, from_three = shift(normed_early, "z", 1), shift(normed_early, "z", 3)
    back_send = add_pack(back_own, swap(back_peer), extra)
    out_own, out_peer = experts_out(core, acted, down)
    back_send, out_own, out_peer, from_one, from_three = together(
        back_send, out_own, out_peer, from_one, from_three
    )
    back = to_owners(back_send)

    acted_late, own_late, peer_late, _ = together(acted, rows_own, rows_peer, back_send)
    grad_gate_up, grad_down = expert_grads(
        core, own_late, peer_late, grad_late, grad_peer, acted_late, d_pair, own_late
    )
    returned = (out_own.astype(F32) + swap(out_peer).astype(F32)).astype(BF)
    from_two = shift(from_one, "z", 1)
    normed_group = turn_parts([normed_early, from_one, from_two, from_three])
    returned, grad_gate_up, grad_down, normed_group = together(returned, grad_gate_up, grad_down, normed_group)
    returned = to_owners(returned)

    gathered = gather_back(back, combine, select, expert_of)
    core_y = jnp.stack([core[0], place[0].astype(jnp.int32)])
    d_logits, d_middle, d_attn, gain_two_local, *d_attn_blocks = middle_back(
        core_y, gathered, swap(gathered), probs, gates, picked_total, member, w_router, middle, cotangent, gain_two
    )

    z_index = place[2].astype(jnp.int32).reshape(1)
    *d_blocks, grad_qk = attend_back(z_index, d_attn, w_out, raw, value_in, gains, table)
    d_group = send_steps(d_blocks, "z")
    normed_group, normed_group_peer, returned, *d_group = together(
        normed_group, swap(normed_group), returned, *d_group
    )

    columns_here = expert_count // 2
    my_logits = lax.dynamic_slice_in_dim(d_logits, core_index * columns_here, columns_here, axis=1)
    partial_grads = group_grads(
        core,
        normed_group,
        normed_group_peer,
        d_group,
        normed_two,
        my_logits,
        gain_two_local,
        grad_qk,
    )
    d_attn_blocks, _ = together(d_attn_blocks, d_blocks)
    d_attn_group = send_steps(d_attn_blocks, "y")
    partial_grads, *d_attn_group = together(partial_grads, *d_attn_group)
    arrived = exchange(partial_grads, ("y", "x"))
    d_attn_group, late_blocks, late_returned, _ = together(d_attn_group, d_blocks, returned, partial_grads)

    grad_out = out_grads(d_attn_group, attended_group)

    grad_out = send_blocks(grad_out.reshape(SIDE, SIDE, rows_here_count, inner), "z", 1)

    d_one = input_grad(z_index, late_blocks, w_parts)
    d_one = d_one.astype(F32) + swap(d_one).astype(F32)

    residual_in = tokens.astype(F32)
    scale_one = rms(residual_in)
    unit_one = residual_in * scale_one
    weighted = d_one * gain_one
    grad_input = d_middle + scale_one * (
        weighted - unit_one * jnp.mean(weighted * unit_one, axis=-1, keepdims=True)
    )

    mix_own = dot(combine, late_returned, TN)
    result_own = (own_half(middle) + mix_own).astype(BF)
    output = side_by_side(result_own, swap(result_own), core_index)

    grad_out = sum(part.astype(F32) for part in grad_out).astype(BF)
    grad_out = sum(part.astype(F32) for part in send_blocks(grad_out, "x", 0))
    arrived, grad_input, output, grad_out = together(arrived, grad_input, output, grad_out)
    parts = send_steps(sum_arrived(z_index, arrived, rows_here_count), "z")
    w_here = lax.dynamic_slice_in_dim(w_parts, dp_index * rows_here_count, rows_here_count, axis=1)
    grad_qkv, small = finish(z_index, parts, w_here)
    grad_qkv = grad_qkv.transpose(1, 0, 2)
    small_peer = swap(small)
    gain_here = lax.dynamic_slice_in_dim(gain_one, dp_index * rows_here_count, rows_here_count, axis=0)
    grad_gain_one = (small[2 * EXTRA] + small_peer[2 * EXTRA])[:rows_here_count] / gain_here
    cut = lambda value: lax.dynamic_slice_in_dim(value, place[2] * rows_here_count, rows_here_count, axis=-1)
    grad_router = jnp.where(
        core_index == 0,
        jnp.concatenate([small[: 2 * EXTRA], small_peer[: 2 * EXTRA]], axis=0),
        jnp.concatenate([small_peer[: 2 * EXTRA], small[: 2 * EXTRA]], axis=0),
    )
    grad_router = cut(grad_router).T
    grad_gain_two = cut(small[2 * EXTRA + 1])
    grad_qk = small[2 * EXTRA + 2 : 2 * EXTRA + 4] + small_peer[2 * EXTRA + 2 : 2 * EXTRA + 4]

    return (
        output,
        grad_input,
        grad_gain_one,
        grad_qkv,
        grad_qk,
        grad_out,
        grad_gain_two,
        grad_router,
        grad_gate_up[None],
        grad_down[None],
    )


def solution(mesh):
    names = AXES + ("tensor",)
    torus = Mesh(mesh.devices.reshape(SIDE, SIDE, SIDE, 2), names)
    return jax.shard_map(
        on_device,
        mesh=torus,
        in_specs=(
            P(AXES, None),
            P(AXES, None),
            P(),
            P(),
            P(None, None, "tensor"),
            P(),
            P(None, "tensor"),
            P(),
            P(),
            P(AXES, None, None, "tensor"),
            P(AXES, "tensor", None),
            P(AXES, None),
        ),
        out_specs=(
            P(AXES, None),
            P(AXES, None),
            P(AXES),
            P(AXES, None, "tensor"),
            P(),
            P(AXES, "tensor"),
            P(AXES),
            P(AXES, None),
            P(AXES, None, None, "tensor"),
            P(AXES, "tensor", None),
        ),
        check_vma=False,
    )
```

```python
import functools
import math

import jax
import jax.numpy as jnp
import numpy as np
from jax import lax
from jax.experimental import pallas as pl
from jax.experimental.pallas import tpu as pltpu
from jax.sharding import Mesh
from jax.sharding import PartitionSpec as P

AXES = ("y", "x", "z")
SIDE = 4
LANE = 128
BF = jnp.bfloat16
F32 = jnp.float32
MIB = 1 << 20


def dot(a, b, dims):
    return lax.dot_general(a, b, (dims, ((), ())), preferred_element_type=F32)


NN = ((1,), (0,))
NT = ((1,), (1,))
TN = ((0,), (0,))


def rms(values):
    return lax.rsqrt(jnp.mean(values * values, axis=-1, keepdims=True) + 1e-06)


def rotary(length, half_dim):
    position = np.arange(length, dtype=np.float32)
    inverse = np.float32(50000.0) ** (-np.arange(half_dim, dtype=np.float32) / np.float32(half_dim))
    angles = position[:, None] * inverse[None, :].astype(np.float32)
    cosine = np.cos(angles).astype(np.float32)
    sine = np.sin(angles).astype(np.float32)
    return np.stack([np.concatenate([cosine, cosine], 1), np.concatenate([-sine, sine], 1)])


def swap(value):
    return lax.ppermute(value, "tensor", [(0, 1), (1, 0)])


def shift(value, axis, step):
    return lax.ppermute(value, axis, [(i, (i + step) % SIDE) for i in range(SIDE)])


def side_by_side(own, peer, core):
    return jnp.where(
        core == 0,
        jnp.concatenate([own, peer], axis=-1),
        jnp.concatenate([peer, own], axis=-1),
    )


def block_at(value, index, dim):
    return lax.dynamic_index_in_dim(value, index, dim, keepdims=False)


def together(*values):
    return lax.optimization_barrier(values)


def share(value, axis):
    return [value] + [shift(value, axis, step) for step in (1, 2, 3)]


def send_blocks(value, axis, dim):
    here = lax.axis_index(axis)
    own = block_at(value, here, dim)
    return [own] + [shift(block_at(value, (here + step) % SIDE, dim), axis, step) for step in (1, 2, 3)]


def send_steps(blocks, axis):
    return [blocks[0]] + [shift(blocks[step], axis, step) for step in (1, 2, 3)]


def exchange(value, axes):
    return lax.all_to_all(value, axes, split_axis=0, concat_axis=0, tiled=True)


def shape(dims, kind):
    return jax.ShapeDtypeStruct(dims, kind)


def main_memory(dims, kind):
    return pltpu.HBM(dims, kind)


def held(*values):
    return [pltpu.with_memory_space_constraint(value, pltpu.HBM) for value in values]


def kernel_call(body, grid, ins, outs, out_shapes, scratch=(), mib=40, scalars=0, name=None):
    return pl.pallas_call(
        body,
        grid_spec=pltpu.PrefetchScalarGridSpec(
            num_scalar_prefetch=scalars, grid=grid, in_specs=ins, out_specs=outs, scratch_shapes=list(scratch)
        ),
        out_shape=out_shapes,
        compiler_params=pltpu.CompilerParams(vmem_limit_bytes=mib * MIB),
        name=name,
    )


def whole(*dims):
    return pl.BlockSpec(dims, lambda *_: (0,) * len(dims))


def rope(values, table):
    return values * table[0] + pltpu.roll(values, values.shape[-1] // 2, 1) * table[1]


def unrope(values, table):
    return values * table[0] - pltpu.roll(values, values.shape[-1] // 2, 1) * table[1]


def attention_weights(query, key):
    scores = dot(query, key, NT) * (1.0 / math.sqrt(query.shape[-1]))
    raised = jnp.exp(scores - jnp.max(scores, axis=-1, keepdims=True))
    return raised / jnp.sum(raised, axis=-1, keepdims=True)


def attend_body(tokens, gain, w_qkv, w_out, gains, table, normed, raw, value_out, attended, partial, total):
    step = pl.program_id(0)

    @pl.when(step == 0)
    def _():
        x = tokens[...].astype(F32)
        normed[...] = (x * rms(x) * gain[...]).astype(BF)
        total[...] = jnp.zeros_like(total)

    h = normed[...]
    query_raw = dot(h, w_qkv[0], NN)
    key_raw = dot(h, w_qkv[1], NN)
    value = dot(h, w_qkv[2], NN).astype(BF)
    raw[0] = query_raw
    raw[1] = key_raw
    value_out[...] = value
    for at in range(query_raw.shape[1] // LANE):
        cut = slice(at * LANE, (at + 1) * LANE)
        q, k = query_raw[:, cut], key_raw[:, cut]
        query = rope(q * rms(q) * gains[0:1], table).astype(BF)
        key = rope(k * rms(k) * gains[1:2], table).astype(BF)
        weights = attention_weights(query, key).astype(BF)
        attended[:, cut] = dot(weights, value[:, cut], NN).astype(BF)
    total[...] += dot(attended[...], w_out[...], NT)

    @pl.when(step == pl.num_programs(0) - 1)
    def _():
        partial[...] = total[...].astype(BF)


def attend(tokens, gain, w_qkv, w_out, gains, table):
    length, width = tokens.shape
    inner = w_qkv.shape[2]
    cols = inner // SIDE
    return kernel_call(
        attend_body,
        (SIDE,),
        [
            whole(length, width),
            whole(1, width),
            pl.BlockSpec((3, width, cols), lambda i: (0, 0, i)),
            pl.BlockSpec((width, cols), lambda i: (0, i)),
            whole(2, LANE),
            whole(2, length, LANE),
        ],
        [
            whole(length, width),
            pl.BlockSpec((2, length, cols), lambda i: (0, 0, i)),
            pl.BlockSpec((length, cols), lambda i: (0, i)),
            pl.BlockSpec((length, cols), lambda i: (0, i)),
            whole(length, width),
        ],
        [
            shape((length, width), BF),
            shape((2, length, inner), F32),
            shape((length, inner), BF),
            shape((length, inner), BF),
            shape((length, width), BF),
        ],
        [pltpu.VMEM((length, width), F32)],
        name="attend",
    )(tokens, gain, w_qkv, w_out, gains, table)


def attend_back_body(z_index, d_attn, w_out, raw, value_in, gains, table, *outs):
    d_gains = outs[SIDE]
    step = pl.program_id(0)
    parts = ([], [], [])

    @pl.when(step == 0)
    def _():
        d_gains[...] = jnp.zeros_like(d_gains)

    d_attended = dot(d_attn[...], w_out[...], NN).astype(BF)
    for at in range(d_attended.shape[1] // LANE):
        cut = slice(at * LANE, (at + 1) * LANE)
        q, k = raw[0, :, cut], raw[1, :, cut]
        rq, rk = rms(q), rms(k)
        unit_q, unit_k = q * rq, k * rk
        query = rope(unit_q * gains[0:1], table).astype(BF)
        key = rope(unit_k * gains[1:2], table).astype(BF)
        weights = attention_weights(query, key)
        grad = d_attended[:, cut]
        d_value = dot(weights.astype(BF), grad, TN)
        d_weights = dot(grad, value_in[:, cut], NT)
        d_scores = (
            weights * (d_weights - jnp.sum(weights * d_weights, axis=-1, keepdims=True))
        ).astype(BF)
        root = 1.0 / math.sqrt(LANE)
        d_query = unrope(dot(d_scores, key, NN) * root, table)
        d_key = unrope(dot(d_scores, query, TN) * root, table)
        d_gains[0:1] += jnp.sum(d_query * unit_q, axis=0, keepdims=True)
        d_gains[1:2] += jnp.sum(d_key * unit_k, axis=0, keepdims=True)
        wq = d_query * gains[0:1]
        wk = d_key * gains[1:2]
        parts[0].append((rq * (wq - unit_q * jnp.mean(wq * unit_q, axis=-1, keepdims=True))).astype(BF))
        parts[1].append((rk * (wk - unit_k * jnp.mean(wk * unit_k, axis=-1, keepdims=True))).astype(BF))
        parts[2].append(d_value.astype(BF))
    for k in range(SIDE):

        @pl.when((z_index[0] + k) % SIDE == step)
        def _():
            for kind in range(3):
                outs[k][kind] = jnp.concatenate(parts[kind], axis=1)


def attend_back(z_index, d_attn, w_out, raw, value_in, gains, table):
    length, width = d_attn.shape
    inner = w_out.shape[1]
    cols = inner // SIDE
    return kernel_call(
        attend_back_body,
        (SIDE,),
        [
            whole(length, width),
            pl.BlockSpec((width, cols), lambda i, z: (0, i)),
            pl.BlockSpec((2, length, cols), lambda i, z: (0, 0, i)),
            pl.BlockSpec((length, cols), lambda i, z: (0, i)),
            whole(2, LANE),
            whole(2, length, LANE),
        ],
        [whole(3, length, cols)] * SIDE + [whole(2, LANE)],
        [shape((3, length, cols), BF)] * SIDE + [shape((2, LANE), F32)],
        scalars=1,
        name="attend_back",
    )(z_index, d_attn, *held(w_out, raw, value_in, gains, table))


def input_grad_body(z_index, *refs):
    w_qkv, out, total = refs[SIDE:]
    step = pl.program_id(0)

    @pl.when(step == 0)
    def _():
        total[...] = jnp.zeros_like(total)

    for k in range(SIDE):

        @pl.when(step == k)
        def _():
            block = refs[k]
            total[...] += dot(block[0], w_qkv[0], NT) + dot(block[1], w_qkv[1], NT) + dot(block[2], w_qkv[2], NT)

    @pl.when(step == pl.num_programs(0) - 1)
    def _():
        out[...] = total[...].astype(BF)


def input_grad(z_index, d_blocks, w_qkv):
    _, length, cols = d_blocks[0].shape
    width = w_qkv.shape[1]
    return kernel_call(
        input_grad_body,
        (SIDE,),
        [whole(3, length, cols)] * SIDE
        + [pl.BlockSpec((3, width, cols), lambda i, z: (0, 0, lax.rem(z[0] + i, SIDE)))],
        whole(length, width),
        shape((length, width), BF),
        [pltpu.VMEM((length, width), F32)],
        scalars=1,
        name="input_grad",
    )(z_index, *d_blocks, *held(w_qkv))


def routing_body(core, capacity, ids, later, expert_of, cotangent, member_out, select, rows):
    experts = expert_of.shape[1]
    length = ids.shape[1]
    at_expert = lax.broadcasted_iota(jnp.int32, (experts, length), 0)
    member = jnp.zeros((experts, length), F32)
    for j in range(ids.shape[0]):
        member = member + (ids[j : j + 1, :] == at_expert).astype(F32)
    member_out[...] = member.T
    ranks = dot(member.astype(BF), later[...], NN)
    row = lax.broadcasted_iota(jnp.int32, (experts, experts), 0)
    column = lax.broadcasted_iota(jnp.int32, (experts, experts), 1)
    limit = jnp.sum(jnp.where(row == column, capacity[...].astype(F32), 0.0), axis=1, keepdims=True)
    code = jnp.where((member > 0.5) & (ranks < limit), ranks, -1.0).astype(BF)
    slots, half = rows.shape
    depth = slots // experts
    chunk = 8 * depth
    slot = lax.broadcasted_iota(jnp.int32, (chunk, length), 0).astype(F32)
    slot = slot - depth * jnp.floor((slot + 0.5) * (1.0 / depth))
    for which in range(2):

        @pl.when(core[0] == which)
        def _():
            for at in range(0, slots, chunk):
                cut = slice(at, at + chunk)
                hit = (dot(expert_of[cut], code, NN) == slot).astype(F32).astype(BF)
                select[cut] = hit
                rows[cut] = dot(hit, cotangent[:, which * half : (which + 1) * half], NN).astype(BF)


def routing(core, capacity, ids, expert_of, cotangent):
    length, width = cotangent.shape
    slots, experts = expert_of.shape
    later = jnp.asarray(np.triu(np.ones((length, length), np.float32), 1), BF)
    return kernel_call(
        routing_body,
        (1,),
        [
            whole(1, experts),
            whole(*ids.shape),
            whole(length, length),
            whole(slots, experts),
            whole(length, width),
        ],
        [whole(length, experts), whole(slots, length), whole(slots, width // 2)],
        [shape((length, experts), F32), main_memory((slots, length), BF), main_memory((slots, width // 2), BF)],
        scalars=1,
        name="routing",
    )(core, *held(capacity.reshape(1, experts), ids, later, expert_of, cotangent))


def middle_body(core, tokens, own, peer, gain, select, w_router, member, expert_of,
                middle, normed, probs_out, gates_out, total_out, combine, rows):
    x2 = tokens[...].astype(F32) + (own[...].astype(F32) + peer[...].astype(F32))
    middle[...] = x2
    normed[...] = (x2 * rms(x2) * gain[...]).astype(BF)
    logits = dot(normed[...], w_router[...], NN)
    raised = jnp.exp(logits - jnp.max(logits, axis=-1, keepdims=True))
    probs = raised / jnp.sum(raised, axis=-1, keepdims=True)
    picked = probs * member[...]
    total = jnp.sum(picked, axis=-1, keepdims=True)
    gates = picked / total
    probs_out[...] = probs
    gates_out[...] = gates
    total_out[...] = total
    low = gates.astype(BF)
    half = rows.shape[1] - LANE
    for at in range(0, rows.shape[0], 256):
        cut = slice(at, at + 256)
        spread = dot(expert_of[cut], low, NT) * select[cut].astype(F32)
        combine[cut] = spread.astype(BF)
        gate = jnp.sum(spread, axis=-1, keepdims=True)
        rows[cut, half:] = jnp.broadcast_to(gate, (256, LANE)).astype(BF)
    for which in range(2):

        @pl.when(core[0] == which)
        def _():
            for at in range(0, rows.shape[0], 256):
                rows[at : at + 256, :half] = dot(
                    select[at : at + 256], normed[:, which * half : (which + 1) * half], NN
                ).astype(BF)


def middle_step(core, tokens, own, peer, gain, select, w_router, member, expert_of):
    length, width = tokens.shape
    slots, experts = expert_of.shape
    columns = width // 2 + LANE
    return kernel_call(
        middle_body,
        (1,),
        [whole(length, width)] * 3
        + [whole(1, width), whole(slots, length), whole(width, experts), whole(length, experts), whole(slots, experts)],
        [
            whole(length, width),
            whole(length, width),
            whole(length, experts),
            whole(length, experts),
            whole(length, 1),
            whole(slots, length),
            whole(slots, columns),
        ],
        [
            main_memory((length, width), F32),
            main_memory((length, width), BF),
            shape((length, experts), F32),
            shape((length, experts), F32),
            shape((length, 1), F32),
            main_memory((slots, length), BF),
            main_memory((slots, columns), BF),
        ],
        scalars=1,
        name="middle",
    )(core, *held(tokens), own, peer, *held(gain, select, w_router, member, expert_of))


def gather_back_body(back, combine, select, expert_of, out):
    half = combine.shape[1]
    half = out.shape[1] - LANE
    out[:, :half] = dot(combine[...], back[:, :half], TN)
    high = back[:, half : half + 1].astype(F32)
    low = back[:, half + 1 : half + 2].astype(F32)
    picked = select[...].astype(F32)
    experts = expert_of.shape[1]
    spread = dot((picked * high).astype(BF), expert_of[...], TN) + dot((picked * low).astype(BF), expert_of[...], TN)
    out[:, half : half + experts] = spread
    out[:, half + experts :] = jnp.zeros((out.shape[0], LANE - experts), F32)


def gather_back(back, combine, select, expert_of):
    slots, columns = back.shape
    length = combine.shape[1]
    experts = expert_of.shape[1]
    return kernel_call(
        gather_back_body,
        (1,),
        [whole(slots, columns), whole(slots, length), whole(slots, length), whole(slots, experts)],
        whole(length, columns),
        shape((length, columns), F32),
        name="gather_back",
    )(back, *held(combine, select, expert_of))


def middle_back_body(core, own, peer, probs, gates, total, member, w_router, middle, cotangent, gain,
                     d_logits_out, d_middle, d_attn, d_gain, *d_attn_blocks):
    half = own.shape[1] - LANE
    experts = probs.shape[1]
    d_gates = own[:, half : half + experts] + peer[:, half : half + experts]
    g, p = gates[...], probs[...]
    d_picked = member[...] * (d_gates - jnp.sum(d_gates * g, axis=-1, keepdims=True)) / total[...]
    d_logits = (p * (d_picked - jnp.sum(p * d_picked, axis=-1, keepdims=True))).astype(BF)
    d_logits_out[...] = d_logits
    d_normed = dot(d_logits, w_router[...], NT)
    for which in range(2):

        @pl.when(core[0] == which)
        def _():
            first, second = (own, peer) if which == 0 else (peer, own)
            d_middle[:, :half] = first[:, :half]
            d_middle[:, half:] = second[:, :half]

    d_normed = d_normed + d_middle[...]
    x2 = middle[...]
    scale = rms(x2)
    unit = x2 * scale
    d_gain[...] = jnp.sum(d_normed * unit, axis=0, keepdims=True)
    weighted = d_normed * gain[...]
    value = cotangent[...].astype(F32) + scale * (
        weighted - unit * jnp.mean(weighted * unit, axis=-1, keepdims=True)
    )
    d_middle[...] = value
    low = value.astype(BF)
    d_attn[...] = low
    cut = d_attn_blocks[0].shape[1]
    for which in range(SIDE):

        @pl.when(core[1] == which)
        def _():
            for k in range(SIDE):
                at = (which + k) % SIDE * cut
                d_attn_blocks[k][...] = low[:, at : at + cut]


def middle_back(core, own, peer, probs, gates, total, member, w_router, middle, cotangent, gain):
    length, width = middle.shape
    experts = probs.shape[1]
    columns = own.shape[1]
    return kernel_call(
        middle_back_body,
        (1,),
        [whole(length, columns)] * 2
        + [whole(length, experts)] * 2
        + [whole(length, 1), whole(length, experts), whole(width, experts), whole(length, width), whole(length, width), whole(1, width)],
        [
            whole(length, experts),
            whole(length, width),
            whole(length, width),
            whole(1, width),
        ]
        + [whole(length, width // SIDE)] * SIDE,
        [
            shape((length, experts), BF),
            shape((length, width), F32),
            shape((length, width), BF),
            shape((1, width), F32),
        ]
        + [shape((length, width // SIDE), BF)] * SIDE,
        scalars=1,
        name="middle_back",
    )(core, *held(own, peer, probs, gates, total, member, w_router, middle, cotangent, gain))


def hidden_grad_body(core, own, peer, down_own, down_peer, out):
    half = down_own.shape[1]
    out[...] = dot(own[:, :half], down_own[...], NT) + dot(peer[:, :half], down_peer[...], NT)


ROWS = 256


def hidden_grad(core, own, peer, down):
    slots, columns = own.shape
    hidden, width = down.shape
    half = width // 2
    return kernel_call(
        hidden_grad_body,
        (slots // ROWS,),
        [
            pl.BlockSpec((ROWS, columns), lambda i, c: (i, 0)),
            pl.BlockSpec((ROWS, columns), lambda i, c: (i, 0)),
            pl.BlockSpec((hidden, half), lambda i, c: (0, c[0])),
            pl.BlockSpec((hidden, half), lambda i, c: (0, 1 - c[0])),
        ],
        pl.BlockSpec((ROWS, hidden), lambda i, c: (i, 0)),
        main_memory((slots, hidden), F32),
        scalars=1,
        name="hidden_grad",
    )(core, *held(own, peer, down, down))


def experts_body(core, own, peer, d_hidden, pair_own, pair_peer, acted, d_pair, back_own, back_peer, extra):
    hidden = d_hidden.shape[1]
    half = pair_own.shape[1]
    mine, other = own[:, :half], peer[:, :half]
    gate = dot(mine, pair_own[0], NN) + dot(other, pair_peer[0], NN)
    up = dot(mine, pair_own[1], NN) + dot(other, pair_peer[1], NN)
    sig = 1.0 / (1.0 + jnp.exp(-gate))
    silu = gate * sig
    act = (silu * up).astype(BF)
    acted[...] = act
    d_act = d_hidden[...]
    slot_grad = jnp.sum(d_act * act.astype(F32), axis=-1, keepdims=True)
    high = slot_grad.astype(BF)
    low = (slot_grad - high.astype(F32)).astype(BF)
    at = lax.broadcasted_iota(jnp.int32, extra.shape, 1)
    extra[...] = jnp.where(at == 0, high.astype(F32), jnp.where(at == 1, low.astype(F32), 0.0)).astype(BF)
    d_gate = (d_act * up * sig * (1.0 + gate * (1.0 - sig))).astype(BF)
    d_up = (d_act * silu).astype(BF)
    d_pair[:, :hidden] = d_gate
    d_pair[:, hidden:] = d_up
    back_peer[...] = (dot(d_gate, pair_peer[0], NT) + dot(d_up, pair_peer[1], NT)).astype(BF)
    back_own[...] = (dot(d_gate, pair_own[0], NT) + dot(d_up, pair_own[1], NT)).astype(BF)


def experts_out_body(core, acted, down_own, down_peer, out_own, out_peer):
    out_peer[...] = dot(acted[...], down_peer[...], NN).astype(BF)
    out_own[...] = dot(acted[...], down_own[...], NN).astype(BF)


def experts_out(core, acted, down):
    slots, hidden = acted.shape
    half = down.shape[1] // 2
    rows = lambda n: pl.BlockSpec((ROWS, n), lambda i, c: (i, 0))
    return kernel_call(
        experts_out_body,
        (slots // ROWS,),
        [
            rows(hidden),
            pl.BlockSpec((hidden, half), lambda i, c: (0, c[0])),
            pl.BlockSpec((hidden, half), lambda i, c: (0, 1 - c[0])),
        ],
        [rows(half), rows(half)],
        [main_memory((slots, half), BF)] * 2,
        scalars=1,
        name="experts_out",
    )(core, *held(acted, down, down))


def experts_step(core, own, peer, d_hidden, pair):
    slots, columns = own.shape
    half = columns - LANE
    hidden = pair.shape[2]
    rows = lambda n: pl.BlockSpec((ROWS, n), lambda i, c: (i, 0))
    return kernel_call(
        experts_body,
        (slots // ROWS,),
        [
            rows(columns),
            rows(columns),
            rows(hidden),
            pl.BlockSpec((2, half, hidden), lambda i, c: (0, c[0], 0)),
            pl.BlockSpec((2, half, hidden), lambda i, c: (0, 1 - c[0], 0)),
        ],
        [rows(hidden), rows(2 * hidden), rows(half), rows(half), rows(LANE)],
        [
            main_memory((slots, hidden), BF),
            main_memory((slots, 2 * hidden), BF),
            main_memory((slots, half), BF),
            main_memory((slots, half), BF),
            shape((slots, LANE), BF),
        ],
        scalars=1,
        name="experts",
    )(core, *held(own, peer, d_hidden, pair, pair))


def add_pack_body(own, peer, extra, out):
    half = own.shape[1]
    out[:, :half] = (own[...].astype(F32) + peer[...].astype(F32)).astype(BF)
    out[:, half:] = extra[...]


def add_pack(own, peer, extra):
    slots, half = own.shape
    rows = lambda n: pl.BlockSpec((ROWS, n), lambda i: (i, 0))
    return kernel_call(
        add_pack_body,
        (slots // ROWS,),
        [rows(half), rows(half), rows(LANE)],
        rows(half + LANE),
        main_memory((slots, half + LANE), BF),
        name="add_pack",
    )(own, peer, extra)


def expert_grads_body(core, own, peer, grad_own, grad_peer, acted, d_pair, gates, grad_pair, grad_down, pair_low, act_low):
    step = pl.program_id(0)
    hidden = acted.shape[1]

    @pl.when(step == 0)
    def _():
        gate = gates[:, :1].astype(F32)
        pair_low[...] = (d_pair[...].astype(F32) * gate).astype(BF)
        act_low[...] = (acted[...].astype(F32) * gate).astype(BF)

    def part(rows, grads):
        value = dot(rows[...], pair_low[...], TN)
        grad_pair[:, 0, :] = value[:, :hidden]
        grad_pair[:, 1, :] = value[:, hidden:]
        grad_down[...] = dot(act_low[...], grads[...], TN)

    @pl.when(step < SIDE)
    def _():
        part(own, grad_own)

    @pl.when(step >= SIDE)
    def _():
        part(peer, grad_peer)


def expert_grads(core, own, peer, grad_own, grad_peer, acted, d_pair, gates):
    slots, half = grad_own.shape
    hidden = acted.shape[1]
    cut = half // SIDE
    first = pl.BlockSpec((slots, cut), lambda i, c: (0, jnp.minimum(i, SIDE - 1)))
    second = pl.BlockSpec((slots, cut), lambda i, c: (0, jnp.maximum(i - SIDE, 0)))

    def target(i, c):
        return jnp.where(i < SIDE, c[0] * SIDE + i, (1 - c[0]) * SIDE + i - SIDE)

    return kernel_call(
        expert_grads_body,
        (2 * SIDE,),
        [first, second, first, second, whole(slots, hidden), whole(slots, 2 * hidden), pl.BlockSpec((slots, LANE), lambda i, c: (0, half // LANE))],
        [
            pl.BlockSpec((cut, 2, hidden), lambda i, c: (target(i, c), 0, 0)),
            pl.BlockSpec((hidden, cut), lambda i, c: (0, target(i, c))),
        ],
        [shape((2 * half, 2, hidden), F32), shape((hidden, 2 * half), F32)],
        [pltpu.VMEM((slots, 2 * hidden), BF), pltpu.VMEM((slots, hidden), BF)],
        mib=48,
        scalars=1,
        name="expert_grads",
    )(core, *held(own, peer, grad_own, grad_peer, acted, d_pair, gates))


EXTRA = 16


def group_grads_body(core, own, peer, *refs):
    step = pl.program_id(0)
    d_group = refs[:SIDE]
    normed_two, d_logits, d_gain, d_qk, out, right = refs[SIDE:]
    _, length, cols = d_group[0].shape
    targets = out.shape[0]
    rows = out.shape[1] - EXTRA

    @pl.when(step == 0)
    def _():
        for k in range(SIDE):
            for which in range(3):
                right[k * length : (k + 1) * length, which * cols : (which + 1) * cols] = d_group[k][which]

    def part(normed):
        value = dot(normed[...], right[...], NN).astype(BF)
        for k in range(targets):
            out[k, :rows] = value[k * rows : (k + 1) * rows]

    @pl.when(step < SIDE)
    def _():
        part(own)

    @pl.when(step >= SIDE)
    def _():
        part(peer)

    router = dot(d_logits[...], normed_two[...], TN).astype(BF)
    for k in range(targets):
        cut = slice(k * rows, (k + 1) * rows)
        out[k, rows:, :LANE] = router[:EXTRA, cut]
        out[k, rows:, LANE : 2 * LANE] = router[EXTRA:, cut]
        out[k, rows:, 2 * LANE : 3 * LANE] = jnp.broadcast_to(d_gain[:, cut], (EXTRA, LANE)).astype(BF)
        out[k, rows:, 3 * LANE : 4 * LANE] = jnp.concatenate([d_qk[...]] * (EXTRA // 2), axis=0).astype(BF)
        out[k, rows:, 4 * LANE :] = jnp.zeros((EXTRA, out.shape[2] - 4 * LANE), BF)


def turn_parts_body(*refs):
    value = jnp.concatenate([part[...].astype(F32) for part in refs[:SIDE]], axis=0)
    refs[SIDE][...] = value.T.astype(BF)


def turn_parts(parts):
    length, width = parts[0].shape
    cut = 256
    return kernel_call(
        turn_parts_body,
        (width // cut,),
        [pl.BlockSpec((length, cut), lambda i: (0, i))] * SIDE,
        pl.BlockSpec((cut, SIDE * length), lambda i: (i, 0)),
        main_memory((width, SIDE * length), BF),
        name="turn_parts",
    )(*held(*parts))


def group_grads(core, own, peer, d_group, normed_two, d_logits, d_gain, d_qk):
    half, depth = own.shape
    length = depth // SIDE
    cols = d_group[0].shape[2]
    cut = half // SIDE
    places = SIDE * SIDE
    rows = 2 * half // places

    def target(i, c):
        return jnp.where(i < SIDE, c[0] * SIDE + i, (1 - c[0]) * SIDE + i - SIDE)

    return kernel_call(
        group_grads_body,
        (2 * SIDE,),
        [
            pl.BlockSpec((cut, depth), lambda i, c: (jnp.minimum(i, SIDE - 1), 0)),
            pl.BlockSpec((cut, depth), lambda i, c: (jnp.maximum(i - SIDE, 0), 0)),
        ]
        + [whole(3, length, cols)] * SIDE
        + [
            pl.BlockSpec((length, cut), lambda i, c: (0, target(i, c))),
            whole(length, d_logits.shape[1]),
            pl.BlockSpec((1, cut), lambda i, c: (0, target(i, c))),
            whole(2, LANE),
        ],
        pl.BlockSpec((cut // rows, rows + EXTRA, 3 * cols), lambda i, c: (target(i, c), 0, 0)),
        main_memory((places, rows + EXTRA, 3 * cols), BF),
        [pltpu.VMEM((depth, 3 * cols), BF)],
        scalars=1,
        name="group_grads",
    )(core, *held(own, peer), *d_group, *held(normed_two), d_logits, d_gain, d_qk)


def out_grads_body(*refs):
    left = jnp.concatenate([part[...] for part in refs[:SIDE]], axis=0)
    right = jnp.concatenate([part[...] for part in refs[SIDE : 2 * SIDE]], axis=0)
    refs[2 * SIDE][...] = dot(left, right, TN).astype(BF)


def out_grads(d_attn, attended):
    length, rows = d_attn[0].shape
    inner = attended[0].shape[1]
    return kernel_call(
        out_grads_body,
        (1,),
        [whole(length, rows)] * SIDE + [whole(length, inner)] * SIDE,
        whole(rows, inner),
        shape((rows, inner), BF),
        name="out_grads",
    )(*d_attn, *held(*attended))


def sum_arrived_body(rows, z_index, arrived, *outs):
    value = arrived[0].astype(F32)
    for k in range(1, arrived.shape[0]):
        value = value + arrived[k].astype(F32)
    value = value.astype(BF)
    main = SIDE * rows
    for which in range(SIDE):

        @pl.when(z_index[0] == which)
        def _():
            for step in range(SIDE):
                at = (which + step) % SIDE * rows
                outs[step][:rows] = value[at : at + rows]

    for step in range(SIDE):
        outs[step][rows:] = value[main:]


def sum_arrived(z_index, arrived, rows):
    places, height, columns = arrived.shape
    cols = columns // 3
    return kernel_call(
        functools.partial(sum_arrived_body, rows),
        (3,),
        [pl.BlockSpec((places, height, cols), lambda i, z: (0, 0, i))],
        [pl.BlockSpec((rows + EXTRA, cols), lambda i, z: (0, i))] * SIDE,
        [shape((rows + EXTRA, columns), BF)] * SIDE,
        scalars=1,
        name="sum_arrived",
    )(z_index, arrived)


def finish_body(z_index, *refs):
    parts, w_here, grad, small = refs[:SIDE], refs[SIDE], refs[SIDE + 1], refs[SIDE + 2]
    rows = grad.shape[1]
    cols = parts[0].shape[1] // 3
    for which in range(SIDE):

        @pl.when(z_index[0] == which)
        def _():
            ordered = [parts[(which - source) % SIDE] for source in range(SIDE)]
            for source in range(SIDE):
                for kind in range(3):
                    grad[kind, :, source * cols : (source + 1) * cols] = ordered[source][
                        :rows, kind * cols : (kind + 1) * cols
                    ].astype(F32)
            extra = [part[rows:].astype(F32) for part in ordered]
            total = (extra[0] + extra[1]) + (extra[2] + extra[3])
            small[:EXTRA] = total[:, :LANE]
            small[EXTRA : 2 * EXTRA] = total[:, LANE : 2 * LANE]
            small[2 * EXTRA + 1 : 2 * EXTRA + 2] = total[0:1, 2 * LANE : 3 * LANE]
            small[2 * EXTRA + 2 : 2 * EXTRA + 4] = total[0:2, 3 * LANE : 4 * LANE]

    product = jnp.sum(grad[0] * w_here[0].astype(F32) + grad[1] * w_here[1].astype(F32) + grad[2] * w_here[2].astype(F32), axis=-1, keepdims=True)
    at_row = lax.broadcasted_iota(jnp.int32, (rows, LANE), 0)
    at_lane = lax.broadcasted_iota(jnp.int32, (rows, LANE), 1)
    small[2 * EXTRA : 2 * EXTRA + 1] = jnp.sum(jnp.where(at_row == at_lane, product, 0.0), axis=0, keepdims=True)
    small[2 * EXTRA + 4 :] = jnp.zeros((small.shape[0] - 2 * EXTRA - 4, LANE), F32)


def finish(z_index, parts, w_here):
    kinds, rows, inner = w_here.shape
    height, columns = parts[0].shape
    return kernel_call(
        finish_body,
        (1,),
        [whole(height, columns)] * SIDE + [whole(kinds, rows, inner)],
        [whole(kinds, rows, inner), whole(2 * EXTRA + 8, LANE)],
        [shape((kinds, rows, inner), F32), shape((2 * EXTRA + 8, LANE), F32)],
        scalars=1,
        name="finish",
    )(z_index, *parts, w_here)


def on_device(
    tokens,
    expert_ids,
    capacity,
    gain_attn,
    w_qkv,
    qk_gain,
    w_out,
    gain_ffn,
    w_router,
    w_gate_up,
    w_down,
    cotangent,
):
    length, width = tokens.shape
    expert_count = capacity.shape[0]
    slot_count = length * expert_ids.shape[1] // expert_count
    slots = expert_count * slot_count
    inner = w_qkv.shape[2]
    half = width // 2
    cols = inner // SIDE
    core_index = lax.axis_index("tensor")
    core = core_index.astype(jnp.int32).reshape(1)
    place = [lax.axis_index(a) for a in AXES]
    dp_index = (place[0] * SIDE + place[1]) * SIDE + place[2]
    rows_here_count = width // SIDE**3

    def own_half(value):
        return lax.dynamic_slice_in_dim(value, core_index * half, half, axis=-1)

    expert_of = jnp.asarray(np.repeat(np.eye(expert_count, dtype=np.float32), slot_count, 0), BF)

    def to_owners(rows):
        columns = rows.shape[1]
        return exchange(rows.reshape(expert_count, slot_count, columns), AXES).reshape(slots, columns)

    member, select, grad_send = routing(core, capacity, expert_ids.T, expert_of, cotangent)
    grad_own = to_owners(grad_send)

    table = jnp.asarray(rotary(length, LANE // 2))
    gains = qk_gain.astype(F32)
    gain_one = gain_attn.astype(F32)
    gain_two = gain_ffn.astype(F32).reshape(1, width)
    w_parts = w_qkv.transpose(1, 0, 2)
    normed_one, raw, value_in, attended, partial = attend(
        tokens, gain_one.reshape(1, width), w_parts, w_out, gains, table
    )
    partial_peer = swap(partial)
    middle, normed_two, probs, gates, picked_total, combine, rows_send = middle_step(
        core, tokens, partial, partial_peer, gain_two, select, w_router, member, expert_of
    )
    rows_own = to_owners(rows_send)

    normed_early, attended_late, pair, grad_late, down, _ = together(
        own_half(normed_one), attended, w_gate_up, grad_own, w_down, rows_send
    )
    down = down[0]
    pair = pair[0].transpose(1, 0, 2)
    grad_peer = swap(grad_late)
    d_hidden = hidden_grad(core, grad_late, grad_peer, down)
    rows_own, d_hidden, pair, normed_early = together(rows_own, d_hidden, pair, normed_early)
    normed_group = share(normed_early, "z")
    rows_peer = swap(rows_own)
    acted, d_pair, back_own, back_peer, extra = experts_step(core, rows_own, rows_peer, d_hidden, pair)
    back_peer, attended_late, *normed_group = together(back_peer, attended_late, *normed_group)
    from_one, from_three = shift(attended_late, "y", 1), shift(attended_late, "y", 3)
    back_send = add_pack(back_own, swap(back_peer), extra)
    out_own, out_peer = experts_out(core, acted, down)
    back_send, out_own, out_peer, from_one, from_three = together(
        back_send, out_own, out_peer, from_one, from_three
    )
    back = to_owners(back_send)

    acted_late, own_late, peer_late, _ = together(acted, rows_own, rows_peer, back_send)
    grad_gate_up, grad_down = expert_grads(
        core, own_late, peer_late, grad_late, grad_peer, acted_late, d_pair, own_late
    )
    returned = (out_own.astype(F32) + swap(out_peer).astype(F32)).astype(BF)
    normed_group, _ = together(normed_group, back_send)
    normed_group = turn_parts(normed_group)
    returned, grad_gate_up, grad_down, normed_group = together(returned, grad_gate_up, grad_down, normed_group)
    returned = to_owners(returned)

    gathered = gather_back(back, combine, select, expert_of)
    core_y = jnp.stack([core[0], place[0].astype(jnp.int32)])
    d_logits, d_middle, d_attn, gain_two_local, *d_attn_blocks = middle_back(
        core_y, gathered, swap(gathered), probs, gates, picked_total, member, w_router, middle, cotangent, gain_two
    )

    z_index = place[2].astype(jnp.int32).reshape(1)
    *d_blocks, grad_qk = attend_back(z_index, d_attn, w_out, raw, value_in, gains, table)
    d_group = send_steps(d_blocks, "z")
    normed_group, normed_group_peer, returned, *d_group = together(
        normed_group, swap(normed_group), returned, *d_group
    )

    columns_here = expert_count // 2
    my_logits = lax.dynamic_slice_in_dim(d_logits, core_index * columns_here, columns_here, axis=1)
    partial_grads = group_grads(
        core,
        normed_group,
        normed_group_peer,
        d_group,
        normed_two,
        my_logits,
        gain_two_local,
        grad_qk,
    )
    d_attn_blocks, from_one, _ = together(d_attn_blocks, from_one, d_blocks)
    d_attn_group = send_steps(d_attn_blocks, "y")
    attended_group = [attended_late, from_one, shift(from_one, "y", 1), from_three]
    partial_grads, attended_group, d_attn_group = together(partial_grads, attended_group, d_attn_group)
    arrived = exchange(partial_grads, ("y", "x"))
    d_attn_group, attended_group, late_blocks, late_returned, _ = together(
        d_attn_group, attended_group, d_blocks, returned, partial_grads
    )

    grad_out = out_grads(d_attn_group, attended_group)

    grad_out = send_blocks(grad_out.reshape(SIDE, SIDE, rows_here_count, inner), "z", 1)

    d_one = input_grad(z_index, late_blocks, w_parts)
    d_one = d_one.astype(F32) + swap(d_one).astype(F32)

    residual_in = tokens.astype(F32)
    scale_one = rms(residual_in)
    unit_one = residual_in * scale_one
    weighted = d_one * gain_one
    grad_input = d_middle + scale_one * (
        weighted - unit_one * jnp.mean(weighted * unit_one, axis=-1, keepdims=True)
    )

    mix_own = dot(combine, late_returned, TN)
    result_own = (own_half(middle) + mix_own).astype(BF)
    output = side_by_side(result_own, swap(result_own), core_index)

    grad_out = sum(part.astype(F32) for part in grad_out).astype(BF)
    grad_out = [block_at(grad_out, (place[1] + step) % SIDE, 0) for step in range(SIDE)]
    arrived, grad_input, output, grad_out = together(arrived, grad_input, output, grad_out)
    grad_out = sum(part.astype(F32) for part in send_steps(grad_out, "x"))
    parts = send_steps(sum_arrived(z_index, arrived, rows_here_count), "z")
    w_here = lax.dynamic_slice_in_dim(w_parts, dp_index * rows_here_count, rows_here_count, axis=1)
    grad_qkv, small = finish(z_index, parts, w_here)
    grad_qkv = grad_qkv.transpose(1, 0, 2)
    small_peer = swap(small)
    gain_here = lax.dynamic_slice_in_dim(gain_one, dp_index * rows_here_count, rows_here_count, axis=0)
    grad_gain_one = (small[2 * EXTRA] + small_peer[2 * EXTRA])[:rows_here_count] / gain_here
    cut = lambda value: lax.dynamic_slice_in_dim(value, place[2] * rows_here_count, rows_here_count, axis=-1)
    grad_router = jnp.where(
        core_index == 0,
        jnp.concatenate([small[: 2 * EXTRA], small_peer[: 2 * EXTRA]], axis=0),
        jnp.concatenate([small_peer[: 2 * EXTRA], small[: 2 * EXTRA]], axis=0),
    )
    grad_router = cut(grad_router).T
    grad_gain_two = cut(small[2 * EXTRA + 1])
    grad_qk = small[2 * EXTRA + 2 : 2 * EXTRA + 4] + small_peer[2 * EXTRA + 2 : 2 * EXTRA + 4]

    return (
        output,
        grad_input,
        grad_gain_one,
        grad_qkv,
        grad_qk,
        grad_out,
        grad_gain_two,
        grad_router,
        grad_gate_up[None],
        grad_down[None],
    )


def solution(mesh):
    names = AXES + ("tensor",)
    torus = Mesh(mesh.devices.reshape(SIDE, SIDE, SIDE, 2), names)
    return jax.shard_map(
        on_device,
        mesh=torus,
        in_specs=(
            P(AXES, None),
            P(AXES, None),
            P(),
            P(),
            P(None, None, "tensor"),
            P(),
            P(None, "tensor"),
            P(),
            P(),
            P(AXES, None, None, "tensor"),
            P(AXES, "tensor", None),
            P(AXES, None),
        ),
        out_specs=(
            P(AXES, None),
            P(AXES, None),
            P(AXES),
            P(AXES, None, "tensor"),
            P(),
            P(AXES, "tensor"),
            P(AXES),
            P(AXES, None),
            P(AXES, None, None, "tensor"),
            P(AXES, "tensor", None),
        ),
        check_vma=False,
    )
```

```python
import functools
import math

import jax
import jax.numpy as jnp
import numpy as np
from jax import lax
from jax.experimental import pallas as pl
from jax.experimental.pallas import tpu as pltpu
from jax.sharding import Mesh
from jax.sharding import PartitionSpec as P

AXES = ("y", "x", "z")
SIDE = 4
LANE = 128
BF = jnp.bfloat16
F32 = jnp.float32
MIB = 1 << 20


def dot(a, b, dims):
    return lax.dot_general(a, b, (dims, ((), ())), preferred_element_type=F32)


NN = ((1,), (0,))
NT = ((1,), (1,))
TN = ((0,), (0,))


def rms(values):
    return lax.rsqrt(jnp.mean(values * values, axis=-1, keepdims=True) + 1e-06)


def rotary(length, half_dim):
    position = np.arange(length, dtype=np.float32)
    inverse = np.float32(50000.0) ** (-np.arange(half_dim, dtype=np.float32) / np.float32(half_dim))
    angles = position[:, None] * inverse[None, :].astype(np.float32)
    cosine = np.cos(angles).astype(np.float32)
    sine = np.sin(angles).astype(np.float32)
    return np.stack([np.concatenate([cosine, cosine], 1), np.concatenate([-sine, sine], 1)])


def swap(value):
    return lax.ppermute(value, "tensor", [(0, 1), (1, 0)])


def shift(value, axis, step):
    return lax.ppermute(value, axis, [(i, (i + step) % SIDE) for i in range(SIDE)])


def side_by_side(own, peer, core):
    return jnp.where(
        core == 0,
        jnp.concatenate([own, peer], axis=-1),
        jnp.concatenate([peer, own], axis=-1),
    )


def block_at(value, index, dim):
    return lax.dynamic_index_in_dim(value, index, dim, keepdims=False)


def together(*values):
    return lax.optimization_barrier(values)


def share(value, axis):
    return [value] + [shift(value, axis, step) for step in (1, 2, 3)]


def send_blocks(value, axis, dim):
    here = lax.axis_index(axis)
    own = block_at(value, here, dim)
    return [own] + [shift(block_at(value, (here + step) % SIDE, dim), axis, step) for step in (1, 2, 3)]


def send_steps(blocks, axis):
    return [blocks[0]] + [shift(blocks[step], axis, step) for step in (1, 2, 3)]


def exchange(value, axes):
    return lax.all_to_all(value, axes, split_axis=0, concat_axis=0, tiled=True)


def shape(dims, kind):
    return jax.ShapeDtypeStruct(dims, kind)


def main_memory(dims, kind):
    return pltpu.HBM(dims, kind)


def held(*values):
    return [pltpu.with_memory_space_constraint(value, pltpu.HBM) for value in values]


def kernel_call(body, grid, ins, outs, out_shapes, scratch=(), mib=40, scalars=0, name=None):
    return pl.pallas_call(
        body,
        grid_spec=pltpu.PrefetchScalarGridSpec(
            num_scalar_prefetch=scalars, grid=grid, in_specs=ins, out_specs=outs, scratch_shapes=list(scratch)
        ),
        out_shape=out_shapes,
        compiler_params=pltpu.CompilerParams(vmem_limit_bytes=mib * MIB),
        name=name,
    )


def whole(*dims):
    return pl.BlockSpec(dims, lambda *_: (0,) * len(dims))


def rope(values, table):
    return values * table[0] + pltpu.roll(values, values.shape[-1] // 2, 1) * table[1]


def unrope(values, table):
    return values * table[0] - pltpu.roll(values, values.shape[-1] // 2, 1) * table[1]


def attention_weights(query, key):
    scores = dot(query, key, NT) * (1.0 / math.sqrt(query.shape[-1]))
    raised = jnp.exp(scores - jnp.max(scores, axis=-1, keepdims=True))
    return raised / jnp.sum(raised, axis=-1, keepdims=True)


def attend_body(tokens, gain, w_qkv, w_out, gains, table, normed, raw, turned, kept, value_out, attended, partial, total):
    step = pl.program_id(0)

    @pl.when(step == 0)
    def _():
        x = tokens[...].astype(F32)
        normed[...] = (x * rms(x) * gain[...]).astype(BF)
        total[...] = jnp.zeros_like(total)

    h = normed[...]
    query_raw = dot(h, w_qkv[0], NN)
    key_raw = dot(h, w_qkv[1], NN)
    value = dot(h, w_qkv[2], NN).astype(BF)
    raw[0] = query_raw
    raw[1] = key_raw
    value_out[...] = value
    for at in range(query_raw.shape[1] // LANE):
        cut = slice(at * LANE, (at + 1) * LANE)
        q, k = query_raw[:, cut], key_raw[:, cut]
        query = rope(q * rms(q) * gains[0:1], table).astype(BF)
        key = rope(k * rms(k) * gains[1:2], table).astype(BF)
        turned[0, :, cut] = query
        turned[1, :, cut] = key
        weights = attention_weights(query, key)
        kept[at] = weights
        attended[:, cut] = dot(weights.astype(BF), value[:, cut], NN).astype(BF)
    total[...] += dot(attended[...], w_out[...], NT)

    @pl.when(step == pl.num_programs(0) - 1)
    def _():
        partial[...] = total[...].astype(BF)


def attend(tokens, gain, w_qkv, w_out, gains, table):
    length, width = tokens.shape
    inner = w_qkv.shape[2]
    cols = inner // SIDE
    return kernel_call(
        attend_body,
        (SIDE,),
        [
            whole(length, width),
            whole(1, width),
            pl.BlockSpec((3, width, cols), lambda i: (0, 0, i)),
            pl.BlockSpec((width, cols), lambda i: (0, i)),
            whole(2, LANE),
            whole(2, length, LANE),
        ],
        [
            whole(length, width),
            pl.BlockSpec((2, length, cols), lambda i: (0, 0, i)),
            pl.BlockSpec((2, length, cols), lambda i: (0, 0, i)),
            pl.BlockSpec((cols // LANE, length, length), lambda i: (i, 0, 0)),
            pl.BlockSpec((length, cols), lambda i: (0, i)),
            pl.BlockSpec((length, cols), lambda i: (0, i)),
            whole(length, width),
        ],
        [
            main_memory((length, width), BF),
            main_memory((2, length, inner), F32),
            main_memory((2, length, inner), BF),
            main_memory((inner // LANE, length, length), F32),
            main_memory((length, inner), BF),
            main_memory((length, inner), BF),
            shape((length, width), BF),
        ],
        [pltpu.VMEM((length, width), F32)],
        name="attend",
    )(tokens, gain, w_qkv, w_out, gains, table)


def attend_back_body(z_index, d_attn, w_out, raw, turned, kept, value_in, gains, table, *outs):
    d_gains = outs[SIDE]
    step = pl.program_id(0)
    parts = ([], [], [])

    @pl.when(step == 0)
    def _():
        d_gains[...] = jnp.zeros_like(d_gains)

    d_attended = dot(d_attn[...], w_out[...], NN).astype(BF)
    for at in range(d_attended.shape[1] // LANE):
        cut = slice(at * LANE, (at + 1) * LANE)
        q, k = raw[0, :, cut], raw[1, :, cut]
        rq, rk = rms(q), rms(k)
        unit_q, unit_k = q * rq, k * rk
        query, key = turned[0, :, cut], turned[1, :, cut]
        weights = kept[at]
        grad = d_attended[:, cut]
        d_value = dot(weights.astype(BF), grad, TN)
        d_weights = dot(grad, value_in[:, cut], NT)
        d_scores = (
            weights * (d_weights - jnp.sum(weights * d_weights, axis=-1, keepdims=True))
        ).astype(BF)
        root = 1.0 / math.sqrt(LANE)
        d_query = unrope(dot(d_scores, key, NN) * root, table)
        d_key = unrope(dot(d_scores, query, TN) * root, table)
        d_gains[0:1] += jnp.sum(d_query * unit_q, axis=0, keepdims=True)
        d_gains[1:2] += jnp.sum(d_key * unit_k, axis=0, keepdims=True)
        wq = d_query * gains[0:1]
        wk = d_key * gains[1:2]
        parts[0].append((rq * (wq - unit_q * jnp.mean(wq * unit_q, axis=-1, keepdims=True))).astype(BF))
        parts[1].append((rk * (wk - unit_k * jnp.mean(wk * unit_k, axis=-1, keepdims=True))).astype(BF))
        parts[2].append(d_value.astype(BF))
    for k in range(SIDE):

        @pl.when((z_index[0] + k) % SIDE == step)
        def _():
            for kind in range(3):
                outs[k][kind] = jnp.concatenate(parts[kind], axis=1)


def attend_back(z_index, d_attn, w_out, raw, turned, kept, value_in, gains, table):
    length, width = d_attn.shape
    inner = w_out.shape[1]
    cols = inner // SIDE
    return kernel_call(
        attend_back_body,
        (SIDE,),
        [
            whole(length, width),
            pl.BlockSpec((width, cols), lambda i, z: (0, i)),
            pl.BlockSpec((2, length, cols), lambda i, z: (0, 0, i)),
            pl.BlockSpec((2, length, cols), lambda i, z: (0, 0, i)),
            pl.BlockSpec((cols // LANE, length, length), lambda i, z: (i, 0, 0)),
            pl.BlockSpec((length, cols), lambda i, z: (0, i)),
            whole(2, LANE),
            whole(2, length, LANE),
        ],
        [whole(3, length, cols)] * SIDE + [whole(2, LANE)],
        [shape((3, length, cols), BF)] * SIDE + [shape((2, LANE), F32)],
        scalars=1,
        name="attend_back",
    )(z_index, d_attn, *held(w_out, raw, turned, kept, value_in, gains, table))


def input_grad_body(z_index, *refs):
    w_qkv, out, total = refs[SIDE:]
    step = pl.program_id(0)

    @pl.when(step == 0)
    def _():
        total[...] = jnp.zeros_like(total)

    for k in range(SIDE):

        @pl.when(step == k)
        def _():
            block = refs[k]
            total[...] += dot(block[0], w_qkv[0], NT) + dot(block[1], w_qkv[1], NT) + dot(block[2], w_qkv[2], NT)

    @pl.when(step == pl.num_programs(0) - 1)
    def _():
        out[...] = total[...].astype(BF)


def input_grad(z_index, d_blocks, w_qkv):
    _, length, cols = d_blocks[0].shape
    width = w_qkv.shape[1]
    return kernel_call(
        input_grad_body,
        (SIDE,),
        [whole(3, length, cols)] * SIDE
        + [pl.BlockSpec((3, width, cols), lambda i, z: (0, 0, lax.rem(z[0] + i, SIDE)))],
        whole(length, width),
        shape((length, width), BF),
        [pltpu.VMEM((length, width), F32)],
        scalars=1,
        name="input_grad",
    )(z_index, *d_blocks, *held(w_qkv))


def routing_body(core, capacity, ids, later, expert_of, cotangent, member_out, select, rows):
    experts = expert_of.shape[1]
    length = ids.shape[1]
    at_expert = lax.broadcasted_iota(jnp.int32, (experts, length), 0)
    member = jnp.zeros((experts, length), F32)
    for j in range(ids.shape[0]):
        member = member + (ids[j : j + 1, :] == at_expert).astype(F32)
    member_out[...] = member.T
    ranks = dot(member.astype(BF), later[...], NN)
    row = lax.broadcasted_iota(jnp.int32, (experts, experts), 0)
    column = lax.broadcasted_iota(jnp.int32, (experts, experts), 1)
    limit = jnp.sum(jnp.where(row == column, capacity[...].astype(F32), 0.0), axis=1, keepdims=True)
    code = jnp.where((member > 0.5) & (ranks < limit), ranks, -1.0).astype(BF)
    slots, half = rows.shape
    depth = slots // experts
    chunk = 8 * depth
    slot = lax.broadcasted_iota(jnp.int32, (chunk, length), 0).astype(F32)
    slot = slot - depth * jnp.floor((slot + 0.5) * (1.0 / depth))
    for which in range(2):

        @pl.when(core[0] == which)
        def _():
            for at in range(0, slots, chunk):
                cut = slice(at, at + chunk)
                hit = (dot(expert_of[cut], code, NN) == slot).astype(F32).astype(BF)
                select[cut] = hit
                rows[cut] = dot(hit, cotangent[:, which * half : (which + 1) * half], NN).astype(BF)


def routing(core, capacity, ids, expert_of, cotangent):
    length, width = cotangent.shape
    slots, experts = expert_of.shape
    later = jnp.asarray(np.triu(np.ones((length, length), np.float32), 1), BF)
    return kernel_call(
        routing_body,
        (1,),
        [
            whole(1, experts),
            whole(*ids.shape),
            whole(length, length),
            whole(slots, experts),
            whole(length, width),
        ],
        [whole(length, experts), whole(slots, length), whole(slots, width // 2)],
        [shape((length, experts), F32), main_memory((slots, length), BF), main_memory((slots, width // 2), BF)],
        scalars=1,
        name="routing",
    )(core, *held(capacity.reshape(1, experts), ids, later, expert_of, cotangent))


def middle_body(core, tokens, own, peer, gain, select, w_router, member, expert_of,
                middle, normed, probs_out, gates_out, total_out, combine, rows):
    x2 = tokens[...].astype(F32) + (own[...].astype(F32) + peer[...].astype(F32))
    middle[...] = x2
    normed[...] = (x2 * rms(x2) * gain[...]).astype(BF)
    logits = dot(normed[...], w_router[...], NN)
    raised = jnp.exp(logits - jnp.max(logits, axis=-1, keepdims=True))
    probs = raised / jnp.sum(raised, axis=-1, keepdims=True)
    picked = probs * member[...]
    total = jnp.sum(picked, axis=-1, keepdims=True)
    gates = picked / total
    probs_out[...] = probs
    gates_out[...] = gates
    total_out[...] = total
    low = gates.astype(BF)
    half = rows.shape[1] - LANE
    for at in range(0, rows.shape[0], 256):
        cut = slice(at, at + 256)
        spread = dot(expert_of[cut], low, NT) * select[cut].astype(F32)
        combine[cut] = spread.astype(BF)
        gate = jnp.sum(spread, axis=-1, keepdims=True)
        rows[cut, half:] = jnp.broadcast_to(gate, (256, LANE)).astype(BF)
    for which in range(2):

        @pl.when(core[0] == which)
        def _():
            for at in range(0, rows.shape[0], 256):
                rows[at : at + 256, :half] = dot(
                    select[at : at + 256], normed[:, which * half : (which + 1) * half], NN
                ).astype(BF)


def middle_step(core, tokens, own, peer, gain, select, w_router, member, expert_of):
    length, width = tokens.shape
    slots, experts = expert_of.shape
    columns = width // 2 + LANE
    return kernel_call(
        middle_body,
        (1,),
        [whole(length, width)] * 3
        + [whole(1, width), whole(slots, length), whole(width, experts), whole(length, experts), whole(slots, experts)],
        [
            whole(length, width),
            whole(length, width),
            whole(length, experts),
            whole(length, experts),
            whole(length, 1),
            whole(slots, length),
            whole(slots, columns),
        ],
        [
            main_memory((length, width), F32),
            main_memory((length, width), BF),
            shape((length, experts), F32),
            shape((length, experts), F32),
            shape((length, 1), F32),
            main_memory((slots, length), BF),
            main_memory((slots, columns), BF),
        ],
        scalars=1,
        name="middle",
    )(core, *held(tokens), own, peer, *held(gain, select, w_router, member, expert_of))


def gather_back_body(back, combine, select, expert_of, out):
    half = out.shape[1] - LANE
    experts = expert_of.shape[1]

    @pl.when(pl.program_id(0) == 0)
    def _():
        out[...] = jnp.zeros_like(out)

    out[:, :half] += dot(combine[...], back[:, :half], TN)
    high = back[:, half : half + 1].astype(F32)
    low = back[:, half + 1 : half + 2].astype(F32)
    picked = select[...].astype(F32)
    spread = dot((picked * high).astype(BF), expert_of[...], TN) + dot((picked * low).astype(BF), expert_of[...], TN)
    out[:, half : half + experts] += spread


def gather_back(back, combine, select, expert_of):
    slots, columns = back.shape
    length = combine.shape[1]
    experts = expert_of.shape[1]
    rows = lambda n: pl.BlockSpec((2 * ROWS, n), lambda i: (i, 0))
    return kernel_call(
        gather_back_body,
        (slots // (2 * ROWS),),
        [rows(columns), rows(length), rows(length), rows(experts)],
        whole(length, columns),
        shape((length, columns), F32),
        name="gather_back",
    )(back, *held(combine, select, expert_of))


def middle_back_body(core, own, peer, probs, gates, total, member, w_router, middle, cotangent, gain,
                     d_logits_out, d_middle, d_attn, d_gain, *d_attn_blocks):
    half = own.shape[1] - LANE
    experts = probs.shape[1]
    d_gates = own[:, half : half + experts] + peer[:, half : half + experts]
    g, p = gates[...], probs[...]
    d_picked = member[...] * (d_gates - jnp.sum(d_gates * g, axis=-1, keepdims=True)) / total[...]
    d_logits = (p * (d_picked - jnp.sum(p * d_picked, axis=-1, keepdims=True))).astype(BF)
    d_logits_out[...] = d_logits
    d_normed = dot(d_logits, w_router[...], NT)
    for which in range(2):

        @pl.when(core[0] == which)
        def _():
            first, second = (own, peer) if which == 0 else (peer, own)
            d_middle[:, :half] = first[:, :half]
            d_middle[:, half:] = second[:, :half]

    d_normed = d_normed + d_middle[...]
    x2 = middle[...]
    scale = rms(x2)
    unit = x2 * scale
    gain_sum = jnp.sum(d_normed * unit, axis=0, keepdims=True)

    @pl.when(pl.program_id(0) == 0)
    def _():
        d_gain[...] = gain_sum

    @pl.when(pl.program_id(0) > 0)
    def _():
        d_gain[...] += gain_sum

    weighted = d_normed * gain[...]
    value = cotangent[...].astype(F32) + scale * (
        weighted - unit * jnp.mean(weighted * unit, axis=-1, keepdims=True)
    )
    d_middle[...] = value
    low = value.astype(BF)
    d_attn[...] = low
    cut = d_attn_blocks[0].shape[1]
    for which in range(SIDE):

        @pl.when(core[1] == which)
        def _():
            for k in range(SIDE):
                at = (which + k) % SIDE * cut
                d_attn_blocks[k][...] = low[:, at : at + cut]


def middle_back(core, own, peer, probs, gates, total, member, w_router, middle, cotangent, gain):
    length, width = middle.shape
    experts = probs.shape[1]
    columns = own.shape[1]
    block = length // 2
    rows = lambda n: pl.BlockSpec((block, n), lambda i, c: (i, 0))
    return kernel_call(
        middle_back_body,
        (length // block,),
        [rows(columns)] * 2
        + [rows(experts)] * 2
        + [rows(1), rows(experts), whole(width, experts), rows(width), rows(width), whole(1, width)],
        [rows(experts), rows(width), rows(width), whole(1, width)] + [rows(width // SIDE)] * SIDE,
        [
            shape((length, experts), BF),
            main_memory((length, width), F32),
            shape((length, width), BF),
            shape((1, width), F32),
        ]
        + [shape((length, width // SIDE), BF)] * SIDE,
        scalars=1,
        name="middle_back",
    )(core, own, peer, *held(probs, gates, total, member, w_router, middle, cotangent, gain))


def hidden_grad_body(core, own, peer, down_own, down_peer, out):
    half = down_own.shape[1]
    out[...] = dot(own[:, :half], down_own[...], NT) + dot(peer[:, :half], down_peer[...], NT)


ROWS = 256


def hidden_grad(core, own, peer, down):
    slots, columns = own.shape
    hidden, width = down.shape
    half = width // 2
    return kernel_call(
        hidden_grad_body,
        (slots // ROWS,),
        [
            pl.BlockSpec((ROWS, columns), lambda i, c: (i, 0)),
            pl.BlockSpec((ROWS, columns), lambda i, c: (i, 0)),
            pl.BlockSpec((hidden, half), lambda i, c: (0, c[0])),
            pl.BlockSpec((hidden, half), lambda i, c: (0, 1 - c[0])),
        ],
        pl.BlockSpec((ROWS, hidden), lambda i, c: (i, 0)),
        main_memory((slots, hidden), F32),
        scalars=1,
        name="hidden_grad",
    )(core, *held(own, peer, down, down))


def experts_body(core, own, peer, d_hidden, pair_own, pair_peer, acted, d_pair, back_own, back_peer, extra):
    hidden = d_hidden.shape[1]
    half = pair_own.shape[1]
    mine, other = own[:, :half], peer[:, :half]
    gate = dot(mine, pair_own[0], NN) + dot(other, pair_peer[0], NN)
    up = dot(mine, pair_own[1], NN) + dot(other, pair_peer[1], NN)
    sig = 1.0 / (1.0 + jnp.exp(-gate))
    silu = gate * sig
    act = (silu * up).astype(BF)
    acted[...] = act
    d_act = d_hidden[...]
    slot_grad = jnp.sum(d_act * act.astype(F32), axis=-1, keepdims=True)
    high = slot_grad.astype(BF)
    low = (slot_grad - high.astype(F32)).astype(BF)
    at = lax.broadcasted_iota(jnp.int32, extra.shape, 1)
    extra[...] = jnp.where(at == 0, high.astype(F32), jnp.where(at == 1, low.astype(F32), 0.0)).astype(BF)
    d_gate = (d_act * up * sig * (1.0 + gate * (1.0 - sig))).astype(BF)
    d_up = (d_act * silu).astype(BF)
    d_pair[:, :hidden] = d_gate
    d_pair[:, hidden:] = d_up
    back_peer[...] = (dot(d_gate, pair_peer[0], NT) + dot(d_up, pair_peer[1], NT)).astype(BF)
    back_own[...] = (dot(d_gate, pair_own[0], NT) + dot(d_up, pair_own[1], NT)).astype(BF)


def experts_out_body(core, acted, acted_peer, down, down_far, out):
    out[...] = (dot(acted[...], down[...], NN) + dot(acted_peer[...], down_far[...], NN)).astype(BF)


def experts_out(core, acted, acted_peer, down, down_far):
    slots, hidden = acted.shape
    half = down_far.shape[1]
    rows = lambda n: pl.BlockSpec((ROWS, n), lambda i, c: (i, 0))
    return kernel_call(
        experts_out_body,
        (slots // ROWS,),
        [
            rows(hidden),
            rows(hidden),
            pl.BlockSpec((hidden, half), lambda i, c: (0, c[0])),
            whole(hidden, half),
        ],
        rows(half),
        main_memory((slots, half), BF),
        scalars=1,
        name="experts_out",
    )(core, *held(acted, acted_peer, down, down_far))


def experts_step(core, own, peer, d_hidden, pair):
    slots, columns = own.shape
    half = columns - LANE
    hidden = pair.shape[2]
    rows = lambda n: pl.BlockSpec((ROWS, n), lambda i, c: (i, 0))
    return kernel_call(
        experts_body,
        (slots // ROWS,),
        [
            rows(columns),
            rows(columns),
            rows(hidden),
            pl.BlockSpec((2, half, hidden), lambda i, c: (0, c[0], 0)),
            pl.BlockSpec((2, half, hidden), lambda i, c: (0, 1 - c[0], 0)),
        ],
        [rows(hidden), rows(2 * hidden), rows(half), rows(half), rows(LANE)],
        [
            main_memory((slots, hidden), BF),
            main_memory((slots, 2 * hidden), BF),
            main_memory((slots, half), BF),
            main_memory((slots, half), BF),
            shape((slots, LANE), BF),
        ],
        scalars=1,
        name="experts",
    )(core, *held(own, peer, d_hidden, pair, pair))


def add_pack_body(own, peer, extra, out):
    half = own.shape[1]
    out[:, :half] = (own[...].astype(F32) + peer[...].astype(F32)).astype(BF)
    out[:, half:] = extra[...]


def add_pack(own, peer, extra):
    slots, half = own.shape
    rows = lambda n: pl.BlockSpec((ROWS, n), lambda i: (i, 0))
    return kernel_call(
        add_pack_body,
        (slots // ROWS,),
        [rows(half), rows(half), rows(LANE)],
        rows(half + LANE),
        main_memory((slots, half + LANE), BF),
        name="add_pack",
    )(own, peer, extra)


def expert_grads_body(core, own, peer, grad_own, grad_peer, acted, d_pair, gates, grad_pair, grad_down, pair_low, act_low):
    step = pl.program_id(0)
    hidden = acted.shape[1]

    @pl.when(step == 0)
    def _():
        gate = gates[:, :1].astype(F32)
        pair_low[...] = (d_pair[...].astype(F32) * gate).astype(BF)
        act_low[...] = (acted[...].astype(F32) * gate).astype(BF)

    def part(rows, grads):
        value = dot(rows[...], pair_low[...], TN)
        grad_pair[:, 0, :] = value[:, :hidden]
        grad_pair[:, 1, :] = value[:, hidden:]
        grad_down[...] = dot(act_low[...], grads[...], TN)

    @pl.when(step < SIDE)
    def _():
        part(own, grad_own)

    @pl.when(step >= SIDE)
    def _():
        part(peer, grad_peer)


def expert_grads(core, own, peer, grad_own, grad_peer, acted, d_pair, gates):
    slots, half = grad_own.shape
    hidden = acted.shape[1]
    cut = half // SIDE
    first = pl.BlockSpec((slots, cut), lambda i, c: (0, jnp.minimum(i, SIDE - 1)))
    second = pl.BlockSpec((slots, cut), lambda i, c: (0, jnp.maximum(i - SIDE, 0)))

    def target(i, c):
        return jnp.where(i < SIDE, c[0] * SIDE + i, (1 - c[0]) * SIDE + i - SIDE)

    return kernel_call(
        expert_grads_body,
        (2 * SIDE,),
        [first, second, first, second, whole(slots, hidden), whole(slots, 2 * hidden), pl.BlockSpec((slots, LANE), lambda i, c: (0, half // LANE))],
        [
            pl.BlockSpec((cut, 2, hidden), lambda i, c: (target(i, c), 0, 0)),
            pl.BlockSpec((hidden, cut), lambda i, c: (0, target(i, c))),
        ],
        [shape((2 * half, 2, hidden), F32), shape((hidden, 2 * half), F32)],
        [pltpu.VMEM((slots, 2 * hidden), BF), pltpu.VMEM((slots, hidden), BF)],
        mib=48,
        scalars=1,
        name="expert_grads",
    )(core, *held(own, peer, grad_own, grad_peer, acted, d_pair, gates))


EXTRA = 8


def group_grads_body(core, own, peer, *refs):
    step = pl.program_id(0)
    d_group = refs[:SIDE]
    normed_two, d_logits, d_gain, d_qk, out, right = refs[SIDE:]
    _, length, cols = d_group[0].shape
    targets = out.shape[0]
    rows = out.shape[1] - EXTRA

    @pl.when(step == 0)
    def _():
        for k in range(SIDE):
            for which in range(3):
                right[k * length : (k + 1) * length, which * cols : (which + 1) * cols] = d_group[k][which]

    def part(normed):
        value = dot(normed[...], right[...], NN).astype(BF)
        for k in range(targets):
            out[k, :rows] = value[k * rows : (k + 1) * rows]

    @pl.when(step < SIDE // 2)
    def _():
        part(own)

    @pl.when(step >= SIDE // 2)
    def _():
        part(peer)

    router = dot(d_logits[...], normed_two[...], TN)
    for k in range(targets):
        cut = slice(k * rows, (k + 1) * rows)
        for at in range(SIDE):
            out[k, rows:, at * LANE : (at + 1) * LANE] = router[at * EXTRA : (at + 1) * EXTRA, cut].astype(BF)
        out[k, rows:, SIDE * LANE : (SIDE + 1) * LANE] = jnp.broadcast_to(d_gain[:, cut], (EXTRA, LANE)).astype(BF)
        out[k, rows:, (SIDE + 1) * LANE :] = jnp.concatenate([d_qk[...]] * (EXTRA // 2), axis=0).astype(BF)


def turn_parts_body(*refs):
    value = jnp.concatenate([part[...].astype(F32) for part in refs[:SIDE]], axis=0)
    refs[SIDE][...] = value.T.astype(BF)


def turn_parts(parts):
    length, width = parts[0].shape
    cut = 256
    return kernel_call(
        turn_parts_body,
        (width // cut,),
        [pl.BlockSpec((length, cut), lambda i: (0, i))] * SIDE,
        pl.BlockSpec((cut, SIDE * length), lambda i: (i, 0)),
        main_memory((width, SIDE * length), BF),
        name="turn_parts",
    )(*held(*parts))


def group_grads(core, own, peer, d_group, normed_two, d_logits, d_gain, d_qk):
    half, depth = own.shape
    length = depth // SIDE
    cols = d_group[0].shape[2]
    steps = SIDE // 2
    cut = half // steps
    places = SIDE * SIDE
    rows = 2 * half // places

    def target(i, c):
        return jnp.where(i < steps, c[0] * steps + i, (1 - c[0]) * steps + i - steps)

    return kernel_call(
        group_grads_body,
        (2 * steps,),
        [
            pl.BlockSpec((cut, depth), lambda i, c: (jnp.minimum(i, steps - 1), 0)),
            pl.BlockSpec((cut, depth), lambda i, c: (jnp.maximum(i - steps, 0), 0)),
        ]
        + [whole(3, length, cols)] * SIDE
        + [
            pl.BlockSpec((length, cut), lambda i, c: (0, target(i, c))),
            whole(length, d_logits.shape[1]),
            pl.BlockSpec((1, cut), lambda i, c: (0, target(i, c))),
            whole(2, LANE),
        ],
        pl.BlockSpec((cut // rows, rows + EXTRA, 3 * cols), lambda i, c: (target(i, c), 0, 0)),
        main_memory((places, rows + EXTRA, 3 * cols), BF),
        [pltpu.VMEM((depth, 3 * cols), BF)],
        scalars=1,
        name="group_grads",
    )(core, *held(own, peer), *d_group, *held(normed_two), d_logits, d_gain, d_qk)


def out_grads_body(*refs):
    out = refs[-1]
    rows = out.shape[0]
    left = jnp.concatenate([part[:, :rows] for part in refs[:SIDE]], axis=0)
    right = jnp.concatenate([refs[SIDE][...], refs[SIDE + 1][...], refs[1][:, rows:], refs[SIDE + 2][...]], axis=0)
    out[...] = dot(left, right, TN).astype(BF)


def out_grads(d_attn, attended):
    length, rows = d_attn[0].shape
    inner = attended[0].shape[1]
    return kernel_call(
        out_grads_body,
        (1,),
        [whole(*part.shape) for part in d_attn] + [whole(length, inner)] * len(attended),
        whole(rows, inner),
        shape((rows, inner), BF),
        name="out_grads",
    )(*d_attn, *held(*attended))


def sum_arrived_body(rows, z_index, arrived, *outs):
    value = arrived[0].astype(F32)
    for k in range(1, arrived.shape[0]):
        value = value + arrived[k].astype(F32)
    value = value.astype(BF)
    main = SIDE * rows
    for which in range(SIDE):

        @pl.when(z_index[0] == which)
        def _():
            for step in range(SIDE):
                at = (which + step) % SIDE * rows
                outs[step][:rows] = value[at : at + rows]

    for step in range(SIDE):
        outs[step][rows:] = value[main:]


def sum_arrived(z_index, arrived, rows):
    places, height, columns = arrived.shape
    cols = columns // 3
    return kernel_call(
        functools.partial(sum_arrived_body, rows),
        (3,),
        [pl.BlockSpec((places, height, cols), lambda i, z: (0, 0, i))],
        [pl.BlockSpec((rows + EXTRA, cols), lambda i, z: (0, i))] * SIDE,
        [shape((rows + EXTRA, columns), BF)] * SIDE,
        scalars=1,
        name="sum_arrived",
    )(z_index, arrived)


def finish_body(z_index, *refs):
    parts, w_here, grad, small = refs[:SIDE], refs[SIDE], refs[SIDE + 1], refs[SIDE + 2]
    rows = grad.shape[1]
    cols = parts[0].shape[1] // 3
    for which in range(SIDE):

        @pl.when(z_index[0] == which)
        def _():
            ordered = [parts[(which - source) % SIDE] for source in range(SIDE)]
            for source in range(SIDE):
                for kind in range(3):
                    grad[kind, :, source * cols : (source + 1) * cols] = ordered[source][
                        :rows, kind * cols : (kind + 1) * cols
                    ].astype(F32)
            extra = [part[rows:].astype(F32) for part in ordered]
            total = (extra[0] + extra[1]) + (extra[2] + extra[3])
            for at in range(SIDE):
                small[at * EXTRA : (at + 1) * EXTRA] = total[:, at * LANE : (at + 1) * LANE]
            small[SIDE * EXTRA + 1 : SIDE * EXTRA + 2] = total[0:1, SIDE * LANE : (SIDE + 1) * LANE]
            small[SIDE * EXTRA + 2 : SIDE * EXTRA + 4] = total[0:2, (SIDE + 1) * LANE :]

    product = jnp.sum(grad[0] * w_here[0].astype(F32) + grad[1] * w_here[1].astype(F32) + grad[2] * w_here[2].astype(F32), axis=-1, keepdims=True)
    at_row = lax.broadcasted_iota(jnp.int32, (rows, LANE), 0)
    at_lane = lax.broadcasted_iota(jnp.int32, (rows, LANE), 1)
    small[SIDE * EXTRA : SIDE * EXTRA + 1] = jnp.sum(jnp.where(at_row == at_lane, product, 0.0), axis=0, keepdims=True)
    small[SIDE * EXTRA + 4 :] = jnp.zeros((small.shape[0] - SIDE * EXTRA - 4, LANE), F32)


def finish(z_index, parts, w_here):
    kinds, rows, inner = w_here.shape
    height, columns = parts[0].shape
    return kernel_call(
        finish_body,
        (1,),
        [whole(height, columns)] * SIDE + [whole(kinds, rows, inner)],
        [whole(kinds, rows, inner), whole(SIDE * EXTRA + 8, LANE)],
        [shape((kinds, rows, inner), F32), shape((SIDE * EXTRA + 8, LANE), F32)],
        scalars=1,
        name="finish",
    )(z_index, *parts, w_here)


def on_device(
    tokens,
    expert_ids,
    capacity,
    gain_attn,
    w_qkv,
    qk_gain,
    w_out,
    gain_ffn,
    w_router,
    w_gate_up,
    w_down,
    cotangent,
):
    length, width = tokens.shape
    expert_count = capacity.shape[0]
    slot_count = length * expert_ids.shape[1] // expert_count
    slots = expert_count * slot_count
    inner = w_qkv.shape[2]
    half = width // 2
    cols = inner // SIDE
    core_index = lax.axis_index("tensor")
    core = core_index.astype(jnp.int32).reshape(1)
    place = [lax.axis_index(a) for a in AXES]
    dp_index = (place[0] * SIDE + place[1]) * SIDE + place[2]
    rows_here_count = width // SIDE**3

    def own_half(value):
        return lax.dynamic_slice_in_dim(value, core_index * half, half, axis=-1)

    expert_of = jnp.asarray(np.repeat(np.eye(expert_count, dtype=np.float32), slot_count, 0), BF)

    def to_owners(rows):
        columns = rows.shape[1]
        return exchange(rows.reshape(expert_count, slot_count, columns), AXES).reshape(slots, columns)

    member, select, grad_send = routing(core, capacity, expert_ids.T, expert_of, cotangent)
    grad_own = to_owners(grad_send)

    table = jnp.asarray(rotary(length, LANE // 2))
    gains = qk_gain.astype(F32)
    gain_one = gain_attn.astype(F32)
    gain_two = gain_ffn.astype(F32).reshape(1, width)
    w_parts = w_qkv.transpose(1, 0, 2)
    normed_one, raw, turned, kept, value_in, attended, partial = attend(
        tokens, gain_one.reshape(1, width), w_parts, w_out, gains, table
    )
    partial_peer = swap(partial)
    middle, normed_two, probs, gates, picked_total, combine, rows_send = middle_step(
        core, tokens, partial, partial_peer, gain_two, select, w_router, member, expert_of
    )
    rows_own = to_owners(rows_send)

    normed_early, attended_late, pair, grad_late, down, _ = together(
        own_half(normed_one), attended, w_gate_up, grad_own, w_down, rows_send
    )
    down = down[0]
    pair = pair[0].transpose(1, 0, 2)
    grad_peer = swap(grad_late)
    d_hidden = hidden_grad(core, grad_late, grad_peer, down)
    down_far = swap(lax.dynamic_slice_in_dim(down, (1 - core_index) * half, half, axis=1))
    rows_own, d_hidden, pair, normed_early, down_far = together(rows_own, d_hidden, pair, normed_early, down_far)
    normed_group = share(normed_early, "z")
    rows_peer = swap(rows_own)
    acted, d_pair, back_own, back_peer, extra = experts_step(core, rows_own, rows_peer, d_hidden, pair)
    back_peer, attended_late, *normed_group = together(back_peer, attended_late, *normed_group)
    from_one, from_three = shift(attended_late, "y", 1), shift(attended_late, "y", 3)
    back_send = add_pack(back_own, swap(back_peer), extra)
    back_send, acted_peer, from_one, from_three = together(back_send, swap(acted), from_one, from_three)
    back = to_owners(back_send)

    acted_late, own_late, peer_late, _ = together(acted, rows_own, rows_peer, back_send)
    grad_gate_up, grad_down = expert_grads(
        core, own_late, peer_late, grad_late, grad_peer, acted_late, d_pair, own_late
    )
    returned = experts_out(core, acted_late, acted_peer, down, down_far)
    normed_group, _ = together(normed_group, back_send)
    normed_group = turn_parts(normed_group)
    returned, grad_gate_up, grad_down, normed_group = together(returned, grad_gate_up, grad_down, normed_group)
    returned = to_owners(returned)

    gathered = gather_back(back, combine, select, expert_of)
    core_y = jnp.stack([core[0], place[0].astype(jnp.int32)])
    d_logits, d_middle, d_attn, gain_two_local, *d_attn_blocks = middle_back(
        core_y, gathered, swap(gathered), probs, gates, picked_total, member, w_router, middle, cotangent, gain_two
    )

    z_index = place[2].astype(jnp.int32).reshape(1)
    d_attn, normed_group_peer = together(d_attn, swap(normed_group))
    *d_blocks, grad_qk = attend_back(z_index, d_attn, w_out, raw, turned, kept, value_in, gains, table)
    d_group = send_steps(d_blocks, "z")
    returned, *d_group = together(returned, *d_group)

    columns_here = expert_count // 2
    my_logits = lax.dynamic_slice_in_dim(d_logits, core_index * columns_here, columns_here, axis=1)
    partial_grads = group_grads(
        core,
        normed_group,
        normed_group_peer,
        d_group,
        normed_two,
        my_logits,
        gain_two_local,
        grad_qk,
    )
    d_attn_blocks, from_one, _ = together(d_attn_blocks, from_one, d_blocks)
    d_attn_group = [
        d_attn_blocks[0],
        shift(jnp.concatenate([d_attn_blocks[1], from_one], axis=1), "y", 1),
        shift(d_attn_blocks[2], "y", 2),
        shift(d_attn_blocks[3], "y", 3),
    ]
    attended_group = [attended_late, from_one, from_three]
    partial_grads, attended_group, d_attn_group = together(partial_grads, attended_group, d_attn_group)
    arrived = exchange(partial_grads, ("y", "x"))
    d_attn_group, attended_group, late_blocks, late_returned, _ = together(
        d_attn_group, attended_group, d_blocks, returned, partial_grads
    )

    grad_out = out_grads(d_attn_group, attended_group)

    grad_out = send_blocks(grad_out.reshape(SIDE, SIDE, rows_here_count, inner), "z", 1)

    d_one = input_grad(z_index, late_blocks, w_parts)
    d_one = d_one.astype(F32) + swap(d_one).astype(F32)

    residual_in = tokens.astype(F32)
    scale_one = rms(residual_in)
    unit_one = residual_in * scale_one
    weighted = d_one * gain_one
    grad_input = d_middle + scale_one * (
        weighted - unit_one * jnp.mean(weighted * unit_one, axis=-1, keepdims=True)
    )

    mix_own = dot(combine, late_returned, TN)
    result_own = (own_half(middle) + mix_own).astype(BF)
    output = side_by_side(result_own, swap(result_own), core_index)

    grad_out = sum(part.astype(F32) for part in grad_out).astype(BF)
    grad_out = [block_at(grad_out, (place[1] + step) % SIDE, 0) for step in range(SIDE)]
    grad_input, output, *grad_out = together(grad_input, output, *grad_out)
    grad_out = send_steps(grad_out, "x")
    arrived, grad_input, output, *grad_out = together(arrived, grad_input, output, *grad_out)
    grad_out = sum(part.astype(F32) for part in grad_out)
    parts = send_steps(sum_arrived(z_index, arrived, rows_here_count), "z")
    w_here = lax.dynamic_slice_in_dim(w_parts, dp_index * rows_here_count, rows_here_count, axis=1)
    grad_qkv, small = finish(z_index, parts, w_here)
    grad_qkv = grad_qkv.transpose(1, 0, 2)
    small_peer = swap(small)
    gain_here = lax.dynamic_slice_in_dim(gain_one, dp_index * rows_here_count, rows_here_count, axis=0)
    grad_gain_one = (small[SIDE * EXTRA] + small_peer[SIDE * EXTRA])[:rows_here_count] / gain_here
    cut = lambda value: lax.dynamic_slice_in_dim(value, place[2] * rows_here_count, rows_here_count, axis=-1)
    grad_router = jnp.where(
        core_index == 0,
        jnp.concatenate([small[: SIDE * EXTRA], small_peer[: SIDE * EXTRA]], axis=0),
        jnp.concatenate([small_peer[: SIDE * EXTRA], small[: SIDE * EXTRA]], axis=0),
    )
    grad_router = cut(grad_router).T
    grad_gain_two = cut(small[SIDE * EXTRA + 1])
    grad_qk = small[SIDE * EXTRA + 2 : SIDE * EXTRA + 4] + small_peer[SIDE * EXTRA + 2 : SIDE * EXTRA + 4]

    return (
        output,
        grad_input,
        grad_gain_one,
        grad_qkv,
        grad_qk,
        grad_out,
        grad_gain_two,
        grad_router,
        grad_gate_up[None],
        grad_down[None],
    )


def solution(mesh):
    names = AXES + ("tensor",)
    torus = Mesh(mesh.devices.reshape(SIDE, SIDE, SIDE, 2), names)
    return jax.shard_map(
        on_device,
        mesh=torus,
        in_specs=(
            P(AXES, None),
            P(AXES, None),
            P(),
            P(),
            P(None, None, "tensor"),
            P(),
            P(None, "tensor"),
            P(),
            P(),
            P(AXES, None, None, "tensor"),
            P(AXES, "tensor", None),
            P(AXES, None),
        ),
        out_specs=(
            P(AXES, None),
            P(AXES, None),
            P(AXES),
            P(AXES, None, "tensor"),
            P(),
            P(AXES, "tensor"),
            P(AXES),
            P(AXES, None),
            P(AXES, None, None, "tensor"),
            P(AXES, "tensor", None),
        ),
        check_vma=False,
    )
```

```python
import functools
import math

import jax
import jax.numpy as jnp
import numpy as np
from jax import lax
from jax.experimental import pallas as pl
from jax.experimental.pallas import tpu as pltpu
from jax.sharding import Mesh
from jax.sharding import PartitionSpec as P

AXES = ("y", "x", "z")
SIDE = 4
LANE = 128
BF = jnp.bfloat16
F32 = jnp.float32
MIB = 1 << 20


def dot(a, b, dims):
    return lax.dot_general(a, b, (dims, ((), ())), preferred_element_type=F32)


NN = ((1,), (0,))
NT = ((1,), (1,))
TN = ((0,), (0,))


def rms(values):
    return lax.rsqrt(jnp.mean(values * values, axis=-1, keepdims=True) + 1e-06)


def rotary(length, half_dim):
    position = np.arange(length, dtype=np.float32)
    inverse = np.float32(50000.0) ** (-np.arange(half_dim, dtype=np.float32) / np.float32(half_dim))
    angles = position[:, None] * inverse[None, :].astype(np.float32)
    cosine = np.cos(angles).astype(np.float32)
    sine = np.sin(angles).astype(np.float32)
    return np.stack([np.concatenate([cosine, cosine], 1), np.concatenate([-sine, sine], 1)])


def swap(value):
    return lax.ppermute(value, "tensor", [(0, 1), (1, 0)])


def shift(value, axis, step):
    return lax.ppermute(value, axis, [(i, (i + step) % SIDE) for i in range(SIDE)])


def side_by_side(own, peer, core):
    return jnp.where(
        core == 0,
        jnp.concatenate([own, peer], axis=-1),
        jnp.concatenate([peer, own], axis=-1),
    )


def block_at(value, index, dim):
    return lax.dynamic_index_in_dim(value, index, dim, keepdims=False)


def together(*values):
    return lax.optimization_barrier(values)


def share(value, axis):
    return [value] + [shift(value, axis, step) for step in (1, 2, 3)]


def send_blocks(value, axis, dim):
    here = lax.axis_index(axis)
    own = block_at(value, here, dim)
    return [own] + [shift(block_at(value, (here + step) % SIDE, dim), axis, step) for step in (1, 2, 3)]


def send_steps(blocks, axis):
    return [blocks[0]] + [shift(blocks[step], axis, step) for step in (1, 2, 3)]


def exchange(value, axes):
    return lax.all_to_all(value, axes, split_axis=0, concat_axis=0, tiled=True)


def shape(dims, kind):
    return jax.ShapeDtypeStruct(dims, kind)


def main_memory(dims, kind):
    return pltpu.HBM(dims, kind)


def held(*values):
    return [pltpu.with_memory_space_constraint(value, pltpu.HBM) for value in values]


def kernel_call(body, grid, ins, outs, out_shapes, scratch=(), mib=40, scalars=0, name=None):
    return pl.pallas_call(
        body,
        grid_spec=pltpu.PrefetchScalarGridSpec(
            num_scalar_prefetch=scalars, grid=grid, in_specs=ins, out_specs=outs, scratch_shapes=list(scratch)
        ),
        out_shape=out_shapes,
        compiler_params=pltpu.CompilerParams(vmem_limit_bytes=mib * MIB),
        name=name,
    )


def whole(*dims):
    return pl.BlockSpec(dims, lambda *_: (0,) * len(dims))


def rope(values, table):
    return values * table[0] + pltpu.roll(values, values.shape[-1] // 2, 1) * table[1]


def unrope(values, table):
    return values * table[0] - pltpu.roll(values, values.shape[-1] // 2, 1) * table[1]


def attention_weights(query, key):
    scores = dot(query, key, NT) * (1.0 / math.sqrt(query.shape[-1]))
    raised = jnp.exp(scores - jnp.max(scores, axis=-1, keepdims=True))
    return raised / jnp.sum(raised, axis=-1, keepdims=True)


def attend_body(tokens, gain, w_qkv, w_out, gains, table, normed, raw, turned, kept, value_out, attended, partial, total):
    step = pl.program_id(0)

    @pl.when(step == 0)
    def _():
        x = tokens[...].astype(F32)
        normed[...] = (x * rms(x) * gain[...]).astype(BF)
        total[...] = jnp.zeros_like(total)

    h = normed[...]
    query_raw = dot(h, w_qkv[0], NN)
    key_raw = dot(h, w_qkv[1], NN)
    value = dot(h, w_qkv[2], NN).astype(BF)
    raw[0] = query_raw
    raw[1] = key_raw
    value_out[...] = value
    for at in range(query_raw.shape[1] // LANE):
        cut = slice(at * LANE, (at + 1) * LANE)
        q, k = query_raw[:, cut], key_raw[:, cut]
        query = rope(q * rms(q) * gains[0:1], table).astype(BF)
        key = rope(k * rms(k) * gains[1:2], table).astype(BF)
        turned[0, :, cut] = query
        turned[1, :, cut] = key
        weights = attention_weights(query, key)
        kept[at] = weights
        attended[:, cut] = dot(weights.astype(BF), value[:, cut], NN).astype(BF)
    total[...] += dot(attended[...], w_out[...], NT)

    @pl.when(step == pl.num_programs(0) - 1)
    def _():
        partial[...] = total[...].astype(BF)


def attend(tokens, gain, w_qkv, w_out, gains, table):
    length, width = tokens.shape
    inner = w_qkv.shape[2]
    cols = inner // SIDE
    return kernel_call(
        attend_body,
        (SIDE,),
        [
            whole(length, width),
            whole(1, width),
            pl.BlockSpec((3, width, cols), lambda i: (0, 0, i)),
            pl.BlockSpec((width, cols), lambda i: (0, i)),
            whole(2, LANE),
            whole(2, length, LANE),
        ],
        [
            whole(length, width),
            pl.BlockSpec((2, length, cols), lambda i: (0, 0, i)),
            pl.BlockSpec((2, length, cols), lambda i: (0, 0, i)),
            pl.BlockSpec((cols // LANE, length, length), lambda i: (i, 0, 0)),
            pl.BlockSpec((length, cols), lambda i: (0, i)),
            pl.BlockSpec((length, cols), lambda i: (0, i)),
            whole(length, width),
        ],
        [
            main_memory((length, width), BF),
            main_memory((2, length, inner), F32),
            main_memory((2, length, inner), BF),
            main_memory((inner // LANE, length, length), F32),
            main_memory((length, inner), BF),
            main_memory((length, inner), BF),
            shape((length, width), BF),
        ],
        [pltpu.VMEM((length, width), F32)],
        name="attend",
    )(tokens, gain, w_qkv, w_out, gains, table)


def attend_back_body(z_index, d_attn, w_out, raw, turned, kept, value_in, gains, table, *outs):
    d_gains = outs[SIDE]
    step = pl.program_id(0)
    parts = ([], [], [])

    @pl.when(step == 0)
    def _():
        d_gains[...] = jnp.zeros_like(d_gains)

    d_attended = dot(d_attn[...], w_out[...], NN).astype(BF)
    for at in range(d_attended.shape[1] // LANE):
        cut = slice(at * LANE, (at + 1) * LANE)
        q, k = raw[0, :, cut], raw[1, :, cut]
        rq, rk = rms(q), rms(k)
        unit_q, unit_k = q * rq, k * rk
        query, key = turned[0, :, cut], turned[1, :, cut]
        weights = kept[at]
        grad = d_attended[:, cut]
        d_value = dot(weights.astype(BF), grad, TN)
        d_weights = dot(grad, value_in[:, cut], NT)
        d_scores = (
            weights * (d_weights - jnp.sum(weights * d_weights, axis=-1, keepdims=True))
        ).astype(BF)
        root = 1.0 / math.sqrt(LANE)
        d_query = unrope(dot(d_scores, key, NN) * root, table)
        d_key = unrope(dot(d_scores, query, TN) * root, table)
        d_gains[0:1] += jnp.sum(d_query * unit_q, axis=0, keepdims=True)
        d_gains[1:2] += jnp.sum(d_key * unit_k, axis=0, keepdims=True)
        wq = d_query * gains[0:1]
        wk = d_key * gains[1:2]
        parts[0].append((rq * (wq - unit_q * jnp.mean(wq * unit_q, axis=-1, keepdims=True))).astype(BF))
        parts[1].append((rk * (wk - unit_k * jnp.mean(wk * unit_k, axis=-1, keepdims=True))).astype(BF))
        parts[2].append(d_value.astype(BF))
    for k in range(SIDE):

        @pl.when((z_index[0] + k) % SIDE == step)
        def _():
            for kind in range(3):
                outs[k][kind] = jnp.concatenate(parts[kind], axis=1)


def attend_back(z_index, d_attn, w_out, raw, turned, kept, value_in, gains, table):
    length, width = d_attn.shape
    inner = w_out.shape[1]
    cols = inner // SIDE
    return kernel_call(
        attend_back_body,
        (SIDE,),
        [
            whole(length, width),
            pl.BlockSpec((width, cols), lambda i, z: (0, i)),
            pl.BlockSpec((2, length, cols), lambda i, z: (0, 0, i)),
            pl.BlockSpec((2, length, cols), lambda i, z: (0, 0, i)),
            pl.BlockSpec((cols // LANE, length, length), lambda i, z: (i, 0, 0)),
            pl.BlockSpec((length, cols), lambda i, z: (0, i)),
            whole(2, LANE),
            whole(2, length, LANE),
        ],
        [whole(3, length, cols)] * SIDE + [whole(2, LANE)],
        [shape((3, length, cols), BF)] * SIDE + [shape((2, LANE), F32)],
        scalars=1,
        name="attend_back",
    )(z_index, d_attn, *held(w_out, raw, turned, kept, value_in, gains, table))


def input_grad_body(z_index, *refs):
    w_qkv, out, total = refs[SIDE:]
    step = pl.program_id(0)

    @pl.when(step == 0)
    def _():
        total[...] = jnp.zeros_like(total)

    for k in range(SIDE):

        @pl.when(step == k)
        def _():
            block = refs[k]
            total[...] += dot(block[0], w_qkv[0], NT) + dot(block[1], w_qkv[1], NT) + dot(block[2], w_qkv[2], NT)

    @pl.when(step == pl.num_programs(0) - 1)
    def _():
        out[...] = total[...].astype(BF)


def input_grad(z_index, d_blocks, w_qkv):
    _, length, cols = d_blocks[0].shape
    width = w_qkv.shape[1]
    return kernel_call(
        input_grad_body,
        (SIDE,),
        [whole(3, length, cols)] * SIDE
        + [pl.BlockSpec((3, width, cols), lambda i, z: (0, 0, lax.rem(z[0] + i, SIDE)))],
        whole(length, width),
        shape((length, width), BF),
        [pltpu.VMEM((length, width), F32)],
        scalars=1,
        name="input_grad",
    )(z_index, *d_blocks, *held(w_qkv))


def routing_body(core, capacity, ids, later, cotangent, member_out, select, rows, code):
    step = pl.program_id(0)
    experts, length = code.shape

    @pl.when(step == 0)
    def _():
        at_expert = lax.broadcasted_iota(jnp.int32, (experts, length), 0)
        member = jnp.zeros((experts, length), F32)
        for j in range(ids.shape[0]):
            member = member + (ids[j : j + 1, :] == at_expert).astype(F32)
        member_out[...] = member.T
        ranks = dot(member.astype(BF), later[...], NN)
        row = lax.broadcasted_iota(jnp.int32, (experts, experts), 0)
        column = lax.broadcasted_iota(jnp.int32, (experts, experts), 1)
        limit = jnp.sum(jnp.where(row == column, capacity[...].astype(F32), 0.0), axis=1, keepdims=True)
        code[...] = jnp.where((member > 0.5) & (ranks < limit), ranks, -1.0)

    chunk = rows.shape[0]
    depth = chunk // 8
    slot = lax.broadcasted_iota(jnp.int32, (depth, length), 0).astype(F32)
    mine = code[pl.ds(pl.multiple_of(step * 8, 8), 8), :]
    hit = jnp.concatenate([(mine[k : k + 1] == slot).astype(F32) for k in range(8)], axis=0).astype(BF)
    select[...] = hit
    rows[...] = dot(hit, cotangent[...], NN).astype(BF)


def routing(core, capacity, ids, cotangent):
    length, width = cotangent.shape
    experts = capacity.shape[0]
    slots = length * ids.shape[0]
    chunk = 8 * (slots // experts)
    half = width // 2
    later = jnp.asarray(np.triu(np.ones((length, length), np.float32), 1), BF)
    return kernel_call(
        routing_body,
        (slots // chunk,),
        [
            whole(1, experts),
            whole(*ids.shape),
            whole(length, length),
            pl.BlockSpec((length, half), lambda i, c: (0, c[0])),
        ],
        [
            whole(length, experts),
            pl.BlockSpec((chunk, length), lambda i, c: (i, 0)),
            pl.BlockSpec((chunk, half), lambda i, c: (i, 0)),
        ],
        [shape((length, experts), F32), main_memory((slots, length), BF), main_memory((slots, half), BF)],
        [pltpu.VMEM((experts, length), F32)],
        scalars=1,
        name="routing",
    )(core, *held(capacity.reshape(1, experts), ids, later, cotangent))


def middle_body(core, tokens, own, peer, gain, select, w_router, member, expert_of,
                middle, normed, probs_out, gates_out, total_out, combine, rows):
    x2 = tokens[...].astype(F32) + (own[...].astype(F32) + peer[...].astype(F32))
    middle[...] = x2
    normed[...] = (x2 * rms(x2) * gain[...]).astype(BF)
    logits = dot(normed[...], w_router[...], NN)
    raised = jnp.exp(logits - jnp.max(logits, axis=-1, keepdims=True))
    probs = raised / jnp.sum(raised, axis=-1, keepdims=True)
    picked = probs * member[...]
    total = jnp.sum(picked, axis=-1, keepdims=True)
    gates = picked / total
    probs_out[...] = probs
    gates_out[...] = gates
    total_out[...] = total
    low = gates.astype(BF)
    half = rows.shape[1] - LANE
    for at in range(0, rows.shape[0], 256):
        cut = slice(at, at + 256)
        spread = dot(expert_of[cut], low, NT) * select[cut].astype(F32)
        combine[cut] = spread.astype(BF)
        gate = jnp.sum(spread, axis=-1, keepdims=True)
        rows[cut, half:] = jnp.broadcast_to(gate, (256, LANE)).astype(BF)
    for which in range(2):

        @pl.when(core[0] == which)
        def _():
            for at in range(0, rows.shape[0], 256):
                rows[at : at + 256, :half] = dot(
                    select[at : at + 256], normed[:, which * half : (which + 1) * half], NN
                ).astype(BF)


def middle_step(core, tokens, own, peer, gain, select, w_router, member, expert_of):
    length, width = tokens.shape
    slots, experts = expert_of.shape
    columns = width // 2 + LANE
    return kernel_call(
        middle_body,
        (1,),
        [whole(length, width)] * 3
        + [whole(1, width), whole(slots, length), whole(width, experts), whole(length, experts), whole(slots, experts)],
        [
            whole(length, width),
            whole(length, width),
            whole(length, experts),
            whole(length, experts),
            whole(length, 1),
            whole(slots, length),
            whole(slots, columns),
        ],
        [
            main_memory((length, width), F32),
            main_memory((length, width), BF),
            shape((length, experts), F32),
            shape((length, experts), F32),
            shape((length, 1), F32),
            main_memory((slots, length), BF),
            main_memory((slots, columns), BF),
        ],
        scalars=1,
        name="middle",
    )(core, *held(tokens), own, peer, *held(gain, select, w_router, member, expert_of))


def gather_back_body(back, combine, select, expert_of, out):
    half = out.shape[1] - LANE
    experts = expert_of.shape[1]
    out[:, :half] = dot(combine[...], back[:, :half], TN)
    high = back[:, half : half + 1].astype(F32)
    low = back[:, half + 1 : half + 2].astype(F32)
    picked = select[...].astype(F32)
    spread = dot((picked * high).astype(BF), expert_of[...], TN) + dot((picked * low).astype(BF), expert_of[...], TN)
    out[:, half : half + experts] = spread
    out[:, half + experts :] = jnp.zeros((out.shape[0], LANE - experts), F32)


def gather_back(back, combine, select, expert_of):
    slots, columns = back.shape
    length = combine.shape[1]
    experts = expert_of.shape[1]
    return kernel_call(
        gather_back_body,
        (1,),
        [whole(slots, columns), whole(slots, length), whole(slots, length), whole(slots, experts)],
        whole(length, columns),
        shape((length, columns), F32),
        name="gather_back",
    )(back, *held(combine, select, expert_of))


def middle_back_body(core, own, peer, probs, gates, total, member, w_router, middle, cotangent, gain, far,
                     d_logits_out, d_middle, d_attn, d_gain, *d_attn_blocks):
    half = own.shape[1] - LANE
    experts = probs.shape[1]
    d_gates = own[:, half : half + experts] + peer[:, half : half + experts]
    g, p = gates[...], probs[...]
    d_picked = member[...] * (d_gates - jnp.sum(d_gates * g, axis=-1, keepdims=True)) / total[...]
    d_logits = (p * (d_picked - jnp.sum(p * d_picked, axis=-1, keepdims=True))).astype(BF)
    d_logits_out[...] = d_logits
    d_normed = dot(d_logits, w_router[...], NT)
    for which in range(2):

        @pl.when(core[0] == which)
        def _():
            first, second = (own, peer) if which == 0 else (peer, own)
            d_middle[:, :half] = first[:, :half]
            d_middle[:, half:] = second[:, :half]

    d_normed = d_normed + d_middle[...]
    x2 = middle[...]
    scale = rms(x2)
    unit = x2 * scale
    d_gain[...] = jnp.sum(d_normed * unit, axis=0, keepdims=True)
    weighted = d_normed * gain[...]
    value = cotangent[...].astype(F32) + scale * (
        weighted - unit * jnp.mean(weighted * unit, axis=-1, keepdims=True)
    )
    d_middle[...] = value
    low = value.astype(BF)
    d_attn[...] = low
    cut = d_attn_blocks[0].shape[1]
    for which in range(SIDE):

        @pl.when(core[1] == which)
        def _():
            for k in range(SIDE):
                at = (which + k) % SIDE * cut
                d_attn_blocks[k][:, :cut] = low[:, at : at + cut]

    d_attn_blocks[1][:, cut:] = far[...]


def middle_back(core, own, peer, probs, gates, total, member, w_router, middle, cotangent, gain, far):
    length, width = middle.shape
    experts = probs.shape[1]
    columns = own.shape[1]
    quarter = width // SIDE
    blocks = [quarter, quarter + far.shape[1], quarter, quarter]
    return kernel_call(
        middle_back_body,
        (1,),
        [whole(length, columns)] * 2
        + [whole(length, experts)] * 2
        + [
            whole(length, 1),
            whole(length, experts),
            whole(width, experts),
            whole(length, width),
            whole(length, width),
            whole(1, width),
            whole(*far.shape),
        ],
        [whole(length, experts), whole(length, width), whole(length, width), whole(1, width)]
        + [whole(length, block) for block in blocks],
        [
            shape((length, experts), BF),
            shape((length, width), F32),
            shape((length, width), BF),
            shape((1, width), F32),
        ]
        + [shape((length, block), BF) for block in blocks],
        scalars=1,
        name="middle_back",
    )(core, own, peer, *held(probs, gates, total, member, w_router, middle, cotangent, gain, far))


def hidden_grad_body(core, own, peer, down_own, down_peer, out):
    half = down_own.shape[1]
    out[...] = dot(own[:, :half], down_own[...], NT) + dot(peer[:, :half], down_peer[...], NT)


ROWS = 256


def hidden_grad(core, own, peer, down):
    slots, columns = own.shape
    hidden, width = down.shape
    half = width // 2
    return kernel_call(
        hidden_grad_body,
        (slots // ROWS,),
        [
            pl.BlockSpec((ROWS, columns), lambda i, c: (i, 0)),
            pl.BlockSpec((ROWS, columns), lambda i, c: (i, 0)),
            pl.BlockSpec((hidden, half), lambda i, c: (0, c[0])),
            pl.BlockSpec((hidden, half), lambda i, c: (0, 1 - c[0])),
        ],
        pl.BlockSpec((ROWS, hidden), lambda i, c: (i, 0)),
        main_memory((slots, hidden), F32),
        scalars=1,
        name="hidden_grad",
    )(core, *held(own, peer, down, down))


def experts_body(core, own, peer, d_hidden, pair_own, pair_peer, acted, d_pair, back_own, back_peer, extra):
    hidden = d_hidden.shape[1]
    half = pair_own.shape[1]
    for start in range(0, own.shape[0], ROWS):
        cut = slice(start, start + ROWS)
        mine, other = own[cut, :half], peer[cut, :half]
        gate = dot(mine, pair_own[0], NN) + dot(other, pair_peer[0], NN)
        up = dot(mine, pair_own[1], NN) + dot(other, pair_peer[1], NN)
        sig = 1.0 / (1.0 + jnp.exp(-gate))
        silu = gate * sig
        act = (silu * up).astype(BF)
        acted[cut] = act
        d_act = d_hidden[cut]
        slot_grad = jnp.sum(d_act * act.astype(F32), axis=-1, keepdims=True)
        high = slot_grad.astype(BF)
        low = (slot_grad - high.astype(F32)).astype(BF)
        at = lax.broadcasted_iota(jnp.int32, (ROWS, LANE), 1)
        extra[cut] = jnp.where(at == 0, high.astype(F32), jnp.where(at == 1, low.astype(F32), 0.0)).astype(BF)
        d_gate = (d_act * up * sig * (1.0 + gate * (1.0 - sig))).astype(BF)
        d_up = (d_act * silu).astype(BF)
        d_pair[cut, :hidden] = d_gate
        d_pair[cut, hidden:] = d_up
        back_peer[cut] = (dot(d_gate, pair_peer[0], NT) + dot(d_up, pair_peer[1], NT)).astype(BF)
        back_own[cut] = (dot(d_gate, pair_own[0], NT) + dot(d_up, pair_own[1], NT)).astype(BF)


def experts_out_body(core, acted, acted_peer, down, down_far, out):
    out[...] = (dot(acted[...], down[...], NN) + dot(acted_peer[...], down_far[...], NN)).astype(BF)


def experts_out(core, acted, acted_peer, down, down_far):
    slots, hidden = acted.shape
    half = down_far.shape[1]
    rows = lambda n: pl.BlockSpec((ROWS, n), lambda i, c: (i, 0))
    return kernel_call(
        experts_out_body,
        (slots // ROWS,),
        [
            rows(hidden),
            rows(hidden),
            pl.BlockSpec((hidden, half), lambda i, c: (0, c[0])),
            whole(hidden, half),
        ],
        rows(half),
        main_memory((slots, half), BF),
        scalars=1,
        name="experts_out",
    )(core, *held(acted, acted_peer, down, down_far))


def experts_step(core, own, peer, d_hidden, pair):
    slots, columns = own.shape
    half = columns - LANE
    hidden = pair.shape[2]
    rows = lambda n: pl.BlockSpec((2 * ROWS, n), lambda i, c: (i, 0))
    return kernel_call(
        experts_body,
        (slots // (2 * ROWS),),
        [
            rows(columns),
            rows(columns),
            rows(hidden),
            pl.BlockSpec((2, half, hidden), lambda i, c: (0, c[0], 0)),
            pl.BlockSpec((2, half, hidden), lambda i, c: (0, 1 - c[0], 0)),
        ],
        [rows(hidden), rows(2 * hidden), rows(half), rows(half), rows(LANE)],
        [
            main_memory((slots, hidden), BF),
            main_memory((slots, 2 * hidden), BF),
            main_memory((slots, half), BF),
            main_memory((slots, half), BF),
            shape((slots, LANE), BF),
        ],
        scalars=1,
        name="experts",
    )(core, *held(own), peer, *held(d_hidden, pair, pair))


def add_pack_body(own, peer, extra, out):
    half = own.shape[1]
    out[:, :half] = (own[...].astype(F32) + peer[...].astype(F32)).astype(BF)
    out[:, half:] = extra[...]


def add_pack(own, peer, extra):
    slots, half = own.shape
    rows = lambda n: pl.BlockSpec((ROWS, n), lambda i: (i, 0))
    return kernel_call(
        add_pack_body,
        (slots // ROWS,),
        [rows(half), rows(half), rows(LANE)],
        rows(half + LANE),
        main_memory((slots, half + LANE), BF),
        name="add_pack",
    )(*held(own), peer, *held(extra))


def expert_grads_body(core, own, peer, grad_own, grad_peer, acted, d_pair, gates, grad_pair, grad_down, pair_low, act_low):
    step = pl.program_id(0)
    hidden = acted.shape[1]

    @pl.when(step == 0)
    def _():
        gate = gates[:, :1].astype(F32)
        pair_low[...] = (d_pair[...].astype(F32) * gate).astype(BF)
        act_low[...] = (acted[...].astype(F32) * gate).astype(BF)

    def part(rows, grads):
        value = dot(rows[...], pair_low[...], TN)
        grad_pair[:, 0, :] = value[:, :hidden]
        grad_pair[:, 1, :] = value[:, hidden:]
        grad_down[...] = dot(act_low[...], grads[...], TN)

    @pl.when(step < SIDE)
    def _():
        part(own, grad_own)

    @pl.when(step >= SIDE)
    def _():
        part(peer, grad_peer)


def expert_grads(core, own, peer, grad_own, grad_peer, acted, d_pair, gates):
    slots, half = grad_own.shape
    hidden = acted.shape[1]
    cut = half // SIDE
    first = pl.BlockSpec((slots, cut), lambda i, c: (0, jnp.minimum(i, SIDE - 1)))
    second = pl.BlockSpec((slots, cut), lambda i, c: (0, jnp.maximum(i - SIDE, 0)))

    def target(i, c):
        return jnp.where(i < SIDE, c[0] * SIDE + i, (1 - c[0]) * SIDE + i - SIDE)

    return kernel_call(
        expert_grads_body,
        (2 * SIDE,),
        [first, second, first, second, whole(slots, hidden), whole(slots, 2 * hidden), pl.BlockSpec((slots, LANE), lambda i, c: (0, half // LANE))],
        [
            pl.BlockSpec((cut, 2, hidden), lambda i, c: (target(i, c), 0, 0)),
            pl.BlockSpec((hidden, cut), lambda i, c: (0, target(i, c))),
        ],
        [shape((2 * half, 2, hidden), F32), shape((hidden, 2 * half), F32)],
        [pltpu.VMEM((slots, 2 * hidden), BF), pltpu.VMEM((slots, hidden), BF)],
        mib=48,
        scalars=1,
        name="expert_grads",
    )(core, *held(own), peer, *held(grad_own, grad_peer, acted, d_pair, gates))


EXTRA = 8


def group_grads_body(core, own, peer, *refs):
    step = pl.program_id(0)
    d_group = refs[:SIDE]
    normed_two, d_logits, d_gain, d_qk, out, right = refs[SIDE:]
    _, length, cols = d_group[0].shape
    targets = out.shape[0]
    rows = out.shape[1] - EXTRA

    @pl.when(step == 0)
    def _():
        for k in range(SIDE):
            for which in range(3):
                right[k * length : (k + 1) * length, which * cols : (which + 1) * cols] = d_group[k][which]

    def part(normed):
        value = dot(normed[...], right[...], NN).astype(BF)
        for k in range(targets):
            out[k, :rows] = value[k * rows : (k + 1) * rows]

    @pl.when(step < SIDE // 2)
    def _():
        part(own)

    @pl.when(step >= SIDE // 2)
    def _():
        part(peer)

    router = dot(d_logits[...], normed_two[...], TN)
    for k in range(targets):
        cut = slice(k * rows, (k + 1) * rows)
        for at in range(SIDE):
            out[k, rows:, at * LANE : (at + 1) * LANE] = router[at * EXTRA : (at + 1) * EXTRA, cut].astype(BF)
        out[k, rows:, SIDE * LANE : (SIDE + 1) * LANE] = jnp.broadcast_to(d_gain[:, cut], (EXTRA, LANE)).astype(BF)
        out[k, rows:, (SIDE + 1) * LANE :] = jnp.concatenate([d_qk[...]] * (EXTRA // 2), axis=0).astype(BF)


def turn_parts_body(*refs):
    value = jnp.concatenate([part[...].astype(F32) for part in refs[:SIDE]], axis=0)
    refs[SIDE][...] = value.T.astype(BF)


def turn_parts(parts):
    length, width = parts[0].shape
    cut = 256
    return kernel_call(
        turn_parts_body,
        (width // cut,),
        [pl.BlockSpec((length, cut), lambda i: (0, i))] * SIDE,
        pl.BlockSpec((cut, SIDE * length), lambda i: (i, 0)),
        main_memory((width, SIDE * length), BF),
        name="turn_parts",
    )(*held(*parts))


def group_grads(core, own, peer, d_group, normed_two, d_logits, d_gain, d_qk):
    half, depth = own.shape
    length = depth // SIDE
    cols = d_group[0].shape[2]
    steps = SIDE // 2
    cut = half // steps
    places = SIDE * SIDE
    rows = 2 * half // places

    def target(i, c):
        return jnp.where(i < steps, c[0] * steps + i, (1 - c[0]) * steps + i - steps)

    return kernel_call(
        group_grads_body,
        (2 * steps,),
        [
            pl.BlockSpec((cut, depth), lambda i, c: (jnp.minimum(i, steps - 1), 0)),
            pl.BlockSpec((cut, depth), lambda i, c: (jnp.maximum(i - steps, 0), 0)),
        ]
        + [whole(3, length, cols)] * SIDE
        + [
            pl.BlockSpec((length, cut), lambda i, c: (0, target(i, c))),
            whole(length, d_logits.shape[1]),
            pl.BlockSpec((1, cut), lambda i, c: (0, target(i, c))),
            whole(2, LANE),
        ],
        pl.BlockSpec((cut // rows, rows + EXTRA, 3 * cols), lambda i, c: (target(i, c), 0, 0)),
        main_memory((places, rows + EXTRA, 3 * cols), BF),
        [pltpu.VMEM((depth, 3 * cols), BF)],
        scalars=1,
        name="group_grads",
    )(core, *held(own, peer), *d_group, *held(normed_two), d_logits, d_gain, d_qk)


def out_grads_body(*refs):
    out = refs[-1]
    rows = out.shape[0]
    left = jnp.concatenate([part[:, :rows] for part in refs[:SIDE]], axis=0)
    right = jnp.concatenate([refs[SIDE][...], refs[SIDE + 1][...], refs[1][:, rows:], refs[SIDE + 2][...]], axis=0)
    out[...] = dot(left, right, TN).astype(BF)


def out_grads(d_attn, attended):
    length, rows = d_attn[0].shape
    inner = attended[0].shape[1]
    return kernel_call(
        out_grads_body,
        (1,),
        [whole(*part.shape) for part in d_attn] + [whole(length, inner)] * len(attended),
        whole(rows, inner),
        shape((rows, inner), BF),
        name="out_grads",
    )(*d_attn, *held(*attended))


def sum_arrived_body(rows, z_index, arrived, *outs):
    value = arrived[0].astype(F32)
    for k in range(1, arrived.shape[0]):
        value = value + arrived[k].astype(F32)
    value = value.astype(BF)
    main = SIDE * rows
    for which in range(SIDE):

        @pl.when(z_index[0] == which)
        def _():
            for step in range(SIDE):
                at = (which + step) % SIDE * rows
                outs[step][:rows] = value[at : at + rows]

    for step in range(SIDE):
        outs[step][rows:] = value[main:]


def sum_arrived(z_index, arrived, rows):
    places, height, columns = arrived.shape
    cols = columns // 3
    return kernel_call(
        functools.partial(sum_arrived_body, rows),
        (3,),
        [pl.BlockSpec((places, height, cols), lambda i, z: (0, 0, i))],
        [pl.BlockSpec((rows + EXTRA, cols), lambda i, z: (0, i))] * SIDE,
        [shape((rows + EXTRA, columns), BF)] * SIDE,
        scalars=1,
        name="sum_arrived",
    )(z_index, arrived)


def finish_body(z_index, *refs):
    parts, w_here, grad, small = refs[:SIDE], refs[SIDE], refs[SIDE + 1], refs[SIDE + 2]
    rows = grad.shape[1]
    cols = parts[0].shape[1] // 3
    for which in range(SIDE):

        @pl.when(z_index[0] == which)
        def _():
            ordered = [parts[(which - source) % SIDE] for source in range(SIDE)]
            for source in range(SIDE):
                for kind in range(3):
                    grad[kind, :, source * cols : (source + 1) * cols] = ordered[source][
                        :rows, kind * cols : (kind + 1) * cols
                    ].astype(F32)
            extra = [part[rows:].astype(F32) for part in ordered]
            total = (extra[0] + extra[1]) + (extra[2] + extra[3])
            for at in range(SIDE):
                small[at * EXTRA : (at + 1) * EXTRA] = total[:, at * LANE : (at + 1) * LANE]
            small[SIDE * EXTRA + 1 : SIDE * EXTRA + 2] = total[0:1, SIDE * LANE : (SIDE + 1) * LANE]
            small[SIDE * EXTRA + 2 : SIDE * EXTRA + 4] = total[0:2, (SIDE + 1) * LANE :]

    product = jnp.sum(grad[0] * w_here[0].astype(F32) + grad[1] * w_here[1].astype(F32) + grad[2] * w_here[2].astype(F32), axis=-1, keepdims=True)
    at_row = lax.broadcasted_iota(jnp.int32, (rows, LANE), 0)
    at_lane = lax.broadcasted_iota(jnp.int32, (rows, LANE), 1)
    small[SIDE * EXTRA : SIDE * EXTRA + 1] = jnp.sum(jnp.where(at_row == at_lane, product, 0.0), axis=0, keepdims=True)
    small[SIDE * EXTRA + 4 :] = jnp.zeros((small.shape[0] - SIDE * EXTRA - 4, LANE), F32)


def finish(z_index, parts, w_here):
    kinds, rows, inner = w_here.shape
    height, columns = parts[0].shape
    return kernel_call(
        finish_body,
        (1,),
        [whole(height, columns)] * SIDE + [whole(kinds, rows, inner)],
        [whole(kinds, rows, inner), whole(SIDE * EXTRA + 8, LANE)],
        [shape((kinds, rows, inner), F32), shape((SIDE * EXTRA + 8, LANE), F32)],
        scalars=1,
        name="finish",
    )(z_index, *parts, w_here)


def on_device(
    tokens,
    expert_ids,
    capacity,
    gain_attn,
    w_qkv,
    qk_gain,
    w_out,
    gain_ffn,
    w_router,
    w_gate_up,
    w_down,
    cotangent,
):
    length, width = tokens.shape
    expert_count = capacity.shape[0]
    slot_count = length * expert_ids.shape[1] // expert_count
    slots = expert_count * slot_count
    inner = w_qkv.shape[2]
    half = width // 2
    cols = inner // SIDE
    core_index = lax.axis_index("tensor")
    core = core_index.astype(jnp.int32).reshape(1)
    place = [lax.axis_index(a) for a in AXES]
    dp_index = (place[0] * SIDE + place[1]) * SIDE + place[2]
    rows_here_count = width // SIDE**3

    def own_half(value):
        return lax.dynamic_slice_in_dim(value, core_index * half, half, axis=-1)

    expert_of = jnp.asarray(np.repeat(np.eye(expert_count, dtype=np.float32), slot_count, 0), BF)

    def to_owners(rows):
        columns = rows.shape[1]
        return exchange(rows.reshape(expert_count, slot_count, columns), AXES).reshape(slots, columns)

    member, select, grad_send = routing(core, capacity, expert_ids.T, cotangent)
    grad_own = to_owners(grad_send)

    table = jnp.asarray(rotary(length, LANE // 2))
    gains = qk_gain.astype(F32)
    gain_one = gain_attn.astype(F32)
    gain_two = gain_ffn.astype(F32).reshape(1, width)
    w_parts = w_qkv.transpose(1, 0, 2)
    normed_one, raw, turned, kept, value_in, attended, partial = attend(
        tokens, gain_one.reshape(1, width), w_parts, w_out, gains, table
    )
    partial_peer = swap(partial)
    middle, normed_two, probs, gates, picked_total, combine, rows_send = middle_step(
        core, tokens, partial, partial_peer, gain_two, select, w_router, member, expert_of
    )
    rows_own = to_owners(rows_send)

    normed_early, attended_late, pair, grad_late, down, _ = together(
        own_half(normed_one), attended, w_gate_up, grad_own, w_down, rows_send
    )
    down = down[0]
    pair = pair[0].transpose(1, 0, 2)
    grad_peer = swap(grad_late)
    d_hidden = hidden_grad(core, grad_late, grad_peer, down)
    down_far = swap(lax.dynamic_slice_in_dim(down, (1 - core_index) * half, half, axis=1))
    rows_own, d_hidden, pair, normed_early, down_far = together(rows_own, d_hidden, pair, normed_early, down_far)
    normed_group = share(normed_early, "z")
    rows_peer = swap(rows_own)
    acted, d_pair, back_own, back_peer, extra = experts_step(core, rows_own, rows_peer, d_hidden, pair)
    back_peer, attended_late, *normed_group = together(back_peer, attended_late, *normed_group)
    from_one, from_three = shift(attended_late, "y", 1), shift(attended_late, "y", 3)
    back_send = add_pack(back_own, swap(back_peer), extra)
    back_send, acted_peer, from_one, from_three = together(back_send, swap(acted), from_one, from_three)
    back = to_owners(back_send)

    acted_late, own_late, peer_late, _ = together(acted, rows_own, rows_peer, back_send)
    grad_gate_up, grad_down = expert_grads(
        core, own_late, peer_late, grad_late, grad_peer, acted_late, d_pair, own_late
    )
    returned = experts_out(core, acted_late, acted_peer, down, down_far)
    normed_group, _ = together(normed_group, back_send)
    normed_group = turn_parts(normed_group)
    returned, grad_gate_up, grad_down, normed_group = together(returned, grad_gate_up, grad_down, normed_group)
    returned = to_owners(returned)

    gathered = gather_back(back, combine, select, expert_of)
    core_y = jnp.stack([core[0], place[0].astype(jnp.int32)])
    d_logits, d_middle, d_attn, gain_two_local, *d_attn_blocks = middle_back(
        core_y, gathered, swap(gathered), probs, gates, picked_total, member, w_router, middle, cotangent, gain_two,
        from_one
    )

    z_index = place[2].astype(jnp.int32).reshape(1)
    d_attn, normed_group_peer = together(d_attn, swap(normed_group))
    *d_blocks, grad_qk = attend_back(z_index, d_attn, w_out, raw, turned, kept, value_in, gains, table)
    d_group = send_steps(d_blocks, "z")
    returned, *d_group = together(returned, *d_group)

    columns_here = expert_count // 2
    my_logits = lax.dynamic_slice_in_dim(d_logits, core_index * columns_here, columns_here, axis=1)
    partial_grads = group_grads(
        core,
        normed_group,
        normed_group_peer,
        d_group,
        normed_two,
        my_logits,
        gain_two_local,
        grad_qk,
    )
    d_attn_blocks, from_one, _ = together(d_attn_blocks, from_one, d_blocks)
    d_attn_group = [
        d_attn_blocks[0],
        shift(d_attn_blocks[1], "y", 1),
        shift(d_attn_blocks[2], "y", 2),
        shift(d_attn_blocks[3], "y", 3),
    ]
    attended_group = [attended_late, from_one, from_three]
    partial_grads, attended_group, d_attn_group = together(partial_grads, attended_group, d_attn_group)
    arrived = exchange(partial_grads, ("y", "x"))
    d_attn_group, attended_group, late_blocks, late_returned, _ = together(
        d_attn_group, attended_group, d_blocks, returned, partial_grads
    )

    grad_out = out_grads(d_attn_group, attended_group)

    grad_out = send_blocks(grad_out.reshape(SIDE, SIDE, rows_here_count, inner), "z", 1)

    d_one = input_grad(z_index, late_blocks, w_parts)
    d_one = d_one.astype(F32) + swap(d_one).astype(F32)

    residual_in = tokens.astype(F32)
    scale_one = rms(residual_in)
    unit_one = residual_in * scale_one
    weighted = d_one * gain_one
    grad_input = d_middle + scale_one * (
        weighted - unit_one * jnp.mean(weighted * unit_one, axis=-1, keepdims=True)
    )

    mix_own = dot(combine, late_returned, TN)
    result_own = (own_half(middle) + mix_own).astype(BF)
    output = side_by_side(result_own, swap(result_own), core_index)

    grad_out = sum(part.astype(F32) for part in grad_out).astype(BF)
    grad_out = [block_at(grad_out, (place[1] + step) % SIDE, 0) for step in range(SIDE)]
    grad_input, output, *grad_out = together(grad_input, output, *grad_out)
    grad_out = send_steps(grad_out, "x")
    arrived, grad_input, output, *grad_out = together(arrived, grad_input, output, *grad_out)
    grad_out = sum(part.astype(F32) for part in grad_out)
    parts = send_steps(sum_arrived(z_index, arrived, rows_here_count), "z")
    w_here = lax.dynamic_slice_in_dim(w_parts, dp_index * rows_here_count, rows_here_count, axis=1)
    grad_qkv, small = finish(z_index, parts, w_here)
    grad_qkv = grad_qkv.transpose(1, 0, 2)
    small_peer = swap(small)
    gain_here = lax.dynamic_slice_in_dim(gain_one, dp_index * rows_here_count, rows_here_count, axis=0)
    grad_gain_one = (small[SIDE * EXTRA] + small_peer[SIDE * EXTRA])[:rows_here_count] / gain_here
    cut = lambda value: lax.dynamic_slice_in_dim(value, place[2] * rows_here_count, rows_here_count, axis=-1)
    grad_router = jnp.where(
        core_index == 0,
        jnp.concatenate([small[: SIDE * EXTRA], small_peer[: SIDE * EXTRA]], axis=0),
        jnp.concatenate([small_peer[: SIDE * EXTRA], small[: SIDE * EXTRA]], axis=0),
    )
    grad_router = cut(grad_router).T
    grad_gain_two = cut(small[SIDE * EXTRA + 1])
    grad_qk = small[SIDE * EXTRA + 2 : SIDE * EXTRA + 4] + small_peer[SIDE * EXTRA + 2 : SIDE * EXTRA + 4]

    return (
        output,
        grad_input,
        grad_gain_one,
        grad_qkv,
        grad_qk,
        grad_out,
        grad_gain_two,
        grad_router,
        grad_gate_up[None],
        grad_down[None],
    )


def solution(mesh):
    names = AXES + ("tensor",)
    torus = Mesh(mesh.devices.reshape(SIDE, SIDE, SIDE, 2), names)
    return jax.shard_map(
        on_device,
        mesh=torus,
        in_specs=(
            P(AXES, None),
            P(AXES, None),
            P(),
            P(),
            P(None, None, "tensor"),
            P(),
            P(None, "tensor"),
            P(),
            P(),
            P(AXES, None, None, "tensor"),
            P(AXES, "tensor", None),
            P(AXES, None),
        ),
        out_specs=(
            P(AXES, None),
            P(AXES, None),
            P(AXES),
            P(AXES, None, "tensor"),
            P(),
            P(AXES, "tensor"),
            P(AXES),
            P(AXES, None),
            P(AXES, None, None, "tensor"),
            P(AXES, "tensor", None),
        ),
        check_vma=False,
    )
```

```python
import functools
import math

import jax
import jax.numpy as jnp
import numpy as np
from jax import lax
from jax.experimental import pallas as pl
from jax.experimental.pallas import tpu as pltpu
from jax.sharding import Mesh
from jax.sharding import PartitionSpec as P

AXES = ("y", "x", "z")
SIDE = 4
LANE = 128
BF = jnp.bfloat16
F32 = jnp.float32
MIB = 1 << 20


def dot(a, b, dims):
    return lax.dot_general(a, b, (dims, ((), ())), preferred_element_type=F32)


NN = ((1,), (0,))
NT = ((1,), (1,))
TN = ((0,), (0,))


def rms(values):
    return lax.rsqrt(jnp.mean(values * values, axis=-1, keepdims=True) + 1e-06)


def rotary(length, half_dim):
    position = np.arange(length, dtype=np.float32)
    inverse = np.float32(50000.0) ** (-np.arange(half_dim, dtype=np.float32) / np.float32(half_dim))
    angles = position[:, None] * inverse[None, :].astype(np.float32)
    cosine = np.cos(angles).astype(np.float32)
    sine = np.sin(angles).astype(np.float32)
    return np.stack([np.concatenate([cosine, cosine], 1), np.concatenate([-sine, sine], 1)])


def swap(value):
    return lax.ppermute(value, "tensor", [(0, 1), (1, 0)])


def shift(value, axis, step):
    return lax.ppermute(value, axis, [(i, (i + step) % SIDE) for i in range(SIDE)])


def side_by_side(own, peer, core):
    return jnp.where(
        core == 0,
        jnp.concatenate([own, peer], axis=-1),
        jnp.concatenate([peer, own], axis=-1),
    )


def block_at(value, index, dim):
    return lax.dynamic_index_in_dim(value, index, dim, keepdims=False)


def together(*values):
    return lax.optimization_barrier(values)


def share(value, axis):
    return [value] + [shift(value, axis, step) for step in (1, 2, 3)]


def send_blocks(value, axis, dim):
    here = lax.axis_index(axis)
    own = block_at(value, here, dim)
    return [own] + [shift(block_at(value, (here + step) % SIDE, dim), axis, step) for step in (1, 2, 3)]


def send_steps(blocks, axis):
    return [blocks[0]] + [shift(blocks[step], axis, step) for step in (1, 2, 3)]


def exchange(value, axes):
    return lax.all_to_all(value, axes, split_axis=0, concat_axis=0, tiled=True)


def shape(dims, kind):
    return jax.ShapeDtypeStruct(dims, kind)


def main_memory(dims, kind):
    return pltpu.HBM(dims, kind)


def held(*values):
    return [pltpu.with_memory_space_constraint(value, pltpu.HBM) for value in values]


def kernel_call(body, grid, ins, outs, out_shapes, scratch=(), mib=40, scalars=0, name=None):
    return pl.pallas_call(
        body,
        grid_spec=pltpu.PrefetchScalarGridSpec(
            num_scalar_prefetch=scalars, grid=grid, in_specs=ins, out_specs=outs, scratch_shapes=list(scratch)
        ),
        out_shape=out_shapes,
        compiler_params=pltpu.CompilerParams(vmem_limit_bytes=mib * MIB),
        name=name,
    )


def whole(*dims):
    return pl.BlockSpec(dims, lambda *_: (0,) * len(dims))


def rope(values, table):
    return values * table[0] + pltpu.roll(values, values.shape[-1] // 2, 1) * table[1]


def unrope(values, table):
    return values * table[0] - pltpu.roll(values, values.shape[-1] // 2, 1) * table[1]


def attention_weights(query, key):
    scores = dot(query, key, NT) * (1.0 / math.sqrt(query.shape[-1]))
    raised = jnp.exp(scores - jnp.max(scores, axis=-1, keepdims=True))
    return raised / jnp.sum(raised, axis=-1, keepdims=True)


def attend_body(tokens, gain, w_qkv, w_out, gains, table, normed, raw, turned, kept, value_out, attended, partial, total):
    step = pl.program_id(0)

    @pl.when(step == 0)
    def _():
        x = tokens[...].astype(F32)
        normed[...] = (x * rms(x) * gain[...]).astype(BF)
        total[...] = jnp.zeros_like(total)

    h = normed[...]
    query_raw = dot(h, w_qkv[0], NN)
    key_raw = dot(h, w_qkv[1], NN)
    value = dot(h, w_qkv[2], NN).astype(BF)
    raw[0] = query_raw
    raw[1] = key_raw
    value_out[...] = value
    for at in range(query_raw.shape[1] // LANE):
        cut = slice(at * LANE, (at + 1) * LANE)
        q, k = query_raw[:, cut], key_raw[:, cut]
        query = rope(q * rms(q) * gains[0:1], table).astype(BF)
        key = rope(k * rms(k) * gains[1:2], table).astype(BF)
        turned[0, :, cut] = query
        turned[1, :, cut] = key
        weights = attention_weights(query, key)
        kept[at] = weights
        attended[:, cut] = dot(weights.astype(BF), value[:, cut], NN).astype(BF)
    total[...] += dot(attended[...], w_out[...], NT)

    @pl.when(step == pl.num_programs(0) - 1)
    def _():
        partial[...] = total[...].astype(BF)


def attend(tokens, gain, w_qkv, w_out, gains, table):
    length, width = tokens.shape
    inner = w_qkv.shape[2]
    cols = inner // SIDE
    return kernel_call(
        attend_body,
        (SIDE,),
        [
            whole(length, width),
            whole(1, width),
            pl.BlockSpec((3, width, cols), lambda i: (0, 0, i)),
            pl.BlockSpec((width, cols), lambda i: (0, i)),
            whole(2, LANE),
            whole(2, length, LANE),
        ],
        [
            whole(length, width),
            pl.BlockSpec((2, length, cols), lambda i: (0, 0, i)),
            pl.BlockSpec((2, length, cols), lambda i: (0, 0, i)),
            pl.BlockSpec((cols // LANE, length, length), lambda i: (i, 0, 0)),
            pl.BlockSpec((length, cols), lambda i: (0, i)),
            pl.BlockSpec((length, cols), lambda i: (0, i)),
            whole(length, width),
        ],
        [
            main_memory((length, width), BF),
            main_memory((2, length, inner), F32),
            main_memory((2, length, inner), BF),
            main_memory((inner // LANE, length, length), F32),
            main_memory((length, inner), BF),
            main_memory((length, inner), BF),
            shape((length, width), BF),
        ],
        [pltpu.VMEM((length, width), F32)],
        name="attend",
    )(tokens, gain, w_qkv, w_out, gains, table)


def attend_back_body(z_index, d_attn, w_out, raw, turned, kept, value_in, gains, table, *outs):
    d_gains = outs[SIDE]
    step = pl.program_id(0)
    parts = ([], [], [])

    @pl.when(step == 0)
    def _():
        d_gains[...] = jnp.zeros_like(d_gains)

    d_attended = dot(d_attn[...], w_out[...], NN).astype(BF)
    for at in range(d_attended.shape[1] // LANE):
        cut = slice(at * LANE, (at + 1) * LANE)
        q, k = raw[0, :, cut], raw[1, :, cut]
        rq, rk = rms(q), rms(k)
        unit_q, unit_k = q * rq, k * rk
        query, key = turned[0, :, cut], turned[1, :, cut]
        weights = kept[at]
        grad = d_attended[:, cut]
        d_value = dot(weights.astype(BF), grad, TN)
        d_weights = dot(grad, value_in[:, cut], NT)
        d_scores = (
            weights * (d_weights - jnp.sum(weights * d_weights, axis=-1, keepdims=True))
        ).astype(BF)
        root = 1.0 / math.sqrt(LANE)
        d_query = unrope(dot(d_scores, key, NN) * root, table)
        d_key = unrope(dot(d_scores, query, TN) * root, table)
        d_gains[0:1] += jnp.sum(d_query * unit_q, axis=0, keepdims=True)
        d_gains[1:2] += jnp.sum(d_key * unit_k, axis=0, keepdims=True)
        wq = d_query * gains[0:1]
        wk = d_key * gains[1:2]
        parts[0].append((rq * (wq - unit_q * jnp.mean(wq * unit_q, axis=-1, keepdims=True))).astype(BF))
        parts[1].append((rk * (wk - unit_k * jnp.mean(wk * unit_k, axis=-1, keepdims=True))).astype(BF))
        parts[2].append(d_value.astype(BF))
    for k in range(SIDE):

        @pl.when((z_index[0] + k) % SIDE == step)
        def _():
            for kind in range(3):
                outs[k][kind] = jnp.concatenate(parts[kind], axis=1)


def attend_back(z_index, d_attn, w_out, raw, turned, kept, value_in, gains, table):
    length, width = d_attn.shape
    inner = w_out.shape[1]
    cols = inner // SIDE
    return kernel_call(
        attend_back_body,
        (SIDE,),
        [
            whole(length, width),
            pl.BlockSpec((width, cols), lambda i, z: (0, i)),
            pl.BlockSpec((2, length, cols), lambda i, z: (0, 0, i)),
            pl.BlockSpec((2, length, cols), lambda i, z: (0, 0, i)),
            pl.BlockSpec((cols // LANE, length, length), lambda i, z: (i, 0, 0)),
            pl.BlockSpec((length, cols), lambda i, z: (0, i)),
            whole(2, LANE),
            whole(2, length, LANE),
        ],
        [whole(3, length, cols)] * SIDE + [whole(2, LANE)],
        [shape((3, length, cols), BF)] * SIDE + [shape((2, LANE), F32)],
        scalars=1,
        name="attend_back",
    )(z_index, d_attn, *held(w_out, raw, turned, kept, value_in, gains, table))


def input_grad_body(z_index, *refs):
    w_qkv, out, total = refs[SIDE:]
    step = pl.program_id(0)

    @pl.when(step == 0)
    def _():
        total[...] = jnp.zeros_like(total)

    for k in range(SIDE):

        @pl.when(step == k)
        def _():
            block = refs[k]
            total[...] += dot(block[0], w_qkv[0], NT) + dot(block[1], w_qkv[1], NT) + dot(block[2], w_qkv[2], NT)

    @pl.when(step == pl.num_programs(0) - 1)
    def _():
        out[...] = total[...].astype(BF)


def input_grad(z_index, d_blocks, w_qkv):
    _, length, cols = d_blocks[0].shape
    width = w_qkv.shape[1]
    return kernel_call(
        input_grad_body,
        (SIDE,),
        [whole(3, length, cols)] * SIDE
        + [pl.BlockSpec((3, width, cols), lambda i, z: (0, 0, lax.rem(z[0] + i, SIDE)))],
        whole(length, width),
        shape((length, width), BF),
        [pltpu.VMEM((length, width), F32)],
        scalars=1,
        name="input_grad",
    )(z_index, *d_blocks, *held(w_qkv))


def routing_body(core, capacity, ids, later, cotangent, member_out, select, rows, code):
    step = pl.program_id(0)
    experts, length = code.shape

    @pl.when(step == 0)
    def _():
        at_expert = lax.broadcasted_iota(jnp.int32, (experts, length), 0)
        member = jnp.zeros((experts, length), F32)
        for j in range(ids.shape[0]):
            member = member + (ids[j : j + 1, :] == at_expert).astype(F32)
        member_out[...] = member.T
        ranks = dot(member.astype(BF), later[...], NN)
        row = lax.broadcasted_iota(jnp.int32, (experts, experts), 0)
        column = lax.broadcasted_iota(jnp.int32, (experts, experts), 1)
        limit = jnp.sum(jnp.where(row == column, capacity[...].astype(F32), 0.0), axis=1, keepdims=True)
        code[...] = jnp.where((member > 0.5) & (ranks < limit), ranks, -1.0)

    chunk = rows.shape[0]
    depth = chunk // 8
    slot = lax.broadcasted_iota(jnp.int32, (depth, length), 0).astype(F32)
    mine = code[pl.ds(pl.multiple_of(step * 8, 8), 8), :]
    hit = jnp.concatenate([(mine[k : k + 1] == slot).astype(F32) for k in range(8)], axis=0).astype(BF)
    select[...] = hit
    rows[...] = dot(hit, cotangent[...], NN).astype(BF)


def routing(core, capacity, ids, cotangent):
    length, width = cotangent.shape
    experts = capacity.shape[0]
    slots = length * ids.shape[0]
    chunk = 8 * (slots // experts)
    half = width // 2
    later = jnp.asarray(np.triu(np.ones((length, length), np.float32), 1), BF)
    return kernel_call(
        routing_body,
        (slots // chunk,),
        [
            whole(1, experts),
            whole(*ids.shape),
            whole(length, length),
            pl.BlockSpec((length, half), lambda i, c: (0, c[0])),
        ],
        [
            whole(length, experts),
            pl.BlockSpec((chunk, length), lambda i, c: (i, 0)),
            pl.BlockSpec((chunk, half), lambda i, c: (i, 0)),
        ],
        [shape((length, experts), F32), main_memory((slots, length), BF), main_memory((slots, half), BF)],
        [pltpu.VMEM((experts, length), F32)],
        scalars=1,
        name="routing",
    )(core, *held(capacity.reshape(1, experts), ids, later, cotangent))


def middle_body(core, tokens, own, peer, gain, select, w_router, member, expert_of,
                middle, normed, probs_out, gates_out, total_out, combine, rows):
    x2 = tokens[...].astype(F32) + (own[...].astype(F32) + peer[...].astype(F32))
    middle[...] = x2
    normed[...] = (x2 * rms(x2) * gain[...]).astype(BF)
    logits = dot(normed[...], w_router[...], NN)
    raised = jnp.exp(logits - jnp.max(logits, axis=-1, keepdims=True))
    probs = raised / jnp.sum(raised, axis=-1, keepdims=True)
    picked = probs * member[...]
    total = jnp.sum(picked, axis=-1, keepdims=True)
    gates = picked / total
    probs_out[...] = probs
    gates_out[...] = gates
    total_out[...] = total
    low = gates.astype(BF)
    half = rows.shape[1] - LANE
    for at in range(0, rows.shape[0], 256):
        cut = slice(at, at + 256)
        spread = dot(expert_of[cut], low, NT) * select[cut].astype(F32)
        combine[cut] = spread.astype(BF)
        gate = jnp.sum(spread, axis=-1, keepdims=True)
        rows[cut, half:] = jnp.broadcast_to(gate, (256, LANE)).astype(BF)
    for which in range(2):

        @pl.when(core[0] == which)
        def _():
            for at in range(0, rows.shape[0], 256):
                rows[at : at + 256, :half] = dot(
                    select[at : at + 256], normed[:, which * half : (which + 1) * half], NN
                ).astype(BF)


def middle_step(core, tokens, own, peer, gain, select, w_router, member, expert_of):
    length, width = tokens.shape
    slots, experts = expert_of.shape
    columns = width // 2 + LANE
    return kernel_call(
        middle_body,
        (1,),
        [whole(length, width)] * 3
        + [whole(1, width), whole(slots, length), whole(width, experts), whole(length, experts), whole(slots, experts)],
        [
            whole(length, width),
            whole(length, width),
            whole(length, experts),
            whole(length, experts),
            whole(length, 1),
            whole(slots, length),
            whole(slots, columns),
        ],
        [
            main_memory((length, width), F32),
            main_memory((length, width), BF),
            shape((length, experts), F32),
            shape((length, experts), F32),
            shape((length, 1), F32),
            main_memory((slots, length), BF),
            main_memory((slots, columns), BF),
        ],
        scalars=1,
        name="middle",
    )(core, *held(tokens), own, peer, *held(gain, select, w_router, member, expert_of))


def gather_back_body(back, combine, select, expert_of, out):
    half = out.shape[1] - LANE
    experts = expert_of.shape[1]
    out[:, :half] = dot(combine[...], back[:, :half], TN)
    high = back[:, half : half + 1].astype(F32)
    low = back[:, half + 1 : half + 2].astype(F32)
    picked = select[...].astype(F32)
    spread = dot((picked * high).astype(BF), expert_of[...], TN) + dot((picked * low).astype(BF), expert_of[...], TN)
    out[:, half : half + experts] = spread
    out[:, half + experts :] = jnp.zeros((out.shape[0], LANE - experts), F32)


def gather_back(back, combine, select, expert_of):
    slots, columns = back.shape
    length = combine.shape[1]
    experts = expert_of.shape[1]
    return kernel_call(
        gather_back_body,
        (1,),
        [whole(slots, columns), whole(slots, length), whole(slots, length), whole(slots, experts)],
        whole(length, columns),
        shape((length, columns), F32),
        name="gather_back",
    )(back, *held(combine, select, expert_of))


def middle_back_body(core, own, peer, probs, gates, total, member, w_router, middle, cotangent, gain, far,
                     d_logits_out, d_middle, d_attn, d_gain, *d_attn_blocks):
    half = own.shape[1] - LANE
    experts = probs.shape[1]
    d_gates = own[:, half : half + experts] + peer[:, half : half + experts]
    g, p = gates[...], probs[...]
    d_picked = member[...] * (d_gates - jnp.sum(d_gates * g, axis=-1, keepdims=True)) / total[...]
    d_logits = (p * (d_picked - jnp.sum(p * d_picked, axis=-1, keepdims=True))).astype(BF)
    d_logits_out[...] = d_logits
    d_normed = dot(d_logits, w_router[...], NT)
    for which in range(2):

        @pl.when(core[0] == which)
        def _():
            first, second = (own, peer) if which == 0 else (peer, own)
            d_middle[:, :half] = first[:, :half]
            d_middle[:, half:] = second[:, :half]

    d_normed = d_normed + d_middle[...]
    x2 = middle[...]
    scale = rms(x2)
    unit = x2 * scale
    d_gain[...] = jnp.sum(d_normed * unit, axis=0, keepdims=True)
    weighted = d_normed * gain[...]
    value = cotangent[...].astype(F32) + scale * (
        weighted - unit * jnp.mean(weighted * unit, axis=-1, keepdims=True)
    )
    d_middle[...] = value
    low = value.astype(BF)
    d_attn[...] = low
    cut = d_attn_blocks[0].shape[1]
    for which in range(SIDE):

        @pl.when(core[1] == which)
        def _():
            for k in range(SIDE):
                at = (which + k) % SIDE * cut
                d_attn_blocks[k][:, :cut] = low[:, at : at + cut]

    d_attn_blocks[1][:, cut:] = far[...]


def middle_back(core, own, peer, probs, gates, total, member, w_router, middle, cotangent, gain, far):
    length, width = middle.shape
    experts = probs.shape[1]
    columns = own.shape[1]
    quarter = width // SIDE
    blocks = [quarter, quarter + far.shape[1], quarter, quarter]
    return kernel_call(
        middle_back_body,
        (1,),
        [whole(length, columns)] * 2
        + [whole(length, experts)] * 2
        + [
            whole(length, 1),
            whole(length, experts),
            whole(width, experts),
            whole(length, width),
            whole(length, width),
            whole(1, width),
            whole(*far.shape),
        ],
        [whole(length, experts), whole(length, width), whole(length, width), whole(1, width)]
        + [whole(length, block) for block in blocks],
        [
            shape((length, experts), BF),
            shape((length, width), F32),
            shape((length, width), BF),
            shape((1, width), F32),
        ]
        + [shape((length, block), BF) for block in blocks],
        scalars=1,
        name="middle_back",
    )(core, own, peer, *held(probs, gates, total, member, w_router, middle, cotangent, gain, far))


def hidden_grad_body(core, own, peer, down_own, down_peer, out):
    half = down_own.shape[1]
    out[...] = dot(own[:, :half], down_own[...], NT) + dot(peer[:, :half], down_peer[...], NT)


ROWS = 256


def hidden_grad(core, own, peer, down):
    slots, columns = own.shape
    hidden, width = down.shape
    half = width // 2
    return kernel_call(
        hidden_grad_body,
        (slots // ROWS,),
        [
            pl.BlockSpec((ROWS, columns), lambda i, c: (i, 0)),
            pl.BlockSpec((ROWS, columns), lambda i, c: (i, 0)),
            pl.BlockSpec((hidden, half), lambda i, c: (0, c[0])),
            pl.BlockSpec((hidden, half), lambda i, c: (0, 1 - c[0])),
        ],
        pl.BlockSpec((ROWS, hidden), lambda i, c: (i, 0)),
        main_memory((slots, hidden), F32),
        scalars=1,
        name="hidden_grad",
    )(core, *held(own, peer, down, down))


def experts_body(core, own, peer, d_hidden, pair_own, pair_peer, acted, d_pair, extra):
    hidden = d_hidden.shape[1]
    half = pair_own.shape[1]
    mine, other = own[:, :half], peer[:, :half]
    gate = dot(mine, pair_own[0], NN) + dot(other, pair_peer[0], NN)
    up = dot(mine, pair_own[1], NN) + dot(other, pair_peer[1], NN)
    sig = 1.0 / (1.0 + jnp.exp(-gate))
    silu = gate * sig
    act = (silu * up).astype(BF)
    acted[...] = act
    d_act = d_hidden[...]
    slot_grad = jnp.sum(d_act * act.astype(F32), axis=-1, keepdims=True)
    high = slot_grad.astype(BF)
    low = (slot_grad - high.astype(F32)).astype(BF)
    at = lax.broadcasted_iota(jnp.int32, extra.shape, 1)
    extra[...] = jnp.where(at == 0, high.astype(F32), jnp.where(at == 1, low.astype(F32), 0.0)).astype(BF)
    d_pair[:, :hidden] = (d_act * up * sig * (1.0 + gate * (1.0 - sig))).astype(BF)
    d_pair[:, hidden:] = (d_act * silu).astype(BF)


def back_first_body(core, d_pair, pair, out):
    hidden = pair.shape[2]
    out[...] = dot(d_pair[:, :hidden], pair[0], NT) + dot(d_pair[:, hidden:], pair[1], NT)


def back_first(core, d_pair, pair):
    slots, columns = d_pair.shape
    _, width, hidden = pair.shape
    half = width // 2
    rows = lambda n: pl.BlockSpec((ROWS, n), lambda i, c: (i, 0))
    return kernel_call(
        back_first_body,
        (slots // ROWS,),
        [rows(columns), pl.BlockSpec((2, half, hidden), lambda i, c: (0, c[0], 0))],
        rows(half),
        shape((slots, half), F32),
        scalars=1,
        mib=24,
        name="back_first",
    )(core, *held(d_pair, pair))


def back_second_body(partial, d_pair, pair, extra, out):
    _, half, hidden = pair.shape
    value = dot(d_pair[:, :hidden], pair[0], NT) + dot(d_pair[:, hidden:], pair[1], NT)
    out[:, :half] = (partial[...] + value).astype(BF)
    out[:, half:] = extra[...]


def back_second(partial, d_pair, pair, extra):
    slots, columns = d_pair.shape
    _, half, hidden = pair.shape
    rows = lambda n: pl.BlockSpec((ROWS, n), lambda i: (i, 0))
    return kernel_call(
        back_second_body,
        (slots // ROWS,),
        [rows(half), rows(columns), whole(2, half, hidden), rows(LANE)],
        rows(half + LANE),
        main_memory((slots, half + LANE), BF),
        mib=24,
        name="back_second",
    )(partial, d_pair, *held(pair, extra))


def experts_out_body(core, acted, acted_peer, down, down_far, out):
    out[...] = (dot(acted[...], down[...], NN) + dot(acted_peer[...], down_far[...], NN)).astype(BF)


def experts_out(core, acted, acted_peer, down, down_far):
    slots, hidden = acted.shape
    half = down_far.shape[1]
    rows = lambda n: pl.BlockSpec((ROWS, n), lambda i, c: (i, 0))
    return kernel_call(
        experts_out_body,
        (slots // ROWS,),
        [
            rows(hidden),
            rows(hidden),
            pl.BlockSpec((hidden, half), lambda i, c: (0, c[0])),
            whole(hidden, half),
        ],
        rows(half),
        main_memory((slots, half), BF),
        scalars=1,
        name="experts_out",
    )(core, *held(acted, acted_peer, down, down_far))


def experts_step(core, own, peer, d_hidden, pair):
    slots, columns = own.shape
    half = columns - LANE
    hidden = pair.shape[2]
    rows = lambda n: pl.BlockSpec((ROWS, n), lambda i, c: (i, 0))
    return kernel_call(
        experts_body,
        (slots // ROWS,),
        [
            rows(columns),
            rows(columns),
            rows(hidden),
            pl.BlockSpec((2, half, hidden), lambda i, c: (0, c[0], 0)),
            pl.BlockSpec((2, half, hidden), lambda i, c: (0, 1 - c[0], 0)),
        ],
        [rows(hidden), rows(2 * hidden), rows(LANE)],
        [
            main_memory((slots, hidden), BF),
            main_memory((slots, 2 * hidden), BF),
            main_memory((slots, LANE), BF),
        ],
        scalars=1,
        mib=28,
        name="experts",
    )(core, *held(own), peer, *held(d_hidden, pair, pair))


def expert_grads_body(core, own, peer, grad_own, grad_peer, acted, d_pair, gates, grad_pair, grad_down, pair_low, act_low):
    step = pl.program_id(0)
    hidden = acted.shape[1]

    @pl.when(step == 0)
    def _():
        gate = gates[:, :1].astype(F32)
        pair_low[...] = (d_pair[...].astype(F32) * gate).astype(BF)
        act_low[...] = (acted[...].astype(F32) * gate).astype(BF)

    def part(rows, grads):
        value = dot(rows[...], pair_low[...], TN)
        grad_pair[:, 0, :] = value[:, :hidden]
        grad_pair[:, 1, :] = value[:, hidden:]
        grad_down[...] = dot(act_low[...], grads[...], TN)

    @pl.when(step < SIDE)
    def _():
        part(own, grad_own)

    @pl.when(step >= SIDE)
    def _():
        part(peer, grad_peer)


def expert_grads(core, own, peer, grad_own, grad_peer, acted, d_pair, gates):
    slots, half = grad_own.shape
    hidden = acted.shape[1]
    cut = half // SIDE
    first = pl.BlockSpec((slots, cut), lambda i, c: (0, jnp.minimum(i, SIDE - 1)))
    second = pl.BlockSpec((slots, cut), lambda i, c: (0, jnp.maximum(i - SIDE, 0)))

    def target(i, c):
        return jnp.where(i < SIDE, c[0] * SIDE + i, (1 - c[0]) * SIDE + i - SIDE)

    return kernel_call(
        expert_grads_body,
        (2 * SIDE,),
        [first, second, first, second, whole(slots, hidden), whole(slots, 2 * hidden), pl.BlockSpec((slots, LANE), lambda i, c: (0, half // LANE))],
        [
            pl.BlockSpec((cut, 2, hidden), lambda i, c: (target(i, c), 0, 0)),
            pl.BlockSpec((hidden, cut), lambda i, c: (0, target(i, c))),
        ],
        [shape((2 * half, 2, hidden), F32), shape((hidden, 2 * half), F32)],
        [pltpu.VMEM((slots, 2 * hidden), BF), pltpu.VMEM((slots, hidden), BF)],
        mib=48,
        scalars=1,
        name="expert_grads",
    )(core, *held(own), peer, *held(grad_own, grad_peer, acted, d_pair, gates))


EXTRA = 8


def group_grads_body(core, own, peer, *refs):
    step = pl.program_id(0)
    d_group = refs[:SIDE]
    normed_two, d_logits, d_gain, d_qk, out, right = refs[SIDE:]
    _, length, cols = d_group[0].shape
    targets = out.shape[0]
    rows = out.shape[1] - EXTRA

    @pl.when(step == 0)
    def _():
        for k in range(SIDE):
            for which in range(3):
                right[k * length : (k + 1) * length, which * cols : (which + 1) * cols] = d_group[k][which]

    def part(normed):
        value = dot(normed[...], right[...], NN).astype(BF)
        for k in range(targets):
            out[k, :rows] = value[k * rows : (k + 1) * rows]

    @pl.when(step < SIDE // 2)
    def _():
        part(own)

    @pl.when(step >= SIDE // 2)
    def _():
        part(peer)

    router = dot(d_logits[...], normed_two[...], TN)
    for k in range(targets):
        cut = slice(k * rows, (k + 1) * rows)
        for at in range(SIDE):
            out[k, rows:, at * LANE : (at + 1) * LANE] = router[at * EXTRA : (at + 1) * EXTRA, cut].astype(BF)
        out[k, rows:, SIDE * LANE : (SIDE + 1) * LANE] = jnp.broadcast_to(d_gain[:, cut], (EXTRA, LANE)).astype(BF)
        out[k, rows:, (SIDE + 1) * LANE :] = jnp.concatenate([d_qk[...]] * (EXTRA // 2), axis=0).astype(BF)


def turn_parts_body(*refs):
    value = jnp.concatenate([part[...].astype(F32) for part in refs[:SIDE]], axis=0)
    refs[SIDE][...] = value.T.astype(BF)


def turn_parts(parts):
    length, width = parts[0].shape
    cut = 256
    return kernel_call(
        turn_parts_body,
        (width // cut,),
        [pl.BlockSpec((length, cut), lambda i: (0, i))] * SIDE,
        pl.BlockSpec((cut, SIDE * length), lambda i: (i, 0)),
        main_memory((width, SIDE * length), BF),
        name="turn_parts",
    )(*held(*parts))


def group_grads(core, own, peer, d_group, normed_two, d_logits, d_gain, d_qk):
    half, depth = own.shape
    length = depth // SIDE
    cols = d_group[0].shape[2]
    steps = SIDE // 2
    cut = half // steps
    places = SIDE * SIDE
    rows = 2 * half // places

    def target(i, c):
        return jnp.where(i < steps, c[0] * steps + i, (1 - c[0]) * steps + i - steps)

    return kernel_call(
        group_grads_body,
        (2 * steps,),
        [
            pl.BlockSpec((cut, depth), lambda i, c: (jnp.minimum(i, steps - 1), 0)),
            pl.BlockSpec((cut, depth), lambda i, c: (jnp.maximum(i - steps, 0), 0)),
        ]
        + [whole(3, length, cols)] * SIDE
        + [
            pl.BlockSpec((length, cut), lambda i, c: (0, target(i, c))),
            whole(length, d_logits.shape[1]),
            pl.BlockSpec((1, cut), lambda i, c: (0, target(i, c))),
            whole(2, LANE),
        ],
        pl.BlockSpec((cut // rows, rows + EXTRA, 3 * cols), lambda i, c: (target(i, c), 0, 0)),
        main_memory((places, rows + EXTRA, 3 * cols), BF),
        [pltpu.VMEM((depth, 3 * cols), BF)],
        scalars=1,
        name="group_grads",
    )(core, *held(own, peer), *d_group, *held(normed_two), d_logits, d_gain, d_qk)


def out_grads_body(*refs):
    out = refs[-1]
    rows = out.shape[0]
    left = jnp.concatenate([part[:, :rows] for part in refs[:SIDE]], axis=0)
    right = jnp.concatenate([refs[SIDE][...], refs[SIDE + 1][...], refs[1][:, rows:], refs[SIDE + 2][...]], axis=0)
    out[...] = dot(left, right, TN).astype(BF)


def out_grads(d_attn, attended):
    length, rows = d_attn[0].shape
    inner = attended[0].shape[1]
    return kernel_call(
        out_grads_body,
        (1,),
        [whole(*part.shape) for part in d_attn] + [whole(length, inner)] * len(attended),
        whole(rows, inner),
        shape((rows, inner), BF),
        name="out_grads",
    )(*d_attn, *held(*attended))


def sum_arrived_body(rows, z_index, arrived, *outs):
    value = arrived[0].astype(F32)
    for k in range(1, arrived.shape[0]):
        value = value + arrived[k].astype(F32)
    value = value.astype(BF)
    main = SIDE * rows
    for which in range(SIDE):

        @pl.when(z_index[0] == which)
        def _():
            for step in range(SIDE):
                at = (which + step) % SIDE * rows
                outs[step][:rows] = value[at : at + rows]

    for step in range(SIDE):
        outs[step][rows:] = value[main:]


def sum_arrived(z_index, arrived, rows):
    places, height, columns = arrived.shape
    cols = columns // 3
    return kernel_call(
        functools.partial(sum_arrived_body, rows),
        (3,),
        [pl.BlockSpec((places, height, cols), lambda i, z: (0, 0, i))],
        [pl.BlockSpec((rows + EXTRA, cols), lambda i, z: (0, i))] * SIDE,
        [shape((rows + EXTRA, columns), BF)] * SIDE,
        scalars=1,
        name="sum_arrived",
    )(z_index, arrived)


def finish_body(z_index, *refs):
    parts, w_here, grad, small = refs[:SIDE], refs[SIDE], refs[SIDE + 1], refs[SIDE + 2]
    rows = grad.shape[1]
    cols = parts[0].shape[1] // 3
    for which in range(SIDE):

        @pl.when(z_index[0] == which)
        def _():
            ordered = [parts[(which - source) % SIDE] for source in range(SIDE)]
            for source in range(SIDE):
                for kind in range(3):
                    grad[kind, :, source * cols : (source + 1) * cols] = ordered[source][
                        :rows, kind * cols : (kind + 1) * cols
                    ].astype(F32)
            extra = [part[rows:].astype(F32) for part in ordered]
            total = (extra[0] + extra[1]) + (extra[2] + extra[3])
            for at in range(SIDE):
                small[at * EXTRA : (at + 1) * EXTRA] = total[:, at * LANE : (at + 1) * LANE]
            small[SIDE * EXTRA + 1 : SIDE * EXTRA + 2] = total[0:1, SIDE * LANE : (SIDE + 1) * LANE]
            small[SIDE * EXTRA + 2 : SIDE * EXTRA + 4] = total[0:2, (SIDE + 1) * LANE :]

    product = jnp.sum(grad[0] * w_here[0].astype(F32) + grad[1] * w_here[1].astype(F32) + grad[2] * w_here[2].astype(F32), axis=-1, keepdims=True)
    at_row = lax.broadcasted_iota(jnp.int32, (rows, LANE), 0)
    at_lane = lax.broadcasted_iota(jnp.int32, (rows, LANE), 1)
    small[SIDE * EXTRA : SIDE * EXTRA + 1] = jnp.sum(jnp.where(at_row == at_lane, product, 0.0), axis=0, keepdims=True)
    small[SIDE * EXTRA + 4 :] = jnp.zeros((small.shape[0] - SIDE * EXTRA - 4, LANE), F32)


def finish(z_index, parts, w_here):
    kinds, rows, inner = w_here.shape
    height, columns = parts[0].shape
    return kernel_call(
        finish_body,
        (1,),
        [whole(height, columns)] * SIDE + [whole(kinds, rows, inner)],
        [whole(kinds, rows, inner), whole(SIDE * EXTRA + 8, LANE)],
        [shape((kinds, rows, inner), F32), shape((SIDE * EXTRA + 8, LANE), F32)],
        scalars=1,
        name="finish",
    )(z_index, *parts, w_here)


def on_device(
    tokens,
    expert_ids,
    capacity,
    gain_attn,
    w_qkv,
    qk_gain,
    w_out,
    gain_ffn,
    w_router,
    w_gate_up,
    w_down,
    cotangent,
):
    length, width = tokens.shape
    expert_count = capacity.shape[0]
    slot_count = length * expert_ids.shape[1] // expert_count
    slots = expert_count * slot_count
    inner = w_qkv.shape[2]
    half = width // 2
    cols = inner // SIDE
    core_index = lax.axis_index("tensor")
    core = core_index.astype(jnp.int32).reshape(1)
    place = [lax.axis_index(a) for a in AXES]
    dp_index = (place[0] * SIDE + place[1]) * SIDE + place[2]
    rows_here_count = width // SIDE**3

    def own_half(value):
        return lax.dynamic_slice_in_dim(value, core_index * half, half, axis=-1)

    expert_of = jnp.asarray(np.repeat(np.eye(expert_count, dtype=np.float32), slot_count, 0), BF)

    def to_owners(rows):
        columns = rows.shape[1]
        return exchange(rows.reshape(expert_count, slot_count, columns), AXES).reshape(slots, columns)

    member, select, grad_send = routing(core, capacity, expert_ids.T, cotangent)
    grad_own = to_owners(grad_send)

    table = jnp.asarray(rotary(length, LANE // 2))
    gains = qk_gain.astype(F32)
    gain_one = gain_attn.astype(F32)
    gain_two = gain_ffn.astype(F32).reshape(1, width)
    w_parts = w_qkv.transpose(1, 0, 2)
    normed_one, raw, turned, kept, value_in, attended, partial = attend(
        tokens, gain_one.reshape(1, width), w_parts, w_out, gains, table
    )
    partial_peer = swap(partial)
    middle, normed_two, probs, gates, picked_total, combine, rows_send = middle_step(
        core, tokens, partial, partial_peer, gain_two, select, w_router, member, expert_of
    )
    rows_own = to_owners(rows_send)

    normed_early, attended_late, pair, grad_late, down, _ = together(
        own_half(normed_one), attended, w_gate_up, grad_own, w_down, rows_send
    )
    down = down[0]
    pair = pair[0].transpose(1, 0, 2)
    grad_peer = swap(grad_late)
    d_hidden = hidden_grad(core, grad_late, grad_peer, down)
    down_far = swap(lax.dynamic_slice_in_dim(down, (1 - core_index) * half, half, axis=1))
    pair_far = swap(lax.dynamic_slice_in_dim(pair, (1 - core_index) * half, half, axis=1))
    rows_own, d_hidden, pair, normed_early, down_far, pair_far = together(
        rows_own, d_hidden, pair, normed_early, down_far, pair_far
    )
    normed_group = share(normed_early, "z")
    rows_peer = swap(rows_own)
    acted, d_pair, extra = experts_step(core, rows_own, rows_peer, d_hidden, pair)
    d_pair, acted, attended_late, *normed_group = together(d_pair, acted, attended_late, *normed_group)
    from_one, from_three = shift(attended_late, "y", 1), shift(attended_late, "y", 3)
    back_send = back_second(back_first(core, d_pair, pair), swap(d_pair), pair_far, extra)
    back_send, acted_peer, from_one, from_three = together(back_send, swap(acted), from_one, from_three)
    back = to_owners(back_send)

    acted_late, own_late, peer_late, _ = together(acted, rows_own, rows_peer, back_send)
    grad_gate_up, grad_down = expert_grads(
        core, own_late, peer_late, grad_late, grad_peer, acted_late, d_pair, own_late
    )
    returned = experts_out(core, acted_late, acted_peer, down, down_far)
    normed_group, _ = together(normed_group, back_send)
    normed_group = turn_parts(normed_group)
    returned, grad_gate_up, grad_down, normed_group = together(returned, grad_gate_up, grad_down, normed_group)
    returned = to_owners(returned)

    gathered = gather_back(back, combine, select, expert_of)
    core_y = jnp.stack([core[0], place[0].astype(jnp.int32)])
    d_logits, d_middle, d_attn, gain_two_local, *d_attn_blocks = middle_back(
        core_y, gathered, swap(gathered), probs, gates, picked_total, member, w_router, middle, cotangent, gain_two,
        from_one
    )

    z_index = place[2].astype(jnp.int32).reshape(1)
    d_attn, normed_group_peer = together(d_attn, swap(normed_group))
    *d_blocks, grad_qk = attend_back(z_index, d_attn, w_out, raw, turned, kept, value_in, gains, table)
    d_group = send_steps(d_blocks, "z")
    returned, *d_group = together(returned, *d_group)

    columns_here = expert_count // 2
    my_logits = lax.dynamic_slice_in_dim(d_logits, core_index * columns_here, columns_here, axis=1)
    partial_grads = group_grads(
        core,
        normed_group,
        normed_group_peer,
        d_group,
        normed_two,
        my_logits,
        gain_two_local,
        grad_qk,
    )
    d_attn_blocks, from_one, _ = together(d_attn_blocks, from_one, d_blocks)
    d_attn_group = [
        d_attn_blocks[0],
        shift(d_attn_blocks[1], "y", 1),
        shift(d_attn_blocks[2], "y", 2),
        shift(d_attn_blocks[3], "y", 3),
    ]
    attended_group = [attended_late, from_one, from_three]
    partial_grads, attended_group, d_attn_group = together(partial_grads, attended_group, d_attn_group)
    arrived = exchange(partial_grads, ("y", "x"))
    d_attn_group, attended_group, late_blocks, late_returned, _ = together(
        d_attn_group, attended_group, d_blocks, returned, partial_grads
    )

    grad_out = out_grads(d_attn_group, attended_group)

    grad_out = send_blocks(grad_out.reshape(SIDE, SIDE, rows_here_count, inner), "z", 1)

    d_one = input_grad(z_index, late_blocks, w_parts)
    d_one = d_one.astype(F32) + swap(d_one).astype(F32)

    residual_in = tokens.astype(F32)
    scale_one = rms(residual_in)
    unit_one = residual_in * scale_one
    weighted = d_one * gain_one
    grad_input = d_middle + scale_one * (
        weighted - unit_one * jnp.mean(weighted * unit_one, axis=-1, keepdims=True)
    )

    mix_own = dot(combine, late_returned, TN)
    result_own = (own_half(middle) + mix_own).astype(BF)
    output = side_by_side(result_own, swap(result_own), core_index)

    grad_out = sum(part.astype(F32) for part in grad_out).astype(BF)
    grad_out = [block_at(grad_out, (place[1] + step) % SIDE, 0) for step in range(SIDE)]
    grad_input, output, *grad_out = together(grad_input, output, *grad_out)
    grad_out = send_steps(grad_out, "x")
    arrived, grad_input, output, *grad_out = together(arrived, grad_input, output, *grad_out)
    grad_out = sum(part.astype(F32) for part in grad_out)
    parts = send_steps(sum_arrived(z_index, arrived, rows_here_count), "z")
    w_here = lax.dynamic_slice_in_dim(w_parts, dp_index * rows_here_count, rows_here_count, axis=1)
    grad_qkv, small = finish(z_index, parts, w_here)
    grad_qkv = grad_qkv.transpose(1, 0, 2)
    small_peer = swap(small)
    gain_here = lax.dynamic_slice_in_dim(gain_one, dp_index * rows_here_count, rows_here_count, axis=0)
    grad_gain_one = (small[SIDE * EXTRA] + small_peer[SIDE * EXTRA])[:rows_here_count] / gain_here
    cut = lambda value: lax.dynamic_slice_in_dim(value, place[2] * rows_here_count, rows_here_count, axis=-1)
    grad_router = jnp.where(
        core_index == 0,
        jnp.concatenate([small[: SIDE * EXTRA], small_peer[: SIDE * EXTRA]], axis=0),
        jnp.concatenate([small_peer[: SIDE * EXTRA], small[: SIDE * EXTRA]], axis=0),
    )
    grad_router = cut(grad_router).T
    grad_gain_two = cut(small[SIDE * EXTRA + 1])
    grad_qk = small[SIDE * EXTRA + 2 : SIDE * EXTRA + 4] + small_peer[SIDE * EXTRA + 2 : SIDE * EXTRA + 4]

    return (
        output,
        grad_input,
        grad_gain_one,
        grad_qkv,
        grad_qk,
        grad_out,
        grad_gain_two,
        grad_router,
        grad_gate_up[None],
        grad_down[None],
    )


def solution(mesh):
    names = AXES + ("tensor",)
    torus = Mesh(mesh.devices.reshape(SIDE, SIDE, SIDE, 2), names)
    return jax.shard_map(
        on_device,
        mesh=torus,
        in_specs=(
            P(AXES, None),
            P(AXES, None),
            P(),
            P(),
            P(None, None, "tensor"),
            P(),
            P(None, "tensor"),
            P(),
            P(),
            P(AXES, None, None, "tensor"),
            P(AXES, "tensor", None),
            P(AXES, None),
        ),
        out_specs=(
            P(AXES, None),
            P(AXES, None),
            P(AXES),
            P(AXES, None, "tensor"),
            P(),
            P(AXES, "tensor"),
            P(AXES),
            P(AXES, None),
            P(AXES, None, None, "tensor"),
            P(AXES, "tensor", None),
        ),
        check_vma=False,
    )
```

```python
import functools
import math

import jax
import jax.numpy as jnp
import numpy as np
from jax import lax
from jax.experimental import pallas as pl
from jax.experimental.pallas import tpu as pltpu
from jax.sharding import Mesh
from jax.sharding import PartitionSpec as P

AXES = ("y", "x", "z")
SIDE = 4
LANE = 128
BF = jnp.bfloat16
F32 = jnp.float32
MIB = 1 << 20


def dot(a, b, dims):
    return lax.dot_general(a, b, (dims, ((), ())), preferred_element_type=F32)


NN = ((1,), (0,))
NT = ((1,), (1,))
TN = ((0,), (0,))


def rms(values):
    return lax.rsqrt(jnp.mean(values * values, axis=-1, keepdims=True) + 1e-06)


def rotary(length, half_dim):
    position = np.arange(length, dtype=np.float32)
    inverse = np.float32(50000.0) ** (-np.arange(half_dim, dtype=np.float32) / np.float32(half_dim))
    angles = position[:, None] * inverse[None, :].astype(np.float32)
    cosine = np.cos(angles).astype(np.float32)
    sine = np.sin(angles).astype(np.float32)
    return np.stack([np.concatenate([cosine, cosine], 1), np.concatenate([-sine, sine], 1)])


def swap(value):
    return lax.ppermute(value, "tensor", [(0, 1), (1, 0)])


def shift(value, axis, step):
    return lax.ppermute(value, axis, [(i, (i + step) % SIDE) for i in range(SIDE)])


def side_by_side(own, peer, core):
    return jnp.where(
        core == 0,
        jnp.concatenate([own, peer], axis=-1),
        jnp.concatenate([peer, own], axis=-1),
    )


def block_at(value, index, dim):
    return lax.dynamic_index_in_dim(value, index, dim, keepdims=False)


def together(*values):
    return lax.optimization_barrier(values)


def share(value, axis):
    return [value] + [shift(value, axis, step) for step in (1, 2, 3)]


def send_blocks(value, axis, dim):
    here = lax.axis_index(axis)
    own = block_at(value, here, dim)
    return [own] + [shift(block_at(value, (here + step) % SIDE, dim), axis, step) for step in (1, 2, 3)]


def send_steps(blocks, axis):
    return [blocks[0]] + [shift(blocks[step], axis, step) for step in (1, 2, 3)]


def exchange(value, axes):
    return lax.all_to_all(value, axes, split_axis=0, concat_axis=0, tiled=True)


def shape(dims, kind):
    return jax.ShapeDtypeStruct(dims, kind)


def main_memory(dims, kind):
    return pltpu.HBM(dims, kind)


def held(*values):
    return [pltpu.with_memory_space_constraint(value, pltpu.HBM) for value in values]


def kernel_call(body, grid, ins, outs, out_shapes, scratch=(), mib=40, scalars=0, name=None):
    return pl.pallas_call(
        body,
        grid_spec=pltpu.PrefetchScalarGridSpec(
            num_scalar_prefetch=scalars, grid=grid, in_specs=ins, out_specs=outs, scratch_shapes=list(scratch)
        ),
        out_shape=out_shapes,
        compiler_params=pltpu.CompilerParams(vmem_limit_bytes=mib * MIB),
        name=name,
    )


def whole(*dims):
    return pl.BlockSpec(dims, lambda *_: (0,) * len(dims))


def rope(values, table):
    return values * table[0] + pltpu.roll(values, values.shape[-1] // 2, 1) * table[1]


def unrope(values, table):
    return values * table[0] - pltpu.roll(values, values.shape[-1] // 2, 1) * table[1]


def attention_weights(query, key):
    scores = dot(query, key, NT) * (1.0 / math.sqrt(query.shape[-1]))
    raised = jnp.exp(scores - jnp.max(scores, axis=-1, keepdims=True))
    return raised / jnp.sum(raised, axis=-1, keepdims=True)


def attend_body(tokens, gain, w_qkv, w_out, gains, table, normed, raw, turned, kept, value_out, attended, partial, total):
    step = pl.program_id(0)

    @pl.when(step == 0)
    def _():
        x = tokens[...].astype(F32)
        normed[...] = (x * rms(x) * gain[...]).astype(BF)
        total[...] = jnp.zeros_like(total)

    h = normed[...]
    query_raw = dot(h, w_qkv[0], NN)
    key_raw = dot(h, w_qkv[1], NN)
    value = dot(h, w_qkv[2], NN).astype(BF)
    raw[0] = query_raw
    raw[1] = key_raw
    value_out[...] = value
    for at in range(query_raw.shape[1] // LANE):
        cut = slice(at * LANE, (at + 1) * LANE)
        q, k = query_raw[:, cut], key_raw[:, cut]
        query = rope(q * rms(q) * gains[0:1], table).astype(BF)
        key = rope(k * rms(k) * gains[1:2], table).astype(BF)
        turned[0, :, cut] = query
        turned[1, :, cut] = key
        weights = attention_weights(query, key)
        kept[at] = weights
        attended[:, cut] = dot(weights.astype(BF), value[:, cut], NN).astype(BF)
    total[...] += dot(attended[...], w_out[...], NT)

    @pl.when(step == pl.num_programs(0) - 1)
    def _():
        partial[...] = total[...].astype(BF)


def attend(tokens, gain, w_qkv, w_out, gains, table):
    length, width = tokens.shape
    inner = w_qkv.shape[2]
    cols = inner // SIDE
    return kernel_call(
        attend_body,
        (SIDE,),
        [
            whole(length, width),
            whole(1, width),
            pl.BlockSpec((3, width, cols), lambda i: (0, 0, i)),
            pl.BlockSpec((width, cols), lambda i: (0, i)),
            whole(2, LANE),
            whole(2, length, LANE),
        ],
        [
            whole(length, width),
            pl.BlockSpec((2, length, cols), lambda i: (0, 0, i)),
            pl.BlockSpec((2, length, cols), lambda i: (0, 0, i)),
            pl.BlockSpec((cols // LANE, length, length), lambda i: (i, 0, 0)),
            pl.BlockSpec((length, cols), lambda i: (0, i)),
            pl.BlockSpec((length, cols), lambda i: (0, i)),
            whole(length, width),
        ],
        [
            main_memory((length, width), BF),
            main_memory((2, length, inner), F32),
            main_memory((2, length, inner), BF),
            main_memory((inner // LANE, length, length), F32),
            main_memory((length, inner), BF),
            main_memory((length, inner), BF),
            shape((length, width), BF),
        ],
        [pltpu.VMEM((length, width), F32)],
        name="attend",
    )(tokens, gain, w_qkv, w_out, gains, table)


def attend_back_body(z_index, d_attn, w_out, raw, turned, kept, value_in, gains, table, *outs):
    d_gains = outs[SIDE]
    step = pl.program_id(0)
    parts = ([], [], [])

    @pl.when(step == 0)
    def _():
        d_gains[...] = jnp.zeros_like(d_gains)

    d_attended = dot(d_attn[...], w_out[...], NN).astype(BF)
    for at in range(d_attended.shape[1] // LANE):
        cut = slice(at * LANE, (at + 1) * LANE)
        q, k = raw[0, :, cut], raw[1, :, cut]
        rq, rk = rms(q), rms(k)
        unit_q, unit_k = q * rq, k * rk
        query, key = turned[0, :, cut], turned[1, :, cut]
        weights = kept[at]
        grad = d_attended[:, cut]
        d_value = dot(weights.astype(BF), grad, TN)
        d_weights = dot(grad, value_in[:, cut], NT)
        d_scores = (
            weights * (d_weights - jnp.sum(weights * d_weights, axis=-1, keepdims=True))
        ).astype(BF)
        root = 1.0 / math.sqrt(LANE)
        d_query = unrope(dot(d_scores, key, NN) * root, table)
        d_key = unrope(dot(d_scores, query, TN) * root, table)
        d_gains[0:1] += jnp.sum(d_query * unit_q, axis=0, keepdims=True)
        d_gains[1:2] += jnp.sum(d_key * unit_k, axis=0, keepdims=True)
        wq = d_query * gains[0:1]
        wk = d_key * gains[1:2]
        parts[0].append((rq * (wq - unit_q * jnp.mean(wq * unit_q, axis=-1, keepdims=True))).astype(BF))
        parts[1].append((rk * (wk - unit_k * jnp.mean(wk * unit_k, axis=-1, keepdims=True))).astype(BF))
        parts[2].append(d_value.astype(BF))
    for k in range(SIDE):

        @pl.when((z_index[0] + k) % SIDE == step)
        def _():
            for kind in range(3):
                outs[k][kind] = jnp.concatenate(parts[kind], axis=1)


def attend_back(z_index, d_attn, w_out, raw, turned, kept, value_in, gains, table):
    length, width = d_attn.shape
    inner = w_out.shape[1]
    cols = inner // SIDE
    return kernel_call(
        attend_back_body,
        (SIDE,),
        [
            whole(length, width),
            pl.BlockSpec((width, cols), lambda i, z: (0, i)),
            pl.BlockSpec((2, length, cols), lambda i, z: (0, 0, i)),
            pl.BlockSpec((2, length, cols), lambda i, z: (0, 0, i)),
            pl.BlockSpec((cols // LANE, length, length), lambda i, z: (i, 0, 0)),
            pl.BlockSpec((length, cols), lambda i, z: (0, i)),
            whole(2, LANE),
            whole(2, length, LANE),
        ],
        [whole(3, length, cols)] * SIDE + [whole(2, LANE)],
        [shape((3, length, cols), BF)] * SIDE + [shape((2, LANE), F32)],
        scalars=1,
        name="attend_back",
    )(z_index, d_attn, *held(w_out, raw, turned, kept, value_in, gains, table))


def input_grad_body(z_index, *refs):
    w_qkv, out, total = refs[SIDE:]
    step = pl.program_id(0)

    @pl.when(step == 0)
    def _():
        total[...] = jnp.zeros_like(total)

    for k in range(SIDE):

        @pl.when(step == k)
        def _():
            block = refs[k]
            total[...] += dot(block[0], w_qkv[0], NT) + dot(block[1], w_qkv[1], NT) + dot(block[2], w_qkv[2], NT)

    @pl.when(step == pl.num_programs(0) - 1)
    def _():
        out[...] = total[...].astype(BF)


def input_grad(z_index, d_blocks, w_qkv):
    _, length, cols = d_blocks[0].shape
    width = w_qkv.shape[1]
    return kernel_call(
        input_grad_body,
        (SIDE,),
        [whole(3, length, cols)] * SIDE
        + [pl.BlockSpec((3, width, cols), lambda i, z: (0, 0, lax.rem(z[0] + i, SIDE)))],
        whole(length, width),
        shape((length, width), BF),
        [pltpu.VMEM((length, width), F32)],
        scalars=1,
        name="input_grad",
    )(z_index, *d_blocks, *held(w_qkv))


def routing_body(select_rows, core, capacity, ids, later, cotangent, member_out, select, rows, code):
    step = pl.program_id(0)
    experts, length = code.shape

    @pl.when(step == 0)
    def _():
        at_expert = lax.broadcasted_iota(jnp.int32, (experts, length), 0)
        member = jnp.zeros((experts, length), F32)
        for j in range(ids.shape[0]):
            member = member + (ids[j : j + 1, :] == at_expert).astype(F32)
        member_out[...] = member.T
        ranks = dot(member.astype(BF), later[...], NN)
        row = lax.broadcasted_iota(jnp.int32, (experts, experts), 0)
        column = lax.broadcasted_iota(jnp.int32, (experts, experts), 1)
        limit = jnp.sum(jnp.where(row == column, capacity[...].astype(F32), 0.0), axis=1, keepdims=True)
        code[...] = jnp.where((member > 0.5) & (ranks < limit), ranks, -1.0)

    chunk = rows.shape[0]
    per = chunk * experts // select_rows
    depth = chunk // per
    slot = lax.broadcasted_iota(jnp.int32, (depth, length), 0).astype(F32)
    mine = code[pl.ds(pl.multiple_of(step * per, per), per), :]
    hit = jnp.concatenate([(mine[k : k + 1] == slot).astype(F32) for k in range(per)], axis=0).astype(BF)
    select[...] = hit
    rows[...] = dot(hit, cotangent[...], NN).astype(BF)


def routing(core, capacity, ids, cotangent):
    length, width = cotangent.shape
    experts = capacity.shape[0]
    slots = length * ids.shape[0]
    chunk = 16 * (slots // experts)
    half = width // 2
    later = jnp.asarray(np.triu(np.ones((length, length), np.float32), 1), BF)
    return kernel_call(
        functools.partial(routing_body, slots),
        (slots // chunk,),
        [
            whole(1, experts),
            whole(*ids.shape),
            whole(length, length),
            pl.BlockSpec((length, half), lambda i, c: (0, c[0])),
        ],
        [
            whole(length, experts),
            pl.BlockSpec((chunk, length), lambda i, c: (i, 0)),
            pl.BlockSpec((chunk, half), lambda i, c: (i, 0)),
        ],
        [shape((length, experts), F32), main_memory((slots, length), BF), main_memory((slots, half), BF)],
        [pltpu.VMEM((experts, length), F32)],
        scalars=1,
        name="routing",
    )(core, *held(capacity.reshape(1, experts), ids, later, cotangent))


def middle_body(core, tokens, own, peer, gain, select, w_router, member, expert_of,
                middle, normed, probs_out, gates_out, total_out, combine, rows):
    x2 = tokens[...].astype(F32) + (own[...].astype(F32) + peer[...].astype(F32))
    middle[...] = x2
    normed[...] = (x2 * rms(x2) * gain[...]).astype(BF)
    logits = dot(normed[...], w_router[...], NN)
    raised = jnp.exp(logits - jnp.max(logits, axis=-1, keepdims=True))
    probs = raised / jnp.sum(raised, axis=-1, keepdims=True)
    picked = probs * member[...]
    total = jnp.sum(picked, axis=-1, keepdims=True)
    gates = picked / total
    probs_out[...] = probs
    gates_out[...] = gates
    total_out[...] = total
    low = gates.astype(BF)
    half = rows.shape[1] - LANE
    for at in range(0, rows.shape[0], 256):
        cut = slice(at, at + 256)
        spread = dot(expert_of[cut], low, NT) * select[cut].astype(F32)
        combine[cut] = spread.astype(BF)
        gate = jnp.sum(spread, axis=-1, keepdims=True)
        rows[cut, half:] = jnp.broadcast_to(gate, (256, LANE)).astype(BF)
    for which in range(2):

        @pl.when(core[0] == which)
        def _():
            for at in range(0, rows.shape[0], 256):
                rows[at : at + 256, :half] = dot(
                    select[at : at + 256], normed[:, which * half : (which + 1) * half], NN
                ).astype(BF)


def middle_step(core, tokens, own, peer, gain, select, w_router, member, expert_of):
    length, width = tokens.shape
    slots, experts = expert_of.shape
    columns = width // 2 + LANE
    return kernel_call(
        middle_body,
        (1,),
        [whole(length, width)] * 3
        + [whole(1, width), whole(slots, length), whole(width, experts), whole(length, experts), whole(slots, experts)],
        [
            whole(length, width),
            whole(length, width),
            whole(length, experts),
            whole(length, experts),
            whole(length, 1),
            whole(slots, length),
            whole(slots, columns),
        ],
        [
            main_memory((length, width), F32),
            main_memory((length, width), BF),
            shape((length, experts), F32),
            shape((length, experts), F32),
            shape((length, 1), F32),
            main_memory((slots, length), BF),
            main_memory((slots, columns), BF),
        ],
        scalars=1,
        name="middle",
    )(core, *held(tokens), own, peer, *held(gain, select, w_router, member, expert_of))


def gather_back_body(back, combine, select, expert_of, out):
    half = out.shape[1] - LANE
    experts = expert_of.shape[1]
    out[:, :half] = dot(combine[...], back[:, :half], TN)
    high = back[:, half : half + 1].astype(F32)
    low = back[:, half + 1 : half + 2].astype(F32)
    picked = select[...].astype(F32)
    spread = dot((picked * high).astype(BF), expert_of[...], TN) + dot((picked * low).astype(BF), expert_of[...], TN)
    out[:, half : half + experts] = spread
    out[:, half + experts :] = jnp.zeros((out.shape[0], LANE - experts), F32)


def gather_back(back, combine, select, expert_of):
    slots, columns = back.shape
    length = combine.shape[1]
    experts = expert_of.shape[1]
    return kernel_call(
        gather_back_body,
        (1,),
        [whole(slots, columns), whole(slots, length), whole(slots, length), whole(slots, experts)],
        whole(length, columns),
        shape((length, columns), F32),
        name="gather_back",
    )(back, *held(combine, select, expert_of))


def middle_back_body(core, own, peer, probs, gates, total, member, w_router, middle, cotangent, gain, far,
                     d_logits_out, d_middle, d_attn, d_gain, *d_attn_blocks):
    half = own.shape[1] - LANE
    experts = probs.shape[1]
    d_gates = own[:, half : half + experts] + peer[:, half : half + experts]
    g, p = gates[...], probs[...]
    d_picked = member[...] * (d_gates - jnp.sum(d_gates * g, axis=-1, keepdims=True)) / total[...]
    d_logits = (p * (d_picked - jnp.sum(p * d_picked, axis=-1, keepdims=True))).astype(BF)
    d_logits_out[...] = d_logits
    d_normed = dot(d_logits, w_router[...], NT)
    for which in range(2):

        @pl.when(core[0] == which)
        def _():
            first, second = (own, peer) if which == 0 else (peer, own)
            d_middle[:, :half] = first[:, :half]
            d_middle[:, half:] = second[:, :half]

    d_normed = d_normed + d_middle[...]
    x2 = middle[...]
    scale = rms(x2)
    unit = x2 * scale
    d_gain[...] = jnp.sum(d_normed * unit, axis=0, keepdims=True)
    weighted = d_normed * gain[...]
    value = cotangent[...].astype(F32) + scale * (
        weighted - unit * jnp.mean(weighted * unit, axis=-1, keepdims=True)
    )
    d_middle[...] = value
    low = value.astype(BF)
    d_attn[...] = low
    cut = d_attn_blocks[0].shape[1]
    for which in range(SIDE):

        @pl.when(core[1] == which)
        def _():
            for k in range(SIDE):
                at = (which + k) % SIDE * cut
                d_attn_blocks[k][:, :cut] = low[:, at : at + cut]

    d_attn_blocks[1][:, cut:] = far[...]


def middle_back(core, own, peer, probs, gates, total, member, w_router, middle, cotangent, gain, far):
    length, width = middle.shape
    experts = probs.shape[1]
    columns = own.shape[1]
    quarter = width // SIDE
    blocks = [quarter, quarter + far.shape[1], quarter, quarter]
    return kernel_call(
        middle_back_body,
        (1,),
        [whole(length, columns)] * 2
        + [whole(length, experts)] * 2
        + [
            whole(length, 1),
            whole(length, experts),
            whole(width, experts),
            whole(length, width),
            whole(length, width),
            whole(1, width),
            whole(*far.shape),
        ],
        [whole(length, experts), whole(length, width), whole(length, width), whole(1, width)]
        + [whole(length, block) for block in blocks],
        [
            shape((length, experts), BF),
            shape((length, width), F32),
            shape((length, width), BF),
            shape((1, width), F32),
        ]
        + [shape((length, block), BF) for block in blocks],
        scalars=1,
        name="middle_back",
    )(core, own, peer, *held(probs, gates, total, member, w_router, middle, cotangent, gain, far))


def hidden_grad_body(core, own, peer, down_own, down_peer, out):
    half = down_own.shape[1]
    out[...] = dot(own[:, :half], down_own[...], NT) + dot(peer[:, :half], down_peer[...], NT)


ROWS = 512


def hidden_grad(core, own, peer, down):
    slots, columns = own.shape
    hidden, width = down.shape
    half = width // 2
    return kernel_call(
        hidden_grad_body,
        (slots // ROWS,),
        [
            pl.BlockSpec((ROWS, columns), lambda i, c: (i, 0)),
            pl.BlockSpec((ROWS, columns), lambda i, c: (i, 0)),
            pl.BlockSpec((hidden, half), lambda i, c: (0, c[0])),
            pl.BlockSpec((hidden, half), lambda i, c: (0, 1 - c[0])),
        ],
        pl.BlockSpec((ROWS, hidden), lambda i, c: (i, 0)),
        main_memory((slots, hidden), F32),
        scalars=1,
        name="hidden_grad",
    )(core, *held(own, peer, down, down))


def gate_first_body(core, own, pair, out):
    half, hidden = pair.shape[1:]
    mine = own[:, :half]
    out[:, :hidden] = dot(mine, pair[0], NN)
    out[:, hidden:] = dot(mine, pair[1], NN)


def gate_first(core, own, pair):
    slots, columns = own.shape
    half = columns - LANE
    hidden = pair.shape[2]
    rows = lambda n: pl.BlockSpec((ROWS, n), lambda i, c: (i, 0))
    return kernel_call(
        gate_first_body,
        (slots // ROWS,),
        [rows(columns), pl.BlockSpec((2, half, hidden), lambda i, c: (0, c[0], 0))],
        rows(2 * hidden),
        shape((slots, 2 * hidden), F32),
        scalars=1,
        mib=28,
        name="gate_first",
    )(core, *held(own, pair))


def experts_body(core, partial, peer, d_hidden, pair, acted, d_pair, extra):
    hidden = d_hidden.shape[1]
    half = pair.shape[1]
    other = peer[:, :half]
    gate = partial[:, :hidden] + dot(other, pair[0], NN)
    up = partial[:, hidden:] + dot(other, pair[1], NN)
    sig = 1.0 / (1.0 + jnp.exp(-gate))
    silu = gate * sig
    act = (silu * up).astype(BF)
    acted[...] = act
    d_act = d_hidden[...]
    slot_grad = jnp.sum(d_act * act.astype(F32), axis=-1, keepdims=True)
    high = slot_grad.astype(BF)
    low = (slot_grad - high.astype(F32)).astype(BF)
    at = lax.broadcasted_iota(jnp.int32, extra.shape, 1)
    extra[...] = jnp.where(at == 0, high.astype(F32), jnp.where(at == 1, low.astype(F32), 0.0)).astype(BF)
    d_pair[:, :hidden] = (d_act * up * sig * (1.0 + gate * (1.0 - sig))).astype(BF)
    d_pair[:, hidden:] = (d_act * silu).astype(BF)


def back_first_body(core, d_pair, pair, out):
    hidden = pair.shape[2]
    out[...] = dot(d_pair[:, :hidden], pair[0], NT) + dot(d_pair[:, hidden:], pair[1], NT)


def back_first(core, d_pair, pair):
    slots, columns = d_pair.shape
    _, width, hidden = pair.shape
    half = width // 2
    rows = lambda n: pl.BlockSpec((ROWS, n), lambda i, c: (i, 0))
    return kernel_call(
        back_first_body,
        (slots // ROWS,),
        [rows(columns), pl.BlockSpec((2, half, hidden), lambda i, c: (0, c[0], 0))],
        rows(half),
        shape((slots, half), F32),
        scalars=1,
        mib=28,
        name="back_first",
    )(core, *held(d_pair, pair))


def back_second_body(partial, d_pair, pair, extra, out):
    _, half, hidden = pair.shape
    value = dot(d_pair[:, :hidden], pair[0], NT) + dot(d_pair[:, hidden:], pair[1], NT)
    out[:, :half] = (partial[...] + value).astype(BF)
    out[:, half:] = extra[...]


def back_second(partial, d_pair, pair, extra):
    slots, columns = d_pair.shape
    _, half, hidden = pair.shape
    rows = lambda n: pl.BlockSpec((ROWS, n), lambda i: (i, 0))
    return kernel_call(
        back_second_body,
        (slots // ROWS,),
        [rows(half), rows(columns), whole(2, half, hidden), rows(LANE)],
        rows(half + LANE),
        main_memory((slots, half + LANE), BF),
        mib=28,
        name="back_second",
    )(partial, d_pair, *held(pair, extra))


def experts_out_body(core, acted, acted_peer, down, down_far, out):
    out[...] = (dot(acted[...], down[...], NN) + dot(acted_peer[...], down_far[...], NN)).astype(BF)


def experts_out(core, acted, acted_peer, down, down_far):
    slots, hidden = acted.shape
    half = down_far.shape[1]
    rows = lambda n: pl.BlockSpec((ROWS, n), lambda i, c: (i, 0))
    return kernel_call(
        experts_out_body,
        (slots // ROWS,),
        [
            rows(hidden),
            rows(hidden),
            pl.BlockSpec((hidden, half), lambda i, c: (0, c[0])),
            whole(hidden, half),
        ],
        rows(half),
        main_memory((slots, half), BF),
        scalars=1,
        name="experts_out",
    )(core, *held(acted, acted_peer, down, down_far))


def experts_step(core, partial, peer, d_hidden, pair):
    slots, columns = peer.shape
    half = columns - LANE
    hidden = pair.shape[2]
    block = ROWS // 2
    rows = lambda n: pl.BlockSpec((block, n), lambda i, c: (i, 0))
    return kernel_call(
        experts_body,
        (slots // block,),
        [
            rows(2 * hidden),
            rows(columns),
            rows(hidden),
            pl.BlockSpec((2, half, hidden), lambda i, c: (0, 1 - c[0], 0)),
        ],
        [rows(hidden), rows(2 * hidden), rows(LANE)],
        [
            main_memory((slots, hidden), BF),
            main_memory((slots, 2 * hidden), BF),
            main_memory((slots, LANE), BF),
        ],
        scalars=1,
        mib=28,
        name="experts",
    )(core, partial, peer, *held(d_hidden, pair))


def expert_grads_body(core, own, peer, grad_own, grad_peer, acted, d_pair, gates, grad_pair, grad_down, pair_low, act_low):
    step = pl.program_id(0)
    hidden = acted.shape[1]

    @pl.when(step == 0)
    def _():
        gate = gates[:, :1].astype(F32)
        pair_low[...] = (d_pair[...].astype(F32) * gate).astype(BF)
        act_low[...] = (acted[...].astype(F32) * gate).astype(BF)

    def part(rows, grads):
        value = dot(rows[...], pair_low[...], TN)
        grad_pair[:, 0, :] = value[:, :hidden]
        grad_pair[:, 1, :] = value[:, hidden:]
        grad_down[...] = dot(act_low[...], grads[...], TN)

    @pl.when(step < SIDE)
    def _():
        part(own, grad_own)

    @pl.when(step >= SIDE)
    def _():
        part(peer, grad_peer)


def expert_grads(core, own, peer, grad_own, grad_peer, acted, d_pair, gates):
    slots, half = grad_own.shape
    hidden = acted.shape[1]
    cut = half // SIDE
    first = pl.BlockSpec((slots, cut), lambda i, c: (0, jnp.minimum(i, SIDE - 1)))
    second = pl.BlockSpec((slots, cut), lambda i, c: (0, jnp.maximum(i - SIDE, 0)))

    def target(i, c):
        return jnp.where(i < SIDE, c[0] * SIDE + i, (1 - c[0]) * SIDE + i - SIDE)

    return kernel_call(
        expert_grads_body,
        (2 * SIDE,),
        [first, second, first, second, whole(slots, hidden), whole(slots, 2 * hidden), pl.BlockSpec((slots, LANE), lambda i, c: (0, half // LANE))],
        [
            pl.BlockSpec((cut, 2, hidden), lambda i, c: (target(i, c), 0, 0)),
            pl.BlockSpec((hidden, cut), lambda i, c: (0, target(i, c))),
        ],
        [shape((2 * half, 2, hidden), F32), shape((hidden, 2 * half), F32)],
        [pltpu.VMEM((slots, 2 * hidden), BF), pltpu.VMEM((slots, hidden), BF)],
        mib=48,
        scalars=1,
        name="expert_grads",
    )(core, *held(own), peer, *held(grad_own, grad_peer, acted, d_pair, gates))


EXTRA = 8


def group_grads_body(core, own, peer, *refs):
    step = pl.program_id(0)
    d_group = refs[:SIDE]
    normed_two, d_logits, d_gain, d_qk, out, right = refs[SIDE:]
    _, length, cols = d_group[0].shape
    targets = out.shape[0]
    rows = out.shape[1] - EXTRA

    @pl.when(step == 0)
    def _():
        for k in range(SIDE):
            for which in range(3):
                right[k * length : (k + 1) * length, which * cols : (which + 1) * cols] = d_group[k][which]

    def part(normed):
        value = dot(normed[...], right[...], NN).astype(BF)
        for k in range(targets):
            out[k, :rows] = value[k * rows : (k + 1) * rows]

    @pl.when(step < SIDE // 2)
    def _():
        part(own)

    @pl.when(step >= SIDE // 2)
    def _():
        part(peer)

    router = dot(d_logits[...], normed_two[...], TN)
    for k in range(targets):
        cut = slice(k * rows, (k + 1) * rows)
        for at in range(SIDE):
            out[k, rows:, at * LANE : (at + 1) * LANE] = router[at * EXTRA : (at + 1) * EXTRA, cut].astype(BF)
        out[k, rows:, SIDE * LANE : (SIDE + 1) * LANE] = jnp.broadcast_to(d_gain[:, cut], (EXTRA, LANE)).astype(BF)
        out[k, rows:, (SIDE + 1) * LANE :] = jnp.concatenate([d_qk[...]] * (EXTRA // 2), axis=0).astype(BF)


def turn_parts_body(*refs):
    value = jnp.concatenate([part[...].astype(F32) for part in refs[:SIDE]], axis=0)
    refs[SIDE][...] = value.T.astype(BF)


def turn_parts(parts):
    length, width = parts[0].shape
    cut = 256
    return kernel_call(
        turn_parts_body,
        (width // cut,),
        [pl.BlockSpec((length, cut), lambda i: (0, i))] * SIDE,
        pl.BlockSpec((cut, SIDE * length), lambda i: (i, 0)),
        main_memory((width, SIDE * length), BF),
        name="turn_parts",
    )(*held(*parts))


def group_grads(core, own, peer, d_group, normed_two, d_logits, d_gain, d_qk):
    half, depth = own.shape
    length = depth // SIDE
    cols = d_group[0].shape[2]
    steps = SIDE // 2
    cut = half // steps
    places = SIDE * SIDE
    rows = 2 * half // places

    def target(i, c):
        return jnp.where(i < steps, c[0] * steps + i, (1 - c[0]) * steps + i - steps)

    return kernel_call(
        group_grads_body,
        (2 * steps,),
        [
            pl.BlockSpec((cut, depth), lambda i, c: (jnp.minimum(i, steps - 1), 0)),
            pl.BlockSpec((cut, depth), lambda i, c: (jnp.maximum(i - steps, 0), 0)),
        ]
        + [whole(3, length, cols)] * SIDE
        + [
            pl.BlockSpec((length, cut), lambda i, c: (0, target(i, c))),
            whole(length, d_logits.shape[1]),
            pl.BlockSpec((1, cut), lambda i, c: (0, target(i, c))),
            whole(2, LANE),
        ],
        pl.BlockSpec((cut // rows, rows + EXTRA, 3 * cols), lambda i, c: (target(i, c), 0, 0)),
        main_memory((places, rows + EXTRA, 3 * cols), BF),
        [pltpu.VMEM((depth, 3 * cols), BF)],
        scalars=1,
        name="group_grads",
    )(core, *held(own, peer), *d_group, *held(normed_two), d_logits, d_gain, d_qk)


def out_grads_body(*refs):
    out = refs[-1]
    rows = out.shape[0]
    left = jnp.concatenate([part[:, :rows] for part in refs[:SIDE]], axis=0)
    right = jnp.concatenate([refs[SIDE][...], refs[SIDE + 1][...], refs[1][:, rows:], refs[SIDE + 2][...]], axis=0)
    out[...] = dot(left, right, TN).astype(BF)


def out_grads(d_attn, attended):
    length, rows = d_attn[0].shape
    inner = attended[0].shape[1]
    return kernel_call(
        out_grads_body,
        (1,),
        [whole(*part.shape) for part in d_attn] + [whole(length, inner)] * len(attended),
        whole(rows, inner),
        shape((rows, inner), BF),
        name="out_grads",
    )(*d_attn, *held(*attended))


def sum_arrived_body(rows, z_index, arrived, *outs):
    value = arrived[0].astype(F32)
    for k in range(1, arrived.shape[0]):
        value = value + arrived[k].astype(F32)
    value = value.astype(BF)
    main = SIDE * rows
    for which in range(SIDE):

        @pl.when(z_index[0] == which)
        def _():
            for step in range(SIDE):
                at = (which + step) % SIDE * rows
                outs[step][:rows] = value[at : at + rows]

    for step in range(SIDE):
        outs[step][rows:] = value[main:]


def sum_arrived(z_index, arrived, rows):
    places, height, columns = arrived.shape
    cols = columns // 3
    return kernel_call(
        functools.partial(sum_arrived_body, rows),
        (3,),
        [pl.BlockSpec((places, height, cols), lambda i, z: (0, 0, i))],
        [pl.BlockSpec((rows + EXTRA, cols), lambda i, z: (0, i))] * SIDE,
        [shape((rows + EXTRA, columns), BF)] * SIDE,
        scalars=1,
        name="sum_arrived",
    )(z_index, arrived)


def finish_body(z_index, *refs):
    parts, w_here, grad, small = refs[:SIDE], refs[SIDE], refs[SIDE + 1], refs[SIDE + 2]
    rows = grad.shape[1]
    cols = parts[0].shape[1] // 3
    for which in range(SIDE):

        @pl.when(z_index[0] == which)
        def _():
            ordered = [parts[(which - source) % SIDE] for source in range(SIDE)]
            for source in range(SIDE):
                for kind in range(3):
                    grad[kind, :, source * cols : (source + 1) * cols] = ordered[source][
                        :rows, kind * cols : (kind + 1) * cols
                    ].astype(F32)
            extra = [part[rows:].astype(F32) for part in ordered]
            total = (extra[0] + extra[1]) + (extra[2] + extra[3])
            for at in range(SIDE):
                small[at * EXTRA : (at + 1) * EXTRA] = total[:, at * LANE : (at + 1) * LANE]
            small[SIDE * EXTRA + 1 : SIDE * EXTRA + 2] = total[0:1, SIDE * LANE : (SIDE + 1) * LANE]
            small[SIDE * EXTRA + 2 : SIDE * EXTRA + 4] = total[0:2, (SIDE + 1) * LANE :]

    product = jnp.sum(grad[0] * w_here[0].astype(F32) + grad[1] * w_here[1].astype(F32) + grad[2] * w_here[2].astype(F32), axis=-1, keepdims=True)
    at_row = lax.broadcasted_iota(jnp.int32, (rows, LANE), 0)
    at_lane = lax.broadcasted_iota(jnp.int32, (rows, LANE), 1)
    small[SIDE * EXTRA : SIDE * EXTRA + 1] = jnp.sum(jnp.where(at_row == at_lane, product, 0.0), axis=0, keepdims=True)
    small[SIDE * EXTRA + 4 :] = jnp.zeros((small.shape[0] - SIDE * EXTRA - 4, LANE), F32)


def finish(z_index, parts, w_here):
    kinds, rows, inner = w_here.shape
    height, columns = parts[0].shape
    return kernel_call(
        finish_body,
        (1,),
        [whole(height, columns)] * SIDE + [whole(kinds, rows, inner)],
        [whole(kinds, rows, inner), whole(SIDE * EXTRA + 8, LANE)],
        [shape((kinds, rows, inner), F32), shape((SIDE * EXTRA + 8, LANE), F32)],
        scalars=1,
        name="finish",
    )(z_index, *parts, w_here)


def on_device(
    tokens,
    expert_ids,
    capacity,
    gain_attn,
    w_qkv,
    qk_gain,
    w_out,
    gain_ffn,
    w_router,
    w_gate_up,
    w_down,
    cotangent,
):
    length, width = tokens.shape
    expert_count = capacity.shape[0]
    slot_count = length * expert_ids.shape[1] // expert_count
    slots = expert_count * slot_count
    inner = w_qkv.shape[2]
    half = width // 2
    cols = inner // SIDE
    core_index = lax.axis_index("tensor")
    core = core_index.astype(jnp.int32).reshape(1)
    place = [lax.axis_index(a) for a in AXES]
    dp_index = (place[0] * SIDE + place[1]) * SIDE + place[2]
    rows_here_count = width // SIDE**3

    def own_half(value):
        return lax.dynamic_slice_in_dim(value, core_index * half, half, axis=-1)

    expert_of = jnp.asarray(np.repeat(np.eye(expert_count, dtype=np.float32), slot_count, 0), BF)

    def to_owners(rows):
        columns = rows.shape[1]
        return exchange(rows.reshape(expert_count, slot_count, columns), AXES).reshape(slots, columns)

    member, select, grad_send = routing(core, capacity, expert_ids.T, cotangent)
    grad_own = to_owners(grad_send)

    table = jnp.asarray(rotary(length, LANE // 2))
    gains = qk_gain.astype(F32)
    gain_one = gain_attn.astype(F32)
    gain_two = gain_ffn.astype(F32).reshape(1, width)
    w_parts = w_qkv.transpose(1, 0, 2)
    normed_one, raw, turned, kept, value_in, attended, partial = attend(
        tokens, gain_one.reshape(1, width), w_parts, w_out, gains, table
    )
    partial_peer = swap(partial)
    middle, normed_two, probs, gates, picked_total, combine, rows_send = middle_step(
        core, tokens, partial, partial_peer, gain_two, select, w_router, member, expert_of
    )
    rows_own = to_owners(rows_send)

    normed_early, attended_late, pair, grad_late, down, _ = together(
        own_half(normed_one), attended, w_gate_up, grad_own, w_down, rows_send
    )
    down = down[0]
    pair = pair[0].transpose(1, 0, 2)
    grad_peer = swap(grad_late)
    d_hidden = hidden_grad(core, grad_late, grad_peer, down)
    down_far = swap(lax.dynamic_slice_in_dim(down, (1 - core_index) * half, half, axis=1))
    pair_far = swap(lax.dynamic_slice_in_dim(pair, (1 - core_index) * half, half, axis=1))
    rows_own, d_hidden, pair, normed_early, down_far, pair_far = together(
        rows_own, d_hidden, pair, normed_early, down_far, pair_far
    )
    normed_group = share(normed_early, "z")
    rows_peer = swap(rows_own)
    acted, d_pair, extra = experts_step(core, gate_first(core, rows_own, pair), rows_peer, d_hidden, pair)
    d_pair, acted, attended_late, *normed_group = together(d_pair, acted, attended_late, *normed_group)
    from_one, from_three = shift(attended_late, "y", 1), shift(attended_late, "y", 3)
    back_send = back_second(back_first(core, d_pair, pair), swap(d_pair), pair_far, extra)
    back_send, acted_peer, from_one, from_three = together(back_send, swap(acted), from_one, from_three)
    back = to_owners(back_send)

    acted_late, own_late, peer_late, _ = together(acted, rows_own, rows_peer, back_send)
    grad_gate_up, grad_down = expert_grads(
        core, own_late, peer_late, grad_late, grad_peer, acted_late, d_pair, own_late
    )
    returned = experts_out(core, acted_late, acted_peer, down, down_far)
    normed_group, _ = together(normed_group, back_send)
    normed_group = turn_parts(normed_group)
    returned, grad_gate_up, grad_down, normed_group = together(returned, grad_gate_up, grad_down, normed_group)
    returned = to_owners(returned)

    gathered = gather_back(back, combine, select, expert_of)
    core_y = jnp.stack([core[0], place[0].astype(jnp.int32)])
    d_logits, d_middle, d_attn, gain_two_local, *d_attn_blocks = middle_back(
        core_y, gathered, swap(gathered), probs, gates, picked_total, member, w_router, middle, cotangent, gain_two,
        from_one
    )

    z_index = place[2].astype(jnp.int32).reshape(1)
    d_attn, normed_group_peer = together(d_attn, swap(normed_group))
    *d_blocks, grad_qk = attend_back(z_index, d_attn, w_out, raw, turned, kept, value_in, gains, table)
    d_group = send_steps(d_blocks, "z")
    returned, *d_group = together(returned, *d_group)

    columns_here = expert_count // 2
    my_logits = lax.dynamic_slice_in_dim(d_logits, core_index * columns_here, columns_here, axis=1)
    partial_grads = group_grads(
        core,
        normed_group,
        normed_group_peer,
        d_group,
        normed_two,
        my_logits,
        gain_two_local,
        grad_qk,
    )
    d_attn_blocks, from_one, _ = together(d_attn_blocks, from_one, d_blocks)
    d_attn_group = [
        d_attn_blocks[0],
        shift(d_attn_blocks[1], "y", 1),
        shift(d_attn_blocks[2], "y", 2),
        shift(d_attn_blocks[3], "y", 3),
    ]
    attended_group = [attended_late, from_one, from_three]
    partial_grads, attended_group, d_attn_group = together(partial_grads, attended_group, d_attn_group)
    arrived = exchange(partial_grads, ("y", "x"))
    d_attn_group, attended_group, late_blocks, late_returned, _ = together(
        d_attn_group, attended_group, d_blocks, returned, partial_grads
    )

    grad_out = out_grads(d_attn_group, attended_group)

    grad_out = send_blocks(grad_out.reshape(SIDE, SIDE, rows_here_count, inner), "z", 1)

    d_one = input_grad(z_index, late_blocks, w_parts)
    d_one = d_one.astype(F32) + swap(d_one).astype(F32)

    residual_in = tokens.astype(F32)
    scale_one = rms(residual_in)
    unit_one = residual_in * scale_one
    weighted = d_one * gain_one
    grad_input = d_middle + scale_one * (
        weighted - unit_one * jnp.mean(weighted * unit_one, axis=-1, keepdims=True)
    )

    mix_own = dot(combine, late_returned, TN)
    result_own = (own_half(middle) + mix_own).astype(BF)
    output = side_by_side(result_own, swap(result_own), core_index)

    grad_out = sum(part.astype(F32) for part in grad_out).astype(BF)
    grad_out = [block_at(grad_out, (place[1] + step) % SIDE, 0) for step in range(SIDE)]
    grad_input, output, *grad_out = together(grad_input, output, *grad_out)
    grad_out = send_steps(grad_out, "x")
    arrived, grad_input, output, *grad_out = together(arrived, grad_input, output, *grad_out)
    grad_out = sum(part.astype(F32) for part in grad_out)
    parts = send_steps(sum_arrived(z_index, arrived, rows_here_count), "z")
    w_here = lax.dynamic_slice_in_dim(w_parts, dp_index * rows_here_count, rows_here_count, axis=1)
    grad_qkv, small = finish(z_index, parts, w_here)
    grad_qkv = grad_qkv.transpose(1, 0, 2)
    small_peer = swap(small)
    gain_here = lax.dynamic_slice_in_dim(gain_one, dp_index * rows_here_count, rows_here_count, axis=0)
    grad_gain_one = (small[SIDE * EXTRA] + small_peer[SIDE * EXTRA])[:rows_here_count] / gain_here
    cut = lambda value: lax.dynamic_slice_in_dim(value, place[2] * rows_here_count, rows_here_count, axis=-1)
    grad_router = jnp.where(
        core_index == 0,
        jnp.concatenate([small[: SIDE * EXTRA], small_peer[: SIDE * EXTRA]], axis=0),
        jnp.concatenate([small_peer[: SIDE * EXTRA], small[: SIDE * EXTRA]], axis=0),
    )
    grad_router = cut(grad_router).T
    grad_gain_two = cut(small[SIDE * EXTRA + 1])
    grad_qk = small[SIDE * EXTRA + 2 : SIDE * EXTRA + 4] + small_peer[SIDE * EXTRA + 2 : SIDE * EXTRA + 4]

    return (
        output,
        grad_input,
        grad_gain_one,
        grad_qkv,
        grad_qk,
        grad_out,
        grad_gain_two,
        grad_router,
        grad_gate_up[None],
        grad_down[None],
    )


def solution(mesh):
    names = AXES + ("tensor",)
    torus = Mesh(mesh.devices.reshape(SIDE, SIDE, SIDE, 2), names)
    return jax.shard_map(
        on_device,
        mesh=torus,
        in_specs=(
            P(AXES, None),
            P(AXES, None),
            P(),
            P(),
            P(None, None, "tensor"),
            P(),
            P(None, "tensor"),
            P(),
            P(),
            P(AXES, None, None, "tensor"),
            P(AXES, "tensor", None),
            P(AXES, None),
        ),
        out_specs=(
            P(AXES, None),
            P(AXES, None),
            P(AXES),
            P(AXES, None, "tensor"),
            P(),
            P(AXES, "tensor"),
            P(AXES),
            P(AXES, None),
            P(AXES, None, None, "tensor"),
            P(AXES, "tensor", None),
        ),
        check_vma=False,
    )
```

```python
import functools
import math

import jax
import jax.numpy as jnp
import numpy as np
from jax import lax
from jax.experimental import pallas as pl
from jax.experimental.pallas import tpu as pltpu
from jax.sharding import Mesh
from jax.sharding import PartitionSpec as P

AXES = ("y", "x", "z")
SIDE = 4
LANE = 128
BF = jnp.bfloat16
F32 = jnp.float32
MIB = 1 << 20


def dot(a, b, dims):
    return lax.dot_general(a, b, (dims, ((), ())), preferred_element_type=F32)


NN = ((1,), (0,))
NT = ((1,), (1,))
TN = ((0,), (0,))


def rms(values):
    return lax.rsqrt(jnp.mean(values * values, axis=-1, keepdims=True) + 1e-06)


def rotary(length, half_dim):
    position = np.arange(length, dtype=np.float32)
    inverse = np.float32(50000.0) ** (-np.arange(half_dim, dtype=np.float32) / np.float32(half_dim))
    angles = position[:, None] * inverse[None, :].astype(np.float32)
    cosine = np.cos(angles).astype(np.float32)
    sine = np.sin(angles).astype(np.float32)
    return np.stack([np.concatenate([cosine, cosine], 1), np.concatenate([-sine, sine], 1)])


def swap(value):
    return lax.ppermute(value, "tensor", [(0, 1), (1, 0)])


def shift(value, axis, step):
    return lax.ppermute(value, axis, [(i, (i + step) % SIDE) for i in range(SIDE)])


def side_by_side(own, peer, core):
    return jnp.where(
        core == 0,
        jnp.concatenate([own, peer], axis=-1),
        jnp.concatenate([peer, own], axis=-1),
    )


def block_at(value, index, dim):
    return lax.dynamic_index_in_dim(value, index, dim, keepdims=False)


def together(*values):
    return lax.optimization_barrier(values)


def share(value, axis):
    return [value] + [shift(value, axis, step) for step in (1, 2, 3)]


def send_blocks(value, axis, dim):
    here = lax.axis_index(axis)
    own = block_at(value, here, dim)
    return [own] + [shift(block_at(value, (here + step) % SIDE, dim), axis, step) for step in (1, 2, 3)]


def send_steps(blocks, axis):
    return [blocks[0]] + [shift(blocks[step], axis, step) for step in (1, 2, 3)]


def exchange(value, axes):
    return lax.all_to_all(value, axes, split_axis=0, concat_axis=0, tiled=True)


def shape(dims, kind):
    return jax.ShapeDtypeStruct(dims, kind)


def main_memory(dims, kind):
    return pltpu.HBM(dims, kind)


def held(*values):
    return [pltpu.with_memory_space_constraint(value, pltpu.HBM) for value in values]


def kernel_call(body, grid, ins, outs, out_shapes, scratch=(), mib=40, scalars=0, name=None):
    return pl.pallas_call(
        body,
        grid_spec=pltpu.PrefetchScalarGridSpec(
            num_scalar_prefetch=scalars, grid=grid, in_specs=ins, out_specs=outs, scratch_shapes=list(scratch)
        ),
        out_shape=out_shapes,
        compiler_params=pltpu.CompilerParams(vmem_limit_bytes=mib * MIB),
        name=name,
    )


def whole(*dims):
    return pl.BlockSpec(dims, lambda *_: (0,) * len(dims))


def rope(values, table):
    return values * table[0] + pltpu.roll(values, values.shape[-1] // 2, 1) * table[1]


def unrope(values, table):
    return values * table[0] - pltpu.roll(values, values.shape[-1] // 2, 1) * table[1]


def attention_weights(query, key):
    scores = dot(query, key, NT) * (1.0 / math.sqrt(query.shape[-1]))
    raised = jnp.exp(scores - jnp.max(scores, axis=-1, keepdims=True))
    return raised / jnp.sum(raised, axis=-1, keepdims=True)


def attend_body(tokens, gain, w_qkv, w_out, gains, table, normed, raw, turned, kept, value_out, attended, partial, total):
    step = pl.program_id(0)

    @pl.when(step == 0)
    def _():
        x = tokens[...].astype(F32)
        normed[...] = (x * rms(x) * gain[...]).astype(BF)
        total[...] = jnp.zeros_like(total)

    h = normed[...]
    query_raw = dot(h, w_qkv[0], NN)
    key_raw = dot(h, w_qkv[1], NN)
    value = dot(h, w_qkv[2], NN).astype(BF)
    raw[0] = query_raw
    raw[1] = key_raw
    value_out[...] = value
    for at in range(query_raw.shape[1] // LANE):
        cut = slice(at * LANE, (at + 1) * LANE)
        q, k = query_raw[:, cut], key_raw[:, cut]
        query = rope(q * rms(q) * gains[0:1], table).astype(BF)
        key = rope(k * rms(k) * gains[1:2], table).astype(BF)
        turned[0, :, cut] = query
        turned[1, :, cut] = key
        weights = attention_weights(query, key)
        kept[at] = weights
        attended[:, cut] = dot(weights.astype(BF), value[:, cut], NN).astype(BF)
    total[...] += dot(attended[...], w_out[...], NT)

    @pl.when(step == pl.num_programs(0) - 1)
    def _():
        partial[...] = total[...].astype(BF)


def attend(tokens, gain, w_qkv, w_out, gains, table):
    length, width = tokens.shape
    inner = w_qkv.shape[2]
    cols = inner // SIDE
    return kernel_call(
        attend_body,
        (SIDE,),
        [
            whole(length, width),
            whole(1, width),
            pl.BlockSpec((3, width, cols), lambda i: (0, 0, i)),
            pl.BlockSpec((width, cols), lambda i: (0, i)),
            whole(2, LANE),
            whole(2, length, LANE),
        ],
        [
            whole(length, width),
            pl.BlockSpec((2, length, cols), lambda i: (0, 0, i)),
            pl.BlockSpec((2, length, cols), lambda i: (0, 0, i)),
            pl.BlockSpec((cols // LANE, length, length), lambda i: (i, 0, 0)),
            pl.BlockSpec((length, cols), lambda i: (0, i)),
            pl.BlockSpec((length, cols), lambda i: (0, i)),
            whole(length, width),
        ],
        [
            main_memory((length, width), BF),
            main_memory((2, length, inner), F32),
            main_memory((2, length, inner), BF),
            main_memory((inner // LANE, length, length), F32),
            main_memory((length, inner), BF),
            main_memory((length, inner), BF),
            shape((length, width), BF),
        ],
        [pltpu.VMEM((length, width), F32)],
        name="attend",
    )(tokens, gain, w_qkv, w_out, gains, table)


def attend_back_body(z_index, d_attn, w_out, raw, turned, kept, value_in, gains, table, *outs):
    d_gains = outs[SIDE]
    step = pl.program_id(0)
    parts = ([], [], [])

    @pl.when(step == 0)
    def _():
        d_gains[...] = jnp.zeros_like(d_gains)

    d_attended = dot(d_attn[...], w_out[...], NN).astype(BF)
    for at in range(d_attended.shape[1] // LANE):
        cut = slice(at * LANE, (at + 1) * LANE)
        q, k = raw[0, :, cut], raw[1, :, cut]
        rq, rk = rms(q), rms(k)
        unit_q, unit_k = q * rq, k * rk
        query, key = turned[0, :, cut], turned[1, :, cut]
        weights = kept[at]
        grad = d_attended[:, cut]
        d_value = dot(weights.astype(BF), grad, TN)
        d_weights = dot(grad, value_in[:, cut], NT)
        d_scores = (
            weights * (d_weights - jnp.sum(weights * d_weights, axis=-1, keepdims=True))
        ).astype(BF)
        root = 1.0 / math.sqrt(LANE)
        d_query = unrope(dot(d_scores, key, NN) * root, table)
        d_key = unrope(dot(d_scores, query, TN) * root, table)
        d_gains[0:1] += jnp.sum(d_query * unit_q, axis=0, keepdims=True)
        d_gains[1:2] += jnp.sum(d_key * unit_k, axis=0, keepdims=True)
        wq = d_query * gains[0:1]
        wk = d_key * gains[1:2]
        parts[0].append((rq * (wq - unit_q * jnp.mean(wq * unit_q, axis=-1, keepdims=True))).astype(BF))
        parts[1].append((rk * (wk - unit_k * jnp.mean(wk * unit_k, axis=-1, keepdims=True))).astype(BF))
        parts[2].append(d_value.astype(BF))
    for k in range(SIDE):

        @pl.when((z_index[0] + k) % SIDE == step)
        def _():
            for kind in range(3):
                outs[k][kind] = jnp.concatenate(parts[kind], axis=1)


def attend_back(z_index, d_attn, w_out, raw, turned, kept, value_in, gains, table):
    length, width = d_attn.shape
    inner = w_out.shape[1]
    cols = inner // SIDE
    return kernel_call(
        attend_back_body,
        (SIDE,),
        [
            whole(length, width),
            pl.BlockSpec((width, cols), lambda i, z: (0, i)),
            pl.BlockSpec((2, length, cols), lambda i, z: (0, 0, i)),
            pl.BlockSpec((2, length, cols), lambda i, z: (0, 0, i)),
            pl.BlockSpec((cols // LANE, length, length), lambda i, z: (i, 0, 0)),
            pl.BlockSpec((length, cols), lambda i, z: (0, i)),
            whole(2, LANE),
            whole(2, length, LANE),
        ],
        [whole(3, length, cols)] * SIDE + [whole(2, LANE)],
        [shape((3, length, cols), BF)] * SIDE + [shape((2, LANE), F32)],
        scalars=1,
        name="attend_back",
    )(z_index, d_attn, *held(w_out, raw, turned, kept, value_in, gains, table))


def input_grad_body(z_index, *refs):
    w_qkv, out, total = refs[SIDE:]
    step = pl.program_id(0)

    @pl.when(step == 0)
    def _():
        total[...] = jnp.zeros_like(total)

    for k in range(SIDE):

        @pl.when(step == k)
        def _():
            block = refs[k]
            total[...] += dot(block[0], w_qkv[0], NT) + dot(block[1], w_qkv[1], NT) + dot(block[2], w_qkv[2], NT)

    @pl.when(step == pl.num_programs(0) - 1)
    def _():
        out[...] = total[...].astype(BF)


def input_grad(z_index, d_blocks, w_qkv):
    _, length, cols = d_blocks[0].shape
    width = w_qkv.shape[1]
    return kernel_call(
        input_grad_body,
        (SIDE,),
        [whole(3, length, cols)] * SIDE
        + [pl.BlockSpec((3, width, cols), lambda i, z: (0, 0, lax.rem(z[0] + i, SIDE)))],
        whole(length, width),
        shape((length, width), BF),
        [pltpu.VMEM((length, width), F32)],
        scalars=1,
        name="input_grad",
    )(z_index, *d_blocks, *held(w_qkv))


def routing_body(select_rows, core, capacity, ids, later, cotangent, member_out, select, rows, code):
    step = pl.program_id(0)
    experts, length = code.shape

    @pl.when(step == 0)
    def _():
        at_expert = lax.broadcasted_iota(jnp.int32, (experts, length), 0)
        member = jnp.zeros((experts, length), F32)
        for j in range(ids.shape[0]):
            member = member + (ids[j : j + 1, :] == at_expert).astype(F32)
        member_out[...] = member.T
        ranks = dot(member.astype(BF), later[...], NN)
        row = lax.broadcasted_iota(jnp.int32, (experts, experts), 0)
        column = lax.broadcasted_iota(jnp.int32, (experts, experts), 1)
        limit = jnp.sum(jnp.where(row == column, capacity[...].astype(F32), 0.0), axis=1, keepdims=True)
        code[...] = jnp.where((member > 0.5) & (ranks < limit), ranks, -1.0)

    chunk = rows.shape[0]
    per = chunk * experts // select_rows
    depth = chunk // per
    slot = lax.broadcasted_iota(jnp.int32, (depth, length), 0).astype(F32)
    mine = code[pl.ds(pl.multiple_of(step * per, per), per), :]
    hit = jnp.concatenate([(mine[k : k + 1] == slot).astype(F32) for k in range(per)], axis=0).astype(BF)
    select[...] = hit
    rows[...] = dot(hit, cotangent[...], NN).astype(BF)


def routing(core, capacity, ids, cotangent):
    length, width = cotangent.shape
    experts = capacity.shape[0]
    slots = length * ids.shape[0]
    chunk = 16 * (slots // experts)
    half = width // 2
    later = jnp.asarray(np.triu(np.ones((length, length), np.float32), 1), BF)
    return kernel_call(
        functools.partial(routing_body, slots),
        (slots // chunk,),
        [
            whole(1, experts),
            whole(*ids.shape),
            whole(length, length),
            pl.BlockSpec((length, half), lambda i, c: (0, c[0])),
        ],
        [
            whole(length, experts),
            pl.BlockSpec((chunk, length), lambda i, c: (i, 0)),
            pl.BlockSpec((chunk, half), lambda i, c: (i, 0)),
        ],
        [shape((length, experts), F32), main_memory((slots, length), BF), main_memory((slots, half), BF)],
        [pltpu.VMEM((experts, length), F32)],
        scalars=1,
        name="routing",
    )(core, *held(capacity.reshape(1, experts), ids, later, cotangent))


def middle_body(core, tokens, own, peer, gain, select, w_router, member, expert_of,
                middle, normed, probs_out, gates_out, total_out, combine, rows):
    x2 = tokens[...].astype(F32) + (own[...].astype(F32) + peer[...].astype(F32))
    middle[...] = x2
    normed[...] = (x2 * rms(x2) * gain[...]).astype(BF)
    logits = dot(normed[...], w_router[...], NN)
    raised = jnp.exp(logits - jnp.max(logits, axis=-1, keepdims=True))
    probs = raised / jnp.sum(raised, axis=-1, keepdims=True)
    picked = probs * member[...]
    total = jnp.sum(picked, axis=-1, keepdims=True)
    gates = picked / total
    probs_out[...] = probs
    gates_out[...] = gates
    total_out[...] = total
    low = gates.astype(BF)
    half = rows.shape[1] - LANE
    for at in range(0, rows.shape[0], 256):
        cut = slice(at, at + 256)
        spread = dot(expert_of[cut], low, NT) * select[cut].astype(F32)
        combine[cut] = spread.astype(BF)
        gate = jnp.sum(spread, axis=-1, keepdims=True)
        rows[cut, half:] = jnp.broadcast_to(gate, (256, LANE)).astype(BF)
    for which in range(2):

        @pl.when(core[0] == which)
        def _():
            for at in range(0, rows.shape[0], 256):
                rows[at : at + 256, :half] = dot(
                    select[at : at + 256], normed[:, which * half : (which + 1) * half], NN
                ).astype(BF)


def middle_step(core, tokens, own, peer, gain, select, w_router, member, expert_of):
    length, width = tokens.shape
    slots, experts = expert_of.shape
    columns = width // 2 + LANE
    return kernel_call(
        middle_body,
        (1,),
        [whole(length, width)] * 3
        + [whole(1, width), whole(slots, length), whole(width, experts), whole(length, experts), whole(slots, experts)],
        [
            whole(length, width),
            whole(length, width),
            whole(length, experts),
            whole(length, experts),
            whole(length, 1),
            whole(slots, length),
            whole(slots, columns),
        ],
        [
            main_memory((length, width), F32),
            main_memory((length, width), BF),
            shape((length, experts), F32),
            shape((length, experts), F32),
            shape((length, 1), F32),
            main_memory((slots, length), BF),
            main_memory((slots, columns), BF),
        ],
        scalars=1,
        name="middle",
    )(core, *held(tokens), own, peer, *held(gain, select, w_router, member, expert_of))


def gather_back_body(back, combine, select, expert_of, out):
    half = out.shape[1] - LANE
    experts = expert_of.shape[1]
    out[:, :half] = dot(combine[...], back[:, :half], TN)
    high = back[:, half : half + 1].astype(F32)
    low = back[:, half + 1 : half + 2].astype(F32)
    picked = select[...].astype(F32)
    spread = dot((picked * high).astype(BF), expert_of[...], TN) + dot((picked * low).astype(BF), expert_of[...], TN)
    out[:, half : half + experts] = spread
    out[:, half + experts :] = jnp.zeros((out.shape[0], LANE - experts), F32)


def gather_back(back, combine, select, expert_of):
    slots, columns = back.shape
    length = combine.shape[1]
    experts = expert_of.shape[1]
    return kernel_call(
        gather_back_body,
        (1,),
        [whole(slots, columns), whole(slots, length), whole(slots, length), whole(slots, experts)],
        whole(length, columns),
        shape((length, columns), F32),
        name="gather_back",
    )(back, *held(combine, select, expert_of))


def middle_back_body(core, own, peer, probs, gates, total, member, w_router, middle, cotangent, gain, far,
                     d_logits_out, d_middle, d_attn, d_gain, *d_attn_blocks):
    half = own.shape[1] - LANE
    experts = probs.shape[1]
    d_gates = own[:, half : half + experts] + peer[:, half : half + experts]
    g, p = gates[...], probs[...]
    d_picked = member[...] * (d_gates - jnp.sum(d_gates * g, axis=-1, keepdims=True)) / total[...]
    d_logits = (p * (d_picked - jnp.sum(p * d_picked, axis=-1, keepdims=True))).astype(BF)
    d_logits_out[...] = d_logits
    d_normed = dot(d_logits, w_router[...], NT)
    for which in range(2):

        @pl.when(core[0] == which)
        def _():
            first, second = (own, peer) if which == 0 else (peer, own)
            d_middle[:, :half] = first[:, :half]
            d_middle[:, half:] = second[:, :half]

    d_normed = d_normed + d_middle[...]
    x2 = middle[...]
    scale = rms(x2)
    unit = x2 * scale
    d_gain[...] = jnp.sum(d_normed * unit, axis=0, keepdims=True)
    weighted = d_normed * gain[...]
    value = cotangent[...].astype(F32) + scale * (
        weighted - unit * jnp.mean(weighted * unit, axis=-1, keepdims=True)
    )
    d_middle[...] = value
    low = value.astype(BF)
    d_attn[...] = low
    cut = d_attn_blocks[0].shape[1]
    for which in range(SIDE):

        @pl.when(core[1] == which)
        def _():
            for k in range(SIDE):
                at = (which + k) % SIDE * cut
                d_attn_blocks[k][:, :cut] = low[:, at : at + cut]

    d_attn_blocks[1][:, cut:] = far[...]


def middle_back(core, own, peer, probs, gates, total, member, w_router, middle, cotangent, gain, far):
    length, width = middle.shape
    experts = probs.shape[1]
    columns = own.shape[1]
    quarter = width // SIDE
    blocks = [quarter, quarter + far.shape[1], quarter, quarter]
    return kernel_call(
        middle_back_body,
        (1,),
        [whole(length, columns)] * 2
        + [whole(length, experts)] * 2
        + [
            whole(length, 1),
            whole(length, experts),
            whole(width, experts),
            whole(length, width),
            whole(length, width),
            whole(1, width),
            whole(*far.shape),
        ],
        [whole(length, experts), whole(length, width), whole(length, width), whole(1, width)]
        + [whole(length, block) for block in blocks],
        [
            shape((length, experts), BF),
            shape((length, width), F32),
            shape((length, width), BF),
            shape((1, width), F32),
        ]
        + [shape((length, block), BF) for block in blocks],
        scalars=1,
        name="middle_back",
    )(core, own, peer, *held(probs, gates, total, member, w_router, middle, cotangent, gain, far))


def hidden_grad_body(core, own, peer, down_own, down_peer, out):
    half = down_own.shape[1]
    out[...] = dot(own[:, :half], down_own[...], NT) + dot(peer[:, :half], down_peer[...], NT)


ROWS = 512


def hidden_grad(core, own, peer, down):
    slots, columns = own.shape
    hidden, width = down.shape
    half = width // 2
    return kernel_call(
        hidden_grad_body,
        (slots // ROWS,),
        [
            pl.BlockSpec((ROWS, columns), lambda i, c: (i, 0)),
            pl.BlockSpec((ROWS, columns), lambda i, c: (i, 0)),
            pl.BlockSpec((hidden, half), lambda i, c: (0, c[0])),
            pl.BlockSpec((hidden, half), lambda i, c: (0, 1 - c[0])),
        ],
        pl.BlockSpec((ROWS, hidden), lambda i, c: (i, 0)),
        main_memory((slots, hidden), F32),
        scalars=1,
        name="hidden_grad",
    )(core, *held(own, peer, down, down))


def gate_first_body(core, own, pair, out):
    half, hidden = pair.shape[1:]
    mine = own[:, :half]
    out[:, :hidden] = dot(mine, pair[0], NN)
    out[:, hidden:] = dot(mine, pair[1], NN)


def gate_first(core, own, pair):
    slots, columns = own.shape
    half = columns - LANE
    hidden = pair.shape[2]
    rows = lambda n: pl.BlockSpec((ROWS, n), lambda i, c: (i, 0))
    return kernel_call(
        gate_first_body,
        (slots // ROWS,),
        [rows(columns), pl.BlockSpec((2, half, hidden), lambda i, c: (0, c[0], 0))],
        rows(2 * hidden),
        shape((slots, 2 * hidden), F32),
        scalars=1,
        mib=28,
        name="gate_first",
    )(core, *held(own, pair))


def experts_body(core, partial, peer, d_hidden, pair, acted, d_pair, extra):
    hidden = d_hidden.shape[1]
    half = pair.shape[1]
    other = peer[:, :half]
    gate = partial[:, :hidden] + dot(other, pair[0], NN)
    up = partial[:, hidden:] + dot(other, pair[1], NN)
    sig = 1.0 / (1.0 + jnp.exp(-gate))
    silu = gate * sig
    act = (silu * up).astype(BF)
    acted[...] = act
    d_act = d_hidden[...]
    slot_grad = jnp.sum(d_act * act.astype(F32), axis=-1, keepdims=True)
    high = slot_grad.astype(BF)
    low = (slot_grad - high.astype(F32)).astype(BF)
    at = lax.broadcasted_iota(jnp.int32, extra.shape, 1)
    extra[...] = jnp.where(at == 0, high.astype(F32), jnp.where(at == 1, low.astype(F32), 0.0)).astype(BF)
    d_pair[:, :hidden] = (d_act * up * sig * (1.0 + gate * (1.0 - sig))).astype(BF)
    d_pair[:, hidden:] = (d_act * silu).astype(BF)


def back_first_body(core, d_pair, pair, out):
    hidden = pair.shape[2]
    out[...] = dot(d_pair[:, :hidden], pair[0], NT) + dot(d_pair[:, hidden:], pair[1], NT)


def back_first(core, d_pair, pair):
    slots, columns = d_pair.shape
    _, width, hidden = pair.shape
    half = width // 2
    rows = lambda n: pl.BlockSpec((ROWS, n), lambda i, c: (i, 0))
    return kernel_call(
        back_first_body,
        (slots // ROWS,),
        [rows(columns), pl.BlockSpec((2, half, hidden), lambda i, c: (0, c[0], 0))],
        rows(half),
        shape((slots, half), F32),
        scalars=1,
        mib=28,
        name="back_first",
    )(core, *held(d_pair, pair))


def back_second_body(partial, d_pair, pair, extra, out):
    _, half, hidden = pair.shape
    value = dot(d_pair[:, :hidden], pair[0], NT) + dot(d_pair[:, hidden:], pair[1], NT)
    out[:, :half] = (partial[...] + value).astype(BF)
    out[:, half:] = extra[...]


def back_second(partial, d_pair, pair, extra):
    slots, columns = d_pair.shape
    _, half, hidden = pair.shape
    rows = lambda n: pl.BlockSpec((ROWS, n), lambda i: (i, 0))
    return kernel_call(
        back_second_body,
        (slots // ROWS,),
        [rows(half), rows(columns), whole(2, half, hidden), rows(LANE)],
        rows(half + LANE),
        main_memory((slots, half + LANE), BF),
        mib=28,
        name="back_second",
    )(partial, d_pair, *held(pair, extra))


def experts_out_body(core, acted, acted_peer, down, down_far, out):
    out[...] = (dot(acted[...], down[...], NN) + dot(acted_peer[...], down_far[...], NN)).astype(BF)


def experts_out(core, acted, acted_peer, down, down_far):
    slots, hidden = acted.shape
    half = down_far.shape[1]
    rows = lambda n: pl.BlockSpec((ROWS, n), lambda i, c: (i, 0))
    return kernel_call(
        experts_out_body,
        (slots // ROWS,),
        [
            rows(hidden),
            rows(hidden),
            pl.BlockSpec((hidden, half), lambda i, c: (0, c[0])),
            whole(hidden, half),
        ],
        rows(half),
        main_memory((slots, half), BF),
        scalars=1,
        name="experts_out",
    )(core, *held(acted, acted_peer, down, down_far))


def experts_step(core, partial, peer, d_hidden, pair):
    slots, columns = peer.shape
    half = columns - LANE
    hidden = pair.shape[2]
    block = ROWS // 2
    rows = lambda n: pl.BlockSpec((block, n), lambda i, c: (i, 0))
    return kernel_call(
        experts_body,
        (slots // block,),
        [
            rows(2 * hidden),
            rows(columns),
            rows(hidden),
            pl.BlockSpec((2, half, hidden), lambda i, c: (0, 1 - c[0], 0)),
        ],
        [rows(hidden), rows(2 * hidden), rows(LANE)],
        [
            main_memory((slots, hidden), BF),
            main_memory((slots, 2 * hidden), BF),
            main_memory((slots, LANE), BF),
        ],
        scalars=1,
        mib=28,
        name="experts",
    )(core, partial, peer, *held(d_hidden, pair))


def expert_grads_body(core, own, peer, grad_own, grad_peer, acted, d_pair, gates, grad_pair, grad_down, pair_low, act_low):
    step = pl.program_id(0)
    hidden = acted.shape[1]

    @pl.when(step == 0)
    def _():
        gate = gates[:, :1].astype(F32)
        pair_low[...] = (d_pair[...].astype(F32) * gate).astype(BF)
        act_low[...] = (acted[...].astype(F32) * gate).astype(BF)

    def part(rows, grads):
        value = dot(rows[...], pair_low[...], TN)
        grad_pair[:, 0, :] = value[:, :hidden]
        grad_pair[:, 1, :] = value[:, hidden:]
        grad_down[...] = dot(act_low[...], grads[...], TN)

    @pl.when(step < SIDE)
    def _():
        part(own, grad_own)

    @pl.when(step >= SIDE)
    def _():
        part(peer, grad_peer)


def expert_grads(core, own, peer, grad_own, grad_peer, acted, d_pair, gates):
    slots, half = grad_own.shape
    hidden = acted.shape[1]
    cut = half // SIDE
    first = pl.BlockSpec((slots, cut), lambda i, c: (0, jnp.minimum(i, SIDE - 1)))
    second = pl.BlockSpec((slots, cut), lambda i, c: (0, jnp.maximum(i - SIDE, 0)))

    def target(i, c):
        return jnp.where(i < SIDE, c[0] * SIDE + i, (1 - c[0]) * SIDE + i - SIDE)

    return kernel_call(
        expert_grads_body,
        (2 * SIDE,),
        [first, second, first, second, whole(slots, hidden), whole(slots, 2 * hidden), pl.BlockSpec((slots, LANE), lambda i, c: (0, half // LANE))],
        [
            pl.BlockSpec((cut, 2, hidden), lambda i, c: (target(i, c), 0, 0)),
            pl.BlockSpec((hidden, cut), lambda i, c: (0, target(i, c))),
        ],
        [shape((2 * half, 2, hidden), F32), shape((hidden, 2 * half), F32)],
        [pltpu.VMEM((slots, 2 * hidden), BF), pltpu.VMEM((slots, hidden), BF)],
        mib=48,
        scalars=1,
        name="expert_grads",
    )(core, *held(own), peer, *held(grad_own, grad_peer, acted, d_pair, gates))


EXTRA = 8


def group_grads_body(index, own, peer, *refs):
    step = pl.program_id(0)
    d_group = refs[:SIDE]
    normed_two, d_logits, d_gain, d_qk = refs[SIDE : SIDE + 4]
    first, second = refs[SIDE + 4 : 2 * SIDE + 4], refs[2 * SIDE + 4 : 3 * SIDE + 4]
    right, value = refs[3 * SIDE + 4 :]
    _, length, cols = d_group[0].shape
    rows = first[0].shape[1] - EXTRA
    middle = first[0].shape[2]

    @pl.when(step == 0)
    def _():
        for k in range(SIDE):
            for which in range(3):
                right[k * length : (k + 1) * length, which * cols : (which + 1) * cols] = d_group[k][which]

    @pl.when(step < SIDE // 2)
    def _():
        value[...] = dot(own[...], right[...], NN).astype(BF)

    @pl.when(step >= SIDE // 2)
    def _():
        value[...] = dot(peer[...], right[...], NN).astype(BF)

    router = dot(d_logits[...], normed_two[...], TN)
    extras = []
    for k in range(SIDE):
        cut = slice(k * rows, (k + 1) * rows)
        groups = [router[at * EXTRA : (at + 1) * EXTRA, cut] for at in range(SIDE)]
        groups.append(jnp.broadcast_to(d_gain[:, cut], (EXTRA, LANE)))
        groups.append(jnp.concatenate([d_qk[...]] * (EXTRA // 2), axis=0))
        extras.append(jnp.concatenate(groups, axis=1).astype(BF))

    half = SIDE // 2
    target = jnp.where(step < half, index[0] * half + step, (1 - index[0]) * half + step - half)
    for away in range(SIDE):

        @pl.when(lax.rem(index[1] + away, SIDE) == target)
        def _():
            for k in range(SIDE):
                first[away][k, :rows] = value[k * rows : (k + 1) * rows, :middle]
                first[away][k, rows:] = extras[k][:, :middle]

    for which in range(SIDE):

        @pl.when(index[2] == which)
        def _():
            for away in range(SIDE):
                k = (which + away) % SIDE
                second[away][target, :rows] = value[k * rows : (k + 1) * rows, middle:]
                second[away][target, rows:] = extras[k][:, middle:]


def turn_parts_body(*refs):
    value = jnp.concatenate([part[...].astype(F32) for part in refs[:SIDE]], axis=0)
    refs[SIDE][...] = value.T.astype(BF)


def turn_parts(parts):
    length, width = parts[0].shape
    cut = 256
    return kernel_call(
        turn_parts_body,
        (width // cut,),
        [pl.BlockSpec((length, cut), lambda i: (0, i))] * SIDE,
        pl.BlockSpec((cut, SIDE * length), lambda i: (i, 0)),
        main_memory((width, SIDE * length), BF),
        name="turn_parts",
    )(*held(*parts))


def group_grads(index, own, peer, d_group, normed_two, d_logits, d_gain, d_qk):
    half, depth = own.shape
    length = depth // SIDE
    cols = d_group[0].shape[2]
    steps = SIDE // 2
    cut = half // steps
    rows = 2 * half // (SIDE * SIDE)
    middle = 3 * cols // 2

    def target(i, c):
        return jnp.where(i < steps, c[0] * steps + i, (1 - c[0]) * steps + i - steps)

    return kernel_call(
        group_grads_body,
        (2 * steps,),
        [
            pl.BlockSpec((cut, depth), lambda i, c: (jnp.minimum(i, steps - 1), 0)),
            pl.BlockSpec((cut, depth), lambda i, c: (jnp.maximum(i - steps, 0), 0)),
        ]
        + [whole(3, length, cols)] * SIDE
        + [
            pl.BlockSpec((length, cut), lambda i, c: (0, target(i, c))),
            whole(length, d_logits.shape[1]),
            pl.BlockSpec((1, cut), lambda i, c: (0, target(i, c))),
            whole(2, LANE),
        ],
        [whole(SIDE, rows + EXTRA, middle)] * (2 * SIDE),
        [shape((SIDE, rows + EXTRA, middle), BF)] * (2 * SIDE),
        [pltpu.VMEM((depth, 3 * cols), BF), pltpu.VMEM((cut, 3 * cols), BF)],
        scalars=1,
        name="group_grads",
    )(index, *held(own, peer), *d_group, *held(normed_two), d_logits, d_gain, d_qk)


def ordered_sum(parts, which, read):
    values = [read(parts[(which - source) % SIDE]).astype(F32) for source in range(SIDE)]
    return ((values[0] + values[1]) + (values[2] + values[3])).astype(BF)


def stage_sums_body(index, *refs):
    sources = refs[:SIDE], refs[SIDE : 2 * SIDE]
    outs = refs[2 * SIDE : 3 * SIDE], refs[3 * SIDE : 4 * SIDE]
    total = refs[4 * SIDE]
    for part in range(2):
        here, there = index[1 + part], index[2 - part]
        for which in range(SIDE):

            @pl.when(here == which)
            def _():
                for k in range(SIDE):
                    total[k] = ordered_sum(sources[part], which, lambda ref: ref[k])

        for which in range(SIDE):

            @pl.when(there == which)
            def _():
                for away in range(SIDE):
                    outs[part][away][...] = total[(which + away) % SIDE]


def stage_sums(index, first, second):
    _, rows, columns = first[0].shape
    return kernel_call(
        stage_sums_body,
        (1,),
        [whole(SIDE, rows, columns)] * (2 * SIDE),
        [whole(rows, columns)] * (2 * SIDE),
        [shape((rows, columns), BF)] * (2 * SIDE),
        [pltpu.VMEM((SIDE, rows, columns), BF)],
        scalars=1,
        name="stage_sums",
    )(index, *first, *second)


def out_grads_body(*refs):
    out = refs[-1]
    rows = out.shape[0]
    left = jnp.concatenate([part[:, :rows] for part in refs[:SIDE]], axis=0)
    right = jnp.concatenate([refs[SIDE][...], refs[SIDE + 1][...], refs[1][:, rows:], refs[SIDE + 2][...]], axis=0)
    out[...] = dot(left, right, TN).astype(BF)


def out_grads(d_attn, attended):
    length, rows = d_attn[0].shape
    inner = attended[0].shape[1]
    return kernel_call(
        out_grads_body,
        (1,),
        [whole(*part.shape) for part in d_attn] + [whole(length, inner)] * len(attended),
        whole(rows, inner),
        shape((rows, inner), BF),
        name="out_grads",
    )(*d_attn, *held(*attended))


def sum_arrived_body(rows, index, *refs):
    sources = refs[:SIDE], refs[SIDE : 2 * SIDE]
    outs, value = refs[2 * SIDE : 3 * SIDE], refs[3 * SIDE]
    main = SIDE * rows
    middle = sources[0][0].shape[1]
    for part in range(2):
        for which in range(SIDE):

            @pl.when(index[2 - part] == which)
            def _():
                value[:, part * middle : (part + 1) * middle] = ordered_sum(sources[part], which, lambda ref: ref[...])

    for which in range(SIDE):

        @pl.when(index[3] == which)
        def _():
            for step in range(SIDE):
                at = (which + step) % SIDE * rows
                outs[step][:rows] = value[at : at + rows]

    for step in range(SIDE):
        outs[step][rows:] = value[main:]


def sum_arrived(index, first, second, rows):
    height, middle = first[0].shape
    return kernel_call(
        functools.partial(sum_arrived_body, rows),
        (1,),
        [whole(height, middle)] * (2 * SIDE),
        [whole(rows + EXTRA, 2 * middle)] * SIDE,
        [shape((rows + EXTRA, 2 * middle), BF)] * SIDE,
        [pltpu.VMEM((height, 2 * middle), BF)],
        scalars=1,
        name="sum_arrived",
    )(index, *first, *second)


def finish_body(z_index, *refs):
    parts, w_here, grad, small = refs[:SIDE], refs[SIDE], refs[SIDE + 1], refs[SIDE + 2]
    rows = grad.shape[1]
    cols = parts[0].shape[1] // 3
    for which in range(SIDE):

        @pl.when(z_index[0] == which)
        def _():
            ordered = [parts[(which - source) % SIDE] for source in range(SIDE)]
            for source in range(SIDE):
                for kind in range(3):
                    grad[kind, :, source * cols : (source + 1) * cols] = ordered[source][
                        :rows, kind * cols : (kind + 1) * cols
                    ].astype(F32)
            extra = [part[rows:].astype(F32) for part in ordered]
            total = (extra[0] + extra[1]) + (extra[2] + extra[3])
            for at in range(SIDE):
                small[at * EXTRA : (at + 1) * EXTRA] = total[:, at * LANE : (at + 1) * LANE]
            small[SIDE * EXTRA + 1 : SIDE * EXTRA + 2] = total[0:1, SIDE * LANE : (SIDE + 1) * LANE]
            small[SIDE * EXTRA + 2 : SIDE * EXTRA + 4] = total[0:2, (SIDE + 1) * LANE :]

    product = jnp.sum(grad[0] * w_here[0].astype(F32) + grad[1] * w_here[1].astype(F32) + grad[2] * w_here[2].astype(F32), axis=-1, keepdims=True)
    at_row = lax.broadcasted_iota(jnp.int32, (rows, LANE), 0)
    at_lane = lax.broadcasted_iota(jnp.int32, (rows, LANE), 1)
    small[SIDE * EXTRA : SIDE * EXTRA + 1] = jnp.sum(jnp.where(at_row == at_lane, product, 0.0), axis=0, keepdims=True)
    small[SIDE * EXTRA + 4 :] = jnp.zeros((small.shape[0] - SIDE * EXTRA - 4, LANE), F32)


def finish(z_index, parts, w_here):
    kinds, rows, inner = w_here.shape
    height, columns = parts[0].shape
    return kernel_call(
        finish_body,
        (1,),
        [whole(height, columns)] * SIDE + [whole(kinds, rows, inner)],
        [whole(kinds, rows, inner), whole(SIDE * EXTRA + 8, LANE)],
        [shape((kinds, rows, inner), F32), shape((SIDE * EXTRA + 8, LANE), F32)],
        scalars=1,
        name="finish",
    )(z_index, *parts, w_here)


def on_device(
    tokens,
    expert_ids,
    capacity,
    gain_attn,
    w_qkv,
    qk_gain,
    w_out,
    gain_ffn,
    w_router,
    w_gate_up,
    w_down,
    cotangent,
):
    length, width = tokens.shape
    expert_count = capacity.shape[0]
    slot_count = length * expert_ids.shape[1] // expert_count
    slots = expert_count * slot_count
    inner = w_qkv.shape[2]
    half = width // 2
    cols = inner // SIDE
    core_index = lax.axis_index("tensor")
    core = core_index.astype(jnp.int32).reshape(1)
    place = [lax.axis_index(a) for a in AXES]
    dp_index = (place[0] * SIDE + place[1]) * SIDE + place[2]
    rows_here_count = width // SIDE**3

    def own_half(value):
        return lax.dynamic_slice_in_dim(value, core_index * half, half, axis=-1)

    expert_of = jnp.asarray(np.repeat(np.eye(expert_count, dtype=np.float32), slot_count, 0), BF)

    def to_owners(rows):
        columns = rows.shape[1]
        return exchange(rows.reshape(expert_count, slot_count, columns), AXES).reshape(slots, columns)

    member, select, grad_send = routing(core, capacity, expert_ids.T, cotangent)
    grad_own = to_owners(grad_send)

    table = jnp.asarray(rotary(length, LANE // 2))
    gains = qk_gain.astype(F32)
    gain_one = gain_attn.astype(F32)
    gain_two = gain_ffn.astype(F32).reshape(1, width)
    w_parts = w_qkv.transpose(1, 0, 2)
    normed_one, raw, turned, kept, value_in, attended, partial = attend(
        tokens, gain_one.reshape(1, width), w_parts, w_out, gains, table
    )
    partial_peer = swap(partial)
    middle, normed_two, probs, gates, picked_total, combine, rows_send = middle_step(
        core, tokens, partial, partial_peer, gain_two, select, w_router, member, expert_of
    )
    rows_own = to_owners(rows_send)

    normed_early, attended_late, pair, grad_late, down, _ = together(
        own_half(normed_one), attended, w_gate_up, grad_own, w_down, rows_send
    )
    down = down[0]
    pair = pair[0].transpose(1, 0, 2)
    grad_peer = swap(grad_late)
    d_hidden = hidden_grad(core, grad_late, grad_peer, down)
    down_far = swap(lax.dynamic_slice_in_dim(down, (1 - core_index) * half, half, axis=1))
    pair_far = swap(lax.dynamic_slice_in_dim(pair, (1 - core_index) * half, half, axis=1))
    rows_own, d_hidden, pair, normed_early, down_far, pair_far = together(
        rows_own, d_hidden, pair, normed_early, down_far, pair_far
    )
    normed_group = share(normed_early, "z")
    rows_peer = swap(rows_own)
    acted, d_pair, extra = experts_step(core, gate_first(core, rows_own, pair), rows_peer, d_hidden, pair)
    d_pair, acted, attended_late, *normed_group = together(d_pair, acted, attended_late, *normed_group)
    from_one, from_three = shift(attended_late, "y", 1), shift(attended_late, "y", 3)
    back_send = back_second(back_first(core, d_pair, pair), swap(d_pair), pair_far, extra)
    back_send, acted_peer, from_one, from_three = together(back_send, swap(acted), from_one, from_three)
    back = to_owners(back_send)

    acted_late, own_late, peer_late, _ = together(acted, rows_own, rows_peer, back_send)
    grad_gate_up, grad_down = expert_grads(
        core, own_late, peer_late, grad_late, grad_peer, acted_late, d_pair, own_late
    )
    returned = experts_out(core, acted_late, acted_peer, down, down_far)
    normed_group, _ = together(normed_group, back_send)
    normed_group = turn_parts(normed_group)
    returned, grad_gate_up, grad_down, normed_group = together(returned, grad_gate_up, grad_down, normed_group)
    returned = to_owners(returned)

    gathered = gather_back(back, combine, select, expert_of)
    core_y = jnp.stack([core[0], place[0].astype(jnp.int32)])
    d_logits, d_middle, d_attn, gain_two_local, *d_attn_blocks = middle_back(
        core_y, gathered, swap(gathered), probs, gates, picked_total, member, w_router, middle, cotangent, gain_two,
        from_one
    )

    z_index = place[2].astype(jnp.int32).reshape(1)
    d_attn, normed_group_peer = together(d_attn, swap(normed_group))
    *d_blocks, grad_qk = attend_back(z_index, d_attn, w_out, raw, turned, kept, value_in, gains, table)
    d_group = send_steps(d_blocks, "z")
    d_one = input_grad(z_index, d_blocks, w_parts)
    returned, d_one, d_one_peer, *d_group = together(returned, d_one, swap(d_one), *d_group)

    columns_here = expert_count // 2
    my_logits = lax.dynamic_slice_in_dim(d_logits, core_index * columns_here, columns_here, axis=1)
    index = jnp.stack([core[0]] + [p.astype(jnp.int32) for p in place])
    partial_grads = group_grads(
        index, normed_group, normed_group_peer, d_group, normed_two, my_logits, gain_two_local, grad_qk
    )
    d_attn_blocks, from_one, _ = together(d_attn_blocks, from_one, d_blocks)
    d_attn_group = [
        d_attn_blocks[0],
        shift(d_attn_blocks[1], "y", 1),
        shift(d_attn_blocks[2], "y", 2),
        shift(d_attn_blocks[3], "y", 3),
    ]
    attended_group = [attended_late, from_one, from_three]
    partial_grads, attended_group, d_attn_group = together(partial_grads, attended_group, d_attn_group)
    first = send_steps(partial_grads[:SIDE], "y")
    second = send_steps(partial_grads[SIDE:], "x")
    d_attn_group, attended_group, late_returned, d_one, d_one_peer, _ = together(
        d_attn_group, attended_group, returned, d_one, d_one_peer, partial_grads
    )

    grad_out = out_grads(d_attn_group, attended_group)
    grad_out, first[1] = together(grad_out, first[1])
    halves = stage_sums(index, first, second)
    first = send_steps(halves[:SIDE], "x")
    second = send_steps(halves[SIDE:], "y")
    grad_out = send_blocks(grad_out.reshape(SIDE, SIDE, rows_here_count, inner), "z", 1)

    d_one = d_one.astype(F32) + d_one_peer.astype(F32)

    residual_in = tokens.astype(F32)
    scale_one = rms(residual_in)
    unit_one = residual_in * scale_one
    weighted = d_one * gain_one
    grad_input = d_middle + scale_one * (
        weighted - unit_one * jnp.mean(weighted * unit_one, axis=-1, keepdims=True)
    )

    mix_own = dot(combine, late_returned, TN)
    result_own, _ = together((own_half(middle) + mix_own).astype(BF), halves)
    output = side_by_side(result_own, swap(result_own), core_index)

    grad_out = sum(part.astype(F32) for part in grad_out).astype(BF)
    grad_out = [block_at(grad_out, (place[1] + step) % SIDE, 0) for step in range(SIDE)]
    w_here = lax.dynamic_slice_in_dim(w_parts, dp_index * rows_here_count, rows_here_count, axis=1)
    first, second, grad_input, output, w_here, grad_out = together(
        first, second, grad_input, output, w_here, grad_out
    )
    grad_out = sum(part.astype(F32) for part in send_steps(grad_out, "x"))
    parts = send_steps(sum_arrived(index, first, second, rows_here_count), "z")
    grad_qkv, small = finish(z_index, parts, w_here)
    grad_qkv = grad_qkv.transpose(1, 0, 2)
    small_peer = swap(small)
    gain_here = lax.dynamic_slice_in_dim(gain_one, dp_index * rows_here_count, rows_here_count, axis=0)
    grad_gain_one = (small[SIDE * EXTRA] + small_peer[SIDE * EXTRA])[:rows_here_count] / gain_here
    cut = lambda value: lax.dynamic_slice_in_dim(value, place[2] * rows_here_count, rows_here_count, axis=-1)
    grad_router = jnp.where(
        core_index == 0,
        jnp.concatenate([small[: SIDE * EXTRA], small_peer[: SIDE * EXTRA]], axis=0),
        jnp.concatenate([small_peer[: SIDE * EXTRA], small[: SIDE * EXTRA]], axis=0),
    )
    grad_router = cut(grad_router).T
    grad_gain_two = cut(small[SIDE * EXTRA + 1])
    grad_qk = small[SIDE * EXTRA + 2 : SIDE * EXTRA + 4] + small_peer[SIDE * EXTRA + 2 : SIDE * EXTRA + 4]

    return (
        output,
        grad_input,
        grad_gain_one,
        grad_qkv,
        grad_qk,
        grad_out,
        grad_gain_two,
        grad_router,
        grad_gate_up[None],
        grad_down[None],
    )


def solution(mesh):
    names = AXES + ("tensor",)
    torus = Mesh(mesh.devices.reshape(SIDE, SIDE, SIDE, 2), names)
    return jax.shard_map(
        on_device,
        mesh=torus,
        in_specs=(
            P(AXES, None),
            P(AXES, None),
            P(),
            P(),
            P(None, None, "tensor"),
            P(),
            P(None, "tensor"),
            P(),
            P(),
            P(AXES, None, None, "tensor"),
            P(AXES, "tensor", None),
            P(AXES, None),
        ),
        out_specs=(
            P(AXES, None),
            P(AXES, None),
            P(AXES),
            P(AXES, None, "tensor"),
            P(),
            P(AXES, "tensor"),
            P(AXES),
            P(AXES, None),
            P(AXES, None, None, "tensor"),
            P(AXES, "tensor", None),
        ),
        check_vma=False,
    )
```

```python
import functools
import math

import jax
import jax.numpy as jnp
import numpy as np
from jax import lax
from jax.experimental import pallas as pl
from jax.experimental.pallas import tpu as pltpu
from jax.sharding import Mesh
from jax.sharding import PartitionSpec as P

AXES = ("y", "x", "z")
SIDE = 4
LANE = 128
BF = jnp.bfloat16
F32 = jnp.float32
MIB = 1 << 20


def dot(a, b, dims):
    return lax.dot_general(a, b, (dims, ((), ())), preferred_element_type=F32)


NN = ((1,), (0,))
NT = ((1,), (1,))
TN = ((0,), (0,))


def rms(values):
    return lax.rsqrt(jnp.mean(values * values, axis=-1, keepdims=True) + 1e-06)


def rotary(length, half_dim):
    position = np.arange(length, dtype=np.float32)
    inverse = np.float32(50000.0) ** (-np.arange(half_dim, dtype=np.float32) / np.float32(half_dim))
    angles = position[:, None] * inverse[None, :].astype(np.float32)
    cosine = np.cos(angles).astype(np.float32)
    sine = np.sin(angles).astype(np.float32)
    return np.stack([np.concatenate([cosine, cosine], 1), np.concatenate([-sine, sine], 1)])


def swap(value):
    return lax.ppermute(value, "tensor", [(0, 1), (1, 0)])


def shift(value, axis, step):
    return lax.ppermute(value, axis, [(i, (i + step) % SIDE) for i in range(SIDE)])


def side_by_side(own, peer, core):
    return jnp.where(
        core == 0,
        jnp.concatenate([own, peer], axis=-1),
        jnp.concatenate([peer, own], axis=-1),
    )


def block_at(value, index, dim):
    return lax.dynamic_index_in_dim(value, index, dim, keepdims=False)


def together(*values):
    return lax.optimization_barrier(values)


def share(value, axis):
    return [value] + [shift(value, axis, step) for step in (1, 2, 3)]


def send_blocks(value, axis, dim):
    here = lax.axis_index(axis)
    own = block_at(value, here, dim)
    return [own] + [shift(block_at(value, (here + step) % SIDE, dim), axis, step) for step in (1, 2, 3)]


def send_steps(blocks, axis):
    return [blocks[0]] + [shift(blocks[step], axis, step) for step in (1, 2, 3)]


def exchange(value, axes):
    return lax.all_to_all(value, axes, split_axis=0, concat_axis=0, tiled=True)


def shape(dims, kind):
    return jax.ShapeDtypeStruct(dims, kind)


def main_memory(dims, kind):
    return pltpu.HBM(dims, kind)


def held(*values):
    return [pltpu.with_memory_space_constraint(value, pltpu.HBM) for value in values]


def kernel_call(body, grid, ins, outs, out_shapes, scratch=(), mib=40, scalars=0, name=None):
    return pl.pallas_call(
        body,
        grid_spec=pltpu.PrefetchScalarGridSpec(
            num_scalar_prefetch=scalars, grid=grid, in_specs=ins, out_specs=outs, scratch_shapes=list(scratch)
        ),
        out_shape=out_shapes,
        compiler_params=pltpu.CompilerParams(vmem_limit_bytes=mib * MIB),
        name=name,
    )


def whole(*dims):
    return pl.BlockSpec(dims, lambda *_: (0,) * len(dims))


def rope(values, table):
    return values * table[0] + pltpu.roll(values, values.shape[-1] // 2, 1) * table[1]


def unrope(values, table):
    return values * table[0] - pltpu.roll(values, values.shape[-1] // 2, 1) * table[1]


def attention_weights(query, key):
    scores = dot(query, key, NT) * (1.0 / math.sqrt(query.shape[-1]))
    raised = jnp.exp(scores - jnp.max(scores, axis=-1, keepdims=True))
    return raised / jnp.sum(raised, axis=-1, keepdims=True)


def attend_body(tokens, gain, w_qkv, w_out, gains, table, normed, raw, turned, kept, value_out, attended, partial, total):
    step = pl.program_id(0)

    @pl.when(step == 0)
    def _():
        x = tokens[...].astype(F32)
        normed[...] = (x * rms(x) * gain[...]).astype(BF)
        total[...] = jnp.zeros_like(total)

    h = normed[...]
    query_raw = dot(h, w_qkv[0], NN)
    key_raw = dot(h, w_qkv[1], NN)
    value = dot(h, w_qkv[2], NN).astype(BF)
    raw[0] = query_raw
    raw[1] = key_raw
    value_out[...] = value
    for at in range(query_raw.shape[1] // LANE):
        cut = slice(at * LANE, (at + 1) * LANE)
        q, k = query_raw[:, cut], key_raw[:, cut]
        query = rope(q * rms(q) * gains[0:1], table).astype(BF)
        key = rope(k * rms(k) * gains[1:2], table).astype(BF)
        turned[0, :, cut] = query
        turned[1, :, cut] = key
        weights = attention_weights(query, key)
        kept[at] = weights
        attended[:, cut] = dot(weights.astype(BF), value[:, cut], NN).astype(BF)
    total[...] += dot(attended[...], w_out[...], NT)

    @pl.when(step == pl.num_programs(0) - 1)
    def _():
        partial[...] = total[...].astype(BF)


def attend(tokens, gain, w_qkv, w_out, gains, table):
    length, width = tokens.shape
    inner = w_qkv.shape[2]
    cols = inner // SIDE
    return kernel_call(
        attend_body,
        (SIDE,),
        [
            whole(length, width),
            whole(1, width),
            pl.BlockSpec((3, width, cols), lambda i: (0, 0, i)),
            pl.BlockSpec((width, cols), lambda i: (0, i)),
            whole(2, LANE),
            whole(2, length, LANE),
        ],
        [
            whole(length, width),
            pl.BlockSpec((2, length, cols), lambda i: (0, 0, i)),
            pl.BlockSpec((2, length, cols), lambda i: (0, 0, i)),
            pl.BlockSpec((cols // LANE, length, length), lambda i: (i, 0, 0)),
            pl.BlockSpec((length, cols), lambda i: (0, i)),
            pl.BlockSpec((length, cols), lambda i: (0, i)),
            whole(length, width),
        ],
        [
            main_memory((length, width), BF),
            main_memory((2, length, inner), F32),
            main_memory((2, length, inner), BF),
            main_memory((inner // LANE, length, length), F32),
            main_memory((length, inner), BF),
            main_memory((length, inner), BF),
            shape((length, width), BF),
        ],
        [pltpu.VMEM((length, width), F32)],
        name="attend",
    )(tokens, gain, w_qkv, w_out, gains, table)


def attend_back_body(z_index, d_attn, w_out, raw, turned, kept, value_in, gains, table, *outs):
    d_gains = outs[SIDE]
    step = pl.program_id(0)
    parts = ([], [], [])

    @pl.when(step == 0)
    def _():
        d_gains[...] = jnp.zeros_like(d_gains)

    d_attended = dot(d_attn[...], w_out[...], NN).astype(BF)
    for at in range(d_attended.shape[1] // LANE):
        cut = slice(at * LANE, (at + 1) * LANE)
        q, k = raw[0, :, cut], raw[1, :, cut]
        rq, rk = rms(q), rms(k)
        unit_q, unit_k = q * rq, k * rk
        query, key = turned[0, :, cut], turned[1, :, cut]
        weights = kept[at]
        grad = d_attended[:, cut]
        d_value = dot(weights.astype(BF), grad, TN)
        d_weights = dot(grad, value_in[:, cut], NT)
        d_scores = (
            weights * (d_weights - jnp.sum(weights * d_weights, axis=-1, keepdims=True))
        ).astype(BF)
        root = 1.0 / math.sqrt(LANE)
        d_query = unrope(dot(d_scores, key, NN) * root, table)
        d_key = unrope(dot(d_scores, query, TN) * root, table)
        d_gains[0:1] += jnp.sum(d_query * unit_q, axis=0, keepdims=True)
        d_gains[1:2] += jnp.sum(d_key * unit_k, axis=0, keepdims=True)
        wq = d_query * gains[0:1]
        wk = d_key * gains[1:2]
        parts[0].append((rq * (wq - unit_q * jnp.mean(wq * unit_q, axis=-1, keepdims=True))).astype(BF))
        parts[1].append((rk * (wk - unit_k * jnp.mean(wk * unit_k, axis=-1, keepdims=True))).astype(BF))
        parts[2].append(d_value.astype(BF))
    for k in range(SIDE):

        @pl.when((z_index[0] + k) % SIDE == step)
        def _():
            for kind in range(3):
                outs[k][kind] = jnp.concatenate(parts[kind], axis=1)


def attend_back(z_index, d_attn, w_out, raw, turned, kept, value_in, gains, table):
    length, width = d_attn.shape
    inner = w_out.shape[1]
    cols = inner // SIDE
    return kernel_call(
        attend_back_body,
        (SIDE,),
        [
            whole(length, width),
            pl.BlockSpec((width, cols), lambda i, z: (0, i)),
            pl.BlockSpec((2, length, cols), lambda i, z: (0, 0, i)),
            pl.BlockSpec((2, length, cols), lambda i, z: (0, 0, i)),
            pl.BlockSpec((cols // LANE, length, length), lambda i, z: (i, 0, 0)),
            pl.BlockSpec((length, cols), lambda i, z: (0, i)),
            whole(2, LANE),
            whole(2, length, LANE),
        ],
        [whole(3, length, cols)] * SIDE + [whole(2, LANE)],
        [shape((3, length, cols), BF)] * SIDE + [shape((2, LANE), F32)],
        scalars=1,
        name="attend_back",
    )(z_index, d_attn, *held(w_out, raw, turned, kept, value_in, gains, table))


def input_grad_body(z_index, *refs):
    w_qkv, out, total = refs[SIDE:]
    step = pl.program_id(0)

    @pl.when(step == 0)
    def _():
        total[...] = jnp.zeros_like(total)

    for k in range(SIDE):

        @pl.when(step == k)
        def _():
            block = refs[k]
            total[...] += dot(block[0], w_qkv[0], NT) + dot(block[1], w_qkv[1], NT) + dot(block[2], w_qkv[2], NT)

    @pl.when(step == pl.num_programs(0) - 1)
    def _():
        out[...] = total[...].astype(BF)


def input_grad(z_index, d_blocks, w_qkv):
    _, length, cols = d_blocks[0].shape
    width = w_qkv.shape[1]
    return kernel_call(
        input_grad_body,
        (SIDE,),
        [whole(3, length, cols)] * SIDE
        + [pl.BlockSpec((3, width, cols), lambda i, z: (0, 0, lax.rem(z[0] + i, SIDE)))],
        whole(length, width),
        shape((length, width), BF),
        [pltpu.VMEM((length, width), F32)],
        scalars=1,
        name="input_grad",
    )(z_index, *d_blocks, *held(w_qkv))


def routing_body(select_rows, core, capacity, ids, later, cotangent, member_out, select, rows, code):
    step = pl.program_id(0)
    experts, length = code.shape

    @pl.when(step == 0)
    def _():
        at_expert = lax.broadcasted_iota(jnp.int32, (experts, length), 0)
        member = jnp.zeros((experts, length), F32)
        for j in range(ids.shape[0]):
            member = member + (ids[j : j + 1, :] == at_expert).astype(F32)
        member_out[...] = member.T
        ranks = dot(member.astype(BF), later[...], NN)
        row = lax.broadcasted_iota(jnp.int32, (experts, experts), 0)
        column = lax.broadcasted_iota(jnp.int32, (experts, experts), 1)
        limit = jnp.sum(jnp.where(row == column, capacity[...].astype(F32), 0.0), axis=1, keepdims=True)
        code[...] = jnp.where((member > 0.5) & (ranks < limit), ranks, -1.0)

    chunk = rows.shape[0]
    per = chunk * experts // select_rows
    depth = chunk // per
    slot = lax.broadcasted_iota(jnp.int32, (depth, length), 0).astype(F32)
    mine = code[pl.ds(pl.multiple_of(step * per, per), per), :]
    hit = jnp.concatenate([(mine[k : k + 1] == slot).astype(F32) for k in range(per)], axis=0).astype(BF)
    select[...] = hit
    rows[...] = dot(hit, cotangent[...], NN).astype(BF)


def routing(core, capacity, ids, cotangent):
    length, width = cotangent.shape
    experts = capacity.shape[0]
    slots = length * ids.shape[0]
    chunk = 16 * (slots // experts)
    half = width // 2
    later = jnp.asarray(np.triu(np.ones((length, length), np.float32), 1), BF)
    return kernel_call(
        functools.partial(routing_body, slots),
        (slots // chunk,),
        [
            whole(1, experts),
            whole(*ids.shape),
            whole(length, length),
            pl.BlockSpec((length, half), lambda i, c: (0, c[0])),
        ],
        [
            whole(length, experts),
            pl.BlockSpec((chunk, length), lambda i, c: (i, 0)),
            pl.BlockSpec((chunk, half), lambda i, c: (i, 0)),
        ],
        [shape((length, experts), F32), main_memory((slots, length), BF), main_memory((slots, half), BF)],
        [pltpu.VMEM((experts, length), F32)],
        scalars=1,
        name="routing",
    )(core, *held(capacity.reshape(1, experts), ids, later, cotangent))


def middle_body(core, tokens, own, peer, gain, select, w_router, member, expert_of,
                middle, normed, probs_out, gates_out, total_out, combine, rows):
    x2 = tokens[...].astype(F32) + (own[...].astype(F32) + peer[...].astype(F32))
    middle[...] = x2
    normed[...] = (x2 * rms(x2) * gain[...]).astype(BF)
    logits = dot(normed[...], w_router[...], NN)
    raised = jnp.exp(logits - jnp.max(logits, axis=-1, keepdims=True))
    probs = raised / jnp.sum(raised, axis=-1, keepdims=True)
    picked = probs * member[...]
    total = jnp.sum(picked, axis=-1, keepdims=True)
    gates = picked / total
    probs_out[...] = probs
    gates_out[...] = gates
    total_out[...] = total
    low = gates.astype(BF)
    half = rows.shape[1] - LANE
    for at in range(0, rows.shape[0], 256):
        cut = slice(at, at + 256)
        spread = dot(expert_of[cut], low, NT) * select[cut].astype(F32)
        combine[cut] = spread.astype(BF)
        gate = jnp.sum(spread, axis=-1, keepdims=True)
        rows[cut, half:] = jnp.broadcast_to(gate, (256, LANE)).astype(BF)
    for which in range(2):

        @pl.when(core[0] == which)
        def _():
            for at in range(0, rows.shape[0], 256):
                rows[at : at + 256, :half] = dot(
                    select[at : at + 256], normed[:, which * half : (which + 1) * half], NN
                ).astype(BF)


def middle_step(core, tokens, own, peer, gain, select, w_router, member, expert_of):
    length, width = tokens.shape
    slots, experts = expert_of.shape
    columns = width // 2 + LANE
    return kernel_call(
        middle_body,
        (1,),
        [whole(length, width)] * 3
        + [whole(1, width), whole(slots, length), whole(width, experts), whole(length, experts), whole(slots, experts)],
        [
            whole(length, width),
            whole(length, width),
            whole(length, experts),
            whole(length, experts),
            whole(length, 1),
            whole(slots, length),
            whole(slots, columns),
        ],
        [
            main_memory((length, width), F32),
            main_memory((length, width), BF),
            shape((length, experts), F32),
            shape((length, experts), F32),
            shape((length, 1), F32),
            main_memory((slots, length), BF),
            main_memory((slots, columns), BF),
        ],
        scalars=1,
        name="middle",
    )(core, *held(tokens), own, peer, *held(gain, select, w_router, member, expert_of))


def gather_back_body(back, combine, select, expert_of, out):
    half = out.shape[1] - LANE
    experts = expert_of.shape[1]
    out[:, :half] = dot(combine[...], back[:, :half], TN)
    high = back[:, half : half + 1].astype(F32)
    low = back[:, half + 1 : half + 2].astype(F32)
    picked = select[...].astype(F32)
    spread = dot((picked * high).astype(BF), expert_of[...], TN) + dot((picked * low).astype(BF), expert_of[...], TN)
    out[:, half : half + experts] = spread
    out[:, half + experts :] = jnp.zeros((out.shape[0], LANE - experts), F32)


def gather_back(back, combine, select, expert_of):
    slots, columns = back.shape
    length = combine.shape[1]
    experts = expert_of.shape[1]
    return kernel_call(
        gather_back_body,
        (1,),
        [whole(slots, columns), whole(slots, length), whole(slots, length), whole(slots, experts)],
        whole(length, columns),
        shape((length, columns), F32),
        name="gather_back",
    )(back, *held(combine, select, expert_of))


def middle_back_body(core, own, peer, probs, gates, total, member, w_router, middle, cotangent, gain, far,
                     d_logits_out, d_middle, d_attn, d_gain, *d_attn_blocks):
    half = own.shape[1] - LANE
    experts = probs.shape[1]
    d_gates = own[:, half : half + experts] + peer[:, half : half + experts]
    g, p = gates[...], probs[...]
    d_picked = member[...] * (d_gates - jnp.sum(d_gates * g, axis=-1, keepdims=True)) / total[...]
    d_logits = (p * (d_picked - jnp.sum(p * d_picked, axis=-1, keepdims=True))).astype(BF)
    d_logits_out[...] = d_logits
    d_normed = dot(d_logits, w_router[...], NT)
    for which in range(2):

        @pl.when(core[0] == which)
        def _():
            first, second = (own, peer) if which == 0 else (peer, own)
            d_middle[:, :half] = first[:, :half]
            d_middle[:, half:] = second[:, :half]

    d_normed = d_normed + d_middle[...]
    x2 = middle[...]
    scale = rms(x2)
    unit = x2 * scale
    d_gain[...] = jnp.sum(d_normed * unit, axis=0, keepdims=True)
    weighted = d_normed * gain[...]
    value = cotangent[...].astype(F32) + scale * (
        weighted - unit * jnp.mean(weighted * unit, axis=-1, keepdims=True)
    )
    d_middle[...] = value
    low = value.astype(BF)
    d_attn[...] = low
    cut = d_attn_blocks[0].shape[1]
    for which in range(SIDE):

        @pl.when(core[1] == which)
        def _():
            for k in range(SIDE):
                at = (which + k) % SIDE * cut
                d_attn_blocks[k][:, :cut] = low[:, at : at + cut]

    d_attn_blocks[1][:, cut:] = far[...]


def middle_back(core, own, peer, probs, gates, total, member, w_router, middle, cotangent, gain, far):
    length, width = middle.shape
    experts = probs.shape[1]
    columns = own.shape[1]
    quarter = width // SIDE
    blocks = [quarter, quarter + far.shape[1], quarter, quarter]
    return kernel_call(
        middle_back_body,
        (1,),
        [whole(length, columns)] * 2
        + [whole(length, experts)] * 2
        + [
            whole(length, 1),
            whole(length, experts),
            whole(width, experts),
            whole(length, width),
            whole(length, width),
            whole(1, width),
            whole(*far.shape),
        ],
        [whole(length, experts), whole(length, width), whole(length, width), whole(1, width)]
        + [whole(length, block) for block in blocks],
        [
            shape((length, experts), BF),
            shape((length, width), F32),
            shape((length, width), BF),
            shape((1, width), F32),
        ]
        + [shape((length, block), BF) for block in blocks],
        scalars=1,
        name="middle_back",
    )(core, own, peer, *held(probs, gates, total, member, w_router, middle, cotangent, gain, far))


def hidden_grad_body(core, own, peer, down_own, down_peer, out):
    half = down_own.shape[1]
    out[...] = dot(own[:, :half], down_own[...], NT) + dot(peer[:, :half], down_peer[...], NT)


ROWS = 512


def hidden_grad(core, own, peer, down):
    slots, columns = own.shape
    hidden, width = down.shape
    half = width // 2
    return kernel_call(
        hidden_grad_body,
        (slots // ROWS,),
        [
            pl.BlockSpec((ROWS, columns), lambda i, c: (i, 0)),
            pl.BlockSpec((ROWS, columns), lambda i, c: (i, 0)),
            pl.BlockSpec((hidden, half), lambda i, c: (0, c[0])),
            pl.BlockSpec((hidden, half), lambda i, c: (0, 1 - c[0])),
        ],
        pl.BlockSpec((ROWS, hidden), lambda i, c: (i, 0)),
        main_memory((slots, hidden), F32),
        scalars=1,
        name="hidden_grad",
    )(core, *held(own, peer, down, down))


def gate_first_body(core, own, pair, out):
    half, hidden = pair.shape[1:]
    mine = own[:, :half]
    out[:, :hidden] = dot(mine, pair[0], NN)
    out[:, hidden:] = dot(mine, pair[1], NN)


def gate_first(core, own, pair):
    slots, columns = own.shape
    half = columns - LANE
    hidden = pair.shape[2]
    rows = lambda n: pl.BlockSpec((ROWS, n), lambda i, c: (i, 0))
    return kernel_call(
        gate_first_body,
        (slots // ROWS,),
        [rows(columns), pl.BlockSpec((2, half, hidden), lambda i, c: (0, c[0], 0))],
        rows(2 * hidden),
        shape((slots, 2 * hidden), F32),
        scalars=1,
        mib=28,
        name="gate_first",
    )(core, *held(own, pair))


def experts_body(core, partial, peer, d_hidden, pair, acted, d_pair, extra):
    hidden = d_hidden.shape[1]
    half = pair.shape[1]
    other = peer[:, :half]
    gate = partial[:, :hidden] + dot(other, pair[0], NN)
    up = partial[:, hidden:] + dot(other, pair[1], NN)
    sig = 1.0 / (1.0 + jnp.exp(-gate))
    silu = gate * sig
    act = (silu * up).astype(BF)
    acted[...] = act
    d_act = d_hidden[...]
    slot_grad = jnp.sum(d_act * act.astype(F32), axis=-1, keepdims=True)
    high = slot_grad.astype(BF)
    low = (slot_grad - high.astype(F32)).astype(BF)
    at = lax.broadcasted_iota(jnp.int32, extra.shape, 1)
    extra[...] = jnp.where(at == 0, high.astype(F32), jnp.where(at == 1, low.astype(F32), 0.0)).astype(BF)
    d_pair[:, :hidden] = (d_act * up * sig * (1.0 + gate * (1.0 - sig))).astype(BF)
    d_pair[:, hidden:] = (d_act * silu).astype(BF)


def back_first_body(core, d_pair, pair, out):
    hidden = pair.shape[2]
    out[...] = dot(d_pair[:, :hidden], pair[0], NT) + dot(d_pair[:, hidden:], pair[1], NT)


def back_first(core, d_pair, pair):
    slots, columns = d_pair.shape
    _, width, hidden = pair.shape
    half = width // 2
    rows = lambda n: pl.BlockSpec((ROWS, n), lambda i, c: (i, 0))
    return kernel_call(
        back_first_body,
        (slots // ROWS,),
        [rows(columns), pl.BlockSpec((2, half, hidden), lambda i, c: (0, c[0], 0))],
        rows(half),
        shape((slots, half), F32),
        scalars=1,
        mib=28,
        name="back_first",
    )(core, *held(d_pair, pair))


def back_second_body(partial, d_pair, pair, extra, out):
    _, half, hidden = pair.shape
    value = dot(d_pair[:, :hidden], pair[0], NT) + dot(d_pair[:, hidden:], pair[1], NT)
    out[:, :half] = (partial[...] + value).astype(BF)
    out[:, half:] = extra[...]


def back_second(partial, d_pair, pair, extra):
    slots, columns = d_pair.shape
    _, half, hidden = pair.shape
    rows = lambda n: pl.BlockSpec((ROWS, n), lambda i: (i, 0))
    return kernel_call(
        back_second_body,
        (slots // ROWS,),
        [rows(half), rows(columns), whole(2, half, hidden), rows(LANE)],
        rows(half + LANE),
        main_memory((slots, half + LANE), BF),
        mib=28,
        name="back_second",
    )(partial, d_pair, *held(pair, extra))


def experts_out_body(core, acted, acted_peer, down, down_far, out):
    out[...] = (dot(acted[...], down[...], NN) + dot(acted_peer[...], down_far[...], NN)).astype(BF)


def experts_out(core, acted, acted_peer, down, down_far):
    slots, hidden = acted.shape
    half = down_far.shape[1]
    rows = lambda n: pl.BlockSpec((ROWS, n), lambda i, c: (i, 0))
    return kernel_call(
        experts_out_body,
        (slots // ROWS,),
        [
            rows(hidden),
            rows(hidden),
            pl.BlockSpec((hidden, half), lambda i, c: (0, c[0])),
            whole(hidden, half),
        ],
        rows(half),
        main_memory((slots, half), BF),
        scalars=1,
        name="experts_out",
    )(core, *held(acted, acted_peer, down, down_far))


def experts_step(core, partial, peer, d_hidden, pair):
    slots, columns = peer.shape
    half = columns - LANE
    hidden = pair.shape[2]
    block = ROWS // 2
    rows = lambda n: pl.BlockSpec((block, n), lambda i, c: (i, 0))
    return kernel_call(
        experts_body,
        (slots // block,),
        [
            rows(2 * hidden),
            rows(columns),
            rows(hidden),
            pl.BlockSpec((2, half, hidden), lambda i, c: (0, 1 - c[0], 0)),
        ],
        [rows(hidden), rows(2 * hidden), rows(LANE)],
        [
            main_memory((slots, hidden), BF),
            main_memory((slots, 2 * hidden), BF),
            main_memory((slots, LANE), BF),
        ],
        scalars=1,
        mib=28,
        name="experts",
    )(core, partial, peer, *held(d_hidden, pair))


def expert_grads_body(core, own, peer, grad_own, grad_peer, acted, d_pair, gates, grad_pair, grad_down, pair_low, act_low):
    step = pl.program_id(0)
    hidden = acted.shape[1]

    @pl.when(step == 0)
    def _():
        gate = gates[:, :1].astype(F32)
        pair_low[...] = (d_pair[...].astype(F32) * gate).astype(BF)
        act_low[...] = (acted[...].astype(F32) * gate).astype(BF)

    def part(rows, grads):
        value = dot(rows[...], pair_low[...], TN)
        grad_pair[:, 0, :] = value[:, :hidden]
        grad_pair[:, 1, :] = value[:, hidden:]
        grad_down[...] = dot(act_low[...], grads[...], TN)

    @pl.when(step < SIDE)
    def _():
        part(own, grad_own)

    @pl.when(step >= SIDE)
    def _():
        part(peer, grad_peer)


def expert_grads(core, own, peer, grad_own, grad_peer, acted, d_pair, gates):
    slots, half = grad_own.shape
    hidden = acted.shape[1]
    cut = half // SIDE
    first = pl.BlockSpec((slots, cut), lambda i, c: (0, jnp.minimum(i, SIDE - 1)))
    second = pl.BlockSpec((slots, cut), lambda i, c: (0, jnp.maximum(i - SIDE, 0)))

    def target(i, c):
        return jnp.where(i < SIDE, c[0] * SIDE + i, (1 - c[0]) * SIDE + i - SIDE)

    return kernel_call(
        expert_grads_body,
        (2 * SIDE,),
        [first, second, first, second, whole(slots, hidden), whole(slots, 2 * hidden), pl.BlockSpec((slots, LANE), lambda i, c: (0, half // LANE))],
        [
            pl.BlockSpec((cut, 2, hidden), lambda i, c: (target(i, c), 0, 0)),
            pl.BlockSpec((hidden, cut), lambda i, c: (0, target(i, c))),
        ],
        [shape((2 * half, 2, hidden), F32), shape((hidden, 2 * half), F32)],
        [pltpu.VMEM((slots, 2 * hidden), BF), pltpu.VMEM((slots, hidden), BF)],
        mib=48,
        scalars=1,
        name="expert_grads",
    )(core, *held(own), peer, *held(grad_own, grad_peer, acted, d_pair, gates))


EXTRA = 8


def group_grads_body(index, own, peer, *refs):
    step = pl.program_id(0)
    d_group = refs[:SIDE]
    normed_two, d_logits, d_gain, d_qk = refs[SIDE : SIDE + 4]
    first, second = refs[SIDE + 4 : 2 * SIDE + 4], refs[2 * SIDE + 4 : 3 * SIDE + 4]
    right, value = refs[3 * SIDE + 4 :]
    _, length, cols = d_group[0].shape
    rows = first[0].shape[1] - EXTRA
    middle = first[0].shape[2]

    @pl.when(step == 0)
    def _():
        for k in range(SIDE):
            for which in range(3):
                right[k * length : (k + 1) * length, which * cols : (which + 1) * cols] = d_group[k][which]

    @pl.when(step < SIDE // 2)
    def _():
        value[...] = dot(own[...], right[...], NN).astype(BF)

    @pl.when(step >= SIDE // 2)
    def _():
        value[...] = dot(peer[...], right[...], NN).astype(BF)

    router = dot(d_logits[...], normed_two[...], TN)
    extras = []
    for k in range(SIDE):
        cut = slice(k * rows, (k + 1) * rows)
        groups = [router[at * EXTRA : (at + 1) * EXTRA, cut] for at in range(SIDE)]
        groups.append(jnp.broadcast_to(d_gain[:, cut], (EXTRA, LANE)))
        groups.append(jnp.concatenate([d_qk[...]] * (EXTRA // 2), axis=0))
        extras.append(jnp.concatenate(groups, axis=1).astype(BF))

    half = SIDE // 2
    target = jnp.where(step < half, index[0] * half + step, (1 - index[0]) * half + step - half)
    for away in range(SIDE):

        @pl.when(lax.rem(index[1] + away, SIDE) == target)
        def _():
            for k in range(SIDE):
                first[away][k, :rows] = value[k * rows : (k + 1) * rows, :middle]
                first[away][k, rows:] = extras[k][:, :middle]

    for which in range(SIDE):

        @pl.when(index[2] == which)
        def _():
            for away in range(SIDE):
                k = (which + away) % SIDE
                second[away][target, :rows] = value[k * rows : (k + 1) * rows, middle:]
                second[away][target, rows:] = extras[k][:, middle:]


def turn_parts_body(*refs):
    value = jnp.concatenate([part[...].astype(F32) for part in refs[:SIDE]], axis=0)
    refs[SIDE][...] = value.T.astype(BF)


def turn_parts(parts):
    length, width = parts[0].shape
    cut = 256
    return kernel_call(
        turn_parts_body,
        (width // cut,),
        [pl.BlockSpec((length, cut), lambda i: (0, i))] * SIDE,
        pl.BlockSpec((cut, SIDE * length), lambda i: (i, 0)),
        main_memory((width, SIDE * length), BF),
        name="turn_parts",
    )(*held(*parts))


def group_grads(index, own, peer, d_group, normed_two, d_logits, d_gain, d_qk):
    half, depth = own.shape
    length = depth // SIDE
    cols = d_group[0].shape[2]
    steps = SIDE // 2
    cut = half // steps
    rows = 2 * half // (SIDE * SIDE)
    middle = 3 * cols // 2

    def target(i, c):
        return jnp.where(i < steps, c[0] * steps + i, (1 - c[0]) * steps + i - steps)

    return kernel_call(
        group_grads_body,
        (2 * steps,),
        [
            pl.BlockSpec((cut, depth), lambda i, c: (jnp.minimum(i, steps - 1), 0)),
            pl.BlockSpec((cut, depth), lambda i, c: (jnp.maximum(i - steps, 0), 0)),
        ]
        + [whole(3, length, cols)] * SIDE
        + [
            pl.BlockSpec((length, cut), lambda i, c: (0, target(i, c))),
            whole(length, d_logits.shape[1]),
            pl.BlockSpec((1, cut), lambda i, c: (0, target(i, c))),
            whole(2, LANE),
        ],
        [whole(SIDE, rows + EXTRA, middle)] * (2 * SIDE),
        [shape((SIDE, rows + EXTRA, middle), BF)] * (2 * SIDE),
        [pltpu.VMEM((depth, 3 * cols), BF), pltpu.VMEM((cut, 3 * cols), BF)],
        scalars=1,
        name="group_grads",
    )(index, *held(own, peer), *d_group, *held(normed_two), d_logits, d_gain, d_qk)


def ordered_sum(parts, which, read):
    values = [read(parts[(which - source) % SIDE]).astype(F32) for source in range(SIDE)]
    return ((values[0] + values[1]) + (values[2] + values[3])).astype(BF)


def stage_sums_body(index, *refs):
    sources = refs[:SIDE], refs[SIDE : 2 * SIDE]
    outs = refs[2 * SIDE : 3 * SIDE], refs[3 * SIDE : 4 * SIDE]
    total = refs[4 * SIDE]
    for part in range(2):
        here, there = index[1 + part], index[2 - part]
        for which in range(SIDE):

            @pl.when(here == which)
            def _():
                for k in range(SIDE):
                    total[k] = ordered_sum(sources[part], which, lambda ref: ref[k])

        for which in range(SIDE):

            @pl.when(there == which)
            def _():
                for away in range(SIDE):
                    outs[part][away][...] = total[(which + away) % SIDE]


def stage_sums(index, first, second):
    _, rows, columns = first[0].shape
    return kernel_call(
        stage_sums_body,
        (1,),
        [whole(SIDE, rows, columns)] * (2 * SIDE),
        [whole(rows, columns)] * (2 * SIDE),
        [shape((rows, columns), BF)] * (2 * SIDE),
        [pltpu.VMEM((SIDE, rows, columns), BF)],
        scalars=1,
        name="stage_sums",
    )(index, *first, *second)


def out_grads_body(*refs):
    out = refs[-1]
    rows = out.shape[0]
    left = jnp.concatenate([part[:, :rows] for part in refs[:SIDE]], axis=0)
    right = jnp.concatenate([refs[SIDE][...], refs[SIDE + 1][...], refs[1][:, rows:], refs[SIDE + 2][...]], axis=0)
    out[...] = dot(left, right, TN).astype(BF)


def out_grads(d_attn, attended):
    length, rows = d_attn[0].shape
    inner = attended[0].shape[1]
    return kernel_call(
        out_grads_body,
        (1,),
        [whole(*part.shape) for part in d_attn] + [whole(length, inner)] * len(attended),
        whole(rows, inner),
        shape((rows, inner), BF),
        name="out_grads",
    )(*d_attn, *held(*attended))


def sum_arrived_body(rows, index, *refs):
    sources = refs[:SIDE], refs[SIDE : 2 * SIDE]
    outs, value = refs[2 * SIDE : 3 * SIDE], refs[3 * SIDE]
    main = SIDE * rows
    middle = sources[0][0].shape[1]
    for part in range(2):
        for which in range(SIDE):

            @pl.when(index[2 - part] == which)
            def _():
                value[:, part * middle : (part + 1) * middle] = ordered_sum(sources[part], which, lambda ref: ref[...])

    for which in range(SIDE):

        @pl.when(index[3] == which)
        def _():
            for step in range(SIDE):
                at = (which + step) % SIDE * rows
                outs[step][:rows] = value[at : at + rows]

    for step in range(SIDE):
        outs[step][rows:] = value[main:]


def sum_arrived(index, first, second, rows):
    height, middle = first[0].shape
    return kernel_call(
        functools.partial(sum_arrived_body, rows),
        (1,),
        [whole(height, middle)] * (2 * SIDE),
        [whole(rows + EXTRA, 2 * middle)] * SIDE,
        [shape((rows + EXTRA, 2 * middle), BF)] * SIDE,
        [pltpu.VMEM((height, 2 * middle), BF)],
        scalars=1,
        name="sum_arrived",
    )(index, *first, *second)


def finish_body(z_index, *refs):
    parts, w_here, grad, small = refs[:SIDE], refs[SIDE], refs[SIDE + 1], refs[SIDE + 2]
    rows = grad.shape[1]
    cols = parts[0].shape[1] // 3
    for which in range(SIDE):

        @pl.when(z_index[0] == which)
        def _():
            ordered = [parts[(which - source) % SIDE] for source in range(SIDE)]
            for source in range(SIDE):
                for kind in range(3):
                    grad[kind, :, source * cols : (source + 1) * cols] = ordered[source][
                        :rows, kind * cols : (kind + 1) * cols
                    ].astype(F32)
            extra = [part[rows:].astype(F32) for part in ordered]
            total = (extra[0] + extra[1]) + (extra[2] + extra[3])
            for at in range(SIDE):
                small[at * EXTRA : (at + 1) * EXTRA] = total[:, at * LANE : (at + 1) * LANE]
            small[SIDE * EXTRA + 1 : SIDE * EXTRA + 2] = total[0:1, SIDE * LANE : (SIDE + 1) * LANE]
            small[SIDE * EXTRA + 2 : SIDE * EXTRA + 4] = total[0:2, (SIDE + 1) * LANE :]

    product = jnp.sum(grad[0] * w_here[0].astype(F32) + grad[1] * w_here[1].astype(F32) + grad[2] * w_here[2].astype(F32), axis=-1, keepdims=True)
    at_row = lax.broadcasted_iota(jnp.int32, (rows, LANE), 0)
    at_lane = lax.broadcasted_iota(jnp.int32, (rows, LANE), 1)
    small[SIDE * EXTRA : SIDE * EXTRA + 1] = jnp.sum(jnp.where(at_row == at_lane, product, 0.0), axis=0, keepdims=True)
    small[SIDE * EXTRA + 4 :] = jnp.zeros((small.shape[0] - SIDE * EXTRA - 4, LANE), F32)


def finish(z_index, parts, w_here):
    kinds, rows, inner = w_here.shape
    height, columns = parts[0].shape
    return kernel_call(
        finish_body,
        (1,),
        [whole(height, columns)] * SIDE + [whole(kinds, rows, inner)],
        [whole(kinds, rows, inner), whole(SIDE * EXTRA + 8, LANE)],
        [shape((kinds, rows, inner), F32), shape((SIDE * EXTRA + 8, LANE), F32)],
        scalars=1,
        name="finish",
    )(z_index, *parts, w_here)


def on_device(
    tokens,
    expert_ids,
    capacity,
    gain_attn,
    w_qkv,
    qk_gain,
    w_out,
    gain_ffn,
    w_router,
    w_gate_up,
    w_down,
    cotangent,
):
    length, width = tokens.shape
    expert_count = capacity.shape[0]
    slot_count = length * expert_ids.shape[1] // expert_count
    slots = expert_count * slot_count
    inner = w_qkv.shape[2]
    half = width // 2
    cols = inner // SIDE
    core_index = lax.axis_index("tensor")
    core = core_index.astype(jnp.int32).reshape(1)
    place = [lax.axis_index(a) for a in AXES]
    dp_index = (place[0] * SIDE + place[1]) * SIDE + place[2]
    rows_here_count = width // SIDE**3

    def own_half(value):
        return lax.dynamic_slice_in_dim(value, core_index * half, half, axis=-1)

    expert_of = jnp.asarray(np.repeat(np.eye(expert_count, dtype=np.float32), slot_count, 0), BF)

    def to_owners(rows):
        columns = rows.shape[1]
        return exchange(rows.reshape(expert_count, slot_count, columns), AXES).reshape(slots, columns)

    member, select, grad_send = routing(core, capacity, expert_ids.T, cotangent)
    grad_own = to_owners(grad_send)

    table = jnp.asarray(rotary(length, LANE // 2))
    gains = qk_gain.astype(F32)
    gain_one = gain_attn.astype(F32)
    gain_two = gain_ffn.astype(F32).reshape(1, width)
    w_parts = w_qkv.transpose(1, 0, 2)
    normed_one, raw, turned, kept, value_in, attended, partial = attend(
        tokens, gain_one.reshape(1, width), w_parts, w_out, gains, table
    )
    partial_peer = swap(partial)
    middle, normed_two, probs, gates, picked_total, combine, rows_send = middle_step(
        core, tokens, partial, partial_peer, gain_two, select, w_router, member, expert_of
    )
    rows_own = to_owners(rows_send)

    normed_early, attended_late, pair, grad_late, down, _ = together(
        own_half(normed_one), attended, w_gate_up, grad_own, w_down, rows_send
    )
    down = down[0]
    pair = pair[0].transpose(1, 0, 2)
    grad_peer = swap(grad_late)
    d_hidden = hidden_grad(core, grad_late, grad_peer, down)
    down_far = swap(lax.dynamic_slice_in_dim(down, (1 - core_index) * half, half, axis=1))
    pair_far = swap(lax.dynamic_slice_in_dim(pair, (1 - core_index) * half, half, axis=1))
    rows_own, d_hidden, pair, normed_early, down_far, pair_far = together(
        rows_own, d_hidden, pair, normed_early, down_far, pair_far
    )
    normed_group = share(normed_early, "z")
    rows_peer = swap(rows_own)
    acted, d_pair, extra = experts_step(core, gate_first(core, rows_own, pair), rows_peer, d_hidden, pair)
    d_pair, acted, attended_late, *normed_group = together(d_pair, acted, attended_late, *normed_group)
    from_one, from_three = shift(attended_late, "y", 1), shift(attended_late, "y", 3)
    back_send = back_second(back_first(core, d_pair, pair), swap(d_pair), pair_far, extra)
    back_send, acted_peer, from_one, from_three = together(back_send, swap(acted), from_one, from_three)
    back = to_owners(back_send)

    acted_late, own_late, peer_late, _ = together(acted, rows_own, rows_peer, back_send)
    grad_gate_up, grad_down = expert_grads(
        core, own_late, peer_late, grad_late, grad_peer, acted_late, d_pair, own_late
    )
    returned = experts_out(core, acted_late, acted_peer, down, down_far)
    normed_group, _ = together(normed_group, back_send)
    normed_group = turn_parts(normed_group)
    returned, grad_gate_up, grad_down, normed_group = together(returned, grad_gate_up, grad_down, normed_group)
    returned = to_owners(returned)

    gathered = gather_back(back, combine, select, expert_of)
    core_y = jnp.stack([core[0], place[0].astype(jnp.int32)])
    d_logits, d_middle, d_attn, gain_two_local, *d_attn_blocks = middle_back(
        core_y, gathered, swap(gathered), probs, gates, picked_total, member, w_router, middle, cotangent, gain_two,
        from_one
    )

    z_index = place[2].astype(jnp.int32).reshape(1)
    d_attn, normed_group_peer = together(d_attn, swap(normed_group))
    *d_blocks, grad_qk = attend_back(z_index, d_attn, w_out, raw, turned, kept, value_in, gains, table)
    d_group = send_steps(d_blocks, "z")
    returned, *d_group = together(returned, *d_group)

    columns_here = expert_count // 2
    my_logits = lax.dynamic_slice_in_dim(d_logits, core_index * columns_here, columns_here, axis=1)
    index = jnp.stack([core[0]] + [p.astype(jnp.int32) for p in place])
    partial_grads = group_grads(
        index, normed_group, normed_group_peer, d_group, normed_two, my_logits, gain_two_local, grad_qk
    )
    d_attn_blocks, from_one, _ = together(d_attn_blocks, from_one, d_blocks)
    d_attn_group = [
        d_attn_blocks[0],
        shift(d_attn_blocks[1], "y", 1),
        shift(d_attn_blocks[2], "y", 2),
        shift(d_attn_blocks[3], "y", 3),
    ]
    attended_group = [attended_late, from_one, from_three]
    partial_grads, attended_group, d_attn_group = together(partial_grads, attended_group, d_attn_group)
    first = send_steps(partial_grads[:SIDE], "y")
    second = send_steps(partial_grads[SIDE:], "x")
    d_attn_group, attended_group, late_returned, late_blocks, _ = together(
        d_attn_group, attended_group, returned, d_blocks, partial_grads
    )
    late_blocks, first[1] = together(late_blocks, first[1])
    d_one = input_grad(z_index, late_blocks, w_parts)

    grad_out = out_grads(d_attn_group, attended_group)
    grad_out, first[1] = together(grad_out, first[1])
    first[2], d_one = together(first[2], d_one)
    halves = stage_sums(index, first, second)
    grad_out = send_blocks(grad_out.reshape(SIDE, SIDE, rows_here_count, inner), "z", 1)
    halves, grad_out = together(halves, grad_out)
    first = send_steps(halves[:SIDE], "x")
    second = send_steps(halves[SIDE:], "y")

    d_one, _ = together(d_one, halves)
    d_one = d_one.astype(F32) + swap(d_one).astype(F32)

    residual_in = tokens.astype(F32)
    scale_one = rms(residual_in)
    unit_one = residual_in * scale_one
    weighted = d_one * gain_one
    grad_input = d_middle + scale_one * (
        weighted - unit_one * jnp.mean(weighted * unit_one, axis=-1, keepdims=True)
    )

    mix_own = dot(combine, late_returned, TN)
    result_own, _ = together((own_half(middle) + mix_own).astype(BF), halves)
    output = side_by_side(result_own, swap(result_own), core_index)

    grad_out = sum(part.astype(F32) for part in grad_out).astype(BF)
    grad_out = [block_at(grad_out, (place[1] + step) % SIDE, 0) for step in range(SIDE)]
    w_here = lax.dynamic_slice_in_dim(w_parts, dp_index * rows_here_count, rows_here_count, axis=1)
    first, second, w_here, grad_out = together(first, second, w_here, grad_out)
    parts = send_steps(sum_arrived(index, first, second, rows_here_count), "z")
    parts, grad_input, output, grad_out = together(parts, grad_input, output, grad_out)
    grad_out = sum(part.astype(F32) for part in send_steps(grad_out, "x"))
    grad_qkv, small = finish(z_index, parts, w_here)
    grad_qkv = grad_qkv.transpose(1, 0, 2)
    small_peer = swap(small)
    gain_here = lax.dynamic_slice_in_dim(gain_one, dp_index * rows_here_count, rows_here_count, axis=0)
    grad_gain_one = (small[SIDE * EXTRA] + small_peer[SIDE * EXTRA])[:rows_here_count] / gain_here
    cut = lambda value: lax.dynamic_slice_in_dim(value, place[2] * rows_here_count, rows_here_count, axis=-1)
    grad_router = jnp.where(
        core_index == 0,
        jnp.concatenate([small[: SIDE * EXTRA], small_peer[: SIDE * EXTRA]], axis=0),
        jnp.concatenate([small_peer[: SIDE * EXTRA], small[: SIDE * EXTRA]], axis=0),
    )
    grad_router = cut(grad_router).T
    grad_gain_two = cut(small[SIDE * EXTRA + 1])
    grad_qk = small[SIDE * EXTRA + 2 : SIDE * EXTRA + 4] + small_peer[SIDE * EXTRA + 2 : SIDE * EXTRA + 4]

    return (
        output,
        grad_input,
        grad_gain_one,
        grad_qkv,
        grad_qk,
        grad_out,
        grad_gain_two,
        grad_router,
        grad_gate_up[None],
        grad_down[None],
    )


def solution(mesh):
    names = AXES + ("tensor",)
    torus = Mesh(mesh.devices.reshape(SIDE, SIDE, SIDE, 2), names)
    return jax.shard_map(
        on_device,
        mesh=torus,
        in_specs=(
            P(AXES, None),
            P(AXES, None),
            P(),
            P(),
            P(None, None, "tensor"),
            P(),
            P(None, "tensor"),
            P(),
            P(),
            P(AXES, None, None, "tensor"),
            P(AXES, "tensor", None),
            P(AXES, None),
        ),
        out_specs=(
            P(AXES, None),
            P(AXES, None),
            P(AXES),
            P(AXES, None, "tensor"),
            P(),
            P(AXES, "tensor"),
            P(AXES),
            P(AXES, None),
            P(AXES, None, None, "tensor"),
            P(AXES, "tensor", None),
        ),
        check_vma=False,
    )
```

```python
import functools
import math

import jax
import jax.numpy as jnp
import numpy as np
from jax import lax
from jax.experimental import pallas as pl
from jax.experimental.pallas import tpu as pltpu
from jax.sharding import Mesh
from jax.sharding import PartitionSpec as P

AXES = ("y", "x", "z")
SIDE = 4
LANE = 128
BF = jnp.bfloat16
F32 = jnp.float32
MIB = 1 << 20


def dot(a, b, dims):
    return lax.dot_general(a, b, (dims, ((), ())), preferred_element_type=F32)


NN = ((1,), (0,))
NT = ((1,), (1,))
TN = ((0,), (0,))


def rms(values):
    return lax.rsqrt(jnp.mean(values * values, axis=-1, keepdims=True) + 1e-06)


def rotary(length, half_dim):
    position = np.arange(length, dtype=np.float32)
    inverse = np.float32(50000.0) ** (-np.arange(half_dim, dtype=np.float32) / np.float32(half_dim))
    angles = position[:, None] * inverse[None, :].astype(np.float32)
    cosine = np.cos(angles).astype(np.float32)
    sine = np.sin(angles).astype(np.float32)
    return np.stack([np.concatenate([cosine, cosine], 1), np.concatenate([-sine, sine], 1)])


def swap(value):
    return lax.ppermute(value, "tensor", [(0, 1), (1, 0)])


def shift(value, axis, step):
    return lax.ppermute(value, axis, [(i, (i + step) % SIDE) for i in range(SIDE)])


def side_by_side(own, peer, core):
    return jnp.where(
        core == 0,
        jnp.concatenate([own, peer], axis=-1),
        jnp.concatenate([peer, own], axis=-1),
    )


def block_at(value, index, dim):
    return lax.dynamic_index_in_dim(value, index, dim, keepdims=False)


def together(*values):
    return lax.optimization_barrier(values)


def share(value, axis):
    return [value] + [shift(value, axis, step) for step in (1, 2, 3)]


def send_blocks(value, axis, dim):
    here = lax.axis_index(axis)
    own = block_at(value, here, dim)
    return [own] + [shift(block_at(value, (here + step) % SIDE, dim), axis, step) for step in (1, 2, 3)]


def send_steps(blocks, axis):
    return [blocks[0]] + [shift(blocks[step], axis, step) for step in (1, 2, 3)]


def exchange(value, axes):
    return lax.all_to_all(value, axes, split_axis=0, concat_axis=0, tiled=True)


def shape(dims, kind):
    return jax.ShapeDtypeStruct(dims, kind)


def main_memory(dims, kind):
    return pltpu.HBM(dims, kind)


def held(*values):
    return [pltpu.with_memory_space_constraint(value, pltpu.HBM) for value in values]


def kernel_call(body, grid, ins, outs, out_shapes, scratch=(), mib=40, scalars=0, name=None):
    return pl.pallas_call(
        body,
        grid_spec=pltpu.PrefetchScalarGridSpec(
            num_scalar_prefetch=scalars, grid=grid, in_specs=ins, out_specs=outs, scratch_shapes=list(scratch)
        ),
        out_shape=out_shapes,
        compiler_params=pltpu.CompilerParams(vmem_limit_bytes=mib * MIB),
        name=name,
    )


def whole(*dims):
    return pl.BlockSpec(dims, lambda *_: (0,) * len(dims))


def rope(values, table):
    return values * table[0] + pltpu.roll(values, values.shape[-1] // 2, 1) * table[1]


def unrope(values, table):
    return values * table[0] - pltpu.roll(values, values.shape[-1] // 2, 1) * table[1]


def attention_weights(query, key):
    scores = dot(query, key, NT) * (1.0 / math.sqrt(query.shape[-1]))
    raised = jnp.exp(scores - jnp.max(scores, axis=-1, keepdims=True))
    return raised / jnp.sum(raised, axis=-1, keepdims=True)


def attend_body(tokens, gain, w_qkv, w_out, gains, table, normed, raw, turned, kept, value_out, attended, partial, total):
    step = pl.program_id(0)

    @pl.when(step == 0)
    def _():
        x = tokens[...].astype(F32)
        normed[...] = (x * rms(x) * gain[...]).astype(BF)
        total[...] = jnp.zeros_like(total)

    h = normed[...]
    query_raw = dot(h, w_qkv[0], NN)
    key_raw = dot(h, w_qkv[1], NN)
    value = dot(h, w_qkv[2], NN).astype(BF)
    raw[0] = query_raw
    raw[1] = key_raw
    value_out[...] = value
    for at in range(query_raw.shape[1] // LANE):
        cut = slice(at * LANE, (at + 1) * LANE)
        q, k = query_raw[:, cut], key_raw[:, cut]
        query = rope(q * rms(q) * gains[0:1], table).astype(BF)
        key = rope(k * rms(k) * gains[1:2], table).astype(BF)
        turned[0, :, cut] = query
        turned[1, :, cut] = key
        weights = attention_weights(query, key)
        kept[at] = weights
        attended[:, cut] = dot(weights.astype(BF), value[:, cut], NN).astype(BF)
    total[...] += dot(attended[...], w_out[...], NT)

    @pl.when(step == pl.num_programs(0) - 1)
    def _():
        partial[...] = total[...].astype(BF)


def attend(tokens, gain, w_qkv, w_out, gains, table):
    length, width = tokens.shape
    inner = w_qkv.shape[2]
    cols = inner // SIDE
    return kernel_call(
        attend_body,
        (SIDE,),
        [
            whole(length, width),
            whole(1, width),
            pl.BlockSpec((3, width, cols), lambda i: (0, 0, i)),
            pl.BlockSpec((width, cols), lambda i: (0, i)),
            whole(2, LANE),
            whole(2, length, LANE),
        ],
        [
            whole(length, width),
            pl.BlockSpec((2, length, cols), lambda i: (0, 0, i)),
            pl.BlockSpec((2, length, cols), lambda i: (0, 0, i)),
            pl.BlockSpec((cols // LANE, length, length), lambda i: (i, 0, 0)),
            pl.BlockSpec((length, cols), lambda i: (0, i)),
            pl.BlockSpec((length, cols), lambda i: (0, i)),
            whole(length, width),
        ],
        [
            main_memory((length, width), BF),
            main_memory((2, length, inner), F32),
            main_memory((2, length, inner), BF),
            main_memory((inner // LANE, length, length), F32),
            main_memory((length, inner), BF),
            main_memory((length, inner), BF),
            shape((length, width), BF),
        ],
        [pltpu.VMEM((length, width), F32)],
        name="attend",
    )(tokens, gain, w_qkv, w_out, gains, table)


def attend_back_body(z_index, d_attn, w_out, raw, turned, kept, value_in, gains, table, *outs):
    d_gains = outs[SIDE]
    step = pl.program_id(0)
    parts = ([], [], [])

    @pl.when(step == 0)
    def _():
        d_gains[...] = jnp.zeros_like(d_gains)

    d_attended = dot(d_attn[...], w_out[...], NN).astype(BF)
    for at in range(d_attended.shape[1] // LANE):
        cut = slice(at * LANE, (at + 1) * LANE)
        q, k = raw[0, :, cut], raw[1, :, cut]
        rq, rk = rms(q), rms(k)
        unit_q, unit_k = q * rq, k * rk
        query, key = turned[0, :, cut], turned[1, :, cut]
        weights = kept[at]
        grad = d_attended[:, cut]
        d_value = dot(weights.astype(BF), grad, TN)
        d_weights = dot(grad, value_in[:, cut], NT)
        d_scores = (
            weights * (d_weights - jnp.sum(weights * d_weights, axis=-1, keepdims=True))
        ).astype(BF)
        root = 1.0 / math.sqrt(LANE)
        d_query = unrope(dot(d_scores, key, NN) * root, table)
        d_key = unrope(dot(d_scores, query, TN) * root, table)
        d_gains[0:1] += jnp.sum(d_query * unit_q, axis=0, keepdims=True)
        d_gains[1:2] += jnp.sum(d_key * unit_k, axis=0, keepdims=True)
        wq = d_query * gains[0:1]
        wk = d_key * gains[1:2]
        parts[0].append((rq * (wq - unit_q * jnp.mean(wq * unit_q, axis=-1, keepdims=True))).astype(BF))
        parts[1].append((rk * (wk - unit_k * jnp.mean(wk * unit_k, axis=-1, keepdims=True))).astype(BF))
        parts[2].append(d_value.astype(BF))
    for k in range(SIDE):

        @pl.when((z_index[0] + k) % SIDE == step)
        def _():
            for kind in range(3):
                outs[k][kind] = jnp.concatenate(parts[kind], axis=1)


def attend_back(z_index, d_attn, w_out, raw, turned, kept, value_in, gains, table):
    length, width = d_attn.shape
    inner = w_out.shape[1]
    cols = inner // SIDE
    return kernel_call(
        attend_back_body,
        (SIDE,),
        [
            whole(length, width),
            pl.BlockSpec((width, cols), lambda i, z: (0, i)),
            pl.BlockSpec((2, length, cols), lambda i, z: (0, 0, i)),
            pl.BlockSpec((2, length, cols), lambda i, z: (0, 0, i)),
            pl.BlockSpec((cols // LANE, length, length), lambda i, z: (i, 0, 0)),
            pl.BlockSpec((length, cols), lambda i, z: (0, i)),
            whole(2, LANE),
            whole(2, length, LANE),
        ],
        [whole(3, length, cols)] * SIDE + [whole(2, LANE)],
        [shape((3, length, cols), BF)] * SIDE + [shape((2, LANE), F32)],
        scalars=1,
        name="attend_back",
    )(z_index, d_attn, *held(w_out, raw, turned, kept, value_in, gains, table))


def input_grad_body(z_index, *refs):
    w_qkv, out, total = refs[SIDE:]
    step = pl.program_id(0)

    @pl.when(step == 0)
    def _():
        total[...] = jnp.zeros_like(total)

    for k in range(SIDE):

        @pl.when(step == k)
        def _():
            block = refs[k]
            total[...] += dot(block[0], w_qkv[0], NT) + dot(block[1], w_qkv[1], NT) + dot(block[2], w_qkv[2], NT)

    @pl.when(step == pl.num_programs(0) - 1)
    def _():
        out[...] = total[...].astype(BF)


def input_grad(z_index, d_blocks, w_qkv):
    _, length, cols = d_blocks[0].shape
    width = w_qkv.shape[1]
    return kernel_call(
        input_grad_body,
        (SIDE,),
        [whole(3, length, cols)] * SIDE
        + [pl.BlockSpec((3, width, cols), lambda i, z: (0, 0, lax.rem(z[0] + i, SIDE)))],
        whole(length, width),
        shape((length, width), BF),
        [pltpu.VMEM((length, width), F32)],
        scalars=1,
        name="input_grad",
    )(z_index, *d_blocks, *held(w_qkv))


def routing_body(select_rows, core, capacity, ids, later, cotangent, member_out, select, rows, code):
    step = pl.program_id(0)
    experts, length = code.shape

    @pl.when(step == 0)
    def _():
        at_expert = lax.broadcasted_iota(jnp.int32, (experts, length), 0)
        member = jnp.zeros((experts, length), F32)
        for j in range(ids.shape[0]):
            member = member + (ids[j : j + 1, :] == at_expert).astype(F32)
        member_out[...] = member.T
        ranks = dot(member.astype(BF), later[...], NN)
        row = lax.broadcasted_iota(jnp.int32, (experts, experts), 0)
        column = lax.broadcasted_iota(jnp.int32, (experts, experts), 1)
        limit = jnp.sum(jnp.where(row == column, capacity[...].astype(F32), 0.0), axis=1, keepdims=True)
        code[...] = jnp.where((member > 0.5) & (ranks < limit), ranks, -1.0)

    chunk = rows.shape[0]
    per = chunk * experts // select_rows
    depth = chunk // per
    slot = lax.broadcasted_iota(jnp.int32, (depth, length), 0).astype(F32)
    mine = code[pl.ds(pl.multiple_of(step * per, per), per), :]
    hit = jnp.concatenate([(mine[k : k + 1] == slot).astype(F32) for k in range(per)], axis=0).astype(BF)
    select[...] = hit
    rows[...] = dot(hit, cotangent[...], NN).astype(BF)


def routing(core, capacity, ids, cotangent):
    length, width = cotangent.shape
    experts = capacity.shape[0]
    slots = length * ids.shape[0]
    chunk = 16 * (slots // experts)
    half = width // 2
    later = jnp.asarray(np.triu(np.ones((length, length), np.float32), 1), BF)
    return kernel_call(
        functools.partial(routing_body, slots),
        (slots // chunk,),
        [
            whole(1, experts),
            whole(*ids.shape),
            whole(length, length),
            pl.BlockSpec((length, half), lambda i, c: (0, c[0])),
        ],
        [
            whole(length, experts),
            pl.BlockSpec((chunk, length), lambda i, c: (i, 0)),
            pl.BlockSpec((chunk, half), lambda i, c: (i, 0)),
        ],
        [shape((length, experts), F32), main_memory((slots, length), BF), main_memory((slots, half), BF)],
        [pltpu.VMEM((experts, length), F32)],
        scalars=1,
        name="routing",
    )(core, *held(capacity.reshape(1, experts), ids, later, cotangent))


def middle_body(core, tokens, own, peer, gain, select, w_router, member, expert_of,
                middle, normed, probs_out, gates_out, total_out, combine, rows):
    x2 = tokens[...].astype(F32) + (own[...].astype(F32) + peer[...].astype(F32))
    middle[...] = x2
    normed[...] = (x2 * rms(x2) * gain[...]).astype(BF)
    logits = dot(normed[...], w_router[...], NN)
    raised = jnp.exp(logits - jnp.max(logits, axis=-1, keepdims=True))
    probs = raised / jnp.sum(raised, axis=-1, keepdims=True)
    picked = probs * member[...]
    total = jnp.sum(picked, axis=-1, keepdims=True)
    gates = picked / total
    probs_out[...] = probs
    gates_out[...] = gates
    total_out[...] = total
    low = gates.astype(BF)
    half = rows.shape[1] - LANE
    for at in range(0, rows.shape[0], 256):
        cut = slice(at, at + 256)
        spread = dot(expert_of[cut], low, NT) * select[cut].astype(F32)
        combine[cut] = spread.astype(BF)
        gate = jnp.sum(spread, axis=-1, keepdims=True)
        rows[cut, half:] = jnp.broadcast_to(gate, (256, LANE)).astype(BF)
    for which in range(2):

        @pl.when(core[0] == which)
        def _():
            for at in range(0, rows.shape[0], 256):
                rows[at : at + 256, :half] = dot(
                    select[at : at + 256], normed[:, which * half : (which + 1) * half], NN
                ).astype(BF)


def middle_step(core, tokens, own, peer, gain, select, w_router, member, expert_of):
    length, width = tokens.shape
    slots, experts = expert_of.shape
    columns = width // 2 + LANE
    return kernel_call(
        middle_body,
        (1,),
        [whole(length, width)] * 3
        + [whole(1, width), whole(slots, length), whole(width, experts), whole(length, experts), whole(slots, experts)],
        [
            whole(length, width),
            whole(length, width),
            whole(length, experts),
            whole(length, experts),
            whole(length, 1),
            whole(slots, length),
            whole(slots, columns),
        ],
        [
            main_memory((length, width), F32),
            main_memory((length, width), BF),
            shape((length, experts), F32),
            shape((length, experts), F32),
            shape((length, 1), F32),
            main_memory((slots, length), BF),
            main_memory((slots, columns), BF),
        ],
        scalars=1,
        name="middle",
    )(core, *held(tokens), own, peer, *held(gain, select, w_router, member, expert_of))


def gather_back_body(back, combine, select, expert_of, out):
    half = out.shape[1] - LANE
    experts = expert_of.shape[1]
    out[:, :half] = dot(combine[...], back[:, :half], TN)
    high = back[:, half : half + 1].astype(F32)
    low = back[:, half + 1 : half + 2].astype(F32)
    picked = select[...].astype(F32)
    spread = dot((picked * high).astype(BF), expert_of[...], TN) + dot((picked * low).astype(BF), expert_of[...], TN)
    out[:, half : half + experts] = spread
    out[:, half + experts :] = jnp.zeros((out.shape[0], LANE - experts), F32)


def gather_back(back, combine, select, expert_of):
    slots, columns = back.shape
    length = combine.shape[1]
    experts = expert_of.shape[1]
    return kernel_call(
        gather_back_body,
        (1,),
        [whole(slots, columns), whole(slots, length), whole(slots, length), whole(slots, experts)],
        whole(length, columns),
        shape((length, columns), F32),
        name="gather_back",
    )(back, *held(combine, select, expert_of))


def middle_back_body(core, own, peer, probs, gates, total, member, w_router, middle, cotangent, gain, far,
                     d_logits_out, d_middle, d_attn, d_gain, *d_attn_blocks):
    half = own.shape[1] - LANE
    experts = probs.shape[1]
    d_gates = own[:, half : half + experts] + peer[:, half : half + experts]
    g, p = gates[...], probs[...]
    d_picked = member[...] * (d_gates - jnp.sum(d_gates * g, axis=-1, keepdims=True)) / total[...]
    d_logits = (p * (d_picked - jnp.sum(p * d_picked, axis=-1, keepdims=True))).astype(BF)
    d_logits_out[...] = d_logits
    d_normed = dot(d_logits, w_router[...], NT)
    for which in range(2):

        @pl.when(core[0] == which)
        def _():
            first, second = (own, peer) if which == 0 else (peer, own)
            d_middle[:, :half] = first[:, :half]
            d_middle[:, half:] = second[:, :half]

    d_normed = d_normed + d_middle[...]
    x2 = middle[...]
    scale = rms(x2)
    unit = x2 * scale
    d_gain[...] = jnp.sum(d_normed * unit, axis=0, keepdims=True)
    weighted = d_normed * gain[...]
    value = cotangent[...].astype(F32) + scale * (
        weighted - unit * jnp.mean(weighted * unit, axis=-1, keepdims=True)
    )
    d_middle[...] = value
    low = value.astype(BF)
    d_attn[...] = low
    cut = d_attn_blocks[0].shape[1]
    for which in range(SIDE):

        @pl.when(core[1] == which)
        def _():
            for k in range(SIDE):
                at = (which + k) % SIDE * cut
                d_attn_blocks[k][:, :cut] = low[:, at : at + cut]

    d_attn_blocks[1][:, cut:] = far[...]


def middle_back(core, own, peer, probs, gates, total, member, w_router, middle, cotangent, gain, far):
    length, width = middle.shape
    experts = probs.shape[1]
    columns = own.shape[1]
    quarter = width // SIDE
    blocks = [quarter, quarter + far.shape[1], quarter, quarter]
    return kernel_call(
        middle_back_body,
        (1,),
        [whole(length, columns)] * 2
        + [whole(length, experts)] * 2
        + [
            whole(length, 1),
            whole(length, experts),
            whole(width, experts),
            whole(length, width),
            whole(length, width),
            whole(1, width),
            whole(*far.shape),
        ],
        [whole(length, experts), whole(length, width), whole(length, width), whole(1, width)]
        + [whole(length, block) for block in blocks],
        [
            shape((length, experts), BF),
            shape((length, width), F32),
            shape((length, width), BF),
            shape((1, width), F32),
        ]
        + [shape((length, block), BF) for block in blocks],
        scalars=1,
        name="middle_back",
    )(core, own, peer, *held(probs, gates, total, member, w_router, middle, cotangent, gain, far))


def hidden_grad_body(core, own, peer, down_own, down_peer, out):
    half = down_own.shape[1]
    out[...] = dot(own[:, :half], down_own[...], NT) + dot(peer[:, :half], down_peer[...], NT)


ROWS = 512


def hidden_grad(core, own, peer, down):
    slots, columns = own.shape
    hidden, width = down.shape
    half = width // 2
    return kernel_call(
        hidden_grad_body,
        (slots // ROWS,),
        [
            pl.BlockSpec((ROWS, columns), lambda i, c: (i, 0)),
            pl.BlockSpec((ROWS, columns), lambda i, c: (i, 0)),
            pl.BlockSpec((hidden, half), lambda i, c: (0, c[0])),
            pl.BlockSpec((hidden, half), lambda i, c: (0, 1 - c[0])),
        ],
        pl.BlockSpec((ROWS, hidden), lambda i, c: (i, 0)),
        main_memory((slots, hidden), F32),
        scalars=1,
        name="hidden_grad",
    )(core, *held(own, peer, down, down))


def gate_first_body(core, own, pair, out):
    half, hidden = pair.shape[1:]
    mine = own[:, :half]
    out[:, :hidden] = dot(mine, pair[0], NN)
    out[:, hidden:] = dot(mine, pair[1], NN)


def gate_first(core, own, pair):
    slots, columns = own.shape
    half = columns - LANE
    hidden = pair.shape[2]
    rows = lambda n: pl.BlockSpec((ROWS, n), lambda i, c: (i, 0))
    return kernel_call(
        gate_first_body,
        (slots // ROWS,),
        [rows(columns), pl.BlockSpec((2, half, hidden), lambda i, c: (0, c[0], 0))],
        rows(2 * hidden),
        shape((slots, 2 * hidden), F32),
        scalars=1,
        mib=28,
        name="gate_first",
    )(core, *held(own, pair))


def experts_body(core, partial, peer, d_hidden, pair, acted, d_pair, extra):
    hidden = d_hidden.shape[1]
    half = pair.shape[1]
    other = peer[:, :half]
    gate = partial[:, :hidden] + dot(other, pair[0], NN)
    up = partial[:, hidden:] + dot(other, pair[1], NN)
    sig = 1.0 / (1.0 + jnp.exp(-gate))
    silu = gate * sig
    act = (silu * up).astype(BF)
    acted[...] = act
    d_act = d_hidden[...]
    slot_grad = jnp.sum(d_act * act.astype(F32), axis=-1, keepdims=True)
    high = slot_grad.astype(BF)
    low = (slot_grad - high.astype(F32)).astype(BF)
    at = lax.broadcasted_iota(jnp.int32, extra.shape, 1)
    extra[...] = jnp.where(at == 0, high.astype(F32), jnp.where(at == 1, low.astype(F32), 0.0)).astype(BF)
    d_pair[:, :hidden] = (d_act * up * sig * (1.0 + gate * (1.0 - sig))).astype(BF)
    d_pair[:, hidden:] = (d_act * silu).astype(BF)


def back_first_body(core, d_pair, pair, out):
    hidden = pair.shape[2]
    out[...] = dot(d_pair[:, :hidden], pair[0], NT) + dot(d_pair[:, hidden:], pair[1], NT)


def back_first(core, d_pair, pair):
    slots, columns = d_pair.shape
    _, width, hidden = pair.shape
    half = width // 2
    rows = lambda n: pl.BlockSpec((ROWS, n), lambda i, c: (i, 0))
    return kernel_call(
        back_first_body,
        (slots // ROWS,),
        [rows(columns), pl.BlockSpec((2, half, hidden), lambda i, c: (0, c[0], 0))],
        rows(half),
        shape((slots, half), F32),
        scalars=1,
        mib=28,
        name="back_first",
    )(core, *held(d_pair, pair))


def back_second_body(partial, d_pair, pair, extra, out):
    _, half, hidden = pair.shape
    value = dot(d_pair[:, :hidden], pair[0], NT) + dot(d_pair[:, hidden:], pair[1], NT)
    out[:, :half] = (partial[...] + value).astype(BF)
    out[:, half:] = extra[...]


def back_second(partial, d_pair, pair, extra):
    slots, columns = d_pair.shape
    _, half, hidden = pair.shape
    rows = lambda n: pl.BlockSpec((ROWS, n), lambda i: (i, 0))
    return kernel_call(
        back_second_body,
        (slots // ROWS,),
        [rows(half), rows(columns), whole(2, half, hidden), rows(LANE)],
        rows(half + LANE),
        main_memory((slots, half + LANE), BF),
        mib=28,
        name="back_second",
    )(partial, d_pair, *held(pair, extra))


def experts_out_body(core, acted, acted_peer, down, down_far, out):
    out[...] = (dot(acted[...], down[...], NN) + dot(acted_peer[...], down_far[...], NN)).astype(BF)


def experts_out(core, acted, acted_peer, down, down_far):
    slots, hidden = acted.shape
    half = down_far.shape[1]
    rows = lambda n: pl.BlockSpec((ROWS, n), lambda i, c: (i, 0))
    return kernel_call(
        experts_out_body,
        (slots // ROWS,),
        [
            rows(hidden),
            rows(hidden),
            pl.BlockSpec((hidden, half), lambda i, c: (0, c[0])),
            whole(hidden, half),
        ],
        rows(half),
        main_memory((slots, half), BF),
        scalars=1,
        name="experts_out",
    )(core, *held(acted, acted_peer, down, down_far))


def experts_step(core, partial, peer, d_hidden, pair):
    slots, columns = peer.shape
    half = columns - LANE
    hidden = pair.shape[2]
    block = ROWS // 2
    rows = lambda n: pl.BlockSpec((block, n), lambda i, c: (i, 0))
    return kernel_call(
        experts_body,
        (slots // block,),
        [
            rows(2 * hidden),
            rows(columns),
            rows(hidden),
            pl.BlockSpec((2, half, hidden), lambda i, c: (0, 1 - c[0], 0)),
        ],
        [rows(hidden), rows(2 * hidden), rows(LANE)],
        [
            main_memory((slots, hidden), BF),
            main_memory((slots, 2 * hidden), BF),
            main_memory((slots, LANE), BF),
        ],
        scalars=1,
        mib=28,
        name="experts",
    )(core, partial, peer, *held(d_hidden, pair))


def expert_grads_body(core, own, peer, grad_own, grad_peer, acted, d_pair, gates, grad_pair, grad_down, pair_low, act_low):
    step = pl.program_id(0)
    hidden = acted.shape[1]

    @pl.when(step == 0)
    def _():
        gate = gates[:, :1].astype(F32)
        pair_low[...] = (d_pair[...].astype(F32) * gate).astype(BF)
        act_low[...] = (acted[...].astype(F32) * gate).astype(BF)

    def part(rows, grads):
        value = dot(rows[...], pair_low[...], TN)
        grad_pair[:, 0, :] = value[:, :hidden]
        grad_pair[:, 1, :] = value[:, hidden:]
        grad_down[...] = dot(act_low[...], grads[...], TN)

    @pl.when(step < SIDE)
    def _():
        part(own, grad_own)

    @pl.when(step >= SIDE)
    def _():
        part(peer, grad_peer)


def expert_grads(core, own, peer, grad_own, grad_peer, acted, d_pair, gates):
    slots, half = grad_own.shape
    hidden = acted.shape[1]
    cut = half // SIDE
    first = pl.BlockSpec((slots, cut), lambda i, c: (0, jnp.minimum(i, SIDE - 1)))
    second = pl.BlockSpec((slots, cut), lambda i, c: (0, jnp.maximum(i - SIDE, 0)))

    def target(i, c):
        return jnp.where(i < SIDE, c[0] * SIDE + i, (1 - c[0]) * SIDE + i - SIDE)

    return kernel_call(
        expert_grads_body,
        (2 * SIDE,),
        [first, second, first, second, whole(slots, hidden), whole(slots, 2 * hidden), pl.BlockSpec((slots, LANE), lambda i, c: (0, half // LANE))],
        [
            pl.BlockSpec((cut, 2, hidden), lambda i, c: (target(i, c), 0, 0)),
            pl.BlockSpec((hidden, cut), lambda i, c: (0, target(i, c))),
        ],
        [shape((2 * half, 2, hidden), F32), shape((hidden, 2 * half), F32)],
        [pltpu.VMEM((slots, 2 * hidden), BF), pltpu.VMEM((slots, hidden), BF)],
        mib=48,
        scalars=1,
        name="expert_grads",
    )(core, *held(own), peer, *held(grad_own, grad_peer, acted, d_pair, gates))


EXTRA = 8


def group_grads_body(index, own, peer, *refs):
    step = pl.program_id(0)
    d_group = refs[:SIDE]
    normed_two, d_logits, d_gain, d_qk = refs[SIDE : SIDE + 4]
    first, second = refs[SIDE + 4 : 2 * SIDE + 4], refs[2 * SIDE + 4 : 3 * SIDE + 4]
    right, value = refs[3 * SIDE + 4 :]
    _, length, cols = d_group[0].shape
    rows = first[0].shape[1] - EXTRA
    middle = first[0].shape[2]

    @pl.when(step == 0)
    def _():
        for k in range(SIDE):
            for which in range(3):
                right[k * length : (k + 1) * length, which * cols : (which + 1) * cols] = d_group[k][which]

    @pl.when(step < SIDE // 2)
    def _():
        value[...] = dot(own[...], right[...], NN).astype(BF)

    @pl.when(step >= SIDE // 2)
    def _():
        value[...] = dot(peer[...], right[...], NN).astype(BF)

    router = dot(d_logits[...], normed_two[...], TN)
    extras = []
    for k in range(SIDE):
        cut = slice(k * rows, (k + 1) * rows)
        groups = [router[at * EXTRA : (at + 1) * EXTRA, cut] for at in range(SIDE)]
        groups.append(jnp.broadcast_to(d_gain[:, cut], (EXTRA, LANE)))
        groups.append(jnp.concatenate([d_qk[...]] * (EXTRA // 2), axis=0))
        extras.append(jnp.concatenate(groups, axis=1).astype(BF))

    half = SIDE // 2
    target = jnp.where(step < half, index[0] * half + step, (1 - index[0]) * half + step - half)
    for away in range(SIDE):

        @pl.when(lax.rem(index[1] + away, SIDE) == target)
        def _():
            for k in range(SIDE):
                first[away][k, :rows] = value[k * rows : (k + 1) * rows, :middle]
                first[away][k, rows:] = extras[k][:, :middle]

    for which in range(SIDE):

        @pl.when(index[2] == which)
        def _():
            for away in range(SIDE):
                k = (which + away) % SIDE
                second[away][target, :rows] = value[k * rows : (k + 1) * rows, middle:]
                second[away][target, rows:] = extras[k][:, middle:]


def turn_parts_body(*refs):
    value = jnp.concatenate([part[...].astype(F32) for part in refs[:SIDE]], axis=0)
    refs[SIDE][...] = value.T.astype(BF)


def turn_parts(parts):
    length, width = parts[0].shape
    cut = 256
    return kernel_call(
        turn_parts_body,
        (width // cut,),
        [pl.BlockSpec((length, cut), lambda i: (0, i))] * SIDE,
        pl.BlockSpec((cut, SIDE * length), lambda i: (i, 0)),
        main_memory((width, SIDE * length), BF),
        name="turn_parts",
    )(*held(*parts))


def group_grads(index, own, peer, d_group, normed_two, d_logits, d_gain, d_qk):
    half, depth = own.shape
    length = depth // SIDE
    cols = d_group[0].shape[2]
    steps = SIDE // 2
    cut = half // steps
    rows = 2 * half // (SIDE * SIDE)
    middle = 3 * cols // 2

    def target(i, c):
        return jnp.where(i < steps, c[0] * steps + i, (1 - c[0]) * steps + i - steps)

    return kernel_call(
        group_grads_body,
        (2 * steps,),
        [
            pl.BlockSpec((cut, depth), lambda i, c: (jnp.minimum(i, steps - 1), 0)),
            pl.BlockSpec((cut, depth), lambda i, c: (jnp.maximum(i - steps, 0), 0)),
        ]
        + [whole(3, length, cols)] * SIDE
        + [
            pl.BlockSpec((length, cut), lambda i, c: (0, target(i, c))),
            whole(length, d_logits.shape[1]),
            pl.BlockSpec((1, cut), lambda i, c: (0, target(i, c))),
            whole(2, LANE),
        ],
        [whole(SIDE, rows + EXTRA, middle)] * (2 * SIDE),
        [shape((SIDE, rows + EXTRA, middle), BF)] * (2 * SIDE),
        [pltpu.VMEM((depth, 3 * cols), BF), pltpu.VMEM((cut, 3 * cols), BF)],
        scalars=1,
        name="group_grads",
    )(index, *held(own, peer), *d_group, *held(normed_two), d_logits, d_gain, d_qk)


def ordered_sum(parts, which, read):
    values = [read(parts[(which - source) % SIDE]).astype(F32) for source in range(SIDE)]
    return ((values[0] + values[1]) + (values[2] + values[3])).astype(BF)


def stage_sums_body(index, *refs):
    sources = refs[:SIDE], refs[SIDE : 2 * SIDE]
    outs = refs[2 * SIDE : 3 * SIDE], refs[3 * SIDE : 4 * SIDE]
    total = refs[4 * SIDE]
    for part in range(2):
        here, there = index[1 + part], index[2 - part]
        for which in range(SIDE):

            @pl.when(here == which)
            def _():
                for k in range(SIDE):
                    total[k] = ordered_sum(sources[part], which, lambda ref: ref[k])

        for which in range(SIDE):

            @pl.when(there == which)
            def _():
                for away in range(SIDE):
                    outs[part][away][...] = total[(which + away) % SIDE]


def stage_sums(index, first, second):
    _, rows, columns = first[0].shape
    return kernel_call(
        stage_sums_body,
        (1,),
        [whole(SIDE, rows, columns)] * (2 * SIDE),
        [whole(rows, columns)] * (2 * SIDE),
        [shape((rows, columns), BF)] * (2 * SIDE),
        [pltpu.VMEM((SIDE, rows, columns), BF)],
        scalars=1,
        name="stage_sums",
    )(index, *first, *second)


def out_grads_body(*refs):
    out = refs[-1]
    rows = out.shape[0]
    left = jnp.concatenate([part[:, :rows] for part in refs[:SIDE]], axis=0)
    right = jnp.concatenate([refs[SIDE][...], refs[SIDE + 1][...], refs[1][:, rows:], refs[SIDE + 2][...]], axis=0)
    out[...] = dot(left, right, TN).astype(BF)


def out_grads(d_attn, attended):
    length, rows = d_attn[0].shape
    inner = attended[0].shape[1]
    return kernel_call(
        out_grads_body,
        (1,),
        [whole(*part.shape) for part in d_attn] + [whole(length, inner)] * len(attended),
        whole(rows, inner),
        shape((rows, inner), BF),
        name="out_grads",
    )(*d_attn, *held(*attended))


def sum_arrived_body(rows, index, *refs):
    sources = refs[:SIDE], refs[SIDE : 2 * SIDE]
    outs, value = refs[2 * SIDE : 3 * SIDE], refs[3 * SIDE]
    main = SIDE * rows
    middle = sources[0][0].shape[1]
    for part in range(2):
        for which in range(SIDE):

            @pl.when(index[2 - part] == which)
            def _():
                value[:, part * middle : (part + 1) * middle] = ordered_sum(sources[part], which, lambda ref: ref[...])

    for which in range(SIDE):

        @pl.when(index[3] == which)
        def _():
            for step in range(SIDE):
                at = (which + step) % SIDE * rows
                outs[step][:rows] = value[at : at + rows]

    for step in range(SIDE):
        outs[step][rows:] = value[main:]


def sum_arrived(index, first, second, rows):
    height, middle = first[0].shape
    return kernel_call(
        functools.partial(sum_arrived_body, rows),
        (1,),
        [whole(height, middle)] * (2 * SIDE),
        [whole(rows + EXTRA, 2 * middle)] * SIDE,
        [shape((rows + EXTRA, 2 * middle), BF)] * SIDE,
        [pltpu.VMEM((height, 2 * middle), BF)],
        scalars=1,
        name="sum_arrived",
    )(index, *first, *second)


def finish_body(z_index, *refs):
    parts, w_here, grad, small = refs[:SIDE], refs[SIDE], refs[SIDE + 1], refs[SIDE + 2]
    rows = grad.shape[1]
    cols = parts[0].shape[1] // 3
    for which in range(SIDE):

        @pl.when(z_index[0] == which)
        def _():
            ordered = [parts[(which - source) % SIDE] for source in range(SIDE)]
            for source in range(SIDE):
                for kind in range(3):
                    grad[kind, :, source * cols : (source + 1) * cols] = ordered[source][
                        :rows, kind * cols : (kind + 1) * cols
                    ].astype(F32)
            extra = [part[rows:].astype(F32) for part in ordered]
            total = (extra[0] + extra[1]) + (extra[2] + extra[3])
            for at in range(SIDE):
                small[at * EXTRA : (at + 1) * EXTRA] = total[:, at * LANE : (at + 1) * LANE]
            small[SIDE * EXTRA + 1 : SIDE * EXTRA + 2] = total[0:1, SIDE * LANE : (SIDE + 1) * LANE]
            small[SIDE * EXTRA + 2 : SIDE * EXTRA + 4] = total[0:2, (SIDE + 1) * LANE :]

    product = jnp.sum(grad[0] * w_here[0].astype(F32) + grad[1] * w_here[1].astype(F32) + grad[2] * w_here[2].astype(F32), axis=-1, keepdims=True)
    at_row = lax.broadcasted_iota(jnp.int32, (rows, LANE), 0)
    at_lane = lax.broadcasted_iota(jnp.int32, (rows, LANE), 1)
    small[SIDE * EXTRA : SIDE * EXTRA + 1] = jnp.sum(jnp.where(at_row == at_lane, product, 0.0), axis=0, keepdims=True)
    small[SIDE * EXTRA + 4 :] = jnp.zeros((small.shape[0] - SIDE * EXTRA - 4, LANE), F32)


def finish(z_index, parts, w_here):
    kinds, rows, inner = w_here.shape
    height, columns = parts[0].shape
    return kernel_call(
        finish_body,
        (1,),
        [whole(height, columns)] * SIDE + [whole(kinds, rows, inner)],
        [whole(kinds, rows, inner), whole(SIDE * EXTRA + 8, LANE)],
        [shape((kinds, rows, inner), F32), shape((SIDE * EXTRA + 8, LANE), F32)],
        scalars=1,
        name="finish",
    )(z_index, *parts, w_here)


def on_device(
    tokens,
    expert_ids,
    capacity,
    gain_attn,
    w_qkv,
    qk_gain,
    w_out,
    gain_ffn,
    w_router,
    w_gate_up,
    w_down,
    cotangent,
):
    length, width = tokens.shape
    expert_count = capacity.shape[0]
    slot_count = length * expert_ids.shape[1] // expert_count
    slots = expert_count * slot_count
    inner = w_qkv.shape[2]
    half = width // 2
    cols = inner // SIDE
    core_index = lax.axis_index("tensor")
    core = core_index.astype(jnp.int32).reshape(1)
    place = [lax.axis_index(a) for a in AXES]
    dp_index = (place[0] * SIDE + place[1]) * SIDE + place[2]
    rows_here_count = width // SIDE**3

    def own_half(value):
        return lax.dynamic_slice_in_dim(value, core_index * half, half, axis=-1)

    expert_of = jnp.asarray(np.repeat(np.eye(expert_count, dtype=np.float32), slot_count, 0), BF)

    def to_owners(rows):
        columns = rows.shape[1]
        return exchange(rows.reshape(expert_count, slot_count, columns), AXES).reshape(slots, columns)

    member, select, grad_send = routing(core, capacity, expert_ids.T, cotangent)
    grad_own = to_owners(grad_send)

    table = jnp.asarray(rotary(length, LANE // 2))
    gains = qk_gain.astype(F32)
    gain_one = gain_attn.astype(F32)
    gain_two = gain_ffn.astype(F32).reshape(1, width)
    w_parts = w_qkv.transpose(1, 0, 2)
    normed_one, raw, turned, kept, value_in, attended, partial = attend(
        tokens, gain_one.reshape(1, width), w_parts, w_out, gains, table
    )
    partial_peer = swap(partial)
    middle, normed_two, probs, gates, picked_total, combine, rows_send = middle_step(
        core, tokens, partial, partial_peer, gain_two, select, w_router, member, expert_of
    )
    rows_own = to_owners(rows_send)

    normed_early, attended_late, pair, grad_late, down, _ = together(
        own_half(normed_one), attended, w_gate_up, grad_own, w_down, rows_send
    )
    down = down[0]
    pair = pair[0].transpose(1, 0, 2)
    grad_peer = swap(grad_late)
    d_hidden = hidden_grad(core, grad_late, grad_peer, down)
    down_far = swap(lax.dynamic_slice_in_dim(down, (1 - core_index) * half, half, axis=1))
    pair_far = swap(lax.dynamic_slice_in_dim(pair, (1 - core_index) * half, half, axis=1))
    rows_own, d_hidden, pair, normed_early, down_far, pair_far = together(
        rows_own, d_hidden, pair, normed_early, down_far, pair_far
    )
    normed_group = share(normed_early, "z")
    rows_peer = swap(rows_own)
    acted, d_pair, extra = experts_step(core, gate_first(core, rows_own, pair), rows_peer, d_hidden, pair)
    d_pair, acted, attended_late, *normed_group = together(d_pair, acted, attended_late, *normed_group)
    from_one, from_three = shift(attended_late, "y", 1), shift(attended_late, "y", 3)
    back_send = back_second(back_first(core, d_pair, pair), swap(d_pair), pair_far, extra)
    back_send, acted_peer, from_one, from_three = together(back_send, swap(acted), from_one, from_three)
    back = to_owners(back_send)

    acted_late, own_late, peer_late, _ = together(acted, rows_own, rows_peer, back_send)
    grad_gate_up, grad_down = expert_grads(
        core, own_late, peer_late, grad_late, grad_peer, acted_late, d_pair, own_late
    )
    returned = experts_out(core, acted_late, acted_peer, down, down_far)
    normed_group, _ = together(normed_group, back_send)
    normed_group = turn_parts(normed_group)
    returned, grad_gate_up, grad_down, normed_group = together(returned, grad_gate_up, grad_down, normed_group)
    returned = to_owners(returned)

    gathered = gather_back(back, combine, select, expert_of)
    core_y = jnp.stack([core[0], place[0].astype(jnp.int32)])
    d_logits, d_middle, d_attn, gain_two_local, *d_attn_blocks = middle_back(
        core_y, gathered, swap(gathered), probs, gates, picked_total, member, w_router, middle, cotangent, gain_two,
        from_one
    )

    z_index = place[2].astype(jnp.int32).reshape(1)
    d_attn, normed_group_peer = together(d_attn, swap(normed_group))
    *d_blocks, grad_qk = attend_back(z_index, d_attn, w_out, raw, turned, kept, value_in, gains, table)
    d_group = send_steps(d_blocks, "z")
    returned, *d_group = together(returned, *d_group)

    columns_here = expert_count // 2
    my_logits = lax.dynamic_slice_in_dim(d_logits, core_index * columns_here, columns_here, axis=1)
    index = jnp.stack([core[0]] + [p.astype(jnp.int32) for p in place])
    partial_grads = group_grads(
        index, normed_group, normed_group_peer, d_group, normed_two, my_logits, gain_two_local, grad_qk
    )
    d_attn_blocks, from_one, _ = together(d_attn_blocks, from_one, d_blocks)
    d_attn_group = [
        d_attn_blocks[0],
        shift(d_attn_blocks[1], "y", 1),
        shift(d_attn_blocks[2], "y", 2),
        shift(d_attn_blocks[3], "y", 3),
    ]
    attended_group = [attended_late, from_one, from_three]
    partial_grads, attended_group, d_attn_group = together(partial_grads, attended_group, d_attn_group)
    first = send_steps(partial_grads[:SIDE], "y")
    second = send_steps(partial_grads[SIDE:], "x")
    d_attn_group, attended_group, late_returned, late_blocks, _ = together(
        d_attn_group, attended_group, returned, d_blocks, partial_grads
    )
    d_one = input_grad(z_index, late_blocks, w_parts)

    grad_out = out_grads(d_attn_group, attended_group)
    mix_own = dot(combine, late_returned, TN)
    result_own = (own_half(middle) + mix_own).astype(BF)
    grad_out, d_one, result_own, first[1] = together(grad_out, d_one, result_own, first[1])
    halves = stage_sums(index, first, second)
    grad_out = send_blocks(grad_out.reshape(SIDE, SIDE, rows_here_count, inner), "z", 1)
    halves, grad_out = together(halves, grad_out)
    first = send_steps(halves[:SIDE], "x")
    second = send_steps(halves[SIDE:], "y")

    d_one, _ = together(d_one, halves)
    d_one = d_one.astype(F32) + swap(d_one).astype(F32)

    residual_in = tokens.astype(F32)
    scale_one = rms(residual_in)
    unit_one = residual_in * scale_one
    weighted = d_one * gain_one
    grad_input = d_middle + scale_one * (
        weighted - unit_one * jnp.mean(weighted * unit_one, axis=-1, keepdims=True)
    )

    result_own, _ = together(result_own, halves)
    output = side_by_side(result_own, swap(result_own), core_index)

    grad_out = sum(part.astype(F32) for part in grad_out).astype(BF)
    grad_out = [block_at(grad_out, (place[1] + step) % SIDE, 0) for step in range(SIDE)]
    w_here = lax.dynamic_slice_in_dim(w_parts, dp_index * rows_here_count, rows_here_count, axis=1)
    first, second, output, w_here, grad_out = together(first, second, output, w_here, grad_out)
    grad_out = sum(part.astype(F32) for part in send_steps(grad_out, "x"))
    parts = send_steps(sum_arrived(index, first, second, rows_here_count), "z")
    parts, grad_input = together(parts, grad_input)
    grad_qkv, small = finish(z_index, parts, w_here)
    grad_qkv = grad_qkv.transpose(1, 0, 2)
    small_peer = swap(small)
    gain_here = lax.dynamic_slice_in_dim(gain_one, dp_index * rows_here_count, rows_here_count, axis=0)
    grad_gain_one = (small[SIDE * EXTRA] + small_peer[SIDE * EXTRA])[:rows_here_count] / gain_here
    cut = lambda value: lax.dynamic_slice_in_dim(value, place[2] * rows_here_count, rows_here_count, axis=-1)
    grad_router = jnp.where(
        core_index == 0,
        jnp.concatenate([small[: SIDE * EXTRA], small_peer[: SIDE * EXTRA]], axis=0),
        jnp.concatenate([small_peer[: SIDE * EXTRA], small[: SIDE * EXTRA]], axis=0),
    )
    grad_router = cut(grad_router).T
    grad_gain_two = cut(small[SIDE * EXTRA + 1])
    grad_qk = small[SIDE * EXTRA + 2 : SIDE * EXTRA + 4] + small_peer[SIDE * EXTRA + 2 : SIDE * EXTRA + 4]

    return (
        output,
        grad_input,
        grad_gain_one,
        grad_qkv,
        grad_qk,
        grad_out,
        grad_gain_two,
        grad_router,
        grad_gate_up[None],
        grad_down[None],
    )


def solution(mesh):
    names = AXES + ("tensor",)
    torus = Mesh(mesh.devices.reshape(SIDE, SIDE, SIDE, 2), names)
    return jax.shard_map(
        on_device,
        mesh=torus,
        in_specs=(
            P(AXES, None),
            P(AXES, None),
            P(),
            P(),
            P(None, None, "tensor"),
            P(),
            P(None, "tensor"),
            P(),
            P(),
            P(AXES, None, None, "tensor"),
            P(AXES, "tensor", None),
            P(AXES, None),
        ),
        out_specs=(
            P(AXES, None),
            P(AXES, None),
            P(AXES),
            P(AXES, None, "tensor"),
            P(),
            P(AXES, "tensor"),
            P(AXES),
            P(AXES, None),
            P(AXES, None, None, "tensor"),
            P(AXES, "tensor", None),
        ),
        check_vma=False,
    )
```

```python
import functools
import math

import jax
import jax.numpy as jnp
import numpy as np
from jax import lax
from jax.experimental import pallas as pl
from jax.experimental.pallas import tpu as pltpu
from jax.sharding import Mesh
from jax.sharding import PartitionSpec as P

AXES = ("y", "x", "z")
SIDE = 4
LANE = 128
BF = jnp.bfloat16
F32 = jnp.float32
MIB = 1 << 20


def dot(a, b, dims):
    return lax.dot_general(a, b, (dims, ((), ())), preferred_element_type=F32)


NN = ((1,), (0,))
NT = ((1,), (1,))
TN = ((0,), (0,))


def rms(values):
    return lax.rsqrt(jnp.mean(values * values, axis=-1, keepdims=True) + 1e-06)


def rotary(length, half_dim):
    position = np.arange(length, dtype=np.float32)
    inverse = np.float32(50000.0) ** (-np.arange(half_dim, dtype=np.float32) / np.float32(half_dim))
    angles = position[:, None] * inverse[None, :].astype(np.float32)
    cosine = np.cos(angles).astype(np.float32)
    sine = np.sin(angles).astype(np.float32)
    return np.stack([np.concatenate([cosine, cosine], 1), np.concatenate([-sine, sine], 1)])


def swap(value):
    return lax.ppermute(value, "tensor", [(0, 1), (1, 0)])


def shift(value, axis, step):
    return lax.ppermute(value, axis, [(i, (i + step) % SIDE) for i in range(SIDE)])


def side_by_side(own, peer, core):
    return jnp.where(
        core == 0,
        jnp.concatenate([own, peer], axis=-1),
        jnp.concatenate([peer, own], axis=-1),
    )


def block_at(value, index, dim):
    return lax.dynamic_index_in_dim(value, index, dim, keepdims=False)


def together(*values):
    return lax.optimization_barrier(values)


def share(value, axis):
    return [value] + [shift(value, axis, step) for step in (1, 2, 3)]


def send_blocks(value, axis, dim):
    here = lax.axis_index(axis)
    own = block_at(value, here, dim)
    return [own] + [shift(block_at(value, (here + step) % SIDE, dim), axis, step) for step in (1, 2, 3)]


def send_steps(blocks, axis):
    return [blocks[0]] + [shift(blocks[step], axis, step) for step in (1, 2, 3)]


def exchange(value, axes):
    return lax.all_to_all(value, axes, split_axis=0, concat_axis=0, tiled=True)


def shape(dims, kind):
    return jax.ShapeDtypeStruct(dims, kind)


def main_memory(dims, kind):
    return pltpu.HBM(dims, kind)


def held(*values):
    return [pltpu.with_memory_space_constraint(value, pltpu.HBM) for value in values]


def kernel_call(body, grid, ins, outs, out_shapes, scratch=(), mib=40, scalars=0, name=None):
    return pl.pallas_call(
        body,
        grid_spec=pltpu.PrefetchScalarGridSpec(
            num_scalar_prefetch=scalars, grid=grid, in_specs=ins, out_specs=outs, scratch_shapes=list(scratch)
        ),
        out_shape=out_shapes,
        compiler_params=pltpu.CompilerParams(vmem_limit_bytes=mib * MIB),
        name=name,
    )


def whole(*dims):
    return pl.BlockSpec(dims, lambda *_: (0,) * len(dims))


def rope(values, table):
    return values * table[0] + pltpu.roll(values, values.shape[-1] // 2, 1) * table[1]


def unrope(values, table):
    return values * table[0] - pltpu.roll(values, values.shape[-1] // 2, 1) * table[1]


def attention_weights(query, key):
    scores = dot(query, key, NT) * (1.0 / math.sqrt(query.shape[-1]))
    raised = jnp.exp(scores - jnp.max(scores, axis=-1, keepdims=True))
    return raised / jnp.sum(raised, axis=-1, keepdims=True)


def attend_body(tokens, gain, w_qkv, w_out, gains, table, normed, raw, turned, kept, value_out, attended, partial, total):
    step = pl.program_id(0)

    @pl.when(step == 0)
    def _():
        x = tokens[...].astype(F32)
        normed[...] = (x * rms(x) * gain[...]).astype(BF)
        total[...] = jnp.zeros_like(total)

    h = normed[...]
    query_raw = dot(h, w_qkv[0], NN)
    key_raw = dot(h, w_qkv[1], NN)
    value = dot(h, w_qkv[2], NN).astype(BF)
    raw[0] = query_raw
    raw[1] = key_raw
    value_out[...] = value
    for at in range(query_raw.shape[1] // LANE):
        cut = slice(at * LANE, (at + 1) * LANE)
        q, k = query_raw[:, cut], key_raw[:, cut]
        query = rope(q * rms(q) * gains[0:1], table).astype(BF)
        key = rope(k * rms(k) * gains[1:2], table).astype(BF)
        turned[0, :, cut] = query
        turned[1, :, cut] = key
        weights = attention_weights(query, key)
        kept[at] = weights
        attended[:, cut] = dot(weights.astype(BF), value[:, cut], NN).astype(BF)
    total[...] += dot(attended[...], w_out[...], NT)

    @pl.when(step == pl.num_programs(0) - 1)
    def _():
        partial[...] = total[...].astype(BF)


def attend(tokens, gain, w_qkv, w_out, gains, table):
    length, width = tokens.shape
    inner = w_qkv.shape[2]
    cols = inner // SIDE
    return kernel_call(
        attend_body,
        (SIDE,),
        [
            whole(length, width),
            whole(1, width),
            pl.BlockSpec((3, width, cols), lambda i: (0, 0, i)),
            pl.BlockSpec((width, cols), lambda i: (0, i)),
            whole(2, LANE),
            whole(2, length, LANE),
        ],
        [
            whole(length, width),
            pl.BlockSpec((2, length, cols), lambda i: (0, 0, i)),
            pl.BlockSpec((2, length, cols), lambda i: (0, 0, i)),
            pl.BlockSpec((cols // LANE, length, length), lambda i: (i, 0, 0)),
            pl.BlockSpec((length, cols), lambda i: (0, i)),
            pl.BlockSpec((length, cols), lambda i: (0, i)),
            whole(length, width),
        ],
        [
            main_memory((length, width), BF),
            main_memory((2, length, inner), F32),
            main_memory((2, length, inner), BF),
            main_memory((inner // LANE, length, length), F32),
            main_memory((length, inner), BF),
            main_memory((length, inner), BF),
            shape((length, width), BF),
        ],
        [pltpu.VMEM((length, width), F32)],
        name="attend",
    )(tokens, gain, w_qkv, w_out, gains, table)


def attend_back_body(z_index, d_attn, w_out, raw, turned, kept, value_in, gains, table, *outs):
    d_gains = outs[SIDE]
    step = pl.program_id(0)
    parts = ([], [], [])

    @pl.when(step == 0)
    def _():
        d_gains[...] = jnp.zeros_like(d_gains)

    d_attended = dot(d_attn[...], w_out[...], NN).astype(BF)
    for at in range(d_attended.shape[1] // LANE):
        cut = slice(at * LANE, (at + 1) * LANE)
        q, k = raw[0, :, cut], raw[1, :, cut]
        rq, rk = rms(q), rms(k)
        unit_q, unit_k = q * rq, k * rk
        query, key = turned[0, :, cut], turned[1, :, cut]
        weights = kept[at]
        grad = d_attended[:, cut]
        d_value = dot(weights.astype(BF), grad, TN)
        d_weights = dot(grad, value_in[:, cut], NT)
        d_scores = (
            weights * (d_weights - jnp.sum(weights * d_weights, axis=-1, keepdims=True))
        ).astype(BF)
        root = 1.0 / math.sqrt(LANE)
        d_query = unrope(dot(d_scores, key, NN) * root, table)
        d_key = unrope(dot(d_scores, query, TN) * root, table)
        d_gains[0:1] += jnp.sum(d_query * unit_q, axis=0, keepdims=True)
        d_gains[1:2] += jnp.sum(d_key * unit_k, axis=0, keepdims=True)
        wq = d_query * gains[0:1]
        wk = d_key * gains[1:2]
        parts[0].append((rq * (wq - unit_q * jnp.mean(wq * unit_q, axis=-1, keepdims=True))).astype(BF))
        parts[1].append((rk * (wk - unit_k * jnp.mean(wk * unit_k, axis=-1, keepdims=True))).astype(BF))
        parts[2].append(d_value.astype(BF))
    for k in range(SIDE):

        @pl.when((z_index[0] + k) % SIDE == step)
        def _():
            for kind in range(3):
                outs[k][kind] = jnp.concatenate(parts[kind], axis=1)


def attend_back(z_index, d_attn, w_out, raw, turned, kept, value_in, gains, table):
    length, width = d_attn.shape
    inner = w_out.shape[1]
    cols = inner // SIDE
    return kernel_call(
        attend_back_body,
        (SIDE,),
        [
            whole(length, width),
            pl.BlockSpec((width, cols), lambda i, z: (0, i)),
            pl.BlockSpec((2, length, cols), lambda i, z: (0, 0, i)),
            pl.BlockSpec((2, length, cols), lambda i, z: (0, 0, i)),
            pl.BlockSpec((cols // LANE, length, length), lambda i, z: (i, 0, 0)),
            pl.BlockSpec((length, cols), lambda i, z: (0, i)),
            whole(2, LANE),
            whole(2, length, LANE),
        ],
        [whole(3, length, cols)] * SIDE + [whole(2, LANE)],
        [shape((3, length, cols), BF)] * SIDE + [shape((2, LANE), F32)],
        scalars=1,
        name="attend_back",
    )(z_index, d_attn, *held(w_out, raw, turned, kept, value_in, gains, table))


def input_grad_body(z_index, *refs):
    w_qkv, out, total = refs[SIDE:]
    step = pl.program_id(0)

    @pl.when(step == 0)
    def _():
        total[...] = jnp.zeros_like(total)

    for k in range(SIDE):

        @pl.when(step == k)
        def _():
            block = refs[k]
            total[...] += dot(block[0], w_qkv[0], NT) + dot(block[1], w_qkv[1], NT) + dot(block[2], w_qkv[2], NT)

    @pl.when(step == pl.num_programs(0) - 1)
    def _():
        out[...] = total[...].astype(BF)


def input_grad(z_index, d_blocks, w_qkv):
    _, length, cols = d_blocks[0].shape
    width = w_qkv.shape[1]
    return kernel_call(
        input_grad_body,
        (SIDE,),
        [whole(3, length, cols)] * SIDE
        + [pl.BlockSpec((3, width, cols), lambda i, z: (0, 0, lax.rem(z[0] + i, SIDE)))],
        whole(length, width),
        shape((length, width), BF),
        [pltpu.VMEM((length, width), F32)],
        scalars=1,
        name="input_grad",
    )(z_index, *d_blocks, *held(w_qkv))


def routing_body(select_rows, core, capacity, ids, later, cotangent, member_out, select, rows, code):
    step = pl.program_id(0)
    experts, length = code.shape

    @pl.when(step == 0)
    def _():
        at_expert = lax.broadcasted_iota(jnp.int32, (experts, length), 0)
        member = jnp.zeros((experts, length), F32)
        for j in range(ids.shape[0]):
            member = member + (ids[j : j + 1, :] == at_expert).astype(F32)
        member_out[...] = member.T
        ranks = dot(member.astype(BF), later[...], NN)
        row = lax.broadcasted_iota(jnp.int32, (experts, experts), 0)
        column = lax.broadcasted_iota(jnp.int32, (experts, experts), 1)
        limit = jnp.sum(jnp.where(row == column, capacity[...].astype(F32), 0.0), axis=1, keepdims=True)
        code[...] = jnp.where((member > 0.5) & (ranks < limit), ranks, -1.0)

    chunk = rows.shape[0]
    per = chunk * experts // select_rows
    depth = chunk // per
    slot = lax.broadcasted_iota(jnp.int32, (depth, length), 0).astype(F32)
    mine = code[pl.ds(pl.multiple_of(step * per, per), per), :]
    hit = jnp.concatenate([(mine[k : k + 1] == slot).astype(F32) for k in range(per)], axis=0).astype(BF)
    select[...] = hit
    rows[...] = dot(hit, cotangent[...], NN).astype(BF)


def routing(core, capacity, ids, cotangent):
    length, width = cotangent.shape
    experts = capacity.shape[0]
    slots = length * ids.shape[0]
    chunk = 16 * (slots // experts)
    half = width // 2
    later = jnp.asarray(np.triu(np.ones((length, length), np.float32), 1), BF)
    return kernel_call(
        functools.partial(routing_body, slots),
        (slots // chunk,),
        [
            whole(1, experts),
            whole(*ids.shape),
            whole(length, length),
            pl.BlockSpec((length, half), lambda i, c: (0, c[0])),
        ],
        [
            whole(length, experts),
            pl.BlockSpec((chunk, length), lambda i, c: (i, 0)),
            pl.BlockSpec((chunk, half), lambda i, c: (i, 0)),
        ],
        [shape((length, experts), F32), main_memory((slots, length), BF), main_memory((slots, half), BF)],
        [pltpu.VMEM((experts, length), F32)],
        scalars=1,
        name="routing",
    )(core, *held(capacity.reshape(1, experts), ids, later, cotangent))


def middle_body(core, tokens, own, peer, gain, select, w_router, member, expert_of,
                middle, normed, probs_out, gates_out, total_out, combine, rows):
    x2 = tokens[...].astype(F32) + (own[...].astype(F32) + peer[...].astype(F32))
    middle[...] = x2
    normed[...] = (x2 * rms(x2) * gain[...]).astype(BF)
    logits = dot(normed[...], w_router[...], NN)
    raised = jnp.exp(logits - jnp.max(logits, axis=-1, keepdims=True))
    probs = raised / jnp.sum(raised, axis=-1, keepdims=True)
    picked = probs * member[...]
    total = jnp.sum(picked, axis=-1, keepdims=True)
    gates = picked / total
    probs_out[...] = probs
    gates_out[...] = gates
    total_out[...] = total
    low = gates.astype(BF)
    half = rows.shape[1] - LANE
    for at in range(0, rows.shape[0], 256):
        cut = slice(at, at + 256)
        spread = dot(expert_of[cut], low, NT) * select[cut].astype(F32)
        combine[cut] = spread.astype(BF)
        gate = jnp.sum(spread, axis=-1, keepdims=True)
        rows[cut, half:] = jnp.broadcast_to(gate, (256, LANE)).astype(BF)
    for which in range(2):

        @pl.when(core[0] == which)
        def _():
            for at in range(0, rows.shape[0], 256):
                rows[at : at + 256, :half] = dot(
                    select[at : at + 256], normed[:, which * half : (which + 1) * half], NN
                ).astype(BF)


def middle_step(core, tokens, own, peer, gain, select, w_router, member, expert_of):
    length, width = tokens.shape
    slots, experts = expert_of.shape
    columns = width // 2 + LANE
    return kernel_call(
        middle_body,
        (1,),
        [whole(length, width)] * 3
        + [whole(1, width), whole(slots, length), whole(width, experts), whole(length, experts), whole(slots, experts)],
        [
            whole(length, width),
            whole(length, width),
            whole(length, experts),
            whole(length, experts),
            whole(length, 1),
            whole(slots, length),
            whole(slots, columns),
        ],
        [
            main_memory((length, width), F32),
            main_memory((length, width), BF),
            shape((length, experts), F32),
            shape((length, experts), F32),
            shape((length, 1), F32),
            main_memory((slots, length), BF),
            main_memory((slots, columns), BF),
        ],
        scalars=1,
        name="middle",
    )(core, *held(tokens), own, peer, *held(gain, select, w_router, member, expert_of))


def gather_back_body(back, combine, select, expert_of, out):
    half = out.shape[1] - LANE
    experts = expert_of.shape[1]
    out[:, :half] = dot(combine[...], back[:, :half], TN)
    high = back[:, half : half + 1].astype(F32)
    low = back[:, half + 1 : half + 2].astype(F32)
    picked = select[...].astype(F32)
    spread = dot((picked * high).astype(BF), expert_of[...], TN) + dot((picked * low).astype(BF), expert_of[...], TN)
    out[:, half : half + experts] = spread
    out[:, half + experts :] = jnp.zeros((out.shape[0], LANE - experts), F32)


def gather_back(back, combine, select, expert_of):
    slots, columns = back.shape
    length = combine.shape[1]
    experts = expert_of.shape[1]
    return kernel_call(
        gather_back_body,
        (1,),
        [whole(slots, columns), whole(slots, length), whole(slots, length), whole(slots, experts)],
        whole(length, columns),
        shape((length, columns), F32),
        name="gather_back",
    )(back, *held(combine, select, expert_of))


def middle_back_body(core, own, peer, probs, gates, total, member, w_router, middle, cotangent, gain, far,
                     d_logits_out, d_middle, d_attn, d_gain, *d_attn_blocks):
    half = own.shape[1] - LANE
    experts = probs.shape[1]
    d_gates = own[:, half : half + experts] + peer[:, half : half + experts]
    g, p = gates[...], probs[...]
    d_picked = member[...] * (d_gates - jnp.sum(d_gates * g, axis=-1, keepdims=True)) / total[...]
    d_logits = (p * (d_picked - jnp.sum(p * d_picked, axis=-1, keepdims=True))).astype(BF)
    d_logits_out[...] = d_logits
    d_normed = dot(d_logits, w_router[...], NT)
    for which in range(2):

        @pl.when(core[0] == which)
        def _():
            first, second = (own, peer) if which == 0 else (peer, own)
            d_middle[:, :half] = first[:, :half]
            d_middle[:, half:] = second[:, :half]

    d_normed = d_normed + d_middle[...]
    x2 = middle[...]
    scale = rms(x2)
    unit = x2 * scale
    d_gain[...] = jnp.sum(d_normed * unit, axis=0, keepdims=True)
    weighted = d_normed * gain[...]
    value = cotangent[...].astype(F32) + scale * (
        weighted - unit * jnp.mean(weighted * unit, axis=-1, keepdims=True)
    )
    d_middle[...] = value
    low = value.astype(BF)
    d_attn[...] = low
    cut = d_attn_blocks[0].shape[1]
    for which in range(SIDE):

        @pl.when(core[1] == which)
        def _():
            for k in range(SIDE):
                at = (which + k) % SIDE * cut
                d_attn_blocks[k][:, :cut] = low[:, at : at + cut]

    d_attn_blocks[1][:, cut:] = far[...]


def middle_back(core, own, peer, probs, gates, total, member, w_router, middle, cotangent, gain, far):
    length, width = middle.shape
    experts = probs.shape[1]
    columns = own.shape[1]
    quarter = width // SIDE
    blocks = [quarter, quarter + far.shape[1], quarter, quarter]
    return kernel_call(
        middle_back_body,
        (1,),
        [whole(length, columns)] * 2
        + [whole(length, experts)] * 2
        + [
            whole(length, 1),
            whole(length, experts),
            whole(width, experts),
            whole(length, width),
            whole(length, width),
            whole(1, width),
            whole(*far.shape),
        ],
        [whole(length, experts), whole(length, width), whole(length, width), whole(1, width)]
        + [whole(length, block) for block in blocks],
        [
            shape((length, experts), BF),
            shape((length, width), F32),
            shape((length, width), BF),
            shape((1, width), F32),
        ]
        + [shape((length, block), BF) for block in blocks],
        scalars=1,
        name="middle_back",
    )(core, own, peer, *held(probs, gates, total, member, w_router, middle, cotangent, gain, far))


def hidden_grad_body(core, own, peer, down_own, down_peer, out):
    half = down_own.shape[1]
    out[...] = dot(own[:, :half], down_own[...], NT) + dot(peer[:, :half], down_peer[...], NT)


ROWS = 512


def hidden_grad(core, own, peer, down):
    slots, columns = own.shape
    hidden, width = down.shape
    half = width // 2
    return kernel_call(
        hidden_grad_body,
        (slots // ROWS,),
        [
            pl.BlockSpec((ROWS, columns), lambda i, c: (i, 0)),
            pl.BlockSpec((ROWS, columns), lambda i, c: (i, 0)),
            pl.BlockSpec((hidden, half), lambda i, c: (0, c[0])),
            pl.BlockSpec((hidden, half), lambda i, c: (0, 1 - c[0])),
        ],
        pl.BlockSpec((ROWS, hidden), lambda i, c: (i, 0)),
        main_memory((slots, hidden), F32),
        scalars=1,
        name="hidden_grad",
    )(core, *held(own, peer, down, down))


def gate_first_body(core, own, pair, out):
    half, hidden = pair.shape[1:]
    mine = own[:, :half]
    out[:, :hidden] = dot(mine, pair[0], NN)
    out[:, hidden:] = dot(mine, pair[1], NN)


def gate_first(core, own, pair):
    slots, columns = own.shape
    half = columns - LANE
    hidden = pair.shape[2]
    rows = lambda n: pl.BlockSpec((ROWS, n), lambda i, c: (i, 0))
    return kernel_call(
        gate_first_body,
        (slots // ROWS,),
        [rows(columns), pl.BlockSpec((2, half, hidden), lambda i, c: (0, c[0], 0))],
        rows(2 * hidden),
        shape((slots, 2 * hidden), F32),
        scalars=1,
        mib=28,
        name="gate_first",
    )(core, *held(own, pair))


def experts_body(core, partial, peer, d_hidden, pair, acted, d_pair, extra):
    hidden = d_hidden.shape[1]
    half = pair.shape[1]
    other = peer[:, :half]
    gate = partial[:, :hidden] + dot(other, pair[0], NN)
    up = partial[:, hidden:] + dot(other, pair[1], NN)
    sig = 1.0 / (1.0 + jnp.exp(-gate))
    silu = gate * sig
    act = (silu * up).astype(BF)
    acted[...] = act
    d_act = d_hidden[...]
    slot_grad = jnp.sum(d_act * act.astype(F32), axis=-1, keepdims=True)
    high = slot_grad.astype(BF)
    low = (slot_grad - high.astype(F32)).astype(BF)
    at = lax.broadcasted_iota(jnp.int32, extra.shape, 1)
    extra[...] = jnp.where(at == 0, high.astype(F32), jnp.where(at == 1, low.astype(F32), 0.0)).astype(BF)
    d_pair[:, :hidden] = (d_act * up * sig * (1.0 + gate * (1.0 - sig))).astype(BF)
    d_pair[:, hidden:] = (d_act * silu).astype(BF)


def back_first_body(core, d_pair, pair, out):
    hidden = pair.shape[2]
    out[...] = dot(d_pair[:, :hidden], pair[0], NT) + dot(d_pair[:, hidden:], pair[1], NT)


def back_first(core, d_pair, pair):
    slots, columns = d_pair.shape
    _, width, hidden = pair.shape
    half = width // 2
    rows = lambda n: pl.BlockSpec((ROWS, n), lambda i, c: (i, 0))
    return kernel_call(
        back_first_body,
        (slots // ROWS,),
        [rows(columns), pl.BlockSpec((2, half, hidden), lambda i, c: (0, c[0], 0))],
        rows(half),
        shape((slots, half), F32),
        scalars=1,
        mib=28,
        name="back_first",
    )(core, *held(d_pair, pair))


def back_second_body(partial, d_pair, pair, extra, out):
    _, half, hidden = pair.shape
    value = dot(d_pair[:, :hidden], pair[0], NT) + dot(d_pair[:, hidden:], pair[1], NT)
    out[:, :half] = (partial[...] + value).astype(BF)
    out[:, half:] = extra[...]


def back_second(partial, d_pair, pair, extra):
    slots, columns = d_pair.shape
    _, half, hidden = pair.shape
    rows = lambda n: pl.BlockSpec((ROWS, n), lambda i: (i, 0))
    return kernel_call(
        back_second_body,
        (slots // ROWS,),
        [rows(half), rows(columns), whole(2, half, hidden), rows(LANE)],
        rows(half + LANE),
        main_memory((slots, half + LANE), BF),
        mib=28,
        name="back_second",
    )(partial, d_pair, *held(pair, extra))


def experts_out_body(core, acted, acted_peer, down, down_far, out):
    out[...] = (dot(acted[...], down[...], NN) + dot(acted_peer[...], down_far[...], NN)).astype(BF)


def experts_out(core, acted, acted_peer, down, down_far):
    slots, hidden = acted.shape
    half = down_far.shape[1]
    rows = lambda n: pl.BlockSpec((ROWS, n), lambda i, c: (i, 0))
    return kernel_call(
        experts_out_body,
        (slots // ROWS,),
        [
            rows(hidden),
            rows(hidden),
            pl.BlockSpec((hidden, half), lambda i, c: (0, c[0])),
            whole(hidden, half),
        ],
        rows(half),
        main_memory((slots, half), BF),
        scalars=1,
        name="experts_out",
    )(core, *held(acted, acted_peer, down, down_far))


def experts_step(core, partial, peer, d_hidden, pair):
    slots, columns = peer.shape
    half = columns - LANE
    hidden = pair.shape[2]
    block = ROWS // 2
    rows = lambda n: pl.BlockSpec((block, n), lambda i, c: (i, 0))
    return kernel_call(
        experts_body,
        (slots // block,),
        [
            rows(2 * hidden),
            rows(columns),
            rows(hidden),
            pl.BlockSpec((2, half, hidden), lambda i, c: (0, 1 - c[0], 0)),
        ],
        [rows(hidden), rows(2 * hidden), rows(LANE)],
        [
            main_memory((slots, hidden), BF),
            main_memory((slots, 2 * hidden), BF),
            main_memory((slots, LANE), BF),
        ],
        scalars=1,
        mib=28,
        name="experts",
    )(core, partial, peer, *held(d_hidden, pair))


def expert_grads_body(core, own, peer, grad_own, grad_peer, acted, d_pair, gates, grad_pair, grad_down, pair_low, act_low):
    step = pl.program_id(0)
    hidden = acted.shape[1]

    @pl.when(step == 0)
    def _():
        gate = gates[:, :1].astype(F32)
        pair_low[...] = (d_pair[...].astype(F32) * gate).astype(BF)
        act_low[...] = (acted[...].astype(F32) * gate).astype(BF)

    def part(rows, grads):
        value = dot(rows[...], pair_low[...], TN)
        grad_pair[:, 0, :] = value[:, :hidden]
        grad_pair[:, 1, :] = value[:, hidden:]
        grad_down[...] = dot(act_low[...], grads[...], TN)

    @pl.when(step < SIDE)
    def _():
        part(own, grad_own)

    @pl.when(step >= SIDE)
    def _():
        part(peer, grad_peer)


def expert_grads(core, own, peer, grad_own, grad_peer, acted, d_pair, gates):
    slots, half = grad_own.shape
    hidden = acted.shape[1]
    cut = half // SIDE
    first = pl.BlockSpec((slots, cut), lambda i, c: (0, jnp.minimum(i, SIDE - 1)))
    second = pl.BlockSpec((slots, cut), lambda i, c: (0, jnp.maximum(i - SIDE, 0)))

    def target(i, c):
        return jnp.where(i < SIDE, c[0] * SIDE + i, (1 - c[0]) * SIDE + i - SIDE)

    return kernel_call(
        expert_grads_body,
        (2 * SIDE,),
        [first, second, first, second, whole(slots, hidden), whole(slots, 2 * hidden), pl.BlockSpec((slots, LANE), lambda i, c: (0, half // LANE))],
        [
            pl.BlockSpec((cut, 2, hidden), lambda i, c: (target(i, c), 0, 0)),
            pl.BlockSpec((hidden, cut), lambda i, c: (0, target(i, c))),
        ],
        [shape((2 * half, 2, hidden), F32), shape((hidden, 2 * half), F32)],
        [pltpu.VMEM((slots, 2 * hidden), BF), pltpu.VMEM((slots, hidden), BF)],
        mib=48,
        scalars=1,
        name="expert_grads",
    )(core, *held(own), peer, *held(grad_own, grad_peer, acted, d_pair, gates))


EXTRA = 8


def group_grads_body(index, own, peer, *refs):
    step = pl.program_id(0)
    d_group = refs[:SIDE]
    normed_two, d_logits, d_gain, d_qk = refs[SIDE : SIDE + 4]
    first, second = refs[SIDE + 4 : 2 * SIDE + 4], refs[2 * SIDE + 4 : 3 * SIDE + 4]
    right, value = refs[3 * SIDE + 4 :]
    _, length, cols = d_group[0].shape
    rows = first[0].shape[1] - EXTRA
    middle = first[0].shape[2]

    @pl.when(step == 0)
    def _():
        for k in range(SIDE):
            for which in range(3):
                right[k * length : (k + 1) * length, which * cols : (which + 1) * cols] = d_group[k][which]

    @pl.when(step < SIDE // 2)
    def _():
        value[...] = dot(own[...], right[...], NN).astype(BF)

    @pl.when(step >= SIDE // 2)
    def _():
        value[...] = dot(peer[...], right[...], NN).astype(BF)

    router = dot(d_logits[...], normed_two[...], TN)
    extras = []
    for k in range(SIDE):
        cut = slice(k * rows, (k + 1) * rows)
        groups = [router[at * EXTRA : (at + 1) * EXTRA, cut] for at in range(SIDE)]
        groups.append(jnp.broadcast_to(d_gain[:, cut], (EXTRA, LANE)))
        groups.append(jnp.concatenate([d_qk[...]] * (EXTRA // 2), axis=0))
        extras.append(jnp.concatenate(groups, axis=1).astype(BF))

    half = SIDE // 2
    target = jnp.where(step < half, index[0] * half + step, (1 - index[0]) * half + step - half)
    for away in range(SIDE):

        @pl.when(lax.rem(index[1] + away, SIDE) == target)
        def _():
            for k in range(SIDE):
                first[away][k, :rows] = value[k * rows : (k + 1) * rows, :middle]
                first[away][k, rows:] = extras[k][:, :middle]

    for which in range(SIDE):

        @pl.when(index[2] == which)
        def _():
            for away in range(SIDE):
                k = (which + away) % SIDE
                second[away][target, :rows] = value[k * rows : (k + 1) * rows, middle:]
                second[away][target, rows:] = extras[k][:, middle:]


def turn_parts_body(*refs):
    value = jnp.concatenate([part[...].astype(F32) for part in refs[:SIDE]], axis=0)
    refs[SIDE][...] = value.T.astype(BF)


def turn_parts(parts):
    length, width = parts[0].shape
    cut = 256
    return kernel_call(
        turn_parts_body,
        (width // cut,),
        [pl.BlockSpec((length, cut), lambda i: (0, i))] * SIDE,
        pl.BlockSpec((cut, SIDE * length), lambda i: (i, 0)),
        main_memory((width, SIDE * length), BF),
        name="turn_parts",
    )(*held(*parts))


def group_grads(index, own, peer, d_group, normed_two, d_logits, d_gain, d_qk):
    half, depth = own.shape
    length = depth // SIDE
    cols = d_group[0].shape[2]
    steps = SIDE // 2
    cut = half // steps
    rows = 2 * half // (SIDE * SIDE)
    middle = 3 * cols // 2

    def target(i, c):
        return jnp.where(i < steps, c[0] * steps + i, (1 - c[0]) * steps + i - steps)

    return kernel_call(
        group_grads_body,
        (2 * steps,),
        [
            pl.BlockSpec((cut, depth), lambda i, c: (jnp.minimum(i, steps - 1), 0)),
            pl.BlockSpec((cut, depth), lambda i, c: (jnp.maximum(i - steps, 0), 0)),
        ]
        + [whole(3, length, cols)] * SIDE
        + [
            pl.BlockSpec((length, cut), lambda i, c: (0, target(i, c))),
            whole(length, d_logits.shape[1]),
            pl.BlockSpec((1, cut), lambda i, c: (0, target(i, c))),
            whole(2, LANE),
        ],
        [whole(SIDE, rows + EXTRA, middle)] * (2 * SIDE),
        [shape((SIDE, rows + EXTRA, middle), BF)] * (2 * SIDE),
        [pltpu.VMEM((depth, 3 * cols), BF), pltpu.VMEM((cut, 3 * cols), BF)],
        scalars=1,
        name="group_grads",
    )(index, *held(own, peer), *d_group, *held(normed_two), d_logits, d_gain, d_qk)


def ordered_sum(parts, which, read):
    values = [read(parts[(which - source) % SIDE]).astype(F32) for source in range(SIDE)]
    return ((values[0] + values[1]) + (values[2] + values[3])).astype(BF)


def stage_sums_body(index, *refs):
    sources = refs[:SIDE], refs[SIDE : 2 * SIDE]
    outs = refs[2 * SIDE : 3 * SIDE], refs[3 * SIDE : 4 * SIDE]
    total = refs[4 * SIDE]
    for part in range(2):
        here, there = index[1 + part], index[2 - part]
        for which in range(SIDE):

            @pl.when(here == which)
            def _():
                for k in range(SIDE):
                    total[k] = ordered_sum(sources[part], which, lambda ref: ref[k])

        for which in range(SIDE):

            @pl.when(there == which)
            def _():
                for away in range(SIDE):
                    outs[part][away][...] = total[(which + away) % SIDE]


def stage_sums(index, first, second):
    _, rows, columns = first[0].shape
    return kernel_call(
        stage_sums_body,
        (1,),
        [whole(SIDE, rows, columns)] * (2 * SIDE),
        [whole(rows, columns)] * (2 * SIDE),
        [shape((rows, columns), BF)] * (2 * SIDE),
        [pltpu.VMEM((SIDE, rows, columns), BF)],
        scalars=1,
        name="stage_sums",
    )(index, *first, *second)


def out_grads_body(*refs):
    out = refs[-1]
    rows = out.shape[0]
    left = jnp.concatenate([part[:, :rows] for part in refs[:SIDE]], axis=0)
    right = jnp.concatenate([refs[SIDE][...], refs[SIDE + 1][...], refs[1][:, rows:], refs[SIDE + 2][...]], axis=0)
    out[...] = dot(left, right, TN).astype(BF)


def out_grads(d_attn, attended):
    length, rows = d_attn[0].shape
    inner = attended[0].shape[1]
    return kernel_call(
        out_grads_body,
        (1,),
        [whole(*part.shape) for part in d_attn] + [whole(length, inner)] * len(attended),
        whole(rows, inner),
        shape((rows, inner), BF),
        name="out_grads",
    )(*d_attn, *held(*attended))


def sum_arrived_body(rows, index, *refs):
    sources = refs[:SIDE], refs[SIDE : 2 * SIDE]
    outs, value = refs[2 * SIDE : 3 * SIDE], refs[3 * SIDE]
    main = SIDE * rows
    middle = sources[0][0].shape[1]
    for part in range(2):
        for which in range(SIDE):

            @pl.when(index[2 - part] == which)
            def _():
                value[:, part * middle : (part + 1) * middle] = ordered_sum(sources[part], which, lambda ref: ref[...])

    for which in range(SIDE):

        @pl.when(index[3] == which)
        def _():
            for step in range(SIDE):
                at = (which + step) % SIDE * rows
                outs[step][:rows] = value[at : at + rows]

    for step in range(SIDE):
        outs[step][rows:] = value[main:]


def sum_arrived(index, first, second, rows):
    height, middle = first[0].shape
    return kernel_call(
        functools.partial(sum_arrived_body, rows),
        (1,),
        [whole(height, middle)] * (2 * SIDE),
        [whole(rows + EXTRA, 2 * middle)] * SIDE,
        [shape((rows + EXTRA, 2 * middle), BF)] * SIDE,
        [pltpu.VMEM((height, 2 * middle), BF)],
        scalars=1,
        name="sum_arrived",
    )(index, *first, *second)


def finish_body(z_index, *refs):
    parts, w_here, grad, small = refs[:SIDE], refs[SIDE], refs[SIDE + 1], refs[SIDE + 2]
    rows = grad.shape[1]
    cols = parts[0].shape[1] // 3
    for which in range(SIDE):

        @pl.when(z_index[0] == which)
        def _():
            ordered = [parts[(which - source) % SIDE] for source in range(SIDE)]
            for source in range(SIDE):
                for kind in range(3):
                    grad[kind, :, source * cols : (source + 1) * cols] = ordered[source][
                        :rows, kind * cols : (kind + 1) * cols
                    ].astype(F32)
            extra = [part[rows:].astype(F32) for part in ordered]
            total = (extra[0] + extra[1]) + (extra[2] + extra[3])
            for at in range(SIDE):
                small[at * EXTRA : (at + 1) * EXTRA] = total[:, at * LANE : (at + 1) * LANE]
            small[SIDE * EXTRA + 1 : SIDE * EXTRA + 2] = total[0:1, SIDE * LANE : (SIDE + 1) * LANE]
            small[SIDE * EXTRA + 2 : SIDE * EXTRA + 4] = total[0:2, (SIDE + 1) * LANE :]

    product = jnp.sum(grad[0] * w_here[0].astype(F32) + grad[1] * w_here[1].astype(F32) + grad[2] * w_here[2].astype(F32), axis=-1, keepdims=True)
    at_row = lax.broadcasted_iota(jnp.int32, (rows, LANE), 0)
    at_lane = lax.broadcasted_iota(jnp.int32, (rows, LANE), 1)
    small[SIDE * EXTRA : SIDE * EXTRA + 1] = jnp.sum(jnp.where(at_row == at_lane, product, 0.0), axis=0, keepdims=True)
    small[SIDE * EXTRA + 4 :] = jnp.zeros((small.shape[0] - SIDE * EXTRA - 4, LANE), F32)


def finish(z_index, parts, w_here):
    kinds, rows, inner = w_here.shape
    height, columns = parts[0].shape
    return kernel_call(
        finish_body,
        (1,),
        [whole(height, columns)] * SIDE + [whole(kinds, rows, inner)],
        [whole(kinds, rows, inner), whole(SIDE * EXTRA + 8, LANE)],
        [shape((kinds, rows, inner), F32), shape((SIDE * EXTRA + 8, LANE), F32)],
        scalars=1,
        name="finish",
    )(z_index, *parts, w_here)


def on_device(
    tokens,
    expert_ids,
    capacity,
    gain_attn,
    w_qkv,
    qk_gain,
    w_out,
    gain_ffn,
    w_router,
    w_gate_up,
    w_down,
    cotangent,
):
    length, width = tokens.shape
    expert_count = capacity.shape[0]
    slot_count = length * expert_ids.shape[1] // expert_count
    slots = expert_count * slot_count
    inner = w_qkv.shape[2]
    half = width // 2
    cols = inner // SIDE
    core_index = lax.axis_index("tensor")
    core = core_index.astype(jnp.int32).reshape(1)
    place = [lax.axis_index(a) for a in AXES]
    dp_index = (place[0] * SIDE + place[1]) * SIDE + place[2]
    rows_here_count = width // SIDE**3

    def own_half(value):
        return lax.dynamic_slice_in_dim(value, core_index * half, half, axis=-1)

    expert_of = jnp.asarray(np.repeat(np.eye(expert_count, dtype=np.float32), slot_count, 0), BF)

    def to_owners(rows):
        columns = rows.shape[1]
        return exchange(rows.reshape(expert_count, slot_count, columns), AXES).reshape(slots, columns)

    member, select, grad_send = routing(core, capacity, expert_ids.T, cotangent)
    grad_own = to_owners(grad_send)

    table = jnp.asarray(rotary(length, LANE // 2))
    gains = qk_gain.astype(F32)
    gain_one = gain_attn.astype(F32)
    gain_two = gain_ffn.astype(F32).reshape(1, width)
    w_parts = w_qkv.transpose(1, 0, 2)
    normed_one, raw, turned, kept, value_in, attended, partial = attend(
        tokens, gain_one.reshape(1, width), w_parts, w_out, gains, table
    )
    partial_peer = swap(partial)
    middle, normed_two, probs, gates, picked_total, combine, rows_send = middle_step(
        core, tokens, partial, partial_peer, gain_two, select, w_router, member, expert_of
    )
    rows_own = to_owners(rows_send)

    normed_early, attended_late, pair, grad_late, down, _ = together(
        own_half(normed_one), attended, w_gate_up, grad_own, w_down, rows_send
    )
    down = down[0]
    pair = pair[0].transpose(1, 0, 2)
    grad_peer = swap(grad_late)
    d_hidden = hidden_grad(core, grad_late, grad_peer, down)
    down_far = swap(lax.dynamic_slice_in_dim(down, (1 - core_index) * half, half, axis=1))
    pair_far = swap(lax.dynamic_slice_in_dim(pair, (1 - core_index) * half, half, axis=1))
    rows_own, d_hidden, pair, normed_early, down_far, pair_far = together(
        rows_own, d_hidden, pair, normed_early, down_far, pair_far
    )
    normed_group = share(normed_early, "z")
    rows_peer = swap(rows_own)
    acted, d_pair, extra = experts_step(core, gate_first(core, rows_own, pair), rows_peer, d_hidden, pair)
    d_pair, acted, attended_late, *normed_group = together(d_pair, acted, attended_late, *normed_group)
    from_one, from_three = shift(attended_late, "y", 1), shift(attended_late, "y", 3)
    back_send = back_second(back_first(core, d_pair, pair), swap(d_pair), pair_far, extra)
    back_send, acted_peer, from_one, from_three = together(back_send, swap(acted), from_one, from_three)
    back = to_owners(back_send)

    acted_late, own_late, peer_late, _ = together(acted, rows_own, rows_peer, back_send)
    grad_gate_up, grad_down = expert_grads(
        core, own_late, peer_late, grad_late, grad_peer, acted_late, d_pair, own_late
    )
    returned = experts_out(core, acted_late, acted_peer, down, down_far)
    normed_group, _ = together(normed_group, back_send)
    normed_group = turn_parts(normed_group)
    returned, grad_gate_up, grad_down, normed_group = together(returned, grad_gate_up, grad_down, normed_group)
    returned = to_owners(returned)

    gathered = gather_back(back, combine, select, expert_of)
    core_y = jnp.stack([core[0], place[0].astype(jnp.int32)])
    d_logits, d_middle, d_attn, gain_two_local, *d_attn_blocks = middle_back(
        core_y, gathered, swap(gathered), probs, gates, picked_total, member, w_router, middle, cotangent, gain_two,
        from_one
    )

    z_index = place[2].astype(jnp.int32).reshape(1)
    d_attn, normed_group_peer = together(d_attn, swap(normed_group))
    *d_blocks, grad_qk = attend_back(z_index, d_attn, w_out, raw, turned, kept, value_in, gains, table)
    d_group = send_steps(d_blocks, "z")
    d_one = input_grad(z_index, d_blocks, w_parts)
    returned, d_one, d_one_peer, *d_group = together(returned, d_one, swap(d_one), *d_group)

    columns_here = expert_count // 2
    my_logits = lax.dynamic_slice_in_dim(d_logits, core_index * columns_here, columns_here, axis=1)
    index = jnp.stack([core[0]] + [p.astype(jnp.int32) for p in place])
    partial_grads = group_grads(
        index, normed_group, normed_group_peer, d_group, normed_two, my_logits, gain_two_local, grad_qk
    )
    d_attn_blocks, from_one, _ = together(d_attn_blocks, from_one, d_blocks)
    d_attn_group = [
        d_attn_blocks[0],
        shift(d_attn_blocks[1], "y", 1),
        shift(d_attn_blocks[2], "y", 2),
        shift(d_attn_blocks[3], "y", 3),
    ]
    attended_group = [attended_late, from_one, from_three]
    second = send_steps(partial_grads[SIDE:], "x")
    first, attended_group, d_attn_group = together(partial_grads[:SIDE], attended_group, d_attn_group)
    first = send_steps(first, "y")
    d_attn_group, attended_group, late_returned, d_one, d_one_peer, _ = together(
        d_attn_group, attended_group, returned, d_one, d_one_peer, partial_grads
    )

    grad_out = out_grads(d_attn_group, attended_group)
    grad_out, first[1] = together(grad_out, first[1])
    halves = stage_sums(index, first, second)
    first = send_steps(halves[:SIDE], "x")
    second = send_steps(halves[SIDE:], "y")
    grad_out = send_blocks(grad_out.reshape(SIDE, SIDE, rows_here_count, inner), "z", 1)

    d_one = d_one.astype(F32) + d_one_peer.astype(F32)

    residual_in = tokens.astype(F32)
    scale_one = rms(residual_in)
    unit_one = residual_in * scale_one
    weighted = d_one * gain_one
    grad_input = d_middle + scale_one * (
        weighted - unit_one * jnp.mean(weighted * unit_one, axis=-1, keepdims=True)
    )

    mix_own = dot(combine, late_returned, TN)
    result_own, _ = together((own_half(middle) + mix_own).astype(BF), halves)
    output = side_by_side(result_own, swap(result_own), core_index)

    grad_out = sum(part.astype(F32) for part in grad_out).astype(BF)
    grad_out = [block_at(grad_out, (place[1] + step) % SIDE, 0) for step in range(SIDE)]
    w_here = lax.dynamic_slice_in_dim(w_parts, dp_index * rows_here_count, rows_here_count, axis=1)
    first, second, grad_input, output, w_here, grad_out = together(
        first, second, grad_input, output, w_here, grad_out
    )
    grad_out = sum(part.astype(F32) for part in send_steps(grad_out, "x"))
    parts = send_steps(sum_arrived(index, first, second, rows_here_count), "z")
    grad_qkv, small = finish(z_index, parts, w_here)
    grad_qkv = grad_qkv.transpose(1, 0, 2)
    small_peer = swap(small)
    gain_here = lax.dynamic_slice_in_dim(gain_one, dp_index * rows_here_count, rows_here_count, axis=0)
    grad_gain_one = (small[SIDE * EXTRA] + small_peer[SIDE * EXTRA])[:rows_here_count] / gain_here
    cut = lambda value: lax.dynamic_slice_in_dim(value, place[2] * rows_here_count, rows_here_count, axis=-1)
    grad_router = jnp.where(
        core_index == 0,
        jnp.concatenate([small[: SIDE * EXTRA], small_peer[: SIDE * EXTRA]], axis=0),
        jnp.concatenate([small_peer[: SIDE * EXTRA], small[: SIDE * EXTRA]], axis=0),
    )
    grad_router = cut(grad_router).T
    grad_gain_two = cut(small[SIDE * EXTRA + 1])
    grad_qk = small[SIDE * EXTRA + 2 : SIDE * EXTRA + 4] + small_peer[SIDE * EXTRA + 2 : SIDE * EXTRA + 4]

    return (
        output,
        grad_input,
        grad_gain_one,
        grad_qkv,
        grad_qk,
        grad_out,
        grad_gain_two,
        grad_router,
        grad_gate_up[None],
        grad_down[None],
    )


def solution(mesh):
    names = AXES + ("tensor",)
    torus = Mesh(mesh.devices.reshape(SIDE, SIDE, SIDE, 2), names)
    return jax.shard_map(
        on_device,
        mesh=torus,
        in_specs=(
            P(AXES, None),
            P(AXES, None),
            P(),
            P(),
            P(None, None, "tensor"),
            P(),
            P(None, "tensor"),
            P(),
            P(),
            P(AXES, None, None, "tensor"),
            P(AXES, "tensor", None),
            P(AXES, None),
        ),
        out_specs=(
            P(AXES, None),
            P(AXES, None),
            P(AXES),
            P(AXES, None, "tensor"),
            P(),
            P(AXES, "tensor"),
            P(AXES),
            P(AXES, None),
            P(AXES, None, None, "tensor"),
            P(AXES, "tensor", None),
        ),
        check_vma=False,
    )
```
